32 devices in a mesh: row: 8 (over y, x, core), col: 4 (over z).
Axes of the slice: x: 2, y: 2, z: 4, core: 2. Of those that a mesh axis runs over, the one named last changes fastest.
Arguments:
- tokens: bfloat16 [16384, 1024], P('row'), may hold values from -6 to 6
- w_qkv: bfloat16 [3, 1024, 1024], P(None, 'row', 'col'), may hold values from -0.1875 to 0.1875
- w_out: bfloat16 [1024, 1024], P('col', 'row'), may hold values from -6 to 6
- w_router: bfloat16 [1024, 32], P('row'), may hold values from -0.09375 to 0.09375
- ln_gains: bfloat16 [2, 1024], P(None, 'row'), may hold values from 0.099609375 to 1.8984375
- ln_biases: bfloat16 [2, 1024], P(None, 'row'), may hold values from -1 to 1
- w_in: bfloat16 [32, 1024, 4096], P('row', None, 'col'), may hold values from -0.1875 to 0.1875
- w_back: bfloat16 [32, 4096, 1024], P('row', 'col'), may hold values from -12 to 12
- expert_ids: int32 [16384, 1], P('row'), may hold values from 0 to 31; in each aligned block of 2048 rows (0 to 2047, 2048 to 4095, ...) at most 128 rows name the same one
- cotangent: bfloat16 [16384, 1024], P('row'), may hold values from -6 to 6
Outputs:
- mixed_out: bfloat16 [16384, 1024], P('row')
- grad_tokens: bfloat16 [16384, 1024], P('row')
- grad_qkv: float32 [3, 1024, 1024], P(None, 'row', 'col')
- grad_out: float32 [1024, 1024], P('col', 'row')
- grad_router: float32 [1024, 32], P('row')
- grad_gains: float32 [2, 1024], P(None, 'row')
- bias_attend: float32 [1024], P('row')
- bias_expert: float32 [1024], P('row')
- grad_in: float32 [32, 1024, 4096], P('row', None, 'col')
- grad_back: float32 [32, 4096, 1024], P('row', 'col')
The draws below stay inside these ranges and needn't reach their ends.
Inputs may be any that keep to these rules, and one draw needn't show every extreme that they name: `expert_ids`: among the 2048 tokens of one sequence (the rows of one index of row) no expert is named more than 128 times, a bound that some block reaches.
All inputs are finite; a program needn't handle non-finite values.
Results may differ from the reference program's by a relative error of at most 0.019.
Values may be sent and summed in bfloat16 or wider, within the bound.
No kernel may reach another device: no remote copies, remote signals or barrier semaphores. Data moves between devices by JAX's collectives and lax.ppermute only.
A program may use at most 320 MiB of HBM per device.

```python
import math
import jax
import jax.numpy as jnp
import numpy as np
from jax import lax

D = 1024
HEADS = 16
HEAD_DIM = 64
FF = 4096
SEQ_LEN = 2048
EXPERTS = 32
CAP = 128
TOKENS = 16384
N_ROW = 8


def shard_levels(own_key, extent, cuts, low, largest):
    level = 1.0
    for axis_at, shards_of in cuts:
        draws = jax.random.uniform(jax.random.fold_in(jax.random.fold_in(own_key, 6), axis_at), (shards_of,), jnp.float32, low / len(cuts), largest / len(cuts))
        level = level * jnp.repeat(jnp.exp(draws), extent[axis_at] // shards_of).reshape((-1,) + (1,) * (len(extent) - 1 - axis_at))
    return level


def deal_out(rng, own, number, rows, count, top, most, lean):
    ranking = jax.random.permutation(rng, count)
    crowded, ordinary = load_shares(count, rows * top, most, lean, True), load_shares(count, rows * top, most, lean, False)
    places = jnp.arange(count)

    def named(tallies, turn):
        used = int((tallies > 0).sum())
        fixed = max(1, used // 4)
        shifted = fixed + (places - fixed + turn * (used - fixed)) % max(1, count - fixed)
        return jnp.zeros((count,), jnp.int32).at[ranking[jnp.where(places < fixed, places, shifted)]].set(jnp.asarray(tallies, jnp.int32))

    tallies = jnp.where(number % 4 == 0, named(crowded, number // 4), named(ordinary, number - number // 4 - 1))
    mixed = jax.random.permutation(jax.random.fold_in(own, 3), count)
    donor, receiver = mixed[0:count // 2 * 2:2], mixed[1:count // 2 * 2:2]
    margin = jnp.minimum(tallies[donor] - 1, most - tallies[receiver]) // 2
    margin = jnp.where((donor == ranking[0]) | (receiver == ranking[0]) | (tallies[receiver] == 0), 0, jnp.maximum(margin, 0))
    shifted = jax.random.randint(jax.random.fold_in(own, 4), (count // 2,), 0, 1 << 20) % (margin + 1)
    tallies = tallies.at[donor].add(-shifted).at[receiver].add(shifted)
    items = jnp.searchsorted(jnp.cumsum(tallies), jnp.arange(rows * top), side="right").astype(jnp.int32)
    table = items.reshape(top, rows).T
    table = table[jax.random.permutation(jax.random.fold_in(own, 1), rows)]
    turn = jax.random.randint(jax.random.fold_in(own, 2), (rows, 1), 0, top)
    return jnp.take_along_axis(table, (jnp.arange(top)[None, :] + turn) % top, axis=1)


def load_shares(number_of, total, reach, lean, full):
    weights = [(1 << 20) // math.isqrt(grade ** lean) + 1 for grade in range(1, number_of + 1)]
    largest = reach if full else min(reach, max(-(-total // number_of), total * weights[0] // sum(weights)))
    least = 1 if total - largest >= number_of - 1 else 0
    given, rest = [largest] + [least] * (number_of - 1), total - largest - least * (number_of - 1)
    while rest > 0:
        free = [i for i in range(1, number_of) if given[i] < largest] or [i for i in range(1, number_of) if given[i] < reach]
        mass, left = sum([weights[i] for i in free]), rest
        for i in free:
            addition = min(reach - given[i], max(1, left * weights[i] // mass), rest)
            given[i] = given[i] + addition
            rest = rest - addition
    return np.array(given)


def bell_draw(stream_key, shape, deviation, bound, shards=(), kind=jnp.bfloat16):
    result = deviation * jax.random.normal(stream_key, shape, jnp.float32)
    if shards:
        result = result * shard_levels(stream_key, shape, shards, -0.22, 0.18)
    return jnp.clip(result, -bound, bound).astype(kind)


def setup_inputs(seed: int = 0) -> dict:
    key_list = jax.random.split(jax.random.key(seed), 11)
    tokens = bell_draw(key_list[0], (TOKENS, D), 1.0, 6.0, ((0, 8),))
    w_qkv = bell_draw(key_list[1], (3, D, D), D ** -0.5, 0.1875, ((1, 8), (2, 4)))
    w_out = bell_draw(key_list[2], (D, D), (max(1, 2 * D // SEQ_LEN)) ** -0.5, 6.0, ((0, 4), (1, 8)))
    w_router = bell_draw(key_list[3], (D, EXPERTS), (4 * D) ** -0.5, 0.09375, ((0, 8),))
    ln_gains = jnp.clip(1.0 + 0.18 * jax.random.normal(key_list[4], (2, D), jnp.float32), 0.099609375, 1.8984375).astype(jnp.bfloat16)
    ln_biases = bell_draw(key_list[5], (2, D), 0.2, 1.0, ((1, 8),))
    w_in = bell_draw(key_list[6], (EXPERTS, D, FF), D ** -0.5, 0.1875, ((0, 8), (2, 4)))
    w_back = bell_draw(key_list[7], (EXPERTS, FF, D), (max(1, EXPERTS // 16)), 12.0, ((0, 8), (1, 4)))
    expert_ids_keys = jax.random.split(jax.random.fold_in(key_list[8], 1), TOKENS // SEQ_LEN)
    expert_ids_turns = jax.random.permutation(jax.random.fold_in(key_list[8], 3), TOKENS // SEQ_LEN)
    expert_ids = jax.vmap(lambda own, number: deal_out(jax.random.fold_in(key_list[8], 2), own, number, SEQ_LEN, EXPERTS, 1, CAP, 2))(expert_ids_keys, expert_ids_turns).reshape((TOKENS, 1))
    cotangent = bell_draw(key_list[9], (TOKENS, D), 1.0, 6.0, ((0, 8),))
    return dict(tokens=tokens, w_qkv=w_qkv, w_out=w_out, w_router=w_router, ln_gains=ln_gains, ln_biases=ln_biases, w_in=w_in, w_back=w_back, expert_ids=expert_ids, cotangent=cotangent)


@jax.custom_vjp
def low(v):
    return lax.optimization_barrier(v.astype(jnp.bfloat16)).astype(jnp.float32)

@jax.custom_vjp
def low_back(v):
    return v

def low_keep(v):
    return (low(v), None)

def low_pass(kept, grad):
    return (grad,)

def back_keep(v):
    return (v, None)

def back_low(kept, grad):
    return (low(grad),)
low.defvjp(low_keep, low_pass)
low_back.defvjp(back_keep, back_low)
EPSILON = 1e-05
MASKED = -1e+30

def highest(left, right):
    return jnp.dot(left, right, precision=lax.Precision.HIGHEST)

def layer_norm(values, gain, bias):
    mean = lax.optimization_barrier(jnp.mean(values, axis=-1, keepdims=True))
    centered = values - mean
    variance = lax.optimization_barrier(jnp.mean(centered * centered, axis=-1, keepdims=True))
    return centered * lax.rsqrt(variance + EPSILON) * gain + bias

def attend(normed, w_qkv, w_out):
    length = normed.shape[0]
    block = min(512, length)
    head_scale = 1.0 / math.sqrt(HEAD_DIM)
    query = low_back(low(highest(normed, w_qkv[0]))).reshape(length, HEADS, HEAD_DIM)
    keys = low_back(low(highest(normed, w_qkv[1]))).reshape(length, HEADS, HEAD_DIM)
    values = low_back(low(highest(normed, w_qkv[2]))).reshape(length, HEADS, HEAD_DIM)

    def one_block(start):
        rows = lax.dynamic_slice_in_dim(query, start, block, 0)
        scores = jnp.einsum('qhd,khd->hqk', rows, keys, precision=lax.Precision.HIGHEST) * head_scale
        scores = low_back(scores)
        places = start + jnp.arange(block, dtype=jnp.int32)
        visible = jnp.arange(length, dtype=jnp.int32)[None, :] <= places[:, None]
        scores = jnp.where(visible[None], scores, MASKED)
        weights = low(jax.nn.softmax(scores, axis=-1))
        mixed = jnp.einsum('hqk,khd->qhd', weights, values, precision=lax.Precision.HIGHEST)
        return mixed.reshape(block, HEADS * HEAD_DIM)
    starts = jnp.arange(length // block, dtype=jnp.int32) * block
    context = lax.map(jax.checkpoint(one_block), starts).reshape(length, HEADS * HEAD_DIM)
    context = low_back(low(context))
    return low_back(highest(context, w_out))

def expert(operands):
    rows, w_first, w_second = operands
    hidden = low_back(highest(rows, w_first))
    active = low(jax.nn.gelu(hidden, approximate=True))
    return highest(active, w_second)

def reference(tokens, w_qkv, w_out, w_router, ln_gains, ln_biases, w_in, w_back, expert_ids, cotangent):
    chosen = expert_ids[:, 0].astype(jnp.int32)
    table = (chosen[:, None] == jnp.arange(EXPERTS, dtype=jnp.int32)[None, :]).astype(jnp.int32)
    per_seq = table.reshape(N_ROW, SEQ_LEN, EXPERTS)
    counted = jnp.cumsum(per_seq, axis=1).astype(jnp.int32)
    ranks = lax.optimization_barrier(jnp.sum((counted - 1) * per_seq, axis=2)).astype(jnp.int32).reshape(TOKENS)
    owners = jnp.arange(TOKENS, dtype=jnp.int32) // SEQ_LEN
    places = (chosen * (N_ROW * CAP) + owners * CAP + ranks).astype(jnp.int32)
    select = table.astype(jnp.float32)

    def forward(resid, qkv, proj, router, gains, biases, first, second):
        normed = low(layer_norm(resid, gains[0], biases[0]))

        def run_sequence(segment):
            return attend(segment, qkv, proj)
        attention = lax.map(jax.checkpoint(run_sequence), normed.reshape(N_ROW, SEQ_LEN, D)).reshape(TOKENS, D)
        middle = resid + attention
        routed = low(layer_norm(middle, gains[1], biases[1]))
        logits = low_back(highest(routed, router))
        probs = jax.nn.softmax(logits, axis=-1)
        gate = lax.optimization_barrier(jnp.sum(probs * select, axis=-1, keepdims=True))
        sent = low_back(routed)
        slots = jnp.zeros((EXPERTS * N_ROW * CAP, D), jnp.float32).at[places].set(sent)
        outputs = lax.map(jax.checkpoint(expert), (slots.reshape(EXPERTS, N_ROW * CAP, D), first, second))
        returned = low_back(low(jnp.take(outputs.reshape(EXPERTS * N_ROW * CAP, D), places, axis=0)))
        return middle + gate * returned
    output, pullback = jax.vjp(forward, tokens.astype(jnp.float32), w_qkv.astype(jnp.float32), w_out.astype(jnp.float32), w_router.astype(jnp.float32), ln_gains.astype(jnp.float32), ln_biases.astype(jnp.float32), w_in.astype(jnp.float32), w_back.astype(jnp.float32))
    grads = pullback(cotangent.astype(jnp.float32))
    return (output.astype(jnp.bfloat16), grads[0].astype(jnp.bfloat16), grads[1], grads[2], grads[3], grads[4], grads[5][0], grads[5][1], grads[6], grads[7])
```

```python
import functools, math
import jax, jax.numpy as jnp
from jax import lax
from jax.experimental import pallas as pl
from jax.experimental.pallas import tpu as pltpu
from jax.sharding import PartitionSpec as P

HEAD_DIM = 64
MASKED = -1e30
VMEM = 60 << 20


def params(*kinds):
    return pltpu.CompilerParams(dimension_semantics=kinds or None, vmem_limit_bytes=VMEM)


def dot(a, b, dims):
    return lax.dot_general(a, b, (dims, ((), ())), preferred_element_type=jnp.float32)

NN = ((1,), (0,))
NT = ((1,), (1,))
TN = ((0,), (0,))


def pack_body(base, step, slots_ref, rows_ref, out_ref):
    length = slots_ref.shape[1]
    first = base + pl.program_id(0) * step
    wanted = first + lax.broadcasted_iota(jnp.int32, (step, length), 0)
    chosen = jnp.where(slots_ref[...] == wanted, 1.0, 0.0).astype(jnp.bfloat16)
    out_ref[...] = dot(chosen, rows_ref[...], NN).astype(out_ref.dtype)


def pack(slots, rows, base, count):
    length, width = rows.shape
    step = min(512, count)
    return pl.pallas_call(
        functools.partial(pack_body, base, step),
        out_shape=jax.ShapeDtypeStruct((count, width), rows.dtype),
        grid=(count // step,),
        in_specs=[
            pl.BlockSpec((1, length), lambda i: (0, 0)),
            pl.BlockSpec((length, width), lambda i: (0, 0)),
        ],
        out_specs=pl.BlockSpec((step, width), lambda i: (i, 0)),
        compiler_params=params("arbitrary"),
        name="pack",
    )(slots.reshape(1, length), rows)


def unpack_body(slots_ref, rows_ref, out_ref):
    step = out_ref.shape[0]
    count = rows_ref.shape[0]
    held = lax.broadcasted_iota(jnp.int32, (step, count), 1)
    chosen = jnp.where(slots_ref[...] == held, 1.0, 0.0).astype(jnp.bfloat16)
    out_ref[...] = dot(chosen, rows_ref[...], NN).astype(out_ref.dtype)


def unpack(slots, rows):
    count, width = rows.shape
    length = slots.shape[0]
    step = min(256, length)
    return pl.pallas_call(
        unpack_body,
        out_shape=jax.ShapeDtypeStruct((length, width), rows.dtype),
        grid=(length // step,),
        in_specs=[
            pl.BlockSpec((step, 1), lambda i: (i, 0)),
            pl.BlockSpec((count, width), lambda i: (0, 0)),
        ],
        out_specs=pl.BlockSpec((step, width), lambda i: (i, 0)),
        compiler_params=params("arbitrary"),
        name="unpack",
    )(slots.reshape(length, 1), rows)


def forward_body(blocks, block, q_ref, k_ref, v_ref, o_ref, lse_ref):
    width = q_ref.shape[1]
    heads = width // HEAD_DIM
    lane = lax.broadcasted_iota(jnp.int32, (block, width), 1)
    hidden = lax.broadcasted_iota(jnp.int32, (block, block), 1) > lax.broadcasted_iota(
        jnp.int32, (block, block), 0
    )
    for at, i in enumerate(blocks):
        span = (i + 1) * block
        here = pl.ds(at * block, block)
        o_ref[here, :] = jnp.zeros((block, width), o_ref.dtype)

        def one_head(h, carry, here=here, span=span, i=i):
            mine = (lane >= h * HEAD_DIM) & (lane < (h + 1) * HEAD_DIM)
            query = q_ref[pl.ds(i * block, block), :].astype(jnp.float32) * 0.125
            query = jnp.where(mine, query, 0.0).astype(jnp.bfloat16)
            edge = jnp.where(hidden, MASKED, dot(query, k_ref[pl.ds(span - block, block), :], NT))
            peak = jnp.max(edge, axis=1, keepdims=True)
            if i:
                past = dot(query, k_ref[pl.ds(0, span - block), :], NT)
                peak = jnp.maximum(peak, jnp.max(past, axis=1, keepdims=True))
            edge = jnp.exp(edge - peak)
            total = jnp.sum(edge, axis=1, keepdims=True)
            if i:
                past = jnp.exp(past - peak)
                total = total + jnp.sum(past, axis=1, keepdims=True)
            share = 1.0 / total
            mixed = dot((edge * share).astype(jnp.bfloat16), v_ref[pl.ds(span - block, block), :], NN)
            if i:
                mixed = mixed + dot(
                    (past * share).astype(jnp.bfloat16), v_ref[pl.ds(0, span - block), :], NN
                )
            o_ref[here, :] = jnp.where(mine, mixed.astype(o_ref.dtype), o_ref[here, :])
            logsum = jnp.broadcast_to(peak + jnp.log(total), (block, 128))
            lse_ref[pl.ds(h, 1), here] = logsum.T[0:1, :]
            return carry

        lax.fori_loop(0, heads, one_head, 0)


def attend_forward(projected, blocks, block):
    length, triple = projected.shape
    width = triple // 3
    heads = width // HEAD_DIM
    rows = len(blocks) * block
    spec = [pl.BlockSpec((length, width), lambda i, j=j: (0, j)) for j in range(3)]
    return pl.pallas_call(
        functools.partial(forward_body, blocks, block),
        out_shape=(
            jax.ShapeDtypeStruct((rows, width), jnp.bfloat16),
            jax.ShapeDtypeStruct((heads, rows), jnp.float32),
        ),
        grid=(1,),
        in_specs=spec,
        out_specs=(
            pl.BlockSpec((rows, width), lambda i: (0, 0)),
            pl.BlockSpec((heads, rows), lambda i: (0, 0)),
        ),
        compiler_params=params("arbitrary"),
        name="attend_forward",
    )(projected, projected, projected)


def backward_body(
    block, q_ref, k_ref, v_ref, do_ref, o_ref, lse_ref, out_ref, dk_ref, dv_ref, p_ref, ds_ref, qm_ref, dom_ref
):
    length, width = q_ref.shape
    heads = width // HEAD_DIM
    count = length // block
    lane = lax.broadcasted_iota(jnp.int32, (block, width), 1)
    hidden = lax.broadcasted_iota(jnp.int32, (block, block), 0) > lax.broadcasted_iota(
        jnp.int32, (block, block), 1
    )
    for i in reversed(range(count)):
        span = (i + 1) * block
        here = pl.ds(i * block, block)

        def one_head(h, carry, here=here, span=span, i=i):
            mine = (lane >= h * HEAD_DIM) & (lane < (h + 1) * HEAD_DIM)
            query = q_ref[here, :].astype(jnp.float32) * 0.125
            query = jnp.where(mine, query, 0.0).astype(jnp.bfloat16)
            grad = jnp.where(mine, do_ref[here, :].astype(jnp.float32), 0.0)
            delta = jnp.sum(grad * o_ref[here, :].astype(jnp.float32), axis=1, keepdims=True)
            delta = jnp.broadcast_to(delta, (block, 128)).T[0:1, :]
            grad = grad.astype(jnp.bfloat16)
            logsum = lse_ref[pl.ds(h, 1), here]
            column = pl.ds(pl.multiple_of(h * block, block), block)
            qm_ref[column, :] = query
            dom_ref[column, :] = grad

            def part(rows, edge):
                scores = dot(k_ref[rows, :], query, NT)
                if edge:
                    scores = jnp.where(hidden, MASKED, scores)
                probs = jnp.exp(scores - logsum)
                p_ref[rows, column] = probs.astype(jnp.bfloat16)
                grad_probs = dot(v_ref[rows, :], grad, NT)
                ds_ref[rows, column] = (probs * (grad_probs - delta)).astype(jnp.bfloat16)

            if i:
                part(pl.ds(0, span - block), False)
            part(pl.ds(span - block, block), True)
            dq = dot(ds_ref[pl.ds(0, span), column], k_ref[pl.ds(0, span), :], TN)
            out_ref[here, pl.ds(0, width)] = jnp.where(
                mine, (dq * 0.125).astype(out_ref.dtype), out_ref[here, pl.ds(0, width)]
            )
            return carry

        lax.fori_loop(0, heads, one_head, 0)
        new_v = dot(p_ref[pl.ds(0, span), :], dom_ref[...], NN)
        new_k = dot(ds_ref[pl.ds(0, span), :], qm_ref[...], NN)
        if i == count - 1:
            dv_ref[...] = new_v
            dk_ref[...] = new_k
        else:
            dv_ref[pl.ds(0, span), :] += new_v
            dk_ref[pl.ds(0, span), :] += new_k
        out_ref[here, pl.ds(width, width)] = dk_ref[here, :].astype(out_ref.dtype)
        out_ref[here, pl.ds(2 * width, width)] = dv_ref[here, :].astype(out_ref.dtype)


def attend_backward(projected, grad_context, context, logsum, block):
    length, triple = projected.shape
    width = triple // 3
    heads = width // HEAD_DIM
    spec = [pl.BlockSpec((length, width), lambda i, j=j: (0, j)) for j in range(3)]
    whole = pl.BlockSpec((length, width), lambda i: (0, 0))
    return pl.pallas_call(
        functools.partial(backward_body, block),
        out_shape=jax.ShapeDtypeStruct((length, triple), jnp.bfloat16),
        grid=(1,),
        in_specs=spec + [whole, whole, pl.BlockSpec((heads, length), lambda i: (0, 0))],
        out_specs=pl.BlockSpec((length, triple), lambda i: (0, 0)),
        scratch_shapes=[
            pltpu.VMEM((length, width), jnp.float32),
            pltpu.VMEM((length, width), jnp.float32),
            pltpu.VMEM((length, heads * block), jnp.bfloat16),
            pltpu.VMEM((length, heads * block), jnp.bfloat16),
            pltpu.VMEM((heads * block, width), jnp.bfloat16),
            pltpu.VMEM((heads * block, width), jnp.bfloat16),
        ],
        compiler_params=params("arbitrary"),
        name="attend_backward",
    )(projected, projected, projected, grad_context, context, logsum)


ROOT = math.sqrt(2.0 / math.pi)
CUBE = 0.044715


def expert_body(given, x_ref, gy_ref, win_ref, wback_ref, *rest):
    out_ref, active_ref, slope_ref, *sent = rest[given:]
    rows, depth = x_ref.shape
    hidden = dot(x_ref[...], win_ref[...], NN)
    square = hidden * hidden
    bent = jnp.tanh(ROOT * hidden * (1.0 + CUBE * square))
    active = (0.5 * hidden * (1.0 + bent)).astype(jnp.bfloat16)
    slope = 0.5 * (1.0 + bent) + 0.5 * hidden * (1.0 - bent * bent) * (
        ROOT * (1.0 + 3.0 * CUBE * square)
    )
    active_ref[...] = active
    parts = out_ref.shape[0]
    wide = depth // parts
    made = dot(active, wback_ref[...], NN).astype(jnp.bfloat16)
    for j in range(parts):
        out_ref[j] = made[:, j * wide : (j + 1) * wide]
    grad_active = dot(gy_ref[...].reshape(rows, depth), wback_ref[...], NT)
    grad_hidden = (grad_active * slope).astype(jnp.bfloat16)
    slope_ref[...] = grad_hidden
    back = dot(grad_hidden, win_ref[...], NT).astype(jnp.bfloat16)
    wide = depth // len(sent)
    for j, ref in enumerate(sent):
        ref[...] = back[:, j * wide : (j + 1) * wide].reshape(ref.shape)


def expert_pass(e, x, grad_y, w_in, w_back, sent, parts, pieces):
    sources, local, cap, depth = grad_y.shape
    width = w_in.shape[2]
    rows = sources * cap
    step = min(256, rows)
    group = step // cap
    sent = list(sent or [])
    piece = jax.ShapeDtypeStruct((sources, local, cap, depth // pieces), jnp.bfloat16)
    piece_spec = pl.BlockSpec((group, None, cap, depth // pieces), lambda i: (i, e, 0, 0))
    made = pl.pallas_call(
        functools.partial(expert_body, len(sent)),
        out_shape=(
            jax.ShapeDtypeStruct((parts, rows, depth // parts), jnp.bfloat16),
            jax.ShapeDtypeStruct((rows, width), jnp.bfloat16),
            jax.ShapeDtypeStruct((rows, width), jnp.bfloat16),
        )
        + (piece,) * pieces,
        grid=(rows // step,),
        in_specs=[
            pl.BlockSpec((step, depth), lambda i: (i, 0)),
            pl.BlockSpec((group, None, cap, depth), lambda i: (i, e, 0, 0)),
            pl.BlockSpec((None, depth, width), lambda i: (e, 0, 0)),
            pl.BlockSpec((None, width, depth), lambda i: (e, 0, 0)),
        ]
        + [pl.BlockSpec(memory_space=pl.ANY)] * len(sent),
        out_specs=(
            pl.BlockSpec((parts, step, depth // parts), lambda i: (0, i, 0)),
            pl.BlockSpec((step, width), lambda i: (i, 0)),
            pl.BlockSpec((step, width), lambda i: (i, 0)),
        )
        + (piece_spec,) * pieces,
        input_output_aliases={4 + j: 3 + j for j in range(len(sent))},
        compiler_params=params("arbitrary"),
        name="expert_pass",
    )(x, grad_y, w_in, w_back, *sent)
    return made[0], made[1], made[2], made[3:]


def weight_body(given, x_ref, gy_ref, gate_ref, active_ref, slope_ref, *rest):
    gin_ref, gback_ref, xt_ref, gyg_ref = rest[given:]
    rows, depth = x_ref.shape

    @pl.when(pl.program_id(0) == 0)
    def _():
        gate = gate_ref[...]
        xt_ref[...] = (x_ref[...].astype(jnp.float32) * gate).T.astype(jnp.bfloat16)
        grad_y = gy_ref[...].reshape(rows, depth).astype(jnp.float32)
        gyg_ref[...] = (grad_y * gate).astype(jnp.bfloat16)

    gin_ref[...] = dot(xt_ref[...], slope_ref[...], NN)
    gback_ref[...] = dot(active_ref[...], gyg_ref[...], TN)


def weight_pass(e, x, grad_y, gate, active, slope, sent):
    sources, local, cap, depth = grad_y.shape
    rows, width = active.shape
    step = min(256, width)
    sent = list(sent or [])
    return pl.pallas_call(
        functools.partial(weight_body, len(sent)),
        out_shape=(
            jax.ShapeDtypeStruct((local, depth, width), jnp.float32),
            jax.ShapeDtypeStruct((local, width, depth), jnp.float32),
        ),
        grid=(width // step,),
        in_specs=[
            pl.BlockSpec((rows, depth), lambda i: (0, 0)),
            pl.BlockSpec((sources, None, cap, depth), lambda i: (0, e, 0, 0)),
            pl.BlockSpec((rows, 1), lambda i: (0, 0)),
            pl.BlockSpec((rows, step), lambda i: (0, i)),
            pl.BlockSpec((rows, step), lambda i: (0, i)),
        ]
        + [pl.BlockSpec(memory_space=pl.ANY)] * len(sent),
        out_specs=(
            pl.BlockSpec((None, depth, step), lambda i: (e, 0, i)),
            pl.BlockSpec((None, step, depth), lambda i: (e, i, 0)),
        ),
        scratch_shapes=[
            pltpu.VMEM((depth, rows), jnp.bfloat16),
            pltpu.VMEM((rows, depth), jnp.bfloat16),
        ],
        input_output_aliases={5 + j: j for j in range(len(sent))},
        compiler_params=params("arbitrary"),
        name="weight_pass",
    )(x, grad_y, gate, active, slope, *sent)


EPSILON = 1e-05


def layer_stats(values):
    mean = jnp.mean(values, axis=-1, keepdims=True)
    centered = values - mean
    variance = jnp.mean(centered * centered, axis=-1, keepdims=True)
    inverse = lax.rsqrt(variance + EPSILON)
    return (centered * inverse, inverse)


def norm_back(grad_normed, normed, inverse, gain):
    grad_hat = grad_normed * gain
    centred_grad = grad_hat - jnp.mean(grad_hat, axis=-1, keepdims=True)
    return inverse * (centred_grad - normed * jnp.mean(grad_hat * normed, axis=-1, keepdims=True))


def slot_layout(expert_ids, experts, cap):
    chosen = expert_ids[:, 0]
    length = chosen.shape[0]
    table = chosen[:, None] == jnp.arange(experts, dtype=jnp.int32)[None, :]
    order = jnp.arange(length, dtype=jnp.int32)
    before = (order[:, None] > order[None, :]).astype(jnp.bfloat16)
    counted = jnp.dot(before, table.astype(jnp.bfloat16), preferred_element_type=jnp.float32)
    ranks = jnp.sum(jnp.where(table, counted, 0.0), axis=1).astype(jnp.int32)
    return (chosen, ranks, table.astype(jnp.float32))


def per_device(
    tokens, w_qkv, w_out, w_router, ln_gains, ln_biases, w_in, w_back, expert_ids, cotangent
):
    rows_all, cols_all = lax.axis_size("row"), lax.axis_size("col")
    col = lax.axis_index("col")
    length, depth = tokens.shape
    share = depth // rows_all
    width = w_qkv.shape[2]
    experts = w_router.shape[1]
    local = w_in.shape[0]
    cap = 2 * length // experts
    block = min(256, length)
    blocks = length // block
    own_length = length // cols_all
    pieces = 4

    def own(values):
        return lax.dynamic_slice_in_dim(values, col * own_length, own_length, 0)

    first = jnp.concatenate(
        [w_qkv.transpose(1, 0, 2).reshape(share, 3 * width), ln_gains.T, ln_biases.T], axis=1
    )
    first = lax.all_gather(first, "row", axis=0, tiled=True)
    qkv_full = first[:, : 3 * width]
    norms = first[:, 3 * width :].astype(jnp.float32).T
    gains, biases = norms[0:2], norms[2:4]
    second = jnp.concatenate([w_out.T, w_router], axis=1)
    second = lax.all_gather(second, "row", axis=0, tiled=True)
    router_full = second[:, width:]
    out_own = second[:, :width]

    chosen, ranks, select = slot_layout(expert_ids, experts, cap)
    slots = chosen * cap + ranks
    slots_by_local = ((chosen % local) * rows_all + chosen // local) * cap + ranks

    grad_packed = pack(slots, cotangent, 0, experts * cap).reshape(rows_all, local, cap, depth)
    grad_arrived = lax.all_to_all(grad_packed, "row", split_axis=0, concat_axis=0, tiled=True)

    resid_in = tokens.astype(jnp.float32)
    normed_one, inverse_one = layer_stats(resid_in)
    normal_in = (normed_one * gains[0] + biases[0]).astype(jnp.bfloat16)
    projected = jnp.dot(normal_in, qkv_full, preferred_element_type=jnp.float32).astype(jnp.bfloat16)

    half = blocks // 2
    context_a, logsum_a = attend_forward(projected, tuple(range(half)), block)
    full_a = lax.all_gather(context_a, "col", axis=0)
    context_b, logsum_b = attend_forward(projected, tuple(range(half, blocks)), block)
    full_b = lax.all_gather(context_b, "col", axis=0)
    out_full = lax.all_gather(out_own, "col", axis=0)
    context = jnp.concatenate([context_a, context_b], axis=0)
    logsum = jnp.concatenate([logsum_a, logsum_b], axis=1)

    def project_out(full):
        return jnp.einsum("ztc,zdc->td", full, out_full, preferred_element_type=jnp.float32)

    middle = resid_in + jnp.concatenate([project_out(full_a), project_out(full_b)], axis=0)
    normed_two, inverse_two = layer_stats(middle)
    routed = (normed_two * gains[1] + biases[1]).astype(jnp.bfloat16)
    logits = jnp.dot(routed, router_full, preferred_element_type=jnp.float32)
    probs = jax.nn.softmax(logits, axis=-1)
    gate = jnp.sum(probs * select, axis=-1, keepdims=True)

    block_rows = rows_all * cap
    arrived, summed, active, slope = [], [], [], []
    sent = None
    for e in range(local):
        packed = pack(slots_by_local, routed, e * block_rows, block_rows)
        packed = packed.reshape(rows_all, cap, depth)
        moved = lax.all_to_all(packed, "row", split_axis=0, concat_axis=0, tiled=True)
        arrived.append(moved.reshape(block_rows, depth))
        made, kept, grads, sent = expert_pass(
            e, arrived[e], grad_arrived, w_in, w_back, sent, cols_all, pieces
        )
        active.append(kept)
        slope.append(grads)
        summed.append(lax.psum_scatter(made, "col", scatter_dimension=0, tiled=True))

    held = jnp.arange(experts * cap, dtype=jnp.int32)
    gate_packed = jnp.sum(jnp.where(held[:, None] == slots[None, :], gate[:, 0][None, :], 0.0), axis=1)
    gate_arrived = lax.all_to_all(
        gate_packed.reshape(rows_all, local * cap), "row", split_axis=0, concat_axis=0, tiled=True
    )
    gate_arrived = gate_arrived.reshape(rows_all, local, cap).transpose(1, 0, 2)

    homed = jnp.stack([s.reshape(rows_all, cap, depth // cols_all) for s in summed], axis=1)
    homed = lax.all_to_all(homed, "row", split_axis=0, concat_axis=0, tiled=True)
    returned = unpack(slots, homed.reshape(experts * cap, depth // cols_all)).astype(jnp.float32)

    grad_sent = []
    for piece in sent:
        back = lax.all_to_all(piece, "row", split_axis=0, concat_axis=0, tiled=True)
        back = unpack(slots, back.reshape(experts * cap, depth // pieces))
        grad_sent.append(lax.psum_scatter(back, "col", scatter_dimension=0, tiled=True))
    grad_sent = jnp.concatenate(grad_sent, axis=1).astype(jnp.float32) * own(gate)

    grad_weights = None
    for e in range(local):
        grad_weights = weight_pass(
            e,
            arrived[e],
            grad_arrived,
            gate_arrived[e].reshape(block_rows, 1),
            active[e],
            slope[e],
            grad_weights,
        )
    grad_in, grad_back = grad_weights

    columns = depth // cols_all

    def own_columns(values):
        return lax.dynamic_slice_in_dim(values, col * columns, columns, 1)

    mixed = (own_columns(middle) + gate * returned).astype(jnp.bfloat16)
    mixed_out = lax.all_gather(mixed, "col", axis=0).transpose(1, 0, 2).reshape(length, depth)
    grad_gate = lax.psum(
        jnp.sum(own_columns(cotangent).astype(jnp.float32) * returned, axis=-1), "col"
    )[:, None]
    grad_logits = (grad_gate * probs * (select - gate)).astype(jnp.bfloat16)
    grad_router = jnp.einsum("td,te->de", routed, grad_logits, preferred_element_type=jnp.float32)

    grad_y = own(cotangent).astype(jnp.float32)
    own_middle = own(middle)
    normed_own, inverse_own = layer_stats(own_middle)
    grad_routed = grad_sent + jnp.einsum(
        "te,de->td", own(grad_logits), router_full, preferred_element_type=jnp.float32
    )
    gain_two = jnp.sum(grad_routed * normed_own, axis=0)
    bias_two = jnp.sum(grad_routed, axis=0)
    grad_middle = grad_y + norm_back(grad_routed, normed_own, inverse_own, gains[1])
    grad_attn = grad_middle.astype(jnp.bfloat16)
    grad_context = jnp.einsum(
        "td,zdc->ztc", grad_attn, out_full, preferred_element_type=jnp.float32
    ).astype(jnp.bfloat16)
    grad_context = lax.all_to_all(grad_context, "col", split_axis=0, concat_axis=0, tiled=True)
    grad_context = grad_context.reshape(length, width)

    full = jnp.concatenate([full_a, full_b], axis=1)
    full_own = lax.dynamic_slice_in_dim(full, col * own_length, own_length, 1)
    grad_out = jnp.einsum("ztc,td->zcd", full_own, grad_attn, preferred_element_type=jnp.float32)
    grad_out = lax.psum_scatter(
        grad_out.astype(jnp.bfloat16), "col", scatter_dimension=0, tiled=False
    )

    grad_proj = attend_backward(projected, grad_context, context, logsum, block)
    grad_qkv = jnp.einsum("td,tc->dc", normal_in, grad_proj, preferred_element_type=jnp.float32)
    partial = jnp.einsum(
        "tc,dc->td", grad_proj, qkv_full, preferred_element_type=jnp.float32
    ).astype(jnp.bfloat16)
    grad_normal = lax.psum_scatter(partial, "col", scatter_dimension=0, tiled=True)
    grad_normal = grad_normal.astype(jnp.float32)
    own_normed, own_inverse = layer_stats(own(tokens).astype(jnp.float32))
    gain_one = jnp.sum(grad_normal * own_normed, axis=0)
    bias_one = jnp.sum(grad_normal, axis=0)
    grad_tokens = (grad_middle + norm_back(grad_normal, own_normed, own_inverse, gains[0])).astype(
        jnp.bfloat16
    )
    grad_tokens = lax.all_gather(grad_tokens, "col", axis=0, tiled=True)

    small = lax.psum(jnp.stack([gain_one, gain_two, bias_one, bias_two]), ("row", "col"))
    small = lax.dynamic_slice_in_dim(small, lax.axis_index("row") * share, share, 1)
    qkv_share = lax.psum_scatter(
        grad_qkv.astype(jnp.bfloat16), "row", scatter_dimension=0, tiled=True
    )
    qkv_share = qkv_share.astype(jnp.float32).reshape(share, 3, width).transpose(1, 0, 2)
    out_share = lax.psum_scatter(grad_out, "row", scatter_dimension=1, tiled=True)
    router_share = lax.psum_scatter(
        grad_router.astype(jnp.bfloat16), "row", scatter_dimension=0, tiled=True
    )
    return (
        mixed_out,
        grad_tokens,
        qkv_share,
        out_share.astype(jnp.float32),
        router_share.astype(jnp.float32),
        small[0:2],
        small[2],
        small[3],
        grad_in,
        grad_back,
    )


def solution(mesh):
    return jax.shard_map(
        per_device,
        mesh=mesh,
        in_specs=(
            P("row", None),
            P(None, "row", "col"),
            P("col", "row"),
            P("row", None),
            P(None, "row"),
            P(None, "row"),
            P("row", None, "col"),
            P("row", "col", None),
            P("row", None),
            P("row", None),
        ),
        out_specs=(
            P("row", None),
            P("row", None),
            P(None, "row", "col"),
            P("col", "row"),
            P("row", None),
            P(None, "row"),
            P("row"),
            P("row"),
            P("row", None, "col"),
            P("row", "col", None),
        ),
        check_vma=False,
    )
```

```python
import functools, math
import jax, jax.numpy as jnp
from jax import lax
from jax.experimental import pallas as pl
from jax.experimental.pallas import tpu as pltpu
from jax.sharding import PartitionSpec as P

HEAD_DIM = 64
MASKED = -1e30
VMEM = 60 << 20


def params(*kinds):
    return pltpu.CompilerParams(dimension_semantics=kinds or None, vmem_limit_bytes=VMEM)


def cost(flops, moved, special=0):
    return pl.CostEstimate(flops=flops, bytes_accessed=moved, transcendentals=special)


def dot(a, b, dims):
    return lax.dot_general(a, b, (dims, ((), ())), preferred_element_type=jnp.float32)

NN = ((1,), (0,))
NT = ((1,), (1,))
TN = ((0,), (0,))


def pack_body(base, step, each, given, slots_ref, rows_ref, *rest):
    outs = rest[given:]
    length = slots_ref.shape[1]
    at = pl.program_id(0)
    wanted = base + at * step + lax.broadcasted_iota(jnp.int32, (step, length), 0)
    chosen = jnp.where(slots_ref[...] == wanted, 1.0, 0.0).astype(jnp.bfloat16)
    made = dot(chosen, rows_ref[...], NN).astype(jnp.bfloat16)
    for j, out_ref in enumerate(outs):

        @pl.when(at // each == j)
        def _(out_ref=out_ref):
            out_ref[...] = made


def pack(slots, rows, base, count, outs, waits=()):
    length, width = rows.shape
    step = min(512, count)
    each = count // step
    return pl.pallas_call(
        functools.partial(pack_body, base, step, each, len(waits)),
        out_shape=(jax.ShapeDtypeStruct((count, width), rows.dtype),) * outs,
        grid=(each * outs,),
        in_specs=[
            pl.BlockSpec((1, length), lambda i: (0, 0)),
            pl.BlockSpec((length, width), lambda i: (0, 0)),
        ]
        + [pl.BlockSpec(memory_space=pl.ANY)] * len(waits),
        out_specs=tuple(
            pl.BlockSpec((step, width), lambda i, j=j: (jnp.clip(i - j * each, 0, each - 1), 0))
            for j in range(outs)
        ),
        compiler_params=params("arbitrary"),
        name="pack",
        cost_estimate=cost(2 * outs * count * length * width, 2 * (length + outs * count) * width),
    )(slots.reshape(1, length), rows, *waits)


def unpack_body(slots_ref, rows_ref, *rest):
    out_ref = rest[-1]
    step = out_ref.shape[0]
    count = rows_ref.shape[0]
    held = lax.broadcasted_iota(jnp.int32, (step, count), 1)
    chosen = jnp.where(slots_ref[...] == held, 1.0, 0.0).astype(jnp.bfloat16)
    out_ref[...] = dot(chosen, rows_ref[...], NN).astype(out_ref.dtype)


def unpack(slots, rows, waits=()):
    count, width = rows.shape
    length = slots.shape[0]
    step = min(256, length)
    return pl.pallas_call(
        unpack_body,
        out_shape=jax.ShapeDtypeStruct((length, width), rows.dtype),
        grid=(length // step,),
        in_specs=[
            pl.BlockSpec((step, 1), lambda i: (i, 0)),
            pl.BlockSpec((count, width), lambda i: (0, 0)),
        ]
        + [pl.BlockSpec(memory_space=pl.ANY)] * len(waits),
        out_specs=pl.BlockSpec((step, width), lambda i: (i, 0)),
        compiler_params=params("arbitrary"),
        name="unpack",
        cost_estimate=cost(2 * count * length * width, 2 * (length + count) * width),
    )(slots.reshape(length, 1), rows, *waits)


def forward_body(blocks, block, q_ref, k_ref, v_ref, *rest):
    o_ref, lse_ref = rest[-2:]
    width = q_ref.shape[1]
    heads = width // HEAD_DIM
    lane = lax.broadcasted_iota(jnp.int32, (block, width), 1)
    hidden = lax.broadcasted_iota(jnp.int32, (block, block), 1) > lax.broadcasted_iota(
        jnp.int32, (block, block), 0
    )
    for at, i in enumerate(blocks):
        span = (i + 1) * block
        here = pl.ds(at * block, block)
        o_ref[here, :] = jnp.zeros((block, width), o_ref.dtype)

        def one_head(h, carry, here=here, span=span, i=i):
            mine = (lane >= h * HEAD_DIM) & (lane < (h + 1) * HEAD_DIM)
            query = q_ref[pl.ds(i * block, block), :].astype(jnp.float32) * 0.125
            query = jnp.where(mine, query, 0.0).astype(jnp.bfloat16)
            edge = jnp.where(hidden, MASKED, dot(query, k_ref[pl.ds(span - block, block), :], NT))
            peak = jnp.max(edge, axis=1, keepdims=True)
            if i:
                past = dot(query, k_ref[pl.ds(0, span - block), :], NT)
                peak = jnp.maximum(peak, jnp.max(past, axis=1, keepdims=True))
            edge = jnp.exp(edge - peak)
            total = jnp.sum(edge, axis=1, keepdims=True)
            if i:
                past = jnp.exp(past - peak)
                total = total + jnp.sum(past, axis=1, keepdims=True)
            share = 1.0 / total
            mixed = dot((edge * share).astype(jnp.bfloat16), v_ref[pl.ds(span - block, block), :], NN)
            if i:
                mixed = mixed + dot(
                    (past * share).astype(jnp.bfloat16), v_ref[pl.ds(0, span - block), :], NN
                )
            o_ref[here, :] = jnp.where(mine, mixed.astype(o_ref.dtype), o_ref[here, :])
            logsum = jnp.broadcast_to(peak + jnp.log(total), (block, 128))
            lse_ref[pl.ds(h, 1), here] = logsum.T[0:1, :]
            return carry

        lax.fori_loop(0, heads, one_head, 0)


def attend_forward(projected, blocks, block, waits=()):
    length, triple = projected.shape
    width = triple // 3
    heads = width // HEAD_DIM
    rows = len(blocks) * block
    spec = [pl.BlockSpec((length, width), lambda i, j=j: (0, j)) for j in range(3)]
    return pl.pallas_call(
        functools.partial(forward_body, blocks, block),
        out_shape=(
            jax.ShapeDtypeStruct((rows, width), jnp.bfloat16),
            jax.ShapeDtypeStruct((heads, rows), jnp.float32),
        ),
        grid=(1,),
        in_specs=spec + [pl.BlockSpec(memory_space=pl.ANY)] * len(waits),
        out_specs=(
            pl.BlockSpec((rows, width), lambda i: (0, 0)),
            pl.BlockSpec((heads, rows), lambda i: (0, 0)),
        ),
        compiler_params=params("arbitrary"),
        name="attend_forward",
        cost_estimate=cost(8 * rows * length * width, 8 * length * width, rows * length * heads),
    )(projected, projected, projected, *waits)


def backward_body(block, q_ref, k_ref, v_ref, do_ref, o_ref, lse_ref, *rest):
    out_ref, dk_ref, dv_ref, p_ref, ds_ref, qm_ref, dom_ref = rest[-7:]
    length, width = q_ref.shape
    heads = width // HEAD_DIM
    count = length // block
    lane = lax.broadcasted_iota(jnp.int32, (block, width), 1)
    hidden = lax.broadcasted_iota(jnp.int32, (block, block), 0) > lax.broadcasted_iota(
        jnp.int32, (block, block), 1
    )
    for i in reversed(range(count)):
        span = (i + 1) * block
        here = pl.ds(i * block, block)

        def one_head(h, carry, here=here, span=span, i=i):
            mine = (lane >= h * HEAD_DIM) & (lane < (h + 1) * HEAD_DIM)
            query = q_ref[here, :].astype(jnp.float32) * 0.125
            query = jnp.where(mine, query, 0.0).astype(jnp.bfloat16)
            grad = jnp.where(mine, do_ref[here, :].astype(jnp.float32), 0.0)
            delta = jnp.sum(grad * o_ref[here, :].astype(jnp.float32), axis=1, keepdims=True)
            delta = jnp.broadcast_to(delta, (block, 128)).T[0:1, :]
            grad = grad.astype(jnp.bfloat16)
            logsum = lse_ref[pl.ds(h, 1), here]
            column = pl.ds(pl.multiple_of(h * block, block), block)
            qm_ref[column, :] = query
            dom_ref[column, :] = grad

            def part(rows, edge):
                scores = dot(k_ref[rows, :], query, NT)
                if edge:
                    scores = jnp.where(hidden, MASKED, scores)
                probs = jnp.exp(scores - logsum)
                p_ref[rows, column] = probs.astype(jnp.bfloat16)
                grad_probs = dot(v_ref[rows, :], grad, NT)
                ds_ref[rows, column] = (probs * (grad_probs - delta)).astype(jnp.bfloat16)

            if i:
                part(pl.ds(0, span - block), False)
            part(pl.ds(span - block, block), True)
            dq = dot(ds_ref[pl.ds(0, span), column], k_ref[pl.ds(0, span), :], TN)
            out_ref[here, pl.ds(0, width)] = jnp.where(
                mine, (dq * 0.125).astype(out_ref.dtype), out_ref[here, pl.ds(0, width)]
            )
            return carry

        lax.fori_loop(0, heads, one_head, 0)
        new_v = dot(p_ref[pl.ds(0, span), :], dom_ref[...], NN)
        new_k = dot(ds_ref[pl.ds(0, span), :], qm_ref[...], NN)
        if i == count - 1:
            dv_ref[...] = new_v
            dk_ref[...] = new_k
        else:
            dv_ref[pl.ds(0, span), :] += new_v
            dk_ref[pl.ds(0, span), :] += new_k
        out_ref[here, pl.ds(width, width)] = dk_ref[here, :].astype(out_ref.dtype)
        out_ref[here, pl.ds(2 * width, width)] = dv_ref[here, :].astype(out_ref.dtype)


def attend_backward(projected, grad_context, context, logsum, block, waits=()):
    length, triple = projected.shape
    width = triple // 3
    heads = width // HEAD_DIM
    spec = [pl.BlockSpec((length, width), lambda i, j=j: (0, j)) for j in range(3)]
    whole = pl.BlockSpec((length, width), lambda i: (0, 0))
    return pl.pallas_call(
        functools.partial(backward_body, block),
        out_shape=jax.ShapeDtypeStruct((length, triple), jnp.bfloat16),
        grid=(1,),
        in_specs=spec + [whole, whole, pl.BlockSpec((heads, length), lambda i: (0, 0))]
        + [pl.BlockSpec(memory_space=pl.ANY)] * len(waits),
        out_specs=pl.BlockSpec((length, triple), lambda i: (0, 0)),
        scratch_shapes=[
            pltpu.VMEM((length, width), jnp.float32),
            pltpu.VMEM((length, width), jnp.float32),
            pltpu.VMEM((length, heads * block), jnp.bfloat16),
            pltpu.VMEM((length, heads * block), jnp.bfloat16),
            pltpu.VMEM((heads * block, width), jnp.bfloat16),
            pltpu.VMEM((heads * block, width), jnp.bfloat16),
        ],
        compiler_params=params("arbitrary"),
        name="attend_backward",
        cost_estimate=cost(20 * length * length * width, 16 * length * width, length * length * heads),
    )(projected, projected, projected, grad_context, context, logsum, *waits)


ROOT = math.sqrt(2.0 / math.pi)
CUBE = 0.044715


def expert_body(given, x_ref, gy_ref, win_ref, wback_ref, *rest):
    out_ref, active_ref, slope_ref, *sent = rest[given:]
    rows, depth = x_ref.shape
    hidden = dot(x_ref[...], win_ref[...], NN)
    square = hidden * hidden
    bent = jnp.tanh(ROOT * hidden * (1.0 + CUBE * square))
    active = (0.5 * hidden * (1.0 + bent)).astype(jnp.bfloat16)
    slope = 0.5 * (1.0 + bent) + 0.5 * hidden * (1.0 - bent * bent) * (
        ROOT * (1.0 + 3.0 * CUBE * square)
    )
    active_ref[...] = active
    parts = out_ref.shape[0]
    wide = depth // parts
    made = dot(active, wback_ref[...], NN).astype(jnp.bfloat16)
    for j in range(parts):
        out_ref[j] = made[:, j * wide : (j + 1) * wide]
    grad_active = dot(gy_ref[...], wback_ref[...], NT)
    grad_hidden = (grad_active * slope).astype(jnp.bfloat16)
    slope_ref[...] = grad_hidden
    back = dot(grad_hidden, win_ref[...], NT).astype(jnp.bfloat16)
    wide = depth // len(sent)
    for j, ref in enumerate(sent):
        ref[...] = back[:, j * wide : (j + 1) * wide].reshape(ref.shape)


def expert_pass(e, cap, x, grad_y, w_in, w_back, sent, parts, pieces, waits=()):
    rows, depth = x.shape
    local, _, width = w_in.shape
    sources = rows // cap
    step = min(256, rows)
    group = step // cap
    sent = list(sent or [])
    piece = jax.ShapeDtypeStruct((sources, local, cap, depth // pieces), jnp.bfloat16)
    piece_spec = pl.BlockSpec((group, None, cap, depth // pieces), lambda i: (i, e, 0, 0))
    made = pl.pallas_call(
        functools.partial(expert_body, len(sent) + len(waits)),
        out_shape=(
            jax.ShapeDtypeStruct((parts, rows, depth // parts), jnp.bfloat16),
            jax.ShapeDtypeStruct((rows, width), jnp.bfloat16),
            jax.ShapeDtypeStruct((rows, width), jnp.bfloat16),
        )
        + (piece,) * pieces,
        grid=(rows // step,),
        in_specs=[
            pl.BlockSpec((step, depth), lambda i: (i, 0)),
            pl.BlockSpec((step, depth), lambda i: (i, 0)),
            pl.BlockSpec((None, depth, width), lambda i: (e, 0, 0)),
            pl.BlockSpec((None, width, depth), lambda i: (e, 0, 0)),
        ]
        + [pl.BlockSpec(memory_space=pl.ANY)] * (len(sent) + len(waits)),
        out_specs=(
            pl.BlockSpec((parts, step, depth // parts), lambda i: (0, i, 0)),
            pl.BlockSpec((step, width), lambda i: (i, 0)),
            pl.BlockSpec((step, width), lambda i: (i, 0)),
        )
        + (piece_spec,) * pieces,
        input_output_aliases={4 + j: 3 + j for j in range(len(sent))},
        compiler_params=params("arbitrary"),
        name="expert_pass",
        cost_estimate=cost(8 * rows * depth * width, 4 * width * depth + 12 * rows * depth, rows * width),
    )(x, grad_y, w_in, w_back, *sent, *waits)
    return made[0], made[1], made[2], made[3:]


def weight_body(given, x_ref, gy_ref, gate_ref, active_ref, slope_ref, *rest):
    gin_ref, gback_ref, token_ref, xt_ref, gyg_ref = rest[given:]
    token_ref[...] = jnp.zeros_like(token_ref)
    rows, depth = x_ref.shape

    @pl.when(pl.program_id(0) == 0)
    def _():
        gate = gate_ref[...]
        xt_ref[...] = (x_ref[...].astype(jnp.float32) * gate).T.astype(jnp.bfloat16)
        gyg_ref[...] = (gy_ref[...].astype(jnp.float32) * gate).astype(jnp.bfloat16)

    gin_ref[...] = dot(xt_ref[...], slope_ref[...], NN)
    gback_ref[...] = dot(active_ref[...], gyg_ref[...], TN)


def weight_pass(e, local, x, grad_y, gate, active, slope, sent, waits=()):
    rows, width = active.shape
    depth = x.shape[1]
    step = min(256, width)
    sent = list(sent or [])
    return pl.pallas_call(
        functools.partial(weight_body, len(sent) + len(waits)),
        out_shape=(
            jax.ShapeDtypeStruct((local, depth, width), jnp.float32),
            jax.ShapeDtypeStruct((local, width, depth), jnp.float32),
            jax.ShapeDtypeStruct((8, 128), jnp.float32),
        ),
        grid=(width // step,),
        in_specs=[
            pl.BlockSpec((rows, depth), lambda i: (0, 0)),
            pl.BlockSpec((rows, depth), lambda i: (0, 0)),
            pl.BlockSpec((rows, 1), lambda i: (0, 0)),
            pl.BlockSpec((rows, step), lambda i: (0, i)),
            pl.BlockSpec((rows, step), lambda i: (0, i)),
        ]
        + [pl.BlockSpec(memory_space=pl.ANY)] * (len(sent) + len(waits)),
        out_specs=(
            pl.BlockSpec((None, depth, step), lambda i: (e, 0, i)),
            pl.BlockSpec((None, step, depth), lambda i: (e, i, 0)),
            pl.BlockSpec((8, 128), lambda i: (0, 0)),
        ),
        scratch_shapes=[
            pltpu.VMEM((depth, rows), jnp.bfloat16),
            pltpu.VMEM((rows, depth), jnp.bfloat16),
        ],
        input_output_aliases={5 + j: j for j in range(len(sent))},
        compiler_params=params("arbitrary"),
        name="weight_pass",
        cost_estimate=cost(4 * rows * depth * width, 8 * width * depth + 8 * rows * depth),
    )(x, grad_y, gate, active, slope, *sent, *waits)


EPSILON = 1e-05


def swap(blocks, axis):
    return lax.all_to_all(blocks, axis, split_axis=0, concat_axis=0, tiled=True)


def tie(*values):
    return lax.optimization_barrier(values)


def relay_steps(shard, axis):
    count = lax.axis_size(axis)
    right = left = shard
    steps = []
    for _ in range(count - 1):
        right = lax.ppermute(right, axis, [(i, i + 1) for i in range(count - 1)])
        left = lax.ppermute(left, axis, [(i + 1, i) for i in range(count - 1)])
        steps.append((right, left))
    return steps


def relay_join(shard, steps, axis, dim):
    count = lax.axis_size(axis)
    me = lax.axis_index(axis)
    size = shard.shape[dim]
    shape = list(shard.shape)
    shape[dim] = size * count
    whole = jnp.zeros(shape, shard.dtype)
    for k in range(count):
        piece = shard if k == 0 else steps[k - 1][0] + steps[count - k - 1][1]
        whole = lax.dynamic_update_slice_in_dim(whole, piece, ((me - k) % count) * size, dim)
    return whole


def layer_stats(values):
    mean = jnp.mean(values, axis=-1, keepdims=True)
    centered = values - mean
    variance = jnp.mean(centered * centered, axis=-1, keepdims=True)
    inverse = lax.rsqrt(variance + EPSILON)
    return (centered * inverse, inverse)


def norm_back(grad_normed, normed, inverse, gain):
    grad_hat = grad_normed * gain
    centred_grad = grad_hat - jnp.mean(grad_hat, axis=-1, keepdims=True)
    return inverse * (centred_grad - normed * jnp.mean(grad_hat * normed, axis=-1, keepdims=True))


def slot_layout(expert_ids, experts, cap):
    chosen = expert_ids[:, 0]
    length = chosen.shape[0]
    table = chosen[:, None] == jnp.arange(experts, dtype=jnp.int32)[None, :]
    order = jnp.arange(length, dtype=jnp.int32)
    before = (order[:, None] > order[None, :]).astype(jnp.bfloat16)
    counted = jnp.dot(before, table.astype(jnp.bfloat16), preferred_element_type=jnp.float32)
    ranks = jnp.sum(jnp.where(table, counted, 0.0), axis=1).astype(jnp.int32)
    return (chosen, ranks, table.astype(jnp.float32))


def per_device(
    tokens, w_qkv, w_out, w_router, ln_gains, ln_biases, w_in, w_back, expert_ids, cotangent
):
    rows_all, cols_all = lax.axis_size("row"), lax.axis_size("col")
    col = lax.axis_index("col")
    length, depth = tokens.shape
    share = depth // rows_all
    width = w_qkv.shape[2]
    experts = w_router.shape[1]
    local = w_in.shape[0]
    cap = 2 * length // experts
    block = min(256, length)
    blocks = length // block
    own_length = length // cols_all
    pieces = 4

    def own(values):
        return lax.dynamic_slice_in_dim(values, col * own_length, own_length, 0)

    stacked = w_qkv.transpose(1, 0, 2).reshape(share, 3 * width)
    weights = jnp.concatenate([stacked, w_router, ln_gains.T, ln_biases.T], axis=1)
    weights = lax.all_gather(weights, "row", axis=0, tiled=True)
    out_block = swap(jnp.broadcast_to(w_out.T[None], (cols_all, share, width)), "col")

    chosen, ranks, select = slot_layout(expert_ids, experts, cap)
    slots = chosen * cap + ranks
    slots_by_local = ((chosen % local) * rows_all + chosen // local) * cap + ranks
    block_rows = rows_all * cap

    def send(packed):
        return swap(packed.reshape(rows_all, cap, depth), "row").reshape(block_rows, depth)

    grad_packed = list(pack(slots_by_local, cotangent, 0, block_rows, local))
    weights, grad_packed[0] = tie(weights, grad_packed[0])
    grad_arrived = [send(grad_packed[0])]
    qkv_full = weights[:, : 3 * width]
    router_full = weights[:, 3 * width : 3 * width + experts]
    norms = weights[:, 3 * width + experts :].astype(jnp.float32).T
    gains, biases = norms[0:2], norms[2:4]

    resid_in = tokens.astype(jnp.float32)
    normed_one, inverse_one = layer_stats(resid_in)
    normal_in = (normed_one * gains[0] + biases[0]).astype(jnp.bfloat16)
    projected = jnp.dot(normal_in, qkv_full, preferred_element_type=jnp.float32).astype(jnp.bfloat16)

    half = blocks // 2
    context_a, logsum_a = attend_forward(projected, tuple(range(half)), block)
    context_a, grad_arrived[0], grad_packed[1] = tie(context_a, grad_arrived[0], grad_packed[1])
    grad_arrived.append(send(grad_packed[1]))
    full_a = lax.all_gather(context_a, "col", axis=0)
    context_b, logsum_b = attend_forward(
        projected, tuple(range(half, blocks)), block, [context_a]
    )
    context_b, out_block, grad_arrived[1], *grad_packed[2:] = tie(
        context_b, out_block, grad_arrived[1], *grad_packed[2:]
    )
    full_b = lax.all_gather(context_b, "col", axis=0)
    out_full = swap(jnp.broadcast_to(out_block[None], (rows_all, *out_block.shape)), "row")
    if local > 2:
        grad_packed[2], out_full = tie(grad_packed[2], out_full)
    out_full = out_full.transpose(1, 0, 2, 3).reshape(cols_all, depth, width)
    for e in range(2, local):
        grad_arrived.append(send(grad_packed[e]))
        if e + 1 < local:
            full_b, grad_arrived[e], grad_packed[e + 1] = tie(
                full_b, grad_arrived[e], grad_packed[e + 1]
            )
    context = jnp.concatenate([context_a, context_b], axis=0)
    logsum = jnp.concatenate([logsum_a, logsum_b], axis=1)

    def project_out(full):
        return jnp.einsum("ztc,zdc->td", full, out_full, preferred_element_type=jnp.float32)

    middle = resid_in + jnp.concatenate([project_out(full_a), project_out(full_b)], axis=0)
    normed_two, inverse_two = layer_stats(middle)
    routed = (normed_two * gains[1] + biases[1]).astype(jnp.bfloat16)
    logits = jnp.dot(routed, router_full, preferred_element_type=jnp.float32)
    probs = jax.nn.softmax(logits, axis=-1)
    gate = jnp.sum(probs * select, axis=-1, keepdims=True)

    packed = list(pack(slots_by_local, routed, 0, block_rows, 1))
    if local > 1:
        packed += pack(slots_by_local, routed, block_rows, block_rows, local - 1)
    packed[0], grad_arrived[-1] = tie(packed[0], grad_arrived[-1])
    held = jnp.arange(experts * cap, dtype=jnp.int32)
    gates = jnp.sum(jnp.where(held[:, None] == slots[None, :], gate[:, 0][None, :], 0.0), axis=1)
    gates = gates.reshape(rows_all, local * cap)
    arrived, summed, active, slope = [], [], [], []
    sent = None
    for e in range(local):
        arrived.append(send(packed[e]))
        after = gates if e + 1 == local else packed[e + 1]
        after, arrived[e] = tie(after, arrived[e])
        if e:
            after, summed[e - 1] = tie(after, summed[e - 1])
            summed[e - 1] = lax.psum_scatter(
                summed[e - 1], "col", scatter_dimension=0, tiled=True
            )
        if e + 1 == local:
            gates = after
        else:
            packed[e + 1] = after
        made, kept, grads, sent = expert_pass(
            e,
            cap,
            arrived[e],
            grad_arrived[e],
            w_in,
            w_back,
            sent,
            cols_all,
            pieces,
            packed[-1:] if e == 0 else summed[e - 3 : e - 2] if e > 2 else [],
        )
        active.append(kept)
        slope.append(grads)
        summed.append(made)
    summed[-1] = lax.psum_scatter(summed[-1], "col", scatter_dimension=0, tiled=True)
    gates = swap(gates, "row")
    gates, *sent = tie(gates, *sent)
    gates = gates.reshape(rows_all, local, cap).transpose(1, 0, 2)

    backs = []
    grad_weights = None
    waits = slope[-1:]
    for e in range(max(local, pieces)):
        if e < local:
            *grad_weights, token = weight_pass(
                e,
                local,
                arrived[e],
                grad_arrived[e],
                gates[e].reshape(block_rows, 1),
                active[e],
                slope[e],
                grad_weights,
                waits + (summed[e - 3 : e - 2] if e < 2 else []),
            )
        if e < pieces:
            back = swap(sent[e], "row")
            if e + 1 < pieces:
                sent[e + 1], back, token, *done = tie(sent[e + 1], back, token, *backs[e - 1 :])
                backs[e - 1 :] = done
            backs.append(unpack(slots, back.reshape(experts * cap, depth // pieces), [token]))
            waits = backs[-1:]
    grad_in, grad_back = grad_weights
    grad_sent = []
    for at in range(0, pieces, 2):
        pair = jnp.concatenate(backs[at : at + 2], axis=1)
        grad_sent.append(lax.psum_scatter(pair, "col", scatter_dimension=0, tiled=True))
    grad_sent = jnp.concatenate(grad_sent, axis=1).astype(jnp.float32) * own(gate)

    homed = jnp.stack([s.reshape(rows_all, cap, depth // cols_all) for s in summed], axis=1)
    homed = swap(homed, "row")
    returned = unpack(slots, homed.reshape(experts * cap, depth // cols_all)).astype(jnp.float32)

    columns = depth // cols_all

    def own_columns(values):
        return lax.dynamic_slice_in_dim(values, col * columns, columns, 1)

    mixed = (own_columns(middle) + gate * returned).astype(jnp.bfloat16)
    steps = relay_steps(mixed, "col")
    grad_gate = lax.psum(
        jnp.sum(own_columns(cotangent).astype(jnp.float32) * returned, axis=-1), "col"
    )[:, None]
    grad_logits = (grad_gate * probs * (select - gate)).astype(jnp.bfloat16)
    grad_router = jnp.einsum("td,te->de", routed, grad_logits, preferred_element_type=jnp.float32)

    grad_y = own(cotangent).astype(jnp.float32)
    if steps:
        grad_sent, *first = tie(grad_sent, *steps[0])
        steps[0] = tuple(first)
    own_middle = own(middle)
    normed_own, inverse_own = layer_stats(own_middle)
    grad_routed = grad_sent + jnp.einsum(
        "te,de->td", own(grad_logits), router_full, preferred_element_type=jnp.float32
    )
    gain_two = jnp.sum(grad_routed * normed_own, axis=0)
    bias_two = jnp.sum(grad_routed, axis=0)
    grad_middle = grad_y + norm_back(grad_routed, normed_own, inverse_own, gains[1])
    grad_attn = grad_middle.astype(jnp.bfloat16)
    grad_context = jnp.einsum(
        "td,zdc->ztc", grad_attn, out_full, preferred_element_type=jnp.float32
    ).astype(jnp.bfloat16)
    grad_context = swap(grad_context, "col").reshape(length, width)

    full = jnp.concatenate([full_a, full_b], axis=1)
    full_own = lax.dynamic_slice_in_dim(full, col * own_length, own_length, 1)
    grad_out = jnp.einsum("td,ztc->dzc", grad_attn, full_own, preferred_element_type=jnp.float32)
    plane = jnp.concatenate([grad_out.reshape(depth, cols_all * width), grad_router], axis=1)
    plane = swap(plane.astype(jnp.bfloat16).reshape(rows_all, share, -1), "row")
    grad_proj = attend_backward(projected, grad_context, context, logsum, block)
    grad_proj, plane = tie(grad_proj, plane)
    plane = jnp.sum(plane.astype(jnp.float32), axis=0)
    router_share = plane[:, cols_all * width :]
    out_share = plane[:, : cols_all * width].reshape(share, cols_all, width).transpose(1, 0, 2)
    out_share = swap(out_share.astype(jnp.bfloat16), "col").astype(jnp.float32)
    out_share = jnp.sum(out_share, axis=0).T
    if len(steps) > 1:
        grad_proj, *second = tie(grad_proj, *steps[1])
        steps[1] = tuple(second)
    grad_qkv = jnp.einsum("td,tc->dc", normal_in, grad_proj, preferred_element_type=jnp.float32)
    partial = jnp.einsum(
        "tc,dc->td", grad_proj, qkv_full, preferred_element_type=jnp.float32
    ).astype(jnp.bfloat16)
    grad_normal = lax.psum_scatter(partial, "col", scatter_dimension=0, tiled=True)
    mixed_out = relay_join(mixed, steps, "col", 1)
    grad_normal, mixed_out, router_share, out_share = tie(
        grad_normal, mixed_out, router_share, out_share
    )
    grad_normal = grad_normal.astype(jnp.float32)
    own_normed, own_inverse = layer_stats(own(tokens).astype(jnp.float32))
    gain_one = jnp.sum(grad_normal * own_normed, axis=0)
    bias_one = jnp.sum(grad_normal, axis=0)
    grad_tokens = (grad_middle + norm_back(grad_normal, own_normed, own_inverse, gains[0])).astype(
        jnp.bfloat16
    )
    grad_tokens = lax.all_gather(grad_tokens, "col", axis=0, tiled=True)

    qkv_share = swap(grad_qkv.astype(jnp.bfloat16).reshape(rows_all, share, -1), "row")
    qkv_share = jnp.sum(qkv_share.astype(jnp.float32), axis=0)
    qkv_share = qkv_share.reshape(share, 3, width).transpose(1, 0, 2)
    small = lax.psum(jnp.stack([gain_one, gain_two, bias_one, bias_two]), ("row", "col"))
    small = lax.dynamic_slice_in_dim(small, lax.axis_index("row") * share, share, 1)
    return (
        mixed_out,
        grad_tokens,
        qkv_share,
        out_share,
        router_share,
        small[0:2],
        small[2],
        small[3],
        grad_in,
        grad_back,
    )


def solution(mesh):
    return jax.shard_map(
        per_device,
        mesh=mesh,
        in_specs=(
            P("row", None),
            P(None, "row", "col"),
            P("col", "row"),
            P("row", None),
            P(None, "row"),
            P(None, "row"),
            P("row", None, "col"),
            P("row", "col", None),
            P("row", None),
            P("row", None),
        ),
        out_specs=(
            P("row", None),
            P("row", None),
            P(None, "row", "col"),
            P("col", "row"),
            P("row", None),
            P(None, "row"),
            P("row"),
            P("row"),
            P("row", None, "col"),
            P("row", "col", None),
        ),
        check_vma=False,
    )
```

```python
import functools, math
import jax, jax.numpy as jnp
from jax import lax
from jax.experimental import pallas as pl
from jax.experimental.pallas import tpu as pltpu
from jax.sharding import PartitionSpec as P

HEAD_DIM = 64
EPSILON = 1e-05
MASKED = -1e30
VMEM = 60 << 20


def params(*kinds):
    return pltpu.CompilerParams(dimension_semantics=kinds or None, vmem_limit_bytes=VMEM)


def cost(flops, moved, special=0):
    return pl.CostEstimate(flops=flops, bytes_accessed=moved, transcendentals=special)


def dot(a, b, dims):
    return lax.dot_general(a, b, (dims, ((), ())), preferred_element_type=jnp.float32)

NN = ((1,), (0,))
NT = ((1,), (1,))
TN = ((0,), (0,))


def pack_body(base, step, each, parts, slots_ref, *rest):
    rows_refs, outs = rest[:parts], rest[-((pl.num_programs(0)) // each) :]
    at = pl.program_id(0)
    made = None
    first = 0
    for rows_ref in rows_refs:
        length = rows_ref.shape[0]
        wanted = base + at * step + lax.broadcasted_iota(jnp.int32, (step, length), 0)
        chosen = jnp.where(slots_ref[:, pl.ds(first, length)] == wanted, 1.0, 0.0)
        more = dot(chosen.astype(jnp.bfloat16), rows_ref[...], NN)
        made = more if made is None else made + more
        first += length
    made = made.astype(jnp.bfloat16)
    for j, out_ref in enumerate(outs):

        @pl.when(at // each == j)
        def _(out_ref=out_ref):
            out_ref[...] = made


def pack(slots, rows, base, count, outs, waits=()):
    length = slots.shape[0]
    width = rows[0].shape[1]
    step = min(512, count)
    each = count // step
    return pl.pallas_call(
        functools.partial(pack_body, base, step, each, len(rows)),
        out_shape=(jax.ShapeDtypeStruct((count, width), jnp.bfloat16),) * outs,
        grid=(each * outs,),
        in_specs=[pl.BlockSpec((1, length), lambda i: (0, 0))]
        + [pl.BlockSpec(r.shape, lambda i: (0, 0)) for r in rows]
        + [pl.BlockSpec(memory_space=pl.ANY)] * len(waits),
        out_specs=tuple(
            pl.BlockSpec((step, width), lambda i, j=j: (jnp.clip(i - j * each, 0, each - 1), 0))
            for j in range(outs)
        ),
        compiler_params=params("arbitrary"),
        name="pack",
        cost_estimate=cost(2 * outs * count * length * width, 2 * (length + outs * count) * width),
    )(slots.reshape(1, length), *rows, *waits)


def unpack_body(parts, *refs):
    out_ref = refs[-1]
    step = out_ref.shape[0]
    made = None
    for slots_ref, rows_ref in zip(refs[:parts], refs[parts : 2 * parts]):
        count = rows_ref.shape[0]
        held = lax.broadcasted_iota(jnp.int32, (step, count), 1)
        chosen = jnp.where(slots_ref[...] == held, 1.0, 0.0).astype(jnp.bfloat16)
        more = dot(chosen, rows_ref[...], NN)
        made = more if made is None else made + more
    out_ref[...] = made.astype(out_ref.dtype)


def unpack(slots, rows, step, place, waits=()):
    length = slots[0].shape[0]
    width = rows[0].shape[1]
    count = sum(r.shape[0] for r in rows)
    return pl.pallas_call(
        functools.partial(unpack_body, len(rows)),
        out_shape=jax.ShapeDtypeStruct((length, width), jnp.bfloat16),
        grid=(length // step,),
        in_specs=[pl.BlockSpec((step, 1), lambda i: (i, 0))] * len(rows)
        + [pl.BlockSpec(r.shape, lambda i: (0, 0)) for r in rows]
        + [pl.BlockSpec(memory_space=pl.ANY)] * len(waits),
        out_specs=pl.BlockSpec((step, width), lambda i: (place(i), 0)),
        compiler_params=params("arbitrary"),
        name="unpack",
        cost_estimate=cost(2 * count * length * width, 2 * (length + count) * width),
    )(*(at.reshape(length, 1) for at in slots), *rows, *waits)


def middle_body(full_ref, out_ref, tokens_ref, gain_ref, bias_ref, middle_ref, routed_ref):
    total = tokens_ref[...].astype(jnp.float32)
    for z in range(full_ref.shape[0]):
        total = total + dot(full_ref[z], out_ref[z], NT)
    middle_ref[...] = total
    mean = jnp.mean(total, axis=1, keepdims=True)
    centered = total - mean
    inverse = lax.rsqrt(jnp.mean(centered * centered, axis=1, keepdims=True) + EPSILON)
    routed_ref[...] = (centered * inverse * gain_ref[...] + bias_ref[...]).astype(jnp.bfloat16)


def middle_pass(full, out_full, tokens, first, gain, bias):
    cols, rows, width = full.shape
    depth = tokens.shape[1]
    step = min(256, rows)
    row = pl.BlockSpec((1, depth), lambda i: (0, 0))
    return pl.pallas_call(
        middle_body,
        out_shape=(
            jax.ShapeDtypeStruct((rows, depth), jnp.float32),
            jax.ShapeDtypeStruct((rows, depth), jnp.bfloat16),
        ),
        grid=(rows // step,),
        in_specs=[
            pl.BlockSpec((cols, step, width), lambda i: (0, i, 0)),
            pl.BlockSpec((cols, depth, width), lambda i: (0, 0, 0)),
            pl.BlockSpec((step, depth), lambda i: (i + first // step, 0)),
            row,
            row,
        ],
        out_specs=(
            pl.BlockSpec((step, depth), lambda i: (i, 0)),
            pl.BlockSpec((step, depth), lambda i: (i, 0)),
        ),
        compiler_params=params("arbitrary"),
        name="middle_pass",
        cost_estimate=cost(2 * rows * depth * width * cols, 10 * rows * depth),
    )(full, out_full, tokens, gain, bias)


def forward_body(blocks, block, q_ref, k_ref, v_ref, *rest):
    o_ref, lse_ref = rest[-2:]
    width = q_ref.shape[1]
    heads = width // HEAD_DIM
    lane = lax.broadcasted_iota(jnp.int32, (block, width), 1)
    hidden = lax.broadcasted_iota(jnp.int32, (block, block), 1) > lax.broadcasted_iota(
        jnp.int32, (block, block), 0
    )
    for at, i in enumerate(blocks):
        span = (i + 1) * block
        here = pl.ds(at * block, block)
        o_ref[here, :] = jnp.zeros((block, width), o_ref.dtype)

        def one_head(h, carry, here=here, span=span, i=i):
            mine = (lane >= h * HEAD_DIM) & (lane < (h + 1) * HEAD_DIM)
            query = q_ref[pl.ds(i * block, block), :].astype(jnp.float32) * 0.125
            query = jnp.where(mine, query, 0.0).astype(jnp.bfloat16)
            edge = jnp.where(hidden, MASKED, dot(query, k_ref[pl.ds(span - block, block), :], NT))
            peak = jnp.max(edge, axis=1, keepdims=True)
            if i:
                past = dot(query, k_ref[pl.ds(0, span - block), :], NT)
                peak = jnp.maximum(peak, jnp.max(past, axis=1, keepdims=True))
            edge = jnp.exp(edge - peak)
            total = jnp.sum(edge, axis=1, keepdims=True)
            if i:
                past = jnp.exp(past - peak)
                total = total + jnp.sum(past, axis=1, keepdims=True)
            share = 1.0 / total
            mixed = dot((edge * share).astype(jnp.bfloat16), v_ref[pl.ds(span - block, block), :], NN)
            if i:
                mixed = mixed + dot(
                    (past * share).astype(jnp.bfloat16), v_ref[pl.ds(0, span - block), :], NN
                )
            o_ref[here, :] = jnp.where(mine, mixed.astype(o_ref.dtype), o_ref[here, :])
            logsum = jnp.broadcast_to(peak + jnp.log(total), (block, 128))
            lse_ref[pl.ds(h, 1), here] = logsum.T[0:1, :]
            return carry

        lax.fori_loop(0, heads, one_head, 0)


def attend_forward(projected, blocks, block, waits=()):
    length, triple = projected.shape
    width = triple // 3
    heads = width // HEAD_DIM
    rows = len(blocks) * block
    spec = [pl.BlockSpec((length, width), lambda i, j=j: (0, j)) for j in range(3)]
    return pl.pallas_call(
        functools.partial(forward_body, blocks, block),
        out_shape=(
            jax.ShapeDtypeStruct((rows, width), jnp.bfloat16),
            jax.ShapeDtypeStruct((heads, rows), jnp.float32),
        ),
        grid=(1,),
        in_specs=spec + [pl.BlockSpec(memory_space=pl.ANY)] * len(waits),
        out_specs=(
            pl.BlockSpec((rows, width), lambda i: (0, 0)),
            pl.BlockSpec((heads, rows), lambda i: (0, 0)),
        ),
        compiler_params=params("arbitrary"),
        name="attend_forward",
        cost_estimate=cost(8 * rows * length * width, 8 * length * width, rows * length * heads),
    )(projected, projected, projected, *waits)


def backward_body(block, first, given, *refs):
    q_ref, do_ref, o_ref, lse_ref, k_ref, v_ref = refs[:6]
    outs = refs[6 + given :]
    out_ref, p_ref, ds_ref, qm_ref, dom_ref, dk_ref, dv_ref = outs[:1] + outs[-6:]
    width = q_ref.shape[1]
    heads = width // HEAD_DIM
    count = q_ref.shape[0] // block
    lane = lax.broadcasted_iota(jnp.int32, (block, width), 1)
    hidden = lax.broadcasted_iota(jnp.int32, (block, block), 0) > lax.broadcasted_iota(
        jnp.int32, (block, block), 1
    )
    for at in reversed(range(count)):
        i = first + at
        span = (i + 1) * block
        here = pl.ds(at * block, block)

        def one_head(h, carry, here=here, span=span, i=i):
            mine = (lane >= h * HEAD_DIM) & (lane < (h + 1) * HEAD_DIM)
            query = q_ref[here, :].astype(jnp.float32) * 0.125
            query = jnp.where(mine, query, 0.0).astype(jnp.bfloat16)
            grad = jnp.where(mine, do_ref[here, :].astype(jnp.float32), 0.0)
            delta = jnp.sum(grad * o_ref[here, :].astype(jnp.float32), axis=1, keepdims=True)
            delta = jnp.broadcast_to(delta, (block, 128)).T[0:1, :]
            grad = grad.astype(jnp.bfloat16)
            logsum = lse_ref[pl.ds(h, 1), here]
            column = pl.ds(pl.multiple_of(h * block, block), block)
            qm_ref[column, :] = query
            dom_ref[column, :] = grad

            def part(rows, edge):
                scores = dot(k_ref[rows, :], query, NT)
                if edge:
                    scores = jnp.where(hidden, MASKED, scores)
                probs = jnp.exp(scores - logsum)
                p_ref[rows, column] = probs.astype(jnp.bfloat16)
                grad_probs = dot(v_ref[rows, :], grad, NT)
                ds_ref[rows, column] = (probs * (grad_probs - delta)).astype(jnp.bfloat16)

            if i:
                part(pl.ds(0, span - block), False)
            part(pl.ds(span - block, block), True)
            dq = dot(ds_ref[pl.ds(0, span), column], k_ref[pl.ds(0, span), :], TN)
            out_ref[here, pl.ds(0, width)] = jnp.where(
                mine, (dq * 0.125).astype(out_ref.dtype), out_ref[here, pl.ds(0, width)]
            )
            return carry

        lax.fori_loop(0, heads, one_head, 0)
        new_v = dot(p_ref[pl.ds(0, span), :], dom_ref[...], NN)
        new_k = dot(ds_ref[pl.ds(0, span), :], qm_ref[...], NN)
        if at == count - 1:
            old_k, old_v = (refs[6][...], refs[7][...]) if given > 1 else (0.0, 0.0)
            dv_ref[...] = old_v + new_v
            dk_ref[...] = old_k + new_k
        else:
            dv_ref[pl.ds(0, span), :] += new_v
            dk_ref[pl.ds(0, span), :] += new_k
        low = pl.ds(i * block, block)
        out_ref[here, pl.ds(width, width)] = dk_ref[low, :].astype(out_ref.dtype)
        out_ref[here, pl.ds(2 * width, width)] = dv_ref[low, :].astype(out_ref.dtype)
    if first:
        outs[1][...] = dk_ref[pl.ds(0, first * block), :]
        outs[2][...] = dv_ref[pl.ds(0, first * block), :]


def attend_backward(projected, grad_context, context, logsum, block, first, carried=()):
    rows, width = context.shape
    heads = width // HEAD_DIM
    length = first * block + rows
    half = lambda j: pl.BlockSpec((rows, width), lambda i: (first * block // rows, j))
    own = pl.BlockSpec((rows, width), lambda i: (0, 0))
    low = pl.BlockSpec((first * block, width), lambda i: (0, 0))
    rest = jax.ShapeDtypeStruct((first * block, width), jnp.float32)
    more = bool(first)
    return pl.pallas_call(
        functools.partial(backward_body, block, first, len(carried)),
        out_shape=(jax.ShapeDtypeStruct((rows, 3 * width), jnp.bfloat16),) + (rest,) * (2 * more),
        grid=(1,),
        in_specs=[
            half(0),
            own,
            own,
            pl.BlockSpec((heads, rows), lambda i: (0, 0)),
            pl.BlockSpec((length, width), lambda i: (0, 1)),
            pl.BlockSpec((length, width), lambda i: (0, 2)),
        ]
        + [own] * len(carried),
        out_specs=(pl.BlockSpec((rows, 3 * width), lambda i: (0, 0)),) + (low,) * (2 * more),
        scratch_shapes=[
            pltpu.VMEM((length, heads * block), jnp.bfloat16),
            pltpu.VMEM((length, heads * block), jnp.bfloat16),
            pltpu.VMEM((heads * block, width), jnp.bfloat16),
            pltpu.VMEM((heads * block, width), jnp.bfloat16),
            pltpu.VMEM((length, width), jnp.float32),
            pltpu.VMEM((length, width), jnp.float32),
        ],
        compiler_params=params("arbitrary"),
        name="attend_backward",
        cost_estimate=cost(
            20 * rows * length * width, 16 * length * width, rows * length * heads
        ),
    )(projected, grad_context, context, logsum, projected, projected, *carried)


ROOT = math.sqrt(2.0 / math.pi)
CUBE = 0.044715


def expert_body(given, x_ref, gy_ref, win_ref, wback_ref, *rest):
    out_ref, active_ref, slope_ref, *sent = rest[given:]
    rows, depth = x_ref.shape
    hidden = dot(x_ref[...], win_ref[...], NN)
    square = hidden * hidden
    bent = jnp.tanh(ROOT * hidden * (1.0 + CUBE * square))
    active = (0.5 * hidden * (1.0 + bent)).astype(jnp.bfloat16)
    slope = 0.5 * (1.0 + bent) + 0.5 * hidden * (1.0 - bent * bent) * (
        ROOT * (1.0 + 3.0 * CUBE * square)
    )
    active_ref[...] = active
    parts = out_ref.shape[0]
    wide = depth // parts
    made = dot(active, wback_ref[...], NN).astype(jnp.bfloat16)
    for j in range(parts):
        out_ref[j] = made[:, j * wide : (j + 1) * wide]
    grad_active = dot(gy_ref[...], wback_ref[...], NT)
    grad_hidden = (grad_active * slope).astype(jnp.bfloat16)
    slope_ref[...] = grad_hidden
    back = dot(grad_hidden, win_ref[...], NT).astype(jnp.bfloat16)
    wide = depth // len(sent)
    for j, ref in enumerate(sent):
        ref[...] = back[:, j * wide : (j + 1) * wide].reshape(ref.shape)


def expert_pass(e, cap, x, grad_y, w_in, w_back, sent, members, parts, pieces, waits=()):
    rows, depth = x.shape
    width = w_in.shape[2]
    sources = rows // cap
    step = min(256, rows)
    group = step // cap
    sent = list(sent or [])
    piece = jax.ShapeDtypeStruct((sources, members, cap, depth // pieces), jnp.bfloat16)
    piece_spec = pl.BlockSpec(
        (group, None, cap, depth // pieces), lambda i: (i, e % members, 0, 0)
    )
    made = pl.pallas_call(
        functools.partial(expert_body, len(sent) + len(waits)),
        out_shape=(
            jax.ShapeDtypeStruct((parts, rows, depth // parts), jnp.bfloat16),
            jax.ShapeDtypeStruct((rows, width), jnp.bfloat16),
            jax.ShapeDtypeStruct((rows, width), jnp.bfloat16),
        )
        + (piece,) * pieces,
        grid=(rows // step,),
        in_specs=[
            pl.BlockSpec((step, depth), lambda i: (i, 0)),
            pl.BlockSpec((step, depth), lambda i: (i, 0)),
            pl.BlockSpec((None, depth, width), lambda i: (e, 0, 0)),
            pl.BlockSpec((None, width, depth), lambda i: (e, 0, 0)),
        ]
        + [pl.BlockSpec(memory_space=pl.ANY)] * (len(sent) + len(waits)),
        out_specs=(
            pl.BlockSpec((parts, step, depth // parts), lambda i: (0, i, 0)),
            pl.BlockSpec((step, width), lambda i: (i, 0)),
            pl.BlockSpec((step, width), lambda i: (i, 0)),
        )
        + (piece_spec,) * pieces,
        input_output_aliases={4 + j: 3 + j for j in range(len(sent))},
        compiler_params=params("arbitrary"),
        name="expert_pass",
        cost_estimate=cost(8 * rows * depth * width, 4 * width * depth + 12 * rows * depth, rows * width),
    )(x, grad_y, w_in, w_back, *sent, *waits)
    return made[0], made[1], made[2], made[3:]


def weight_body(given, x_ref, gy_ref, gate_ref, active_ref, slope_ref, *rest):
    gin_ref, gback_ref, token_ref, xt_ref, gyg_ref = rest[given:]
    token_ref[...] = jnp.zeros_like(token_ref)
    rows, depth = x_ref.shape

    @pl.when(pl.program_id(0) == 0)
    def _():
        gate = gate_ref[...]
        xt_ref[...] = (x_ref[...].astype(jnp.float32) * gate).T.astype(jnp.bfloat16)
        gyg_ref[...] = (gy_ref[...].astype(jnp.float32) * gate).astype(jnp.bfloat16)

    gin_ref[...] = dot(xt_ref[...], slope_ref[...], NN)
    gback_ref[...] = dot(active_ref[...], gyg_ref[...], TN)


def weight_pass(e, local, x, grad_y, gate, active, slope, sent, waits=()):
    rows, width = active.shape
    depth = x.shape[1]
    step = min(256, width)
    sent = list(sent or [])
    return pl.pallas_call(
        functools.partial(weight_body, len(sent) + len(waits)),
        out_shape=(
            jax.ShapeDtypeStruct((local, depth, width), jnp.float32),
            jax.ShapeDtypeStruct((local, width, depth), jnp.float32),
            jax.ShapeDtypeStruct((8, 128), jnp.float32),
        ),
        grid=(width // step,),
        in_specs=[
            pl.BlockSpec((rows, depth), lambda i: (0, 0)),
            pl.BlockSpec((rows, depth), lambda i: (0, 0)),
            pl.BlockSpec((rows, 1), lambda i: (0, 0)),
            pl.BlockSpec((rows, step), lambda i: (0, i)),
            pl.BlockSpec((rows, step), lambda i: (0, i)),
        ]
        + [pl.BlockSpec(memory_space=pl.ANY)] * (len(sent) + len(waits)),
        out_specs=(
            pl.BlockSpec((None, depth, step), lambda i: (e, 0, i)),
            pl.BlockSpec((None, step, depth), lambda i: (e, i, 0)),
            pl.BlockSpec((8, 128), lambda i: (0, 0)),
        ),
        scratch_shapes=[
            pltpu.VMEM((depth, rows), jnp.bfloat16),
            pltpu.VMEM((rows, depth), jnp.bfloat16),
        ],
        input_output_aliases={5 + j: j for j in range(len(sent))},
        compiler_params=params("arbitrary"),
        name="weight_pass",
        cost_estimate=cost(4 * rows * depth * width, 8 * width * depth + 8 * rows * depth),
    )(x, grad_y, gate, active, slope, *sent, *waits)


def swap(blocks, axis):
    return lax.all_to_all(blocks, axis, split_axis=0, concat_axis=0, tiled=True)


def tie(*values):
    return lax.optimization_barrier(values)


def relay_steps(shard, axis):
    count = lax.axis_size(axis)
    right = left = shard
    steps = []
    for _ in range(count - 1):
        right = lax.ppermute(right, axis, [(i, i + 1) for i in range(count - 1)])
        left = lax.ppermute(left, axis, [(i + 1, i) for i in range(count - 1)])
        steps.append((right, left))
    return steps


def relay_join(shard, steps, axis, dim):
    count = lax.axis_size(axis)
    me = lax.axis_index(axis)
    size = shard.shape[dim]
    shape = list(shard.shape)
    shape[dim] = size * count
    whole = jnp.zeros(shape, shard.dtype)
    for k in range(count):
        piece = shard if k == 0 else steps[k - 1][0] + steps[count - k - 1][1]
        whole = lax.dynamic_update_slice_in_dim(whole, piece, ((me - k) % count) * size, dim)
    return whole


def layer_stats(values):
    mean = jnp.mean(values, axis=-1, keepdims=True)
    centered = values - mean
    variance = jnp.mean(centered * centered, axis=-1, keepdims=True)
    inverse = lax.rsqrt(variance + EPSILON)
    return (centered * inverse, inverse)


def norm_back(grad_normed, normed, inverse, gain):
    grad_hat = grad_normed * gain
    centred_grad = grad_hat - jnp.mean(grad_hat, axis=-1, keepdims=True)
    return inverse * (centred_grad - normed * jnp.mean(grad_hat * normed, axis=-1, keepdims=True))


def slot_layout(expert_ids, experts, cap):
    chosen = expert_ids[:, 0]
    length = chosen.shape[0]
    table = chosen[:, None] == jnp.arange(experts, dtype=jnp.int32)[None, :]
    order = jnp.arange(length, dtype=jnp.int32)
    before = (order[:, None] > order[None, :]).astype(jnp.bfloat16)
    counted = jnp.dot(before, table.astype(jnp.bfloat16), preferred_element_type=jnp.float32)
    ranks = jnp.sum(jnp.where(table, counted, 0.0), axis=1).astype(jnp.int32)
    return (chosen, ranks, table.astype(jnp.float32))


def per_device(
    tokens, w_qkv, w_out, w_router, ln_gains, ln_biases, w_in, w_back, expert_ids, cotangent
):
    rows_all, cols_all = lax.axis_size("row"), lax.axis_size("col")
    col = lax.axis_index("col")
    length, depth = tokens.shape
    share = depth // rows_all
    width = w_qkv.shape[2]
    experts = w_router.shape[1]
    local = w_in.shape[0]
    cap = 2 * length // experts
    block_rows = rows_all * cap
    block = min(256, length // 2)
    half = length // 2
    part = half // cols_all
    members = max(1, local // 2)
    pieces = 2

    def own(low, high):
        both = (lax.dynamic_slice_in_dim(v, col * part, part, 0) for v in (low, high))
        return jnp.concatenate(list(both), axis=0)

    def own_of(values):
        return own(values[:half], values[half:])

    def send(packed):
        return swap(packed.reshape(rows_all, cap, depth), "row").reshape(block_rows, depth)

    stacked = w_qkv.transpose(1, 0, 2).reshape(share, 3 * width)
    weights = jnp.concatenate([stacked, w_router, ln_gains.T, ln_biases.T], axis=1)
    weights = lax.all_gather(weights, "row", axis=0, tiled=True)
    out_block = swap(jnp.broadcast_to(w_out.T[None], (cols_all, share, width)), "col")

    chosen, ranks, select = slot_layout(expert_ids, experts, cap)
    slots = chosen * cap + ranks
    slots_by_local = ((chosen % local) * rows_all + chosen // local) * cap + ranks
    member = chosen % local
    slots_by_group = [
        jnp.where(
            member // members == g,
            ((chosen // local) * members + member % members) * cap + ranks,
            -1,
        )
        for g in range(local // members)
    ]

    grad_packed = list(pack(slots_by_local, [cotangent], 0, block_rows, local))
    weights, grad_packed[0], out_block = tie(weights, grad_packed[0], out_block)
    grad_arrived = [send(grad_packed[0])]
    qkv_full = weights[:, : 3 * width]
    router_full = weights[:, 3 * width : 3 * width + experts]
    norms = weights[:, 3 * width + experts :].astype(jnp.float32).T
    gains, biases = norms[0:2], norms[2:4]

    resid_in = tokens.astype(jnp.float32)
    normed_one, inverse_one = layer_stats(resid_in)
    normal_in = (normed_one * gains[0] + biases[0]).astype(jnp.bfloat16)
    projected = jnp.dot(normal_in, qkv_full, preferred_element_type=jnp.float32).astype(jnp.bfloat16)

    count = half // block
    context_a, logsum_a = attend_forward(projected, tuple(range(count)), block)
    context_a, grad_arrived[0], *grad_packed[1:2] = tie(
        context_a, grad_arrived[0], *grad_packed[1:2]
    )
    full_a = lax.all_gather(context_a, "col", axis=0)
    grad_arrived += [send(p) for p in grad_packed[1:2]]
    context_b, logsum_b = attend_forward(
        projected, tuple(range(count, 2 * count)), block, [context_a]
    )
    context_b, out_block, *grad_arrived[1:] = tie(context_b, out_block, *grad_arrived[1:])
    full_b = lax.all_gather(context_b, "col", axis=0)
    out_full = swap(jnp.broadcast_to(out_block[None], (rows_all, *out_block.shape)), "row")
    out_full, *grad_packed[2:] = tie(out_full, *grad_packed[2:])
    out_full = out_full.transpose(1, 0, 2, 3).reshape(cols_all, depth, width)
    gain, bias = gains[1:2], biases[1:2]
    middle_a, routed_a = middle_pass(full_a, out_full, tokens, 0, gain, bias)
    for e in range(2, local):
        grad_arrived.append(send(grad_packed[e]))
        if e + 1 < local:
            full_b, grad_arrived[e], grad_packed[e + 1], middle_a = tie(
                full_b, grad_arrived[e], grad_packed[e + 1], middle_a
            )
    middle_b, routed_b = middle_pass(full_b, out_full, tokens, half, gain, bias)

    routed = [routed_a, routed_b]
    packed = list(pack(slots_by_local, routed, 0, block_rows, 1))
    if local > 1:
        packed += pack(slots_by_local, routed, block_rows, block_rows, local - 1)
    packed[0], grad_arrived[-1] = tie(packed[0], grad_arrived[-1])

    def route(rows):
        return jnp.dot(rows, router_full, preferred_element_type=jnp.float32)

    logits = jnp.concatenate([route(routed_a), route(routed_b)], axis=0)
    probs = jax.nn.softmax(logits, axis=-1)
    gate = jnp.sum(probs * select, axis=-1, keepdims=True)

    arrived, summed, active, slope, sent = [], [], [], [], []
    for e in range(local):
        arrived.append(send(packed[e]))
        if e + 1 < local:
            packed[e + 1], arrived[e] = tie(packed[e + 1], arrived[e])
        if e:
            then = packed[e + 1] if e + 1 < local else sent[0][0]
            then, summed[e - 1], arrived[e] = tie(then, summed[e - 1], arrived[e])
            summed[e - 1] = lax.psum_scatter(
                summed[e - 1], "col", scatter_dimension=0, tiled=True
            )
            if e + 1 < local:
                packed[e + 1] = then
            else:
                sent[0] = (then, *sent[0][1:])
        made, kept, grads, pair = expert_pass(
            e,
            cap,
            arrived[e],
            grad_arrived[e],
            w_in,
            w_back,
            sent.pop() if e % members else None,
            members,
            cols_all,
            pieces,
            packed[-1:] if e == 0 else summed[e - 3 : e - 2] if e > 2 else [],
        )
        active.append(kept)
        slope.append(grads)
        summed.append(made)
        sent.append(pair)
    summed[-1] = lax.psum_scatter(summed[-1], "col", scatter_dimension=0, tiled=True)

    def place(i):
        return (i % cols_all) * 2 + i // cols_all

    order = [(g, f) for f in range(pieces) for g in range(len(sent))]
    back = {}
    grad_sent = []
    last = None
    for at, (g, f) in enumerate(order):
        piece = sent[g][f]
        if last is not None:
            piece, last = tie(piece, last)
            back[order[at - 1]] = last
        if at == 1:
            piece, slope[-1] = tie(piece, slope[-1])
        if at == len(order) - 1:
            homed = jnp.stack(
                [v.reshape(rows_all, cap, depth // cols_all) for v in summed], axis=1
            )
            homed, piece = tie(homed, piece)
            homed = swap(homed, "row")
            homed, piece = tie(homed, piece)
        last = swap(piece, "row")
        back[(g, f)] = last
        if g == len(sent) - 1:
            rows = [back[(k, f)].reshape(-1, depth // pieces) for k in range(len(sent))]
            whole = unpack(slots_by_group, rows, part, place)
            if f == 0:
                whole, *summed = tie(whole, *summed)
            grad_sent.append(lax.psum_scatter(whole, "col", scatter_dimension=0, tiled=True))

    returned = unpack(
        [slots], [homed.reshape(experts * cap, depth // cols_all)], part, lambda i: i
    ).astype(jnp.float32)
    columns = depth // cols_all

    def own_columns(values):
        return lax.dynamic_slice_in_dim(values, col * columns, columns, 1)

    middle_cols = jnp.concatenate([own_columns(middle_a), own_columns(middle_b)], axis=0)
    mixed = (middle_cols + gate * returned).astype(jnp.bfloat16)
    grad_gate = jnp.sum(own_columns(cotangent).astype(jnp.float32) * returned, axis=-1)
    grad_gate = swap(grad_gate.reshape(2, cols_all, part).transpose(1, 0, 2), "col")
    grad_gate = jnp.sum(grad_gate, axis=0).reshape(2 * part, 1)
    held = jnp.arange(experts * cap, dtype=jnp.int32)
    gates = jnp.sum(jnp.where(held[:, None] == slots[None, :], gate[:, 0][None, :], 0.0), axis=1)
    mixed, grad_gate, gates = tie(mixed, grad_gate, gates.reshape(rows_all, local * cap))
    steps = relay_steps(mixed, "col")

    own_gate, own_probs, own_select = own_of(gate), own_of(probs), own_of(select)
    grad_logits = (grad_gate * own_probs * (own_select - own_gate)).astype(jnp.bfloat16)
    own_routed = own(routed_a, routed_b)
    grad_router = jnp.einsum(
        "td,te->de", own_routed, grad_logits, preferred_element_type=jnp.float32
    )
    grad_y = own_of(cotangent).astype(jnp.float32)
    normed_own, inverse_own = layer_stats(own(middle_a, middle_b))
    grad_sent = jnp.concatenate(grad_sent, axis=1).astype(jnp.float32) * own_gate
    grad_routed = grad_sent + jnp.einsum(
        "te,de->td", grad_logits, router_full, preferred_element_type=jnp.float32
    )
    gain_two = jnp.sum(grad_routed * normed_own, axis=0)
    bias_two = jnp.sum(grad_routed, axis=0)
    grad_middle = grad_y + norm_back(grad_routed, normed_own, inverse_own, gains[1])
    grad_attn = grad_middle.astype(jnp.bfloat16)
    grad_context = jnp.einsum(
        "td,zdc->ztc", grad_attn, out_full, preferred_element_type=jnp.float32
    ).astype(jnp.bfloat16)
    gates = swap(gates, "row")
    if steps:
        grad_context, *first = tie(grad_context, *steps[0])
        steps[0] = tuple(first)
    grad_context = swap(grad_context, "col").reshape(cols_all, 2, part, width)
    grad_context = grad_context.transpose(1, 0, 2, 3).reshape(2, half, width)

    context_own = jnp.concatenate(
        [lax.dynamic_slice_in_dim(v, col * part, part, 1) for v in (full_a, full_b)], axis=1
    )
    grad_out = jnp.einsum("td,ztc->dzc", grad_attn, context_own, preferred_element_type=jnp.float32)
    plane = jnp.concatenate([grad_out.reshape(depth, cols_all * width), grad_router], axis=1)
    plane = swap(plane.astype(jnp.bfloat16).reshape(rows_all, share, -1), "row")

    proj_b, *carried = attend_backward(
        projected, grad_context[1], context_b, logsum_b, block, count
    )
    tied = steps[1] if len(steps) > 1 else ()
    proj_b, gates, *second = tie(proj_b, gates, *tied)
    proj_a = attend_backward(
        projected, grad_context[0], context_a, logsum_a, block, 0, carried
    )[0]
    tied = steps[2] if len(steps) > 2 else ()
    proj_a, plane, *third = tie(proj_a, plane, *tied)
    steps[1:3] = [tuple(v) for v in (second, third) if v]

    def spread(grads):
        made = jnp.einsum("tc,dc->td", grads, qkv_full, preferred_element_type=jnp.float32)
        return lax.psum_scatter(
            made.astype(jnp.bfloat16), "col", scatter_dimension=0, tiled=True
        ).astype(jnp.float32)

    normal_b, normal_a = spread(proj_b), spread(proj_a)
    grad_qkv = jnp.einsum(
        "td,tc->dc", normal_in[:half], proj_a, preferred_element_type=jnp.float32
    ) + jnp.einsum("td,tc->dc", normal_in[half:], proj_b, preferred_element_type=jnp.float32)

    gates = gates.reshape(rows_all, local, cap).transpose(1, 0, 2)
    grad_weights = None
    for e in range(local):
        *grad_weights, token = weight_pass(
            e,
            local,
            arrived[e],
            grad_arrived[e],
            gates[e].reshape(block_rows, 1),
            active[e],
            slope[e],
            grad_weights,
            [token if e else proj_a],
        )
        if e == max(local // 2 - 1, 0):
            normal_b, token = tie(normal_b, token)
    grad_in, grad_back = grad_weights

    plane = jnp.sum(plane.astype(jnp.float32), axis=0)
    router_share = plane[:, cols_all * width :].reshape(1, share, experts)
    out_share = plane[:, : cols_all * width].reshape(share, cols_all, width).transpose(1, 0, 2)
    router_share = jnp.broadcast_to(router_share, (cols_all, share, experts))
    plane = jnp.concatenate([out_share, router_share], axis=2).astype(jnp.bfloat16)
    plane = jnp.sum(swap(plane, "col").astype(jnp.float32), axis=0)
    out_share, router_share = plane[:, :width].T, plane[:, width:]

    tokens_own = [lax.dynamic_slice_in_dim(v, col * part, part, 0) for v in (tokens[:half], tokens[half:])]
    normed = [layer_stats(v.astype(jnp.float32)) for v in tokens_own]
    finished = [None, None]
    sums = [jnp.stack([gain_two, bias_two])]
    for c in (1, 0):
        grads = (normal_a, normal_b)[c]
        own_normed, own_inverse = normed[c]
        made = grad_middle[c * part : (c + 1) * part] + norm_back(
            grads, own_normed, own_inverse, gains[0]
        )
        finished[c] = made.astype(jnp.bfloat16)
        sums.append(
            jnp.stack([jnp.sum(grads * own_normed, axis=0), jnp.sum(grads, axis=0)])
        )
        if c:
            moves = relay_steps(finished[1], "col")
            flat = [v for move in moves for v in move]
            normal_a, out_share, router_share, *flat = tie(
                normal_a, out_share, router_share, *flat
            )
            moves = list(zip(flat[0::2], flat[1::2]))
    grad_tokens = jnp.concatenate(
        [relay_join(finished[1], moves, "col", 0), lax.all_gather(finished[0], "col", axis=0, tiled=True)][::-1],
        axis=0,
    )
    mixed_out = relay_join(mixed, steps, "col", 1)

    small = jnp.concatenate([sums[1] + sums[2], sums[0]], axis=0)
    small = swap(small.reshape(4, rows_all, share).transpose(1, 0, 2), "row")
    small = jnp.sum(small, axis=0)
    small = jnp.sum(swap(jnp.broadcast_to(small[None], (cols_all, 4, share)), "col"), axis=0)
    qkv_share = swap(grad_qkv.astype(jnp.bfloat16).reshape(rows_all, share, -1), "row")
    qkv_share = jnp.sum(qkv_share.astype(jnp.float32), axis=0)
    qkv_share = qkv_share.reshape(share, 3, width).transpose(1, 0, 2)
    return (
        mixed_out,
        grad_tokens,
        qkv_share,
        out_share,
        router_share,
        jnp.stack([small[0], small[2]]),
        small[1],
        small[3],
        grad_in,
        grad_back,
    )


def solution(mesh):
    return jax.shard_map(
        per_device,
        mesh=mesh,
        in_specs=(
            P("row", None),
            P(None, "row", "col"),
            P("col", "row"),
            P("row", None),
            P(None, "row"),
            P(None, "row"),
            P("row", None, "col"),
            P("row", "col", None),
            P("row", None),
            P("row", None),
        ),
        out_specs=(
            P("row", None),
            P("row", None),
            P(None, "row", "col"),
            P("col", "row"),
            P("row", None),
            P(None, "row"),
            P("row"),
            P("row"),
            P("row", None, "col"),
            P("row", "col", None),
        ),
        check_vma=False,
    )
```

```python
import functools, math
import jax, jax.numpy as jnp
from jax import lax
from jax.experimental import pallas as pl
from jax.experimental.pallas import tpu as pltpu
from jax.sharding import PartitionSpec as P

HEAD_DIM = 64
EPSILON = 1e-05
MASKED = -1e30
VMEM = 60 << 20


def params(*kinds):
    return pltpu.CompilerParams(dimension_semantics=kinds or None, vmem_limit_bytes=VMEM)


def cost(flops, moved, special=0):
    return pl.CostEstimate(flops=flops, bytes_accessed=moved, transcendentals=special)


def dot(a, b, dims):
    return lax.dot_general(a, b, (dims, ((), ())), preferred_element_type=jnp.float32)

NN = ((1,), (0,))
NT = ((1,), (1,))
TN = ((0,), (0,))


def pack_body(base, step, each, parts, slots_ref, *rest):
    rows_refs, outs = rest[:parts], rest[-((pl.num_programs(0)) // each) :]
    at = pl.program_id(0)
    made = None
    first = 0
    for rows_ref in rows_refs:
        length = rows_ref.shape[0]
        wanted = base + at * step + lax.broadcasted_iota(jnp.int32, (step, length), 0)
        chosen = jnp.where(slots_ref[:, pl.ds(first, length)] == wanted, 1.0, 0.0)
        more = dot(chosen.astype(jnp.bfloat16), rows_ref[...], NN)
        made = more if made is None else made + more
        first += length
    made = made.astype(jnp.bfloat16)
    for j, out_ref in enumerate(outs):

        @pl.when(at // each == j)
        def _(out_ref=out_ref):
            out_ref[...] = made


def pack(slots, rows, base, count, outs, waits=()):
    length = slots.shape[0]
    width = rows[0].shape[1]
    step = min(512, count)
    each = count // step
    return pl.pallas_call(
        functools.partial(pack_body, base, step, each, len(rows)),
        out_shape=(jax.ShapeDtypeStruct((count, width), jnp.bfloat16),) * outs,
        grid=(each * outs,),
        in_specs=[pl.BlockSpec((1, length), lambda i: (0, 0))]
        + [pl.BlockSpec(r.shape, lambda i: (0, 0)) for r in rows]
        + [pl.BlockSpec(memory_space=pl.ANY)] * len(waits),
        out_specs=tuple(
            pl.BlockSpec((step, width), lambda i, j=j: (jnp.clip(i - j * each, 0, each - 1), 0))
            for j in range(outs)
        ),
        compiler_params=params("arbitrary"),
        name="pack",
        cost_estimate=cost(count * width, count * width),
    )(slots.reshape(1, length), *rows, *waits)


def unpack_body(parts, *refs):
    out_ref = refs[-1]
    step = out_ref.shape[0]
    made = None
    for slots_ref, rows_ref in zip(refs[:parts], refs[parts : 2 * parts]):
        count = rows_ref.shape[0]
        held = lax.broadcasted_iota(jnp.int32, (step, count), 1)
        chosen = jnp.where(slots_ref[...] == held, 1.0, 0.0).astype(jnp.bfloat16)
        more = dot(chosen, rows_ref[...], NN)
        made = more if made is None else made + more
    out_ref[...] = made.astype(out_ref.dtype)


def unpack(slots, rows, step, place, waits=()):
    length = slots[0].shape[0]
    width = rows[0].shape[1]
    count = sum(r.shape[0] for r in rows)
    return pl.pallas_call(
        functools.partial(unpack_body, len(rows)),
        out_shape=jax.ShapeDtypeStruct((length, width), jnp.bfloat16),
        grid=(length // step,),
        in_specs=[pl.BlockSpec((step, 1), lambda i: (i, 0))] * len(rows)
        + [pl.BlockSpec(r.shape, lambda i: (0, 0)) for r in rows]
        + [pl.BlockSpec(memory_space=pl.ANY)] * len(waits),
        out_specs=pl.BlockSpec((step, width), lambda i: (place(i), 0)),
        compiler_params=params("arbitrary"),
        name="unpack",
        cost_estimate=cost(2 * count * length * width, 2 * (length + count) * width),
    )(*(at.reshape(length, 1) for at in slots), *rows, *waits)


def middle_body(full_ref, out_ref, tokens_ref, gain_ref, bias_ref, middle_ref, routed_ref):
    total = tokens_ref[...].astype(jnp.float32)
    for z in range(full_ref.shape[0]):
        total = total + dot(full_ref[z], out_ref[z], NT)
    middle_ref[...] = total
    mean = jnp.mean(total, axis=1, keepdims=True)
    centered = total - mean
    inverse = lax.rsqrt(jnp.mean(centered * centered, axis=1, keepdims=True) + EPSILON)
    routed_ref[...] = (centered * inverse * gain_ref[...] + bias_ref[...]).astype(jnp.bfloat16)


def middle_pass(full, out_full, tokens, first, gain, bias):
    cols, rows, width = full.shape
    depth = tokens.shape[1]
    step = min(256, rows)
    row = pl.BlockSpec((1, depth), lambda i: (0, 0))
    return pl.pallas_call(
        middle_body,
        out_shape=(
            jax.ShapeDtypeStruct((rows, depth), jnp.float32),
            jax.ShapeDtypeStruct((rows, depth), jnp.bfloat16),
        ),
        grid=(rows // step,),
        in_specs=[
            pl.BlockSpec((cols, step, width), lambda i: (0, i, 0)),
            pl.BlockSpec((cols, depth, width), lambda i: (0, 0, 0)),
            pl.BlockSpec((step, depth), lambda i: (i + first // step, 0)),
            row,
            row,
        ],
        out_specs=(
            pl.BlockSpec((step, depth), lambda i: (i, 0)),
            pl.BlockSpec((step, depth), lambda i: (i, 0)),
        ),
        compiler_params=params("arbitrary"),
        name="middle_pass",
        cost_estimate=cost(2 * rows * depth * width * cols, 10 * rows * depth),
    )(full, out_full, tokens, gain, bias)


def forward_body(blocks, block, q_ref, k_ref, v_ref, *rest):
    o_ref, lse_ref = rest[-2:]
    width = q_ref.shape[1]
    heads = width // HEAD_DIM
    lane = lax.broadcasted_iota(jnp.int32, (block, width), 1)
    hidden = lax.broadcasted_iota(jnp.int32, (block, block), 1) > lax.broadcasted_iota(
        jnp.int32, (block, block), 0
    )
    for at, i in enumerate(blocks):
        span = (i + 1) * block
        here = pl.ds(at * block, block)
        o_ref[here, :] = jnp.zeros((block, width), o_ref.dtype)

        def one_head(h, carry, here=here, span=span, i=i):
            mine = (lane >= h * HEAD_DIM) & (lane < (h + 1) * HEAD_DIM)
            query = q_ref[pl.ds(i * block, block), :].astype(jnp.float32) * 0.125
            query = jnp.where(mine, query, 0.0).astype(jnp.bfloat16)
            edge = jnp.where(hidden, MASKED, dot(query, k_ref[pl.ds(span - block, block), :], NT))
            peak = jnp.max(edge, axis=1, keepdims=True)
            if i:
                past = dot(query, k_ref[pl.ds(0, span - block), :], NT)
                peak = jnp.maximum(peak, jnp.max(past, axis=1, keepdims=True))
            edge = jnp.exp(edge - peak)
            total = jnp.sum(edge, axis=1, keepdims=True)
            if i:
                past = jnp.exp(past - peak)
                total = total + jnp.sum(past, axis=1, keepdims=True)
            share = 1.0 / total
            mixed = dot((edge * share).astype(jnp.bfloat16), v_ref[pl.ds(span - block, block), :], NN)
            if i:
                mixed = mixed + dot(
                    (past * share).astype(jnp.bfloat16), v_ref[pl.ds(0, span - block), :], NN
                )
            o_ref[here, :] = jnp.where(mine, mixed.astype(o_ref.dtype), o_ref[here, :])
            logsum = jnp.broadcast_to(peak + jnp.log(total), (block, 128))
            lse_ref[pl.ds(h, 1), here] = logsum.T[0:1, :]
            return carry

        lax.fori_loop(0, heads, one_head, 0, unroll=heads)


def attend_forward(projected, blocks, block, waits=()):
    length, triple = projected.shape
    width = triple // 3
    heads = width // HEAD_DIM
    rows = len(blocks) * block
    spec = [pl.BlockSpec((length, width), lambda i, j=j: (0, j)) for j in range(3)]
    return pl.pallas_call(
        functools.partial(forward_body, blocks, block),
        out_shape=(
            jax.ShapeDtypeStruct((rows, width), jnp.bfloat16),
            jax.ShapeDtypeStruct((heads, rows), jnp.float32),
        ),
        grid=(1,),
        in_specs=spec + [pl.BlockSpec(memory_space=pl.ANY)] * len(waits),
        out_specs=(
            pl.BlockSpec((rows, width), lambda i: (0, 0)),
            pl.BlockSpec((heads, rows), lambda i: (0, 0)),
        ),
        compiler_params=params("arbitrary"),
        name="attend_forward",
        cost_estimate=cost(rows * width, rows * width),
    )(projected, projected, projected, *waits)


def backward_body(block, first, given, *refs):
    q_ref, do_ref, o_ref, lse_ref, k_ref, v_ref = refs[:6]
    outs = refs[6 + given :]
    out_ref, p_ref, ds_ref, qm_ref, dom_ref, dk_ref, dv_ref = outs[:1] + outs[-6:]
    width = q_ref.shape[1]
    heads = width // HEAD_DIM
    count = q_ref.shape[0] // block
    lane = lax.broadcasted_iota(jnp.int32, (block, width), 1)
    hidden = lax.broadcasted_iota(jnp.int32, (block, block), 0) > lax.broadcasted_iota(
        jnp.int32, (block, block), 1
    )
    for at in reversed(range(count)):
        i = first + at
        span = (i + 1) * block
        here = pl.ds(at * block, block)

        def one_head(h, carry, here=here, span=span, i=i):
            mine = (lane >= h * HEAD_DIM) & (lane < (h + 1) * HEAD_DIM)
            query = q_ref[here, :].astype(jnp.float32) * 0.125
            query = jnp.where(mine, query, 0.0).astype(jnp.bfloat16)
            grad = jnp.where(mine, do_ref[here, :].astype(jnp.float32), 0.0)
            delta = jnp.sum(grad * o_ref[here, :].astype(jnp.float32), axis=1, keepdims=True)
            delta = jnp.broadcast_to(delta, (block, 128)).T[0:1, :]
            grad = grad.astype(jnp.bfloat16)
            logsum = lse_ref[pl.ds(h, 1), here]
            column = pl.ds(pl.multiple_of(h * block, block), block)
            qm_ref[column, :] = query
            dom_ref[column, :] = grad

            def part(rows, edge):
                scores = dot(k_ref[rows, :], query, NT)
                if edge:
                    scores = jnp.where(hidden, MASKED, scores)
                probs = jnp.exp(scores - logsum)
                p_ref[rows, column] = probs.astype(jnp.bfloat16)
                grad_probs = dot(v_ref[rows, :], grad, NT)
                ds_ref[rows, column] = (probs * (grad_probs - delta)).astype(jnp.bfloat16)

            if i:
                part(pl.ds(0, span - block), False)
            part(pl.ds(span - block, block), True)
            dq = dot(ds_ref[pl.ds(0, span), column], k_ref[pl.ds(0, span), :], TN)
            out_ref[here, pl.ds(0, width)] = jnp.where(
                mine, (dq * 0.125).astype(out_ref.dtype), out_ref[here, pl.ds(0, width)]
            )
            return carry

        lax.fori_loop(0, heads, one_head, 0, unroll=heads)
        new_v = dot(p_ref[pl.ds(0, span), :], dom_ref[...], NN)
        new_k = dot(ds_ref[pl.ds(0, span), :], qm_ref[...], NN)
        if at == count - 1:
            old_k, old_v = (refs[6][...], refs[7][...]) if given > 1 else (0.0, 0.0)
            dv_ref[...] = old_v + new_v
            dk_ref[...] = old_k + new_k
        else:
            dv_ref[pl.ds(0, span), :] += new_v
            dk_ref[pl.ds(0, span), :] += new_k
        low = pl.ds(i * block, block)
        out_ref[here, pl.ds(width, width)] = dk_ref[low, :].astype(out_ref.dtype)
        out_ref[here, pl.ds(2 * width, width)] = dv_ref[low, :].astype(out_ref.dtype)
    if first:
        outs[1][...] = dk_ref[pl.ds(0, first * block), :]
        outs[2][...] = dv_ref[pl.ds(0, first * block), :]


def attend_backward(projected, grad_context, context, logsum, block, first, carried=()):
    rows, width = context.shape
    heads = width // HEAD_DIM
    length = first * block + rows
    half = lambda j: pl.BlockSpec((rows, width), lambda i: (first * block // rows, j))
    own = pl.BlockSpec((rows, width), lambda i: (0, 0))
    low = pl.BlockSpec((first * block, width), lambda i: (0, 0))
    rest = jax.ShapeDtypeStruct((first * block, width), jnp.float32)
    more = bool(first)
    return pl.pallas_call(
        functools.partial(backward_body, block, first, len(carried)),
        out_shape=(jax.ShapeDtypeStruct((rows, 3 * width), jnp.bfloat16),) + (rest,) * (2 * more),
        grid=(1,),
        in_specs=[
            half(0),
            own,
            own,
            pl.BlockSpec((heads, rows), lambda i: (0, 0)),
            pl.BlockSpec((length, width), lambda i: (0, 1)),
            pl.BlockSpec((length, width), lambda i: (0, 2)),
        ]
        + [own] * len(carried),
        out_specs=(pl.BlockSpec((rows, 3 * width), lambda i: (0, 0)),) + (low,) * (2 * more),
        scratch_shapes=[
            pltpu.VMEM((length, heads * block), jnp.bfloat16),
            pltpu.VMEM((length, heads * block), jnp.bfloat16),
            pltpu.VMEM((heads * block, width), jnp.bfloat16),
            pltpu.VMEM((heads * block, width), jnp.bfloat16),
            pltpu.VMEM((length, width), jnp.float32),
            pltpu.VMEM((length, width), jnp.float32),
        ],
        compiler_params=params("arbitrary"),
        name="attend_backward",
        cost_estimate=cost(
            20 * rows * length * width, 16 * length * width, rows * length * heads
        ),
    )(projected, grad_context, context, logsum, projected, projected, *carried)


ROOT = math.sqrt(2.0 / math.pi)
CUBE = 0.044715


def expert_body(given, x_ref, gy_ref, win_ref, wback_ref, *rest):
    out_ref, active_ref, slope_ref, *sent = rest[given:]
    rows, depth = x_ref.shape
    hidden = dot(x_ref[...], win_ref[...], NN)
    square = hidden * hidden
    bent = jnp.tanh(ROOT * hidden * (1.0 + CUBE * square))
    active = (0.5 * hidden * (1.0 + bent)).astype(jnp.bfloat16)
    slope = 0.5 * (1.0 + bent) + 0.5 * hidden * (1.0 - bent * bent) * (
        ROOT * (1.0 + 3.0 * CUBE * square)
    )
    active_ref[...] = active
    parts = out_ref.shape[0]
    wide = depth // parts
    made = dot(active, wback_ref[...], NN).astype(jnp.bfloat16)
    for j in range(parts):
        out_ref[j] = made[:, j * wide : (j + 1) * wide]
    grad_active = dot(gy_ref[...], wback_ref[...], NT)
    grad_hidden = (grad_active * slope).astype(jnp.bfloat16)
    slope_ref[...] = grad_hidden
    back = dot(grad_hidden, win_ref[...], NT).astype(jnp.bfloat16)
    wide = depth // len(sent)
    for j, ref in enumerate(sent):
        ref[...] = back[:, j * wide : (j + 1) * wide].reshape(ref.shape)


def expert_pass(e, cap, x, grad_y, w_in, w_back, sent, members, parts, pieces, waits=()):
    rows, depth = x.shape
    width = w_in.shape[2]
    sources = rows // cap
    step = min(256, rows)
    group = step // cap
    sent = list(sent or [])
    piece = jax.ShapeDtypeStruct((sources, members, cap, depth // pieces), jnp.bfloat16)
    piece_spec = pl.BlockSpec(
        (group, None, cap, depth // pieces), lambda i: (i, e % members, 0, 0)
    )
    made = pl.pallas_call(
        functools.partial(expert_body, len(sent) + len(waits)),
        out_shape=(
            jax.ShapeDtypeStruct((parts, rows, depth // parts), jnp.bfloat16),
            jax.ShapeDtypeStruct((rows, width), jnp.bfloat16),
            jax.ShapeDtypeStruct((rows, width), jnp.bfloat16),
        )
        + (piece,) * pieces,
        grid=(rows // step,),
        in_specs=[
            pl.BlockSpec((step, depth), lambda i: (i, 0)),
            pl.BlockSpec((step, depth), lambda i: (i, 0)),
            pl.BlockSpec((None, depth, width), lambda i: (e, 0, 0)),
            pl.BlockSpec((None, width, depth), lambda i: (e, 0, 0)),
        ]
        + [pl.BlockSpec(memory_space=pl.ANY)] * (len(sent) + len(waits)),
        out_specs=(
            pl.BlockSpec((parts, step, depth // parts), lambda i: (0, i, 0)),
            pl.BlockSpec((step, width), lambda i: (i, 0)),
            pl.BlockSpec((step, width), lambda i: (i, 0)),
        )
        + (piece_spec,) * pieces,
        input_output_aliases={4 + j: 3 + j for j in range(len(sent))},
        compiler_params=params("arbitrary"),
        name="expert_pass",
        cost_estimate=cost(8 * rows * depth * width, 4 * width * depth + 12 * rows * depth, rows * width),
    )(x, grad_y, w_in, w_back, *sent, *waits)
    return made[0], made[1], made[2], made[3:]


def weight_body(given, x_ref, gy_ref, router_ref, pick_ref, active_ref, slope_ref, *rest):
    gin_ref, gback_ref, token_ref, xt_ref, gyg_ref = rest[given:]
    token_ref[...] = jnp.zeros_like(token_ref)
    rows, depth = x_ref.shape

    @pl.when(pl.program_id(0) == 0)
    def _():
        logits = dot(x_ref[...], router_ref[...], NN)
        raised = jnp.exp(logits - jnp.max(logits, axis=1, keepdims=True))
        gate = jnp.sum(raised * pick_ref[...], axis=1, keepdims=True)
        gate = gate / jnp.sum(raised, axis=1, keepdims=True)
        xt_ref[...] = (x_ref[...].astype(jnp.float32) * gate).T.astype(jnp.bfloat16)
        gyg_ref[...] = (gy_ref[...].astype(jnp.float32) * gate).astype(jnp.bfloat16)

    gin_ref[...] = dot(xt_ref[...], slope_ref[...], NN)
    gback_ref[...] = dot(active_ref[...], gyg_ref[...], TN)


def weight_pass(e, local, x, grad_y, router, pick, active, slope, sent, waits=()):
    rows, width = active.shape
    depth = x.shape[1]
    step = min(256, width)
    sent = list(sent or [])
    return pl.pallas_call(
        functools.partial(weight_body, len(sent) + len(waits)),
        out_shape=(
            jax.ShapeDtypeStruct((local, depth, width), jnp.float32),
            jax.ShapeDtypeStruct((local, width, depth), jnp.float32),
            jax.ShapeDtypeStruct((8, 128), jnp.float32),
        ),
        grid=(width // step,),
        in_specs=[
            pl.BlockSpec((rows, depth), lambda i: (0, 0)),
            pl.BlockSpec((rows, depth), lambda i: (0, 0)),
            pl.BlockSpec(router.shape, lambda i: (0, 0)),
            pl.BlockSpec(pick.shape, lambda i: (0, 0)),
            pl.BlockSpec((rows, step), lambda i: (0, i)),
            pl.BlockSpec((rows, step), lambda i: (0, i)),
        ]
        + [pl.BlockSpec(memory_space=pl.ANY)] * (len(sent) + len(waits)),
        out_specs=(
            pl.BlockSpec((None, depth, step), lambda i: (e, 0, i)),
            pl.BlockSpec((None, step, depth), lambda i: (e, i, 0)),
            pl.BlockSpec((8, 128), lambda i: (0, 0)),
        ),
        scratch_shapes=[
            pltpu.VMEM((depth, rows), jnp.bfloat16),
            pltpu.VMEM((rows, depth), jnp.bfloat16),
        ],
        input_output_aliases={6 + j: j for j in range(len(sent))},
        compiler_params=params("arbitrary"),
        name="weight_pass",
        cost_estimate=cost(4 * rows * depth * width, 8 * width * depth + 8 * rows * depth),
    )(x, grad_y, router, pick, active, slope, *sent, *waits)


def swap(blocks, axis):
    return lax.all_to_all(blocks, axis, split_axis=0, concat_axis=0, tiled=True)


def tie(*values):
    return lax.optimization_barrier(values)


def relay_steps(shard, axis):
    count = lax.axis_size(axis)
    right = left = shard
    steps = []
    for _ in range(count - 1):
        right = lax.ppermute(right, axis, [(i, i + 1) for i in range(count - 1)])
        left = lax.ppermute(left, axis, [(i + 1, i) for i in range(count - 1)])
        steps.append([right, left])
    return steps


def relay_join(shard, steps, axis, dim):
    count = lax.axis_size(axis)
    me = lax.axis_index(axis)
    size = shard.shape[dim]
    shape = list(shard.shape)
    shape[dim] = size * count
    whole = jnp.zeros(shape, shard.dtype)
    for k in range(count):
        piece = shard if k == 0 else steps[k - 1][0] + steps[count - k - 1][1]
        whole = lax.dynamic_update_slice_in_dim(whole, piece, ((me - k) % count) * size, dim)
    return whole


def layer_stats(values):
    mean = jnp.mean(values, axis=-1, keepdims=True)
    centered = values - mean
    variance = jnp.mean(centered * centered, axis=-1, keepdims=True)
    inverse = lax.rsqrt(variance + EPSILON)
    return (centered * inverse, inverse)


def norm_back(grad_normed, normed, inverse, gain):
    grad_hat = grad_normed * gain
    centred_grad = grad_hat - jnp.mean(grad_hat, axis=-1, keepdims=True)
    return inverse * (centred_grad - normed * jnp.mean(grad_hat * normed, axis=-1, keepdims=True))


def slot_layout(expert_ids, experts, cap):
    chosen = expert_ids[:, 0]
    length = chosen.shape[0]
    table = chosen[:, None] == jnp.arange(experts, dtype=jnp.int32)[None, :]
    order = jnp.arange(length, dtype=jnp.int32)
    before = (order[:, None] > order[None, :]).astype(jnp.bfloat16)
    counted = jnp.dot(before, table.astype(jnp.bfloat16), preferred_element_type=jnp.float32)
    ranks = jnp.sum(jnp.where(table, counted, 0.0), axis=1).astype(jnp.int32)
    return (chosen, ranks, table.astype(jnp.float32))


def per_device(
    tokens, w_qkv, w_out, w_router, ln_gains, ln_biases, w_in, w_back, expert_ids, cotangent
):
    rows_all, cols_all = lax.axis_size("row"), lax.axis_size("col")
    col = lax.axis_index("col")
    length, depth = tokens.shape
    share = depth // rows_all
    width = w_qkv.shape[2]
    experts = w_router.shape[1]
    local = w_in.shape[0]
    cap = 2 * length // experts
    block_rows = rows_all * cap
    block = min(256, length // 2)
    half = length // 2
    part = half // cols_all
    members = max(1, local // 2)
    pieces = 2

    def own(low, high):
        both = (lax.dynamic_slice_in_dim(v, col * part, part, 0) for v in (low, high))
        return jnp.concatenate(list(both), axis=0)

    def own_of(values):
        return own(values[:half], values[half:])

    def send(packed):
        return swap(packed.reshape(rows_all, cap, depth), "row").reshape(block_rows, depth)

    stacked = w_qkv.transpose(1, 0, 2).reshape(share, 3 * width)
    weights = jnp.concatenate([stacked, w_router, ln_gains.T, ln_biases.T], axis=1)
    weights = lax.all_gather(weights, "row", axis=0, tiled=True)

    chosen, ranks, select = slot_layout(expert_ids, experts, cap)
    out_block, ranks = tie(w_out.T, ranks)
    out_block = swap(jnp.broadcast_to(out_block[None], (cols_all, share, width)), "col")
    slots = chosen * cap + ranks
    slots_by_local = ((chosen % local) * rows_all + chosen // local) * cap + ranks
    member = chosen % local
    slots_by_group = [
        jnp.where(
            member // members == g,
            ((chosen // local) * members + member % members) * cap + ranks,
            -1,
        )
        for g in range(local // members)
    ]

    early = min(2, local)
    grad_packed = list(pack(slots_by_local, [cotangent], 0, block_rows, early))
    weights, grad_packed[0], out_block = tie(weights, grad_packed[0], out_block)
    grad_arrived = [send(grad_packed[0])]
    qkv_full = weights[:, : 3 * width]
    router_full = weights[:, 3 * width : 3 * width + experts]
    norms = weights[:, 3 * width + experts :].astype(jnp.float32).T
    gains, biases = norms[0:2], norms[2:4]

    resid_in = tokens.astype(jnp.float32)
    normed_one, inverse_one = layer_stats(resid_in)
    normal_in = (normed_one * gains[0] + biases[0]).astype(jnp.bfloat16)
    projected = jnp.dot(normal_in, qkv_full, preferred_element_type=jnp.float32).astype(jnp.bfloat16)

    count = half // block
    context_a, logsum_a = attend_forward(projected, tuple(range(count)), block)
    full_a = lax.all_gather(context_a, "col", axis=0)
    grad_arrived[0], *grad_packed[1:] = tie(grad_arrived[0], *grad_packed[1:])
    grad_arrived += [send(p) for p in grad_packed[1:]]
    if local > early:
        grad_packed += pack(
            slots_by_local, [cotangent], early * block_rows, block_rows, local - early, [context_a]
        )
    context_b, logsum_b = attend_forward(
        projected, tuple(range(count, 2 * count)), block, grad_packed[-1:]
    )
    context_b, out_block, *grad_arrived[1:] = tie(context_b, out_block, *grad_arrived[1:])
    full_b = lax.all_gather(context_b, "col", axis=0)
    out_full = swap(jnp.broadcast_to(out_block[None], (rows_all, *out_block.shape)), "row")
    out_full, *grad_packed[early:] = tie(out_full, *grad_packed[early:])
    out_full = out_full.transpose(1, 0, 2, 3).reshape(cols_all, depth, width)
    gain, bias = gains[1:2], biases[1:2]
    middle_a, routed_a = middle_pass(full_a, out_full, tokens, 0, gain, bias)
    for e in range(early, local):
        grad_arrived.append(send(grad_packed[e]))
        if e + 1 < local:
            full_b, grad_arrived[e], grad_packed[e + 1], middle_a = tie(
                full_b, grad_arrived[e], grad_packed[e + 1], middle_a
            )
    middle_b, routed_b = middle_pass(full_b, out_full, tokens, half, gain, bias)

    routed = [routed_a, routed_b]
    packed = list(pack(slots_by_local, routed, 0, block_rows, 1))
    if local > 1:
        packed += pack(slots_by_local, routed, block_rows, block_rows, local - 1)
    packed[0], grad_arrived[-1] = tie(packed[0], grad_arrived[-1])

    def route(rows):
        return jnp.dot(rows, router_full, preferred_element_type=jnp.float32)

    logits = jnp.concatenate([route(routed_a), route(routed_b)], axis=0)
    probs = jax.nn.softmax(logits, axis=-1)
    gate = jnp.sum(probs * select, axis=-1, keepdims=True)

    arrived, summed, active, slope, sent = [], [], [], [], []
    for e in range(local):
        arrived.append(send(packed[e]))
        if e + 1 < local:
            packed[e + 1], arrived[e] = tie(packed[e + 1], arrived[e])
        if e:
            then = packed[e + 1] if e + 1 < local else sent[0][0]
            then, summed[e - 1], arrived[e] = tie(then, summed[e - 1], arrived[e])
            summed[e - 1] = lax.psum_scatter(
                summed[e - 1], "col", scatter_dimension=0, tiled=True
            )
            if e + 1 < local:
                packed[e + 1] = then
            else:
                sent[0] = (then, *sent[0][1:])
        made, kept, grads, pair = expert_pass(
            e,
            cap,
            arrived[e],
            grad_arrived[e],
            w_in,
            w_back,
            sent.pop() if e % members else None,
            members,
            cols_all,
            pieces,
            packed[-1:] if e == 0 else summed[e - 3 : e - 2] if e > 2 else [],
        )
        active.append(kept)
        slope.append(grads)
        summed.append(made)
        sent.append(pair)
    summed[-1] = lax.psum_scatter(summed[-1], "col", scatter_dimension=0, tiled=True)

    def place(i):
        return (i % cols_all) * 2 + i // cols_all

    order = [(g, f) for f in range(pieces) for g in range(len(sent))]
    back = {}
    grad_sent = []
    grad_weights = None
    token = None
    row = lax.axis_index("row")

    def weigh(e, waits):
        pick = jnp.arange(experts, dtype=jnp.int32)[None, :] == row * local + e
        return weight_pass(
            e,
            local,
            arrived[e],
            grad_arrived[e],
            router_full,
            pick.astype(jnp.float32),
            active[e],
            slope[e],
            grad_weights,
            waits,
        )

    waits = slope[-1:]
    last = None
    for at, (g, f) in enumerate(order):
        piece = sent[g][f]
        if last is not None:
            piece, last = tie(piece, last)
            back[order[at - 1]] = last
        if at == 1:
            piece, slope[-1] = tie(piece, slope[-1])
        last = swap(piece, "row")
        back[(g, f)] = last
        if g == len(sent) - 1:
            rows = [back[(k, f)].reshape(-1, depth // pieces) for k in range(len(sent))]
            for e in range(f * local // pieces, (f + 1) * local // pieces):
                *grad_weights, token = weigh(e, waits)
                waits = [token]
            whole = unpack(slots_by_group, rows, part, place, waits)
            waits = [whole]
            grad_sent.append(lax.psum_scatter(whole, "col", scatter_dimension=0, tiled=True))

    grad_in, grad_back = grad_weights
    homed = jnp.stack([v.reshape(rows_all, cap, depth // cols_all) for v in summed], axis=1)
    homed, last = tie(homed, last)
    back[order[-1]] = last
    homed = swap(homed, "row")
    returned = unpack(
        [slots], [homed.reshape(experts * cap, depth // cols_all)], part, lambda i: i
    ).astype(jnp.float32)
    columns = depth // cols_all

    def own_columns(values):
        return lax.dynamic_slice_in_dim(values, col * columns, columns, 1)

    middle_cols = jnp.concatenate([own_columns(middle_a), own_columns(middle_b)], axis=0)
    mixed = (middle_cols + gate * returned).astype(jnp.bfloat16)
    grad_gate = jnp.sum(own_columns(cotangent).astype(jnp.float32) * returned, axis=-1)
    grad_gate = swap(grad_gate.reshape(2, cols_all, part).transpose(1, 0, 2), "col")
    grad_gate = jnp.sum(grad_gate, axis=0).reshape(2 * part, 1)

    own_gate, own_probs, own_select = own_of(gate), own_of(probs), own_of(select)
    grad_logits = (grad_gate * own_probs * (own_select - own_gate)).astype(jnp.bfloat16)
    own_routed = own(routed_a, routed_b)
    grad_router = jnp.einsum(
        "td,te->de", own_routed, grad_logits, preferred_element_type=jnp.float32
    )
    grad_y = own_of(cotangent).astype(jnp.float32)
    normed_own, inverse_own = layer_stats(own(middle_a, middle_b))
    grad_sent = jnp.concatenate(grad_sent, axis=1).astype(jnp.float32) * own_gate
    grad_routed = grad_sent + jnp.einsum(
        "te,de->td", grad_logits, router_full, preferred_element_type=jnp.float32
    )
    gain_two = jnp.sum(grad_routed * normed_own, axis=0)
    bias_two = jnp.sum(grad_routed, axis=0)
    grad_middle = grad_y + norm_back(grad_routed, normed_own, inverse_own, gains[1])
    grad_attn = grad_middle.astype(jnp.bfloat16)
    grad_context = jnp.einsum(
        "td,zdc->ztc", grad_attn, out_full, preferred_element_type=jnp.float32
    ).astype(jnp.bfloat16)
    grad_context = swap(grad_context, "col")
    grad_context, mixed = tie(grad_context, mixed)
    steps = relay_steps(mixed, "col")
    grad_context = grad_context.reshape(cols_all, 2, part, width)
    grad_context = grad_context.transpose(1, 0, 2, 3).reshape(2, half, width)


    proj_b, *carried = attend_backward(
        projected, grad_context[1], context_b, logsum_b, block, count
    )
    proj_b, *steps[0] = tie(proj_b, *steps[0])
    proj_a = attend_backward(
        projected, grad_context[0], context_a, logsum_a, block, 0, carried
    )[0]

    def spread(grads):
        made = jnp.einsum("tc,dc->td", grads, qkv_full, preferred_element_type=jnp.float32)
        return lax.psum_scatter(
            made.astype(jnp.bfloat16), "col", scatter_dimension=0, tiled=True
        ).astype(jnp.float32)

    tied = steps[1] if len(steps) > 1 else []
    proj_a, grad_attn, *tied[:] = tie(proj_a, grad_attn, *tied)
    context_own = jnp.concatenate(
        [lax.dynamic_slice_in_dim(v, col * part, part, 1) for v in (full_a, full_b)], axis=1
    )
    grad_out = jnp.einsum("td,ztc->dzc", grad_attn, context_own, preferred_element_type=jnp.float32)
    plane = jnp.concatenate([grad_out.reshape(depth, cols_all * width), grad_router], axis=1)
    plane = swap(plane.astype(jnp.bfloat16).reshape(rows_all, share, -1), "row")
    normal_b, normal_a = spread(proj_b), spread(proj_a)
    normal_a, plane = tie(normal_a, plane)
    for step in steps[2:]:
        normal_b, *step[:] = tie(normal_b, *step)
    grad_qkv = jnp.einsum(
        "td,tc->dc", normal_in[:half], proj_a, preferred_element_type=jnp.float32
    ) + jnp.einsum("td,tc->dc", normal_in[half:], proj_b, preferred_element_type=jnp.float32)

    plane = jnp.sum(plane.astype(jnp.float32), axis=0)
    router_share = plane[:, cols_all * width :].reshape(1, share, experts)
    out_share = plane[:, : cols_all * width].reshape(share, cols_all, width).transpose(1, 0, 2)
    router_share = jnp.broadcast_to(router_share, (cols_all, share, experts))
    plane = jnp.concatenate([out_share, router_share], axis=2).astype(jnp.bfloat16)
    plane = jnp.sum(swap(plane, "col").astype(jnp.float32), axis=0)
    out_share, router_share = plane[:, :width].T, plane[:, width:]

    tokens_own = [lax.dynamic_slice_in_dim(v, col * part, part, 0) for v in (tokens[:half], tokens[half:])]
    normed = [layer_stats(v.astype(jnp.float32)) for v in tokens_own]
    finished = [None, None]
    sums = [jnp.stack([gain_two, bias_two])]
    for c in (1, 0):
        grads = (normal_a, normal_b)[c]
        own_normed, own_inverse = normed[c]
        made = grad_middle[c * part : (c + 1) * part] + norm_back(
            grads, own_normed, own_inverse, gains[0]
        )
        finished[c] = made.astype(jnp.bfloat16)
        sums.append(
            jnp.stack([jnp.sum(grads * own_normed, axis=0), jnp.sum(grads, axis=0)])
        )
        if c:
            moves = relay_steps(finished[1], "col")
            flat = [v for move in moves for v in move]
            normal_a, *flat = tie(normal_a, *flat)
            moves = list(zip(flat[0::2], flat[1::2]))
    grad_tokens = jnp.concatenate(
        [relay_join(finished[1], moves, "col", 0), lax.all_gather(finished[0], "col", axis=0, tiled=True)][::-1],
        axis=0,
    )
    mixed_out = relay_join(mixed, steps, "col", 1)

    small = jnp.concatenate([sums[1] + sums[2], sums[0]], axis=0)
    small = swap(small.reshape(4, rows_all, share).transpose(1, 0, 2), "row")
    small = jnp.sum(small, axis=0)
    small = jnp.sum(swap(jnp.broadcast_to(small[None], (cols_all, 4, share)), "col"), axis=0)
    qkv_share = swap(grad_qkv.astype(jnp.bfloat16).reshape(rows_all, share, -1), "row")
    qkv_share = jnp.sum(qkv_share.astype(jnp.float32), axis=0)
    qkv_share = qkv_share.reshape(share, 3, width).transpose(1, 0, 2)
    return (
        mixed_out,
        grad_tokens,
        qkv_share,
        out_share,
        router_share,
        jnp.stack([small[0], small[2]]),
        small[1],
        small[3],
        grad_in,
        grad_back,
    )


def solution(mesh):
    return jax.shard_map(
        per_device,
        mesh=mesh,
        in_specs=(
            P("row", None),
            P(None, "row", "col"),
            P("col", "row"),
            P("row", None),
            P(None, "row"),
            P(None, "row"),
            P("row", None, "col"),
            P("row", "col", None),
            P("row", None),
            P("row", None),
        ),
        out_specs=(
            P("row", None),
            P("row", None),
            P(None, "row", "col"),
            P("col", "row"),
            P("row", None),
            P(None, "row"),
            P("row"),
            P("row"),
            P("row", None, "col"),
            P("row", "col", None),
        ),
        check_vma=False,
    )
```

```python
import functools, math
import jax, jax.numpy as jnp
from jax import lax
from jax.experimental import pallas as pl
from jax.experimental.pallas import tpu as pltpu
from jax.sharding import PartitionSpec as P

HEAD_DIM = 64
EPSILON = 1e-05
MASKED = -1e30
VMEM = 60 << 20


def params(*kinds):
    return pltpu.CompilerParams(dimension_semantics=kinds or None, vmem_limit_bytes=VMEM)


def cost(flops, moved, special=0):
    return pl.CostEstimate(flops=flops, bytes_accessed=moved, transcendentals=special)


def dot(a, b, dims):
    return lax.dot_general(a, b, (dims, ((), ())), preferred_element_type=jnp.float32)

NN = ((1,), (0,))
NT = ((1,), (1,))
TN = ((0,), (0,))


def pack_body(base, step, each, parts, slots_ref, *rest):
    rows_refs, outs = rest[:parts], rest[-((pl.num_programs(0)) // each) :]
    at = pl.program_id(0)
    made = None
    first = 0
    for rows_ref in rows_refs:
        length = rows_ref.shape[0]
        wanted = base + at * step + lax.broadcasted_iota(jnp.int32, (step, length), 0)
        chosen = jnp.where(slots_ref[:, pl.ds(first, length)] == wanted, 1.0, 0.0)
        more = dot(chosen.astype(jnp.bfloat16), rows_ref[...], NN)
        made = more if made is None else made + more
        first += length
    made = made.astype(jnp.bfloat16)
    for j, out_ref in enumerate(outs):

        @pl.when(at // each == j)
        def _(out_ref=out_ref):
            out_ref[...] = made


def pack(slots, rows, base, count, outs, waits=()):
    length = slots.shape[0]
    width = rows[0].shape[1]
    step = min(512, count)
    each = count // step
    return pl.pallas_call(
        functools.partial(pack_body, base, step, each, len(rows)),
        out_shape=(jax.ShapeDtypeStruct((count, width), jnp.bfloat16),) * outs,
        grid=(each * outs,),
        in_specs=[pl.BlockSpec((1, length), lambda i: (0, 0))]
        + [pl.BlockSpec(r.shape, lambda i: (0, 0)) for r in rows]
        + [pl.BlockSpec(memory_space=pl.ANY)] * len(waits),
        out_specs=tuple(
            pl.BlockSpec((step, width), lambda i, j=j: (jnp.clip(i - j * each, 0, each - 1), 0))
            for j in range(outs)
        ),
        compiler_params=params("arbitrary"),
        name="pack",
        cost_estimate=cost(count * width, count * width),
    )(slots.reshape(1, length), *rows, *waits)


def unpack_body(parts, *refs):
    out_ref = refs[-1]
    step = out_ref.shape[0]
    made = None
    for slots_ref, rows_ref in zip(refs[:parts], refs[parts : 2 * parts]):
        count = rows_ref.shape[0]
        held = lax.broadcasted_iota(jnp.int32, (step, count), 1)
        chosen = jnp.where(slots_ref[...] == held, 1.0, 0.0).astype(jnp.bfloat16)
        more = dot(chosen, rows_ref[...], NN)
        made = more if made is None else made + more
    out_ref[...] = made.astype(out_ref.dtype)


def unpack(slots, rows, step, waits=()):
    length = slots[0].shape[0]
    width = rows[0].shape[1]
    count = sum(r.shape[0] for r in rows)
    return pl.pallas_call(
        functools.partial(unpack_body, len(rows)),
        out_shape=jax.ShapeDtypeStruct((length, width), jnp.bfloat16),
        grid=(length // step,),
        in_specs=[pl.BlockSpec((step, 1), lambda i: (i, 0))] * len(rows)
        + [pl.BlockSpec(r.shape, lambda i: (0, 0)) for r in rows]
        + [pl.BlockSpec(memory_space=pl.ANY)] * len(waits),
        out_specs=pl.BlockSpec((step, width), lambda i: (i, 0)),
        compiler_params=params("arbitrary"),
        name="unpack",
        cost_estimate=cost(2 * count * length * width, 2 * (length + count) * width),
    )(*(at.reshape(length, 1) for at in slots), *rows, *waits)


def middle_body(full_ref, out_ref, tokens_ref, gain_ref, bias_ref, middle_ref, routed_ref):
    total = tokens_ref[...].astype(jnp.float32)
    for z in range(full_ref.shape[0]):
        total = total + dot(full_ref[z], out_ref[z], NT)
    middle_ref[...] = total
    mean = jnp.mean(total, axis=1, keepdims=True)
    centered = total - mean
    inverse = lax.rsqrt(jnp.mean(centered * centered, axis=1, keepdims=True) + EPSILON)
    routed_ref[...] = (centered * inverse * gain_ref[...] + bias_ref[...]).astype(jnp.bfloat16)


def middle_pass(full, out_full, tokens, first, gain, bias):
    cols, rows, width = full.shape
    depth = tokens.shape[1]
    step = min(256, rows)
    row = pl.BlockSpec((1, depth), lambda i: (0, 0))
    return pl.pallas_call(
        middle_body,
        out_shape=(
            jax.ShapeDtypeStruct((rows, depth), jnp.float32),
            jax.ShapeDtypeStruct((rows, depth), jnp.bfloat16),
        ),
        grid=(rows // step,),
        in_specs=[
            pl.BlockSpec((cols, step, width), lambda i: (0, i, 0)),
            pl.BlockSpec((cols, depth, width), lambda i: (0, 0, 0)),
            pl.BlockSpec((step, depth), lambda i: (i + first // step, 0)),
            row,
            row,
        ],
        out_specs=(
            pl.BlockSpec((step, depth), lambda i: (i, 0)),
            pl.BlockSpec((step, depth), lambda i: (i, 0)),
        ),
        compiler_params=params("arbitrary"),
        name="middle_pass",
        cost_estimate=cost(2 * rows * depth * width * cols, 10 * rows * depth),
    )(full, out_full, tokens, gain, bias)


def forward_body(blocks, block, q_ref, k_ref, v_ref, *rest):
    o_ref, lse_ref = rest[-2:]
    width = q_ref.shape[1]
    heads = width // HEAD_DIM
    lane = lax.broadcasted_iota(jnp.int32, (block, width), 1)
    hidden = lax.broadcasted_iota(jnp.int32, (block, block), 1) > lax.broadcasted_iota(
        jnp.int32, (block, block), 0
    )
    for at, i in enumerate(blocks):
        span = (i + 1) * block
        here = pl.ds(at * block, block)
        o_ref[here, :] = jnp.zeros((block, width), o_ref.dtype)

        def one_head(h, carry, here=here, span=span, i=i):
            mine = (lane >= h * HEAD_DIM) & (lane < (h + 1) * HEAD_DIM)
            query = q_ref[pl.ds(i * block, block), :].astype(jnp.float32) * 0.125
            query = jnp.where(mine, query, 0.0).astype(jnp.bfloat16)
            edge = jnp.where(hidden, MASKED, dot(query, k_ref[pl.ds(span - block, block), :], NT))
            peak = jnp.max(edge, axis=1, keepdims=True)
            if i:
                past = dot(query, k_ref[pl.ds(0, span - block), :], NT)
                peak = jnp.maximum(peak, jnp.max(past, axis=1, keepdims=True))
            edge = jnp.exp(edge - peak)
            total = jnp.sum(edge, axis=1, keepdims=True)
            if i:
                past = jnp.exp(past - peak)
                total = total + jnp.sum(past, axis=1, keepdims=True)
            share = 1.0 / total
            mixed = dot((edge * share).astype(jnp.bfloat16), v_ref[pl.ds(span - block, block), :], NN)
            if i:
                mixed = mixed + dot(
                    (past * share).astype(jnp.bfloat16), v_ref[pl.ds(0, span - block), :], NN
                )
            o_ref[here, :] = jnp.where(mine, mixed.astype(o_ref.dtype), o_ref[here, :])
            logsum = jnp.broadcast_to(peak + jnp.log(total), (block, 128))
            lse_ref[pl.ds(h, 1), here] = logsum.T[0:1, :]
            return carry

        lax.fori_loop(0, heads, one_head, 0, unroll=heads)


def attend_forward(projected, blocks, block, waits=()):
    length, triple = projected.shape
    width = triple // 3
    heads = width // HEAD_DIM
    rows = len(blocks) * block
    spec = [pl.BlockSpec((length, width), lambda i, j=j: (0, j)) for j in range(3)]
    return pl.pallas_call(
        functools.partial(forward_body, blocks, block),
        out_shape=(
            jax.ShapeDtypeStruct((rows, width), jnp.bfloat16),
            jax.ShapeDtypeStruct((heads, rows), jnp.float32),
        ),
        grid=(1,),
        in_specs=spec + [pl.BlockSpec(memory_space=pl.ANY)] * len(waits),
        out_specs=(
            pl.BlockSpec((rows, width), lambda i: (0, 0)),
            pl.BlockSpec((heads, rows), lambda i: (0, 0)),
        ),
        compiler_params=params("arbitrary"),
        name="attend_forward",
        cost_estimate=cost(rows * width, rows * width),
    )(projected, projected, projected, *waits)


def backward_body(block, first, given, *refs):
    q_ref, do_ref, o_ref, lse_ref, k_ref, v_ref = refs[:6]
    outs = refs[6 + given :]
    out_ref, p_ref, ds_ref, qm_ref, dom_ref, dk_ref, dv_ref = outs[:1] + outs[-6:]
    width = q_ref.shape[1]
    heads = width // HEAD_DIM
    count = q_ref.shape[0] // block
    lane = lax.broadcasted_iota(jnp.int32, (block, width), 1)
    hidden = lax.broadcasted_iota(jnp.int32, (block, block), 0) > lax.broadcasted_iota(
        jnp.int32, (block, block), 1
    )
    for at in reversed(range(count)):
        i = first + at
        span = (i + 1) * block
        here = pl.ds(at * block, block)

        def one_head(h, carry, here=here, span=span, i=i):
            mine = (lane >= h * HEAD_DIM) & (lane < (h + 1) * HEAD_DIM)
            query = q_ref[here, :].astype(jnp.float32) * 0.125
            query = jnp.where(mine, query, 0.0).astype(jnp.bfloat16)
            grad = jnp.where(mine, do_ref[here, :].astype(jnp.float32), 0.0)
            delta = jnp.sum(grad * o_ref[here, :].astype(jnp.float32), axis=1, keepdims=True)
            delta = jnp.broadcast_to(delta, (block, 128)).T[0:1, :]
            grad = grad.astype(jnp.bfloat16)
            logsum = lse_ref[pl.ds(h, 1), here]
            column = pl.ds(pl.multiple_of(h * block, block), block)
            qm_ref[column, :] = query
            dom_ref[column, :] = grad

            def part(rows, edge):
                scores = dot(k_ref[rows, :], query, NT)
                if edge:
                    scores = jnp.where(hidden, MASKED, scores)
                probs = jnp.exp(scores - logsum)
                p_ref[rows, column] = probs.astype(jnp.bfloat16)
                grad_probs = dot(v_ref[rows, :], grad, NT)
                ds_ref[rows, column] = (probs * (grad_probs - delta)).astype(jnp.bfloat16)

            if i:
                part(pl.ds(0, span - block), False)
            part(pl.ds(span - block, block), True)
            dq = dot(ds_ref[pl.ds(0, span), column], k_ref[pl.ds(0, span), :], TN)
            out_ref[here, pl.ds(0, width)] = jnp.where(
                mine, (dq * 0.125).astype(out_ref.dtype), out_ref[here, pl.ds(0, width)]
            )
            return carry

        lax.fori_loop(0, heads, one_head, 0, unroll=heads)
        new_v = dot(p_ref[pl.ds(0, span), :], dom_ref[...], NN)
        new_k = dot(ds_ref[pl.ds(0, span), :], qm_ref[...], NN)
        if at == count - 1:
            old_k, old_v = (refs[6][...], refs[7][...]) if given > 1 else (0.0, 0.0)
            dv_ref[...] = old_v + new_v
            dk_ref[...] = old_k + new_k
        else:
            dv_ref[pl.ds(0, span), :] += new_v
            dk_ref[pl.ds(0, span), :] += new_k
        low = pl.ds(i * block, block)
        out_ref[here, pl.ds(width, width)] = dk_ref[low, :].astype(out_ref.dtype)
        out_ref[here, pl.ds(2 * width, width)] = dv_ref[low, :].astype(out_ref.dtype)
    if first:
        outs[1][...] = dk_ref[pl.ds(0, first * block), :]
        outs[2][...] = dv_ref[pl.ds(0, first * block), :]


def attend_backward(projected, grad_context, context, logsum, block, first, carried=()):
    rows, width = context.shape
    heads = width // HEAD_DIM
    length = first * block + rows
    half = lambda j: pl.BlockSpec((rows, width), lambda i: (first * block // rows, j))
    own = pl.BlockSpec((rows, width), lambda i: (0, 0))
    low = pl.BlockSpec((first * block, width), lambda i: (0, 0))
    rest = jax.ShapeDtypeStruct((first * block, width), jnp.float32)
    more = bool(first)
    return pl.pallas_call(
        functools.partial(backward_body, block, first, len(carried)),
        out_shape=(jax.ShapeDtypeStruct((rows, 3 * width), jnp.bfloat16),) + (rest,) * (2 * more),
        grid=(1,),
        in_specs=[
            half(0),
            own,
            own,
            pl.BlockSpec((heads, rows), lambda i: (0, 0)),
            pl.BlockSpec((length, width), lambda i: (0, 1)),
            pl.BlockSpec((length, width), lambda i: (0, 2)),
        ]
        + [own] * len(carried),
        out_specs=(pl.BlockSpec((rows, 3 * width), lambda i: (0, 0)),) + (low,) * (2 * more),
        scratch_shapes=[
            pltpu.VMEM((length, heads * block), jnp.bfloat16),
            pltpu.VMEM((length, heads * block), jnp.bfloat16),
            pltpu.VMEM((heads * block, width), jnp.bfloat16),
            pltpu.VMEM((heads * block, width), jnp.bfloat16),
            pltpu.VMEM((length, width), jnp.float32),
            pltpu.VMEM((length, width), jnp.float32),
        ],
        compiler_params=params("arbitrary"),
        name="attend_backward",
        cost_estimate=cost(
            20 * rows * length * width, 16 * length * width, rows * length * heads
        ),
    )(projected, grad_context, context, logsum, projected, projected, *carried)


ROOT = math.sqrt(2.0 / math.pi)
CUBE = 0.044715


def expert_body(given, x_ref, gy_ref, win_ref, wback_ref, *rest):
    out_ref, active_ref, slope_ref, *sent = rest[given:]
    rows, depth = x_ref.shape
    hidden = dot(x_ref[...], win_ref[...], NN)
    square = hidden * hidden
    bent = jnp.tanh(ROOT * hidden * (1.0 + CUBE * square))
    active = (0.5 * hidden * (1.0 + bent)).astype(jnp.bfloat16)
    slope = 0.5 * (1.0 + bent) + 0.5 * hidden * (1.0 - bent * bent) * (
        ROOT * (1.0 + 3.0 * CUBE * square)
    )
    active_ref[...] = active
    parts = out_ref.shape[0]
    wide = depth // parts
    made = dot(active, wback_ref[...], NN).astype(jnp.bfloat16)
    for j in range(parts):
        out_ref[j] = made[:, j * wide : (j + 1) * wide]
    grad_active = dot(gy_ref[...], wback_ref[...], NT)
    grad_hidden = (grad_active * slope).astype(jnp.bfloat16)
    slope_ref[...] = grad_hidden
    back = dot(grad_hidden, win_ref[...], NT).astype(jnp.bfloat16)
    wide = depth // len(sent)
    for j, ref in enumerate(sent):
        ref[...] = back[:, j * wide : (j + 1) * wide].reshape(ref.shape)


def expert_pass(e, cap, x, grad_y, w_in, w_back, sent, members, parts, pieces, waits=()):
    rows, depth = x.shape
    width = w_in.shape[2]
    sources = rows // cap
    step = min(256, rows)
    group = step // cap
    sent = list(sent or [])
    piece = jax.ShapeDtypeStruct((sources, members, cap, depth // pieces), jnp.bfloat16)
    piece_spec = pl.BlockSpec(
        (group, None, cap, depth // pieces), lambda i: (i, e % members, 0, 0)
    )
    made = pl.pallas_call(
        functools.partial(expert_body, len(sent) + len(waits)),
        out_shape=(
            jax.ShapeDtypeStruct((parts, rows, depth // parts), jnp.bfloat16),
            jax.ShapeDtypeStruct((rows, width), jnp.bfloat16),
            jax.ShapeDtypeStruct((rows, width), jnp.bfloat16),
        )
        + (piece,) * pieces,
        grid=(rows // step,),
        in_specs=[
            pl.BlockSpec((step, depth), lambda i: (i, 0)),
            pl.BlockSpec((step, depth), lambda i: (i, 0)),
            pl.BlockSpec((None, depth, width), lambda i: (e, 0, 0)),
            pl.BlockSpec((None, width, depth), lambda i: (e, 0, 0)),
        ]
        + [pl.BlockSpec(memory_space=pl.ANY)] * (len(sent) + len(waits)),
        out_specs=(
            pl.BlockSpec((parts, step, depth // parts), lambda i: (0, i, 0)),
            pl.BlockSpec((step, width), lambda i: (i, 0)),
            pl.BlockSpec((step, width), lambda i: (i, 0)),
        )
        + (piece_spec,) * pieces,
        input_output_aliases={4 + j: 3 + j for j in range(len(sent))},
        compiler_params=params("arbitrary"),
        name="expert_pass",
        cost_estimate=cost(8 * rows * depth * width, 4 * width * depth + 12 * rows * depth, rows * width),
    )(x, grad_y, w_in, w_back, *sent, *waits)
    return made[0], made[1], made[2], made[3:]


def weight_body(given, x_ref, gy_ref, router_ref, pick_ref, active_ref, slope_ref, *rest):
    gin_ref, gback_ref, token_ref, xt_ref, gyg_ref = rest[given:]
    token_ref[...] = jnp.zeros_like(token_ref)
    rows, depth = x_ref.shape

    @pl.when(pl.program_id(0) == 0)
    def _():
        logits = dot(x_ref[...], router_ref[...], NN)
        raised = jnp.exp(logits - jnp.max(logits, axis=1, keepdims=True))
        gate = jnp.sum(raised * pick_ref[...], axis=1, keepdims=True)
        gate = gate / jnp.sum(raised, axis=1, keepdims=True)
        xt_ref[...] = (x_ref[...].astype(jnp.float32) * gate).T.astype(jnp.bfloat16)
        gyg_ref[...] = (gy_ref[...].astype(jnp.float32) * gate).astype(jnp.bfloat16)

    gin_ref[...] = dot(xt_ref[...], slope_ref[...], NN)
    gback_ref[...] = dot(active_ref[...], gyg_ref[...], TN)


def weight_pass(e, local, x, grad_y, router, pick, active, slope, sent, waits=()):
    rows, width = active.shape
    depth = x.shape[1]
    step = min(256, width)
    sent = list(sent or [])
    return pl.pallas_call(
        functools.partial(weight_body, len(sent) + len(waits)),
        out_shape=(
            jax.ShapeDtypeStruct((local, depth, width), jnp.float32),
            jax.ShapeDtypeStruct((local, width, depth), jnp.float32),
            jax.ShapeDtypeStruct((8, 128), jnp.float32),
        ),
        grid=(width // step,),
        in_specs=[
            pl.BlockSpec((rows, depth), lambda i: (0, 0)),
            pl.BlockSpec((rows, depth), lambda i: (0, 0)),
            pl.BlockSpec(router.shape, lambda i: (0, 0)),
            pl.BlockSpec(pick.shape, lambda i: (0, 0)),
            pl.BlockSpec((rows, step), lambda i: (0, i)),
            pl.BlockSpec((rows, step), lambda i: (0, i)),
        ]
        + [pl.BlockSpec(memory_space=pl.ANY)] * (len(sent) + len(waits)),
        out_specs=(
            pl.BlockSpec((None, depth, step), lambda i: (e, 0, i)),
            pl.BlockSpec((None, step, depth), lambda i: (e, i, 0)),
            pl.BlockSpec((8, 128), lambda i: (0, 0)),
        ),
        scratch_shapes=[
            pltpu.VMEM((depth, rows), jnp.bfloat16),
            pltpu.VMEM((rows, depth), jnp.bfloat16),
        ],
        input_output_aliases={6 + j: j for j in range(len(sent))},
        compiler_params=params("arbitrary"),
        name="weight_pass",
        cost_estimate=cost(4 * rows * depth * width, 8 * width * depth + 8 * rows * depth),
    )(x, grad_y, router, pick, active, slope, *sent, *waits)


def swap(blocks, axis):
    return lax.all_to_all(blocks, axis, split_axis=0, concat_axis=0, tiled=True)


def tie(*values):
    return lax.optimization_barrier(values)


def layer_stats(values):
    mean = jnp.mean(values, axis=-1, keepdims=True)
    centered = values - mean
    variance = jnp.mean(centered * centered, axis=-1, keepdims=True)
    inverse = lax.rsqrt(variance + EPSILON)
    return (centered * inverse, inverse)


def norm_back(grad_normed, normed, inverse, gain):
    grad_hat = grad_normed * gain
    centred_grad = grad_hat - jnp.mean(grad_hat, axis=-1, keepdims=True)
    return inverse * (centred_grad - normed * jnp.mean(grad_hat * normed, axis=-1, keepdims=True))


def slot_layout(expert_ids, experts, cap):
    chosen = expert_ids[:, 0]
    length = chosen.shape[0]
    table = chosen[:, None] == jnp.arange(experts, dtype=jnp.int32)[None, :]
    order = jnp.arange(length, dtype=jnp.int32)
    before = (order[:, None] > order[None, :]).astype(jnp.bfloat16)
    counted = jnp.dot(before, table.astype(jnp.bfloat16), preferred_element_type=jnp.float32)
    ranks = jnp.sum(jnp.where(table, counted, 0.0), axis=1).astype(jnp.int32)
    return (chosen, ranks, table.astype(jnp.float32))


def per_device(
    tokens, w_qkv, w_out, w_router, ln_gains, ln_biases, w_in, w_back, expert_ids, cotangent
):
    rows_all, cols_all = lax.axis_size("row"), lax.axis_size("col")
    col = lax.axis_index("col")
    length, depth = tokens.shape
    share = depth // rows_all
    width = w_qkv.shape[2]
    experts = w_router.shape[1]
    local = w_in.shape[0]
    cap = 2 * length // experts
    block_rows = rows_all * cap
    block = min(256, length // 2)
    half = length // 2
    part = length // cols_all
    members = max(1, local // 2)
    pieces = 2

    def own_of(values):
        return lax.dynamic_slice_in_dim(values, col * part, part, 0)

    def own(low, high, axis=0):
        first = lax.dynamic_slice_in_dim(low, col * part, part, axis)
        second = lax.dynamic_slice_in_dim(high, col * part - half, part, axis)
        return jnp.where(col * part < half, first, second)

    def send(packed):
        return swap(packed.reshape(rows_all, cap, depth), "row").reshape(block_rows, depth)

    stacked = w_qkv.transpose(1, 0, 2).reshape(share, 3 * width)
    weights = jnp.concatenate([stacked, w_router, ln_gains.T, ln_biases.T], axis=1)
    weights = lax.all_gather(weights, "row", axis=0, tiled=True)

    chosen, ranks, select = slot_layout(expert_ids, experts, cap)
    out_block, ranks = tie(w_out.T, ranks)
    out_block = swap(jnp.broadcast_to(out_block[None], (cols_all, share, width)), "col")
    slots = chosen * cap + ranks
    slots_by_local = ((chosen % local) * rows_all + chosen // local) * cap + ranks
    member = chosen % local
    slots_by_group = [
        jnp.where(
            member // members == g,
            ((chosen // local) * members + member % members) * cap + ranks,
            -1,
        )
        for g in range(local // members)
    ]

    early = min(2, local)
    grad_packed = list(pack(slots_by_local, [cotangent], 0, block_rows, early))
    weights, grad_packed[0], out_block = tie(weights, grad_packed[0], out_block)
    grad_arrived = [send(grad_packed[0])]
    qkv_full = weights[:, : 3 * width]
    router_full = weights[:, 3 * width : 3 * width + experts]
    norms = weights[:, 3 * width + experts :].astype(jnp.float32).T
    gains, biases = norms[0:2], norms[2:4]

    resid_in = tokens.astype(jnp.float32)
    normed_one, inverse_one = layer_stats(resid_in)
    normal_in = (normed_one * gains[0] + biases[0]).astype(jnp.bfloat16)
    projected = jnp.dot(normal_in, qkv_full, preferred_element_type=jnp.float32).astype(jnp.bfloat16)

    count = half // block
    context_a, logsum_a = attend_forward(projected, tuple(range(count)), block)
    full_a = lax.all_gather(context_a, "col", axis=0)
    grad_arrived[0], *grad_packed[1:] = tie(grad_arrived[0], *grad_packed[1:])
    grad_arrived += [send(p) for p in grad_packed[1:]]
    if local > early:
        grad_packed += pack(
            slots_by_local, [cotangent], early * block_rows, block_rows, local - early, [context_a]
        )
    out_full = lax.all_gather(out_block, "row", axis=1, tiled=True)
    context_b, logsum_b = attend_forward(
        projected, tuple(range(count, 2 * count)), block, [grad_packed[-1], out_full]
    )
    context_b, *both = tie(context_b, *grad_arrived[1:], *grad_packed[early:])
    grad_arrived[1:], grad_packed[early:] = both[: len(grad_arrived) - 1], both[len(grad_arrived) - 1 :]
    full_b = lax.all_gather(context_b, "col", axis=0)
    gain, bias = gains[1:2], biases[1:2]
    middle_a, routed_a = middle_pass(full_a, out_full, tokens, 0, gain, bias)
    full_b, middle_a = tie(full_b, middle_a)
    for e in range(early, local):
        grad_arrived.append(send(grad_packed[e]))
        if e + 1 < local:
            grad_arrived[e], grad_packed[e + 1] = tie(grad_arrived[e], grad_packed[e + 1])
    middle_b, routed_b = middle_pass(full_b, out_full, tokens, half, gain, bias)

    routed = [routed_a, routed_b]
    packed = list(pack(slots_by_local, routed, 0, block_rows, 1))
    if local > 1:
        packed += pack(slots_by_local, routed, block_rows, block_rows, local - 1)
    packed[0], grad_arrived[-1] = tie(packed[0], grad_arrived[-1])

    def route(rows):
        return jnp.dot(rows, router_full, preferred_element_type=jnp.float32)

    logits = jnp.concatenate([route(routed_a), route(routed_b)], axis=0)
    probs = jax.nn.softmax(logits, axis=-1)
    gate = jnp.sum(probs * select, axis=-1, keepdims=True)

    arrived, summed, active, slope, sent = [], [], [], [], []
    for e in range(local):
        arrived.append(send(packed[e]))
        if e + 1 < local:
            packed[e + 1], arrived[e] = tie(packed[e + 1], arrived[e])
        if e:
            then = packed[e + 1] if e + 1 < local else sent[0][0]
            then, summed[e - 1], arrived[e] = tie(then, summed[e - 1], arrived[e])
            summed[e - 1] = lax.psum_scatter(
                summed[e - 1], "col", scatter_dimension=0, tiled=True
            )
            if e + 1 < local:
                packed[e + 1] = then
            else:
                sent[0] = (then, *sent[0][1:])
        made, kept, grads, pair = expert_pass(
            e,
            cap,
            arrived[e],
            grad_arrived[e],
            w_in,
            w_back,
            sent.pop() if e % members else None,
            members,
            cols_all,
            pieces,
            packed[-1:] if e == 0 else summed[e - 3 : e - 2] if e > 2 else [],
        )
        active.append(kept)
        slope.append(grads)
        summed.append(made)
        sent.append(pair)
    summed[-1] = lax.psum_scatter(summed[-1], "col", scatter_dimension=0, tiled=True)

    step = min(256, length)
    order = [(g, f) for f in range(pieces) for g in range(len(sent))]
    back = {}
    grad_sent = []
    grad_weights = None
    token = None
    row = lax.axis_index("row")

    def weigh(e, waits):
        pick = jnp.arange(experts, dtype=jnp.int32)[None, :] == row * local + e
        return weight_pass(
            e,
            local,
            arrived[e],
            grad_arrived[e],
            router_full,
            pick.astype(jnp.float32),
            active[e],
            slope[e],
            grad_weights,
            waits,
        )

    waits = slope[-1:]
    last = None
    for at, (g, f) in enumerate(order):
        piece = sent[g][f]
        if last is not None:
            piece, last = tie(piece, last)
            back[order[at - 1]] = last
        if at == 1:
            piece, slope[-1] = tie(piece, slope[-1])
        last = swap(piece, "row")
        back[(g, f)] = last
        if g == len(sent) - 1:
            rows = [back[(k, f)].reshape(-1, depth // pieces) for k in range(len(sent))]
            for e in range(f * local // pieces, (f + 1) * local // pieces):
                *grad_weights, token = weigh(e, waits)
                waits = [token]
            whole = unpack(slots_by_group, rows, step, waits)
            waits = [whole]
            grad_sent.append(lax.psum_scatter(whole, "col", scatter_dimension=0, tiled=True))

    grad_in, grad_back = grad_weights
    homed = jnp.stack([v.reshape(rows_all, cap, depth // cols_all) for v in summed], axis=1)
    homed, last = tie(homed, last)
    back[order[-1]] = last
    homed = swap(homed, "row")
    returned = unpack(
        [slots], [homed.reshape(experts * cap, depth // cols_all)], step
    ).astype(jnp.float32)
    columns = depth // cols_all

    def own_columns(values):
        return lax.dynamic_slice_in_dim(values, col * columns, columns, 1)

    middle_cols = jnp.concatenate([own_columns(middle_a), own_columns(middle_b)], axis=0)
    mixed = (middle_cols + gate * returned).astype(jnp.bfloat16)
    grad_gate = jnp.sum(own_columns(cotangent).astype(jnp.float32) * returned, axis=-1)
    grad_gate = swap(grad_gate.reshape(cols_all, part), "col")
    grad_gate = jnp.sum(grad_gate, axis=0)[:, None]
    mixed_full = lax.all_gather(mixed, "col", axis=0)

    own_gate, own_probs, own_select = own_of(gate), own_of(probs), own_of(select)
    grad_logits = (grad_gate * own_probs * (own_select - own_gate)).astype(jnp.bfloat16)
    own_routed = own(routed_a, routed_b)
    grad_router = jnp.einsum(
        "td,te->de", own_routed, grad_logits, preferred_element_type=jnp.float32
    )
    grad_y = own_of(cotangent).astype(jnp.float32)
    normed_own, inverse_own = layer_stats(own(middle_a, middle_b))
    grad_sent = jnp.concatenate(grad_sent, axis=1).astype(jnp.float32) * own_gate
    grad_routed = grad_sent + jnp.einsum(
        "te,de->td", grad_logits, router_full, preferred_element_type=jnp.float32
    )
    gain_two = jnp.sum(grad_routed * normed_own, axis=0)
    bias_two = jnp.sum(grad_routed, axis=0)
    grad_middle = grad_y + norm_back(grad_routed, normed_own, inverse_own, gains[1])
    grad_attn = grad_middle.astype(jnp.bfloat16)
    grad_context = jnp.einsum(
        "td,zdc->ztc", grad_attn, out_full, preferred_element_type=jnp.float32
    ).astype(jnp.bfloat16)
    grad_context = swap(grad_context, "col")
    grad_context = grad_context.reshape(length, width)
    context = jnp.concatenate([context_a, context_b], axis=0)
    logsum = jnp.concatenate([logsum_a, logsum_b], axis=1)
    grad_proj = attend_backward(projected, grad_context, context, logsum, block, 0)[0]
    grad_proj, grad_attn, mixed_full = tie(grad_proj, grad_attn, mixed_full)

    def spread(grads):
        made = jnp.einsum("tc,dc->td", grads, qkv_full, preferred_element_type=jnp.float32)
        return lax.psum_scatter(
            made.astype(jnp.bfloat16), "col", scatter_dimension=0, tiled=True
        ).astype(jnp.float32)

    grad_normal = spread(grad_proj)
    context_own = own(full_a, full_b, 1)
    grad_out = jnp.einsum("td,ztc->dzc", grad_attn, context_own, preferred_element_type=jnp.float32)
    plane = jnp.concatenate([grad_out.reshape(depth, cols_all * width), grad_router], axis=1)
    plane = swap(plane.astype(jnp.bfloat16).reshape(rows_all, share, -1), "row")
    mixed_out = mixed_full.transpose(1, 0, 2).reshape(length, depth)
    grad_qkv = jnp.einsum("td,tc->dc", normal_in, grad_proj, preferred_element_type=jnp.float32)
    grad_normal, plane, mixed_out, grad_qkv = tie(grad_normal, plane, mixed_out, grad_qkv)

    plane = jnp.sum(plane.astype(jnp.float32), axis=0)
    router_share = plane[:, cols_all * width :].reshape(1, share, experts)
    out_share = plane[:, : cols_all * width].reshape(share, cols_all, width).transpose(1, 0, 2)
    router_share = jnp.broadcast_to(router_share, (cols_all, share, experts))
    plane = jnp.concatenate([out_share, router_share], axis=2).astype(jnp.bfloat16)
    plane = jnp.sum(swap(plane, "col").astype(jnp.float32), axis=0)
    out_share, router_share = plane[:, :width].T, plane[:, width:]

    own_normed, own_inverse = layer_stats(own_of(tokens).astype(jnp.float32))
    grad_tokens = (
        grad_middle + norm_back(grad_normal, own_normed, own_inverse, gains[0])
    ).astype(jnp.bfloat16)
    grad_tokens = lax.all_gather(grad_tokens, "col", axis=0, tiled=True)
    small = [
        jnp.sum(grad_normal * own_normed, axis=0),
        jnp.sum(grad_normal, axis=0),
        gain_two,
        bias_two,
    ]
    small = swap(jnp.stack(small).reshape(4, rows_all, share).transpose(1, 0, 2), "row")
    small = jnp.sum(small, axis=0)
    small = jnp.sum(swap(jnp.broadcast_to(small[None], (cols_all, 4, share)), "col"), axis=0)
    qkv_share = swap(grad_qkv.astype(jnp.bfloat16).reshape(rows_all, share, -1), "row")
    qkv_share = jnp.sum(qkv_share.astype(jnp.float32), axis=0)
    qkv_share = qkv_share.reshape(share, 3, width).transpose(1, 0, 2)
    return (
        mixed_out,
        grad_tokens,
        qkv_share,
        out_share,
        router_share,
        jnp.stack([small[0], small[2]]),
        small[1],
        small[3],
        grad_in,
        grad_back,
    )


def solution(mesh):
    return jax.shard_map(
        per_device,
        mesh=mesh,
        in_specs=(
            P("row", None),
            P(None, "row", "col"),
            P("col", "row"),
            P("row", None),
            P(None, "row"),
            P(None, "row"),
            P("row", None, "col"),
            P("row", "col", None),
            P("row", None),
            P("row", None),
        ),
        out_specs=(
            P("row", None),
            P("row", None),
            P(None, "row", "col"),
            P("col", "row"),
            P("row", None),
            P(None, "row"),
            P("row"),
            P("row"),
            P("row", None, "col"),
            P("row", "col", None),
        ),
        check_vma=False,
    )
```

```python
import functools, math
import jax, jax.numpy as jnp
from jax import lax
from jax.experimental import pallas as pl
from jax.experimental.pallas import tpu as pltpu
from jax.sharding import PartitionSpec as P

HEAD_DIM = 64
EPSILON = 1e-05
MASKED = -1e30
VMEM = 60 << 20


def params(*kinds):
    return pltpu.CompilerParams(dimension_semantics=kinds or None, vmem_limit_bytes=VMEM)


def cost(flops, moved, special=0):
    return pl.CostEstimate(flops=flops, bytes_accessed=moved, transcendentals=special)


def dot(a, b, dims):
    return lax.dot_general(a, b, (dims, ((), ())), preferred_element_type=jnp.float32)

NN = ((1,), (0,))
NT = ((1,), (1,))
TN = ((0,), (0,))


def pack_body(base, step, each, parts, slots_ref, *rest):
    rows_refs, outs = rest[:parts], rest[-((pl.num_programs(0)) // each) :]
    at = pl.program_id(0)
    made = None
    first = 0
    for rows_ref in rows_refs:
        length = rows_ref.shape[0]
        wanted = base + at * step + lax.broadcasted_iota(jnp.int32, (step, length), 0)
        chosen = jnp.where(slots_ref[:, pl.ds(first, length)] == wanted, 1.0, 0.0)
        more = dot(chosen.astype(jnp.bfloat16), rows_ref[...], NN)
        made = more if made is None else made + more
        first += length
    made = made.astype(jnp.bfloat16)
    for j, out_ref in enumerate(outs):

        @pl.when(at // each == j)
        def _(out_ref=out_ref):
            out_ref[...] = made


def pack(slots, rows, base, count, outs, waits=()):
    length = slots.shape[0]
    width = rows[0].shape[1]
    step = min(512, count)
    each = count // step
    return pl.pallas_call(
        functools.partial(pack_body, base, step, each, len(rows)),
        out_shape=(jax.ShapeDtypeStruct((count, width), jnp.bfloat16),) * outs,
        grid=(each * outs,),
        in_specs=[pl.BlockSpec((1, length), lambda i: (0, 0))]
        + [pl.BlockSpec(r.shape, lambda i: (0, 0)) for r in rows]
        + [pl.BlockSpec(memory_space=pl.ANY)] * len(waits),
        out_specs=tuple(
            pl.BlockSpec((step, width), lambda i, j=j: (jnp.clip(i - j * each, 0, each - 1), 0))
            for j in range(outs)
        ),
        compiler_params=params("arbitrary"),
        name="pack",
        cost_estimate=cost(count * width, count * width),
    )(slots.reshape(1, length), *rows, *waits)


def unpack_body(parts, *refs):
    out_ref = refs[-1]
    step = out_ref.shape[0]
    made = None
    for slots_ref, rows_ref in zip(refs[:parts], refs[parts : 2 * parts]):
        count = rows_ref.shape[0]
        held = lax.broadcasted_iota(jnp.int32, (step, count), 1)
        chosen = jnp.where(slots_ref[...] == held, 1.0, 0.0).astype(jnp.bfloat16)
        more = dot(chosen, rows_ref[...], NN)
        made = more if made is None else made + more
    out_ref[...] = made.astype(out_ref.dtype)


def unpack(slots, rows, step, waits=()):
    length = slots[0].shape[0]
    width = rows[0].shape[1]
    count = sum(r.shape[0] for r in rows)
    return pl.pallas_call(
        functools.partial(unpack_body, len(rows)),
        out_shape=jax.ShapeDtypeStruct((length, width), jnp.bfloat16),
        grid=(length // step,),
        in_specs=[pl.BlockSpec((step, 1), lambda i: (i, 0))] * len(rows)
        + [pl.BlockSpec(r.shape, lambda i: (0, 0)) for r in rows]
        + [pl.BlockSpec(memory_space=pl.ANY)] * len(waits),
        out_specs=pl.BlockSpec((step, width), lambda i: (i, 0)),
        compiler_params=params("arbitrary"),
        name="unpack",
        cost_estimate=cost(2 * count * length * width, 2 * (length + count) * width),
    )(*(at.reshape(length, 1) for at in slots), *rows, *waits)


def middle_body(full_ref, out_ref, tokens_ref, gain_ref, bias_ref, middle_ref, routed_ref):
    total = tokens_ref[...].astype(jnp.float32)
    for z in range(full_ref.shape[0]):
        total = total + dot(full_ref[z], out_ref[z], NT)
    middle_ref[...] = total
    mean = jnp.mean(total, axis=1, keepdims=True)
    centered = total - mean
    inverse = lax.rsqrt(jnp.mean(centered * centered, axis=1, keepdims=True) + EPSILON)
    routed_ref[...] = (centered * inverse * gain_ref[...] + bias_ref[...]).astype(jnp.bfloat16)


def middle_pass(full, out_full, tokens, first, gain, bias):
    cols, rows, width = full.shape
    depth = tokens.shape[1]
    step = min(256, rows)
    row = pl.BlockSpec((1, depth), lambda i: (0, 0))
    return pl.pallas_call(
        middle_body,
        out_shape=(
            jax.ShapeDtypeStruct((rows, depth), jnp.float32),
            jax.ShapeDtypeStruct((rows, depth), jnp.bfloat16),
        ),
        grid=(rows // step,),
        in_specs=[
            pl.BlockSpec((cols, step, width), lambda i: (0, i, 0)),
            pl.BlockSpec((cols, depth, width), lambda i: (0, 0, 0)),
            pl.BlockSpec((step, depth), lambda i: (i + first // step, 0)),
            row,
            row,
        ],
        out_specs=(
            pl.BlockSpec((step, depth), lambda i: (i, 0)),
            pl.BlockSpec((step, depth), lambda i: (i, 0)),
        ),
        compiler_params=params("arbitrary"),
        name="middle_pass",
        cost_estimate=cost(2 * rows * depth * width * cols, 10 * rows * depth),
    )(full, out_full, tokens, gain, bias)


def forward_body(blocks, block, q_ref, k_ref, v_ref, *rest):
    o_ref, lse_ref = rest[-2:]
    width = q_ref.shape[1]
    heads = width // HEAD_DIM
    lane = lax.broadcasted_iota(jnp.int32, (block, width), 1)
    hidden = lax.broadcasted_iota(jnp.int32, (block, block), 1) > lax.broadcasted_iota(
        jnp.int32, (block, block), 0
    )
    for at, i in enumerate(blocks):
        span = (i + 1) * block
        here = pl.ds(at * block, block)
        o_ref[here, :] = jnp.zeros((block, width), o_ref.dtype)

        def one_head(h, carry, here=here, span=span, i=i):
            mine = (lane >= h * HEAD_DIM) & (lane < (h + 1) * HEAD_DIM)
            query = q_ref[pl.ds(i * block, block), :].astype(jnp.float32) * 0.125
            query = jnp.where(mine, query, 0.0).astype(jnp.bfloat16)
            edge = jnp.where(hidden, MASKED, dot(query, k_ref[pl.ds(span - block, block), :], NT))
            peak = jnp.max(edge, axis=1, keepdims=True)
            if i:
                past = dot(query, k_ref[pl.ds(0, span - block), :], NT)
                peak = jnp.maximum(peak, jnp.max(past, axis=1, keepdims=True))
            edge = jnp.exp(edge - peak)
            total = jnp.sum(edge, axis=1, keepdims=True)
            if i:
                past = jnp.exp(past - peak)
                total = total + jnp.sum(past, axis=1, keepdims=True)
            share = 1.0 / total
            mixed = dot((edge * share).astype(jnp.bfloat16), v_ref[pl.ds(span - block, block), :], NN)
            if i:
                mixed = mixed + dot(
                    (past * share).astype(jnp.bfloat16), v_ref[pl.ds(0, span - block), :], NN
                )
            o_ref[here, :] = jnp.where(mine, mixed.astype(o_ref.dtype), o_ref[here, :])
            logsum = jnp.broadcast_to(peak + jnp.log(total), (block, 128))
            lse_ref[pl.ds(h, 1), here] = logsum.T[0:1, :]
            return carry

        lax.fori_loop(0, heads, one_head, 0, unroll=heads)


def attend_forward(projected, blocks, block, waits=()):
    length, triple = projected.shape
    width = triple // 3
    heads = width // HEAD_DIM
    rows = len(blocks) * block
    spec = [pl.BlockSpec((length, width), lambda i, j=j: (0, j)) for j in range(3)]
    return pl.pallas_call(
        functools.partial(forward_body, blocks, block),
        out_shape=(
            jax.ShapeDtypeStruct((rows, width), jnp.bfloat16),
            jax.ShapeDtypeStruct((heads, rows), jnp.float32),
        ),
        grid=(1,),
        in_specs=spec + [pl.BlockSpec(memory_space=pl.ANY)] * len(waits),
        out_specs=(
            pl.BlockSpec((rows, width), lambda i: (0, 0)),
            pl.BlockSpec((heads, rows), lambda i: (0, 0)),
        ),
        compiler_params=params("arbitrary"),
        name="attend_forward",
        cost_estimate=cost(rows * width, rows * width),
    )(projected, projected, projected, *waits)


def backward_body(block, first, given, *refs):
    q_ref, do_ref, o_ref, lse_ref, k_ref, v_ref = refs[:6]
    outs = refs[6 + given :]
    out_ref, p_ref, ds_ref, qm_ref, dom_ref, dk_ref, dv_ref = outs[:1] + outs[-6:]
    width = q_ref.shape[1]
    heads = width // HEAD_DIM
    count = q_ref.shape[0] // block
    lane = lax.broadcasted_iota(jnp.int32, (block, width), 1)
    hidden = lax.broadcasted_iota(jnp.int32, (block, block), 0) > lax.broadcasted_iota(
        jnp.int32, (block, block), 1
    )
    for at in reversed(range(count)):
        i = first + at
        span = (i + 1) * block
        here = pl.ds(at * block, block)

        def one_head(h, carry, here=here, span=span, i=i):
            mine = (lane >= h * HEAD_DIM) & (lane < (h + 1) * HEAD_DIM)
            query = q_ref[here, :].astype(jnp.float32) * 0.125
            query = jnp.where(mine, query, 0.0).astype(jnp.bfloat16)
            grad = jnp.where(mine, do_ref[here, :].astype(jnp.float32), 0.0)
            delta = jnp.sum(grad * o_ref[here, :].astype(jnp.float32), axis=1, keepdims=True)
            delta = jnp.broadcast_to(delta, (block, 128)).T[0:1, :]
            grad = grad.astype(jnp.bfloat16)
            logsum = lse_ref[pl.ds(h, 1), here]
            column = pl.ds(pl.multiple_of(h * block, block), block)
            qm_ref[column, :] = query
            dom_ref[column, :] = grad

            def part(rows, edge):
                scores = dot(k_ref[rows, :], query, NT)
                if edge:
                    scores = jnp.where(hidden, MASKED, scores)
                probs = jnp.exp(scores - logsum)
                p_ref[rows, column] = probs.astype(jnp.bfloat16)
                grad_probs = dot(v_ref[rows, :], grad, NT)
                ds_ref[rows, column] = (probs * (grad_probs - delta)).astype(jnp.bfloat16)

            if i:
                part(pl.ds(0, span - block), False)
            part(pl.ds(span - block, block), True)
            dq = dot(ds_ref[pl.ds(0, span), column], k_ref[pl.ds(0, span), :], TN)
            out_ref[here, pl.ds(0, width)] = jnp.where(
                mine, (dq * 0.125).astype(out_ref.dtype), out_ref[here, pl.ds(0, width)]
            )
            return carry

        lax.fori_loop(0, heads, one_head, 0, unroll=heads)
        new_v = dot(p_ref[pl.ds(0, span), :], dom_ref[...], NN)
        new_k = dot(ds_ref[pl.ds(0, span), :], qm_ref[...], NN)
        if at == count - 1:
            old_k, old_v = (refs[6][...], refs[7][...]) if given > 1 else (0.0, 0.0)
            dv_ref[...] = old_v + new_v
            dk_ref[...] = old_k + new_k
        else:
            dv_ref[pl.ds(0, span), :] += new_v
            dk_ref[pl.ds(0, span), :] += new_k
        low = pl.ds(i * block, block)
        out_ref[here, pl.ds(width, width)] = dk_ref[low, :].astype(out_ref.dtype)
        out_ref[here, pl.ds(2 * width, width)] = dv_ref[low, :].astype(out_ref.dtype)
    if first:
        outs[1][...] = dk_ref[pl.ds(0, first * block), :]
        outs[2][...] = dv_ref[pl.ds(0, first * block), :]


def attend_backward(projected, grad_context, context, logsum, block, first, carried=()):
    rows, width = context.shape
    heads = width // HEAD_DIM
    length = first * block + rows
    half = lambda j: pl.BlockSpec((rows, width), lambda i: (first * block // rows, j))
    own = pl.BlockSpec((rows, width), lambda i: (0, 0))
    low = pl.BlockSpec((first * block, width), lambda i: (0, 0))
    rest = jax.ShapeDtypeStruct((first * block, width), jnp.float32)
    more = bool(first)
    return pl.pallas_call(
        functools.partial(backward_body, block, first, len(carried)),
        out_shape=(jax.ShapeDtypeStruct((rows, 3 * width), jnp.bfloat16),) + (rest,) * (2 * more),
        grid=(1,),
        in_specs=[
            half(0),
            own,
            own,
            pl.BlockSpec((heads, rows), lambda i: (0, 0)),
            pl.BlockSpec((length, width), lambda i: (0, 1)),
            pl.BlockSpec((length, width), lambda i: (0, 2)),
        ]
        + [own] * len(carried),
        out_specs=(pl.BlockSpec((rows, 3 * width), lambda i: (0, 0)),) + (low,) * (2 * more),
        scratch_shapes=[
            pltpu.VMEM((length, heads * block), jnp.bfloat16),
            pltpu.VMEM((length, heads * block), jnp.bfloat16),
            pltpu.VMEM((heads * block, width), jnp.bfloat16),
            pltpu.VMEM((heads * block, width), jnp.bfloat16),
            pltpu.VMEM((length, width), jnp.float32),
            pltpu.VMEM((length, width), jnp.float32),
        ],
        compiler_params=params("arbitrary"),
        name="attend_backward",
        cost_estimate=cost(
            20 * rows * length * width, 16 * length * width, rows * length * heads
        ),
    )(projected, grad_context, context, logsum, projected, projected, *carried)


ROOT = math.sqrt(2.0 / math.pi)
CUBE = 0.044715


def expert_body(given, x_ref, gy_ref, win_ref, wback_ref, *rest):
    out_ref, active_ref, slope_ref, *sent = rest[given:]
    rows, depth = x_ref.shape
    hidden = dot(x_ref[...], win_ref[...], NN)
    square = hidden * hidden
    bent = jnp.tanh(ROOT * hidden * (1.0 + CUBE * square))
    active = (0.5 * hidden * (1.0 + bent)).astype(jnp.bfloat16)
    slope = 0.5 * (1.0 + bent) + 0.5 * hidden * (1.0 - bent * bent) * (
        ROOT * (1.0 + 3.0 * CUBE * square)
    )
    active_ref[...] = active.reshape(active_ref.shape)
    parts = out_ref.shape[0]
    wide = depth // parts
    made = dot(active, wback_ref[...], NN).astype(jnp.bfloat16)
    for j in range(parts):
        out_ref[j] = made[:, j * wide : (j + 1) * wide]
    grad_active = dot(gy_ref[...].reshape(rows, depth), wback_ref[...], NT)
    grad_hidden = (grad_active * slope).astype(jnp.bfloat16)
    slope_ref[...] = grad_hidden.reshape(slope_ref.shape)
    back = dot(grad_hidden, win_ref[...], NT).astype(jnp.bfloat16)
    wide = depth // len(sent)
    for j, ref in enumerate(sent):
        ref[...] = back[:, j * wide : (j + 1) * wide].reshape(ref.shape)


def expert_pass(chunk, x, grad_y, w_in, w_back, kept, sent, members, parts, pieces, waits=()):
    e, low, size = chunk
    sources, cap, depth = grad_y.shape
    rows = sources * size
    width = w_in.shape[2]
    step = min(256, rows)
    group = step // size
    at = low // size
    given = [*kept, *sent]
    aliases = {4 + j: (1 if kept else 3) + j for j in range(len(given))}
    keep = jax.ShapeDtypeStruct((sources, cap, width), jnp.bfloat16)
    keep_spec = pl.BlockSpec((group, size, width), lambda i: (i, at, 0))
    piece = jax.ShapeDtypeStruct((sources, members, cap, depth // pieces), jnp.bfloat16)
    piece_spec = pl.BlockSpec(
        (group, None, size, depth // pieces), lambda i: (i, e % members, at, 0)
    )
    made = pl.pallas_call(
        functools.partial(expert_body, len(given) + len(waits)),
        out_shape=(jax.ShapeDtypeStruct((parts, rows, depth // parts), jnp.bfloat16), keep, keep)
        + (piece,) * pieces,
        grid=(rows // step,),
        in_specs=[
            pl.BlockSpec((step, depth), lambda i: (i, 0)),
            pl.BlockSpec((group, size, depth), lambda i: (i, at, 0)),
            pl.BlockSpec((None, depth, width), lambda i: (e, 0, 0)),
            pl.BlockSpec((None, width, depth), lambda i: (e, 0, 0)),
        ]
        + [pl.BlockSpec(memory_space=pl.ANY)] * (len(given) + len(waits)),
        out_specs=(
            pl.BlockSpec((parts, step, depth // parts), lambda i: (0, i, 0)),
            keep_spec,
            keep_spec,
        )
        + (piece_spec,) * pieces,
        input_output_aliases=aliases,
        compiler_params=params("arbitrary"),
        name="expert_pass",
        cost_estimate=cost(
            8 * rows * depth * width, 4 * width * depth + 12 * rows * depth, rows * width
        ),
    )(x, grad_y, w_in, w_back, *given, *waits)
    return made[0], made[1:3], list(made[3:])


def weight_body(given, x_ref, gy_ref, router_ref, pick_ref, active_ref, slope_ref, *rest):
    gin_ref, gback_ref, token_ref, xt_ref, gyg_ref = rest[given:]
    token_ref[...] = jnp.zeros_like(token_ref)
    rows, depth = x_ref.shape

    @pl.when(pl.program_id(0) == 0)
    def _():
        logits = dot(x_ref[...], router_ref[...], NN)
        raised = jnp.exp(logits - jnp.max(logits, axis=1, keepdims=True))
        gate = jnp.sum(raised * pick_ref[...], axis=1, keepdims=True)
        gate = gate / jnp.sum(raised, axis=1, keepdims=True)
        xt_ref[...] = (x_ref[...].astype(jnp.float32) * gate).T.astype(jnp.bfloat16)
        gyg_ref[...] = (gy_ref[...].astype(jnp.float32) * gate).astype(jnp.bfloat16)

    gin_ref[...] = dot(xt_ref[...], slope_ref[...], NN)
    gback_ref[...] = dot(active_ref[...], gyg_ref[...], TN)


def weight_pass(e, local, x, grad_y, router, pick, active, slope, sent, waits=()):
    rows, width = active.shape
    depth = x.shape[1]
    step = min(256, width)
    sent = list(sent or [])
    return pl.pallas_call(
        functools.partial(weight_body, len(sent) + len(waits)),
        out_shape=(
            jax.ShapeDtypeStruct((local, depth, width), jnp.float32),
            jax.ShapeDtypeStruct((local, width, depth), jnp.float32),
            jax.ShapeDtypeStruct((8, 128), jnp.float32),
        ),
        grid=(width // step,),
        in_specs=[
            pl.BlockSpec((rows, depth), lambda i: (0, 0)),
            pl.BlockSpec((rows, depth), lambda i: (0, 0)),
            pl.BlockSpec(router.shape, lambda i: (0, 0)),
            pl.BlockSpec(pick.shape, lambda i: (0, 0)),
            pl.BlockSpec((rows, step), lambda i: (0, i)),
            pl.BlockSpec((rows, step), lambda i: (0, i)),
        ]
        + [pl.BlockSpec(memory_space=pl.ANY)] * (len(sent) + len(waits)),
        out_specs=(
            pl.BlockSpec((None, depth, step), lambda i: (e, 0, i)),
            pl.BlockSpec((None, step, depth), lambda i: (e, i, 0)),
            pl.BlockSpec((8, 128), lambda i: (0, 0)),
        ),
        scratch_shapes=[
            pltpu.VMEM((depth, rows), jnp.bfloat16),
            pltpu.VMEM((rows, depth), jnp.bfloat16),
        ],
        input_output_aliases={6 + j: j for j in range(len(sent))},
        compiler_params=params("arbitrary"),
        name="weight_pass",
        cost_estimate=cost(4 * rows * depth * width, 8 * width * depth + 8 * rows * depth),
    )(x, grad_y, router, pick, active, slope, *sent, *waits)


def swap(blocks, axis):
    return lax.all_to_all(blocks, axis, split_axis=0, concat_axis=0, tiled=True)


def tie(*values):
    return lax.optimization_barrier(values)


def row_stats(values):
    mean = jnp.mean(values, axis=-1, keepdims=True)
    centered = values - mean
    variance = jnp.mean(centered * centered, axis=-1, keepdims=True)
    return (mean, lax.rsqrt(variance + EPSILON))


def layer_stats(values):
    mean = jnp.mean(values, axis=-1, keepdims=True)
    centered = values - mean
    variance = jnp.mean(centered * centered, axis=-1, keepdims=True)
    inverse = lax.rsqrt(variance + EPSILON)
    return (centered * inverse, inverse)


def norm_back(grad_normed, normed, inverse, gain):
    grad_hat = grad_normed * gain
    centred_grad = grad_hat - jnp.mean(grad_hat, axis=-1, keepdims=True)
    return inverse * (centred_grad - normed * jnp.mean(grad_hat * normed, axis=-1, keepdims=True))


def slot_layout(expert_ids, experts, cap):
    chosen = expert_ids[:, 0]
    length = chosen.shape[0]
    table = chosen[:, None] == jnp.arange(experts, dtype=jnp.int32)[None, :]
    order = jnp.arange(length, dtype=jnp.int32)
    before = (order[:, None] > order[None, :]).astype(jnp.bfloat16)
    counted = jnp.dot(before, table.astype(jnp.bfloat16), preferred_element_type=jnp.float32)
    ranks = jnp.sum(jnp.where(table, counted, 0.0), axis=1).astype(jnp.int32)
    return (chosen, ranks, table.astype(jnp.float32))


def per_device(
    tokens, w_qkv, w_out, w_router, ln_gains, ln_biases, w_in, w_back, expert_ids, cotangent
):
    rows_all, cols_all = lax.axis_size("row"), lax.axis_size("col")
    col = lax.axis_index("col")
    length, depth = tokens.shape
    share = depth // rows_all
    width = w_qkv.shape[2]
    experts = w_router.shape[1]
    local = w_in.shape[0]
    cap = 2 * length // experts
    block_rows = rows_all * cap
    block = min(256, length // 2)
    half = length // 2
    part = length // cols_all
    members = max(1, local // 2)
    pieces = 2

    def own_of(values):
        return lax.dynamic_slice_in_dim(values, col * part, part, 0)

    def own(low, high, axis=0):
        first = lax.dynamic_slice_in_dim(low, col * part, part, axis)
        second = lax.dynamic_slice_in_dim(high, col * part - half, part, axis)
        return jnp.where(col * part < half, first, second)

    def send(packed):
        return swap(packed.reshape(rows_all, cap, depth), "row").reshape(block_rows, depth)

    stacked = w_qkv.transpose(1, 0, 2).reshape(share, 3 * width)
    weights = jnp.concatenate([stacked, w_router, ln_gains.T, ln_biases.T], axis=1)
    weights = lax.all_gather(weights, "row", axis=0, tiled=True)
    mean_one, inverse_one = row_stats(tokens.astype(jnp.float32))

    chosen, ranks, select = slot_layout(expert_ids, experts, cap)
    out_block, ranks = tie(w_out.T, ranks)
    out_block = swap(jnp.broadcast_to(out_block[None], (cols_all, share, width)), "col")
    slots = chosen * cap + ranks
    slots_by_local = ((chosen % local) * rows_all + chosen // local) * cap + ranks
    member = chosen % local
    slots_by_group = [
        jnp.where(
            member // members == g,
            ((chosen // local) * members + member % members) * cap + ranks,
            -1,
        )
        for g in range(local // members)
    ]

    early = min(2, local)
    grad_packed = list(pack(slots_by_local, [cotangent], 0, block_rows, early))
    weights, grad_packed[0], out_block, mean_one, inverse_one = tie(
        weights, grad_packed[0], out_block, mean_one, inverse_one
    )
    qkv_full = weights[:, : 3 * width]
    router_full = weights[:, 3 * width : 3 * width + experts]
    norms = weights[:, 3 * width + experts :].astype(jnp.float32).T
    gains, biases = norms[0:2], norms[2:4]

    resid_in = tokens.astype(jnp.float32)
    normed_one = (resid_in - mean_one) * inverse_one
    normal_in = (normed_one * gains[0] + biases[0]).astype(jnp.bfloat16)
    projected = jnp.dot(normal_in, qkv_full, preferred_element_type=jnp.float32).astype(jnp.bfloat16)

    count = half // block
    context_a, logsum_a = attend_forward(projected, tuple(range(count)), block)
    context_a, grad_packed[0] = tie(context_a, grad_packed[0])
    full_a = lax.all_gather(context_a, "col", axis=0)
    grad_arrived = [send(grad_packed[0])]
    later = [context_a]
    if local > early:
        later = pack(
            slots_by_local, [cotangent], early * block_rows, block_rows, local - early, later
        )
        grad_packed += later
    grad_arrived[0], *grad_packed[1:] = tie(grad_arrived[0], *grad_packed[1:])
    grad_arrived += [send(p) for p in grad_packed[1:early]]
    out_full = lax.all_gather(out_block, "row", axis=1, tiled=True)
    context_b, logsum_b = attend_forward(
        projected, tuple(range(count, 2 * count)), block, [later[-1], out_full]
    )
    context_b, *both = tie(context_b, *grad_arrived[1:], *grad_packed[early:])
    grad_arrived[1:], grad_packed[early:] = both[: len(grad_arrived) - 1], both[len(grad_arrived) - 1 :]
    full_b = lax.all_gather(context_b, "col", axis=0)
    gain, bias = gains[1:2], biases[1:2]
    middle_a, routed_a = middle_pass(full_a, out_full, tokens, 0, gain, bias)
    full_b, middle_a = tie(full_b, middle_a)
    for e in range(early, local):
        grad_arrived.append(send(grad_packed[e]))
        if e + 1 < local:
            grad_arrived[e], grad_packed[e + 1] = tie(grad_arrived[e], grad_packed[e + 1])
    middle_b, routed_b = middle_pass(full_b, out_full, tokens, half, gain, bias)

    routed = [routed_a, routed_b]
    short = cap // 2
    chunks = [(0, 0, short), (0, short, short)] + [(e, 0, cap) for e in range(1, local)]
    split = (ranks // short * rows_all + chosen // local) * short + ranks % short
    slots_by_chunk = jnp.where(chosen % local == 0, split, slots_by_local)

    def pack_chunk(k, waits):
        e, low, size = chunks[k]
        base = (e * cap + low) * rows_all
        return pack(slots_by_chunk, routed, base, size * rows_all, 1, waits)[0]

    packed = [pack_chunk(k, []) for k in range(min(3, len(chunks)))]
    packed[0], grad_arrived[-1] = tie(packed[0], grad_arrived[-1])

    def route(rows):
        return jnp.dot(rows, router_full, preferred_element_type=jnp.float32)

    logits = jnp.concatenate([route(routed_a), route(routed_b)], axis=0)
    probs = jax.nn.softmax(logits, axis=-1)
    gate = jnp.sum(probs * select, axis=-1, keepdims=True)

    arrived, summed, kept, sent = [], [], [], []
    final = len(chunks) - 1
    for k, (e, low, size) in enumerate(chunks):
        moved = swap(packed[k].reshape(rows_all, size, depth), "row")
        arrived.append(moved.reshape(rows_all * size, depth))
        if k < final:
            packed[k + 1], arrived[k] = tie(packed[k + 1], arrived[k])
        if k:
            then = packed[k + 1] if k < final else sent[0][0]
            then, summed[k - 1], arrived[k] = tie(then, summed[k - 1], arrived[k])
            summed[k - 1] = lax.psum_scatter(
                summed[k - 1], "col", scatter_dimension=0, tiled=True
            )
            if k < final:
                packed[k + 1] = then
            else:
                sent[0][0] = then
        waits = packed[2:3] if k == 0 else summed[:1] if k == final else []
        made, both, pair = expert_pass(
            chunks[k],
            arrived[k],
            grad_arrived[e].reshape(rows_all, cap, depth),
            w_in,
            w_back,
            kept.pop() if low else [],
            sent.pop() if low or e % members else [],
            members,
            cols_all,
            pieces,
            waits,
        )
        kept.append(both)
        summed.append(made)
        sent.append(pair)
        if k + 3 <= final:
            packed.append(pack_chunk(k + 3, [made]))
    summed[-1] = lax.psum_scatter(summed[-1], "col", scatter_dimension=0, tiled=True)
    active = [v[0].reshape(block_rows, -1) for v in kept]
    slope = [v[1].reshape(block_rows, -1) for v in kept]

    def joined(values):
        first = [v.reshape(rows_all, short, -1) for v in values[:2]]
        whole = [v.reshape(rows_all, cap, -1) for v in values[2:]]
        return [jnp.concatenate(first, axis=1)] + whole

    arrived = [v.reshape(block_rows, depth) for v in joined(arrived)]

    step = min(256, length)
    order = [(g, f) for f in range(pieces) for g in range(len(sent))]
    back = {}
    grad_sent = []
    grad_weights = None
    token = None
    row = lax.axis_index("row")

    def weigh(e, waits):
        pick = jnp.arange(experts, dtype=jnp.int32)[None, :] == row * local + e
        return weight_pass(
            e,
            local,
            arrived[e],
            grad_arrived[e],
            router_full,
            pick.astype(jnp.float32),
            active[e],
            slope[e],
            grad_weights,
            waits,
        )

    waits = slope[-1:]
    last = None
    for at, (g, f) in enumerate(order):
        piece = sent[g][f]
        if last is not None:
            piece, last = tie(piece, last)
            back[order[at - 1]] = last
        if at == 1:
            piece, slope[-1] = tie(piece, slope[-1])
        last = swap(piece, "row")
        back[(g, f)] = last
        if g == len(sent) - 1:
            rows = [back[(k, f)].reshape(-1, depth // pieces) for k in range(len(sent))]
            for e in range(f * local // pieces, (f + 1) * local // pieces):
                *grad_weights, token = weigh(e, waits)
                waits = [token]
            whole = unpack(slots_by_group, rows, step, waits)
            waits = [whole]
            grad_sent.append(lax.psum_scatter(whole, "col", scatter_dimension=0, tiled=True))

    grad_in, grad_back = grad_weights
    homed = jnp.stack(joined(summed), axis=1)
    homed, last = tie(homed, last)
    back[order[-1]] = last
    homed = swap(homed, "row")
    returned = unpack(
        [slots], [homed.reshape(experts * cap, depth // cols_all)], step
    ).astype(jnp.float32)
    columns = depth // cols_all

    def own_columns(values):
        return lax.dynamic_slice_in_dim(values, col * columns, columns, 1)

    middle_cols = jnp.concatenate([own_columns(middle_a), own_columns(middle_b)], axis=0)
    mixed = (middle_cols + gate * returned).astype(jnp.bfloat16)
    grad_gate = jnp.sum(own_columns(cotangent).astype(jnp.float32) * returned, axis=-1)
    grad_gate = swap(grad_gate.reshape(cols_all, part), "col")
    grad_gate = jnp.sum(grad_gate, axis=0)[:, None]
    mixed_full = lax.all_gather(mixed, "col", axis=0)

    own_gate, own_probs, own_select = own_of(gate), own_of(probs), own_of(select)
    grad_logits = (grad_gate * own_probs * (own_select - own_gate)).astype(jnp.bfloat16)
    own_routed = own(routed_a, routed_b)
    grad_router = jnp.einsum(
        "td,te->de", own_routed, grad_logits, preferred_element_type=jnp.float32
    )
    grad_y = own_of(cotangent).astype(jnp.float32)
    normed_own, inverse_own = layer_stats(own(middle_a, middle_b))
    grad_sent = jnp.concatenate(grad_sent, axis=1).astype(jnp.float32) * own_gate
    grad_routed = grad_sent + jnp.einsum(
        "te,de->td", grad_logits, router_full, preferred_element_type=jnp.float32
    )
    gain_two = jnp.sum(grad_routed * normed_own, axis=0)
    bias_two = jnp.sum(grad_routed, axis=0)
    grad_middle = grad_y + norm_back(grad_routed, normed_own, inverse_own, gains[1])
    grad_attn = grad_middle.astype(jnp.bfloat16)
    grad_context = jnp.einsum(
        "td,zdc->ztc", grad_attn, out_full, preferred_element_type=jnp.float32
    ).astype(jnp.bfloat16)
    grad_context = swap(grad_context, "col")
    grad_context = grad_context.reshape(length, width)
    context = jnp.concatenate([context_a, context_b], axis=0)
    logsum = jnp.concatenate([logsum_a, logsum_b], axis=1)
    grad_proj = attend_backward(projected, grad_context, context, logsum, block, 0)[0]
    grad_proj, grad_attn, mixed_full = tie(grad_proj, grad_attn, mixed_full)

    def spread(grads):
        made = jnp.einsum("tc,dc->td", grads, qkv_full, preferred_element_type=jnp.float32)
        return lax.psum_scatter(
            made.astype(jnp.bfloat16), "col", scatter_dimension=0, tiled=True
        ).astype(jnp.float32)

    grad_normal = spread(grad_proj)
    context_own = own(full_a, full_b, 1)
    grad_out = jnp.einsum("td,ztc->dzc", grad_attn, context_own, preferred_element_type=jnp.float32)
    plane = jnp.concatenate([grad_out.reshape(depth, cols_all * width), grad_router], axis=1)
    plane = swap(plane.astype(jnp.bfloat16).reshape(rows_all, share, -1), "row")
    mixed_out = mixed_full.transpose(1, 0, 2).reshape(length, depth)
    grad_qkv = jnp.einsum("td,tc->dc", normal_in, grad_proj, preferred_element_type=jnp.float32)
    grad_normal, plane, mixed_out, grad_qkv = tie(grad_normal, plane, mixed_out, grad_qkv)

    plane = jnp.sum(plane.astype(jnp.float32), axis=0)
    router_share = plane[:, cols_all * width :].reshape(1, share, experts)
    out_share = plane[:, : cols_all * width].reshape(share, cols_all, width).transpose(1, 0, 2)
    router_share = jnp.broadcast_to(router_share, (cols_all, share, experts))
    plane = jnp.concatenate([out_share, router_share], axis=2).astype(jnp.bfloat16)
    plane = jnp.sum(swap(plane, "col").astype(jnp.float32), axis=0)
    out_share, router_share = plane[:, :width].T, plane[:, width:]

    own_normed, own_inverse = layer_stats(own_of(tokens).astype(jnp.float32))
    grad_tokens = (
        grad_middle + norm_back(grad_normal, own_normed, own_inverse, gains[0])
    ).astype(jnp.bfloat16)
    grad_tokens = lax.all_gather(grad_tokens, "col", axis=0, tiled=True)
    small = [
        jnp.sum(grad_normal * own_normed, axis=0),
        jnp.sum(grad_normal, axis=0),
        gain_two,
        bias_two,
    ]
    small = swap(jnp.stack(small).reshape(4, rows_all, share).transpose(1, 0, 2), "row")
    small = jnp.sum(small, axis=0)
    small = jnp.sum(swap(jnp.broadcast_to(small[None], (cols_all, 4, share)), "col"), axis=0)
    qkv_share = swap(grad_qkv.astype(jnp.bfloat16).reshape(rows_all, share, -1), "row")
    qkv_share = jnp.sum(qkv_share.astype(jnp.float32), axis=0)
    qkv_share = qkv_share.reshape(share, 3, width).transpose(1, 0, 2)
    return (
        mixed_out,
        grad_tokens,
        qkv_share,
        out_share,
        router_share,
        jnp.stack([small[0], small[2]]),
        small[1],
        small[3],
        grad_in,
        grad_back,
    )


def solution(mesh):
    return jax.shard_map(
        per_device,
        mesh=mesh,
        in_specs=(
            P("row", None),
            P(None, "row", "col"),
            P("col", "row"),
            P("row", None),
            P(None, "row"),
            P(None, "row"),
            P("row", None, "col"),
            P("row", "col", None),
            P("row", None),
            P("row", None),
        ),
        out_specs=(
            P("row", None),
            P("row", None),
            P(None, "row", "col"),
            P("col", "row"),
            P("row", None),
            P(None, "row"),
            P("row"),
            P("row"),
            P("row", None, "col"),
            P("row", "col", None),
        ),
        check_vma=False,
    )
```

```python
import functools, math
import jax, jax.numpy as jnp
from jax import lax
from jax.experimental import pallas as pl
from jax.experimental.pallas import tpu as pltpu
from jax.sharding import PartitionSpec as P

HEAD_DIM = 64
EPSILON = 1e-05
MASKED = -1e30
VMEM = 60 << 20


def params(*kinds):
    return pltpu.CompilerParams(dimension_semantics=kinds or None, vmem_limit_bytes=VMEM)


def cost(flops, moved, special=0):
    return pl.CostEstimate(flops=flops, bytes_accessed=moved, transcendentals=special)


def dot(a, b, dims):
    return lax.dot_general(a, b, (dims, ((), ())), preferred_element_type=jnp.float32)

NN = ((1,), (0,))
NT = ((1,), (1,))
TN = ((0,), (0,))


def pack_body(base, step, each, parts, slots_ref, *rest):
    rows_refs, outs = rest[:parts], rest[-((pl.num_programs(0)) // each) :]
    at = pl.program_id(0)
    made = None
    first = 0
    for rows_ref in rows_refs:
        length = rows_ref.shape[0]
        wanted = base + at * step + lax.broadcasted_iota(jnp.int32, (step, length), 0)
        chosen = jnp.where(slots_ref[:, pl.ds(first, length)] == wanted, 1.0, 0.0)
        more = dot(chosen.astype(jnp.bfloat16), rows_ref[...], NN)
        made = more if made is None else made + more
        first += length
    made = made.astype(jnp.bfloat16)
    for j, out_ref in enumerate(outs):

        @pl.when(at // each == j)
        def _(out_ref=out_ref):
            out_ref[...] = made


def pack(slots, rows, base, count, outs, waits=()):
    length = slots.shape[0]
    width = rows[0].shape[1]
    step = min(512, count)
    each = count // step
    return pl.pallas_call(
        functools.partial(pack_body, base, step, each, len(rows)),
        out_shape=(jax.ShapeDtypeStruct((count, width), jnp.bfloat16),) * outs,
        grid=(each * outs,),
        in_specs=[pl.BlockSpec((1, length), lambda i: (0, 0))]
        + [pl.BlockSpec(r.shape, lambda i: (0, 0)) for r in rows]
        + [pl.BlockSpec(memory_space=pl.ANY)] * len(waits),
        out_specs=tuple(
            pl.BlockSpec((step, width), lambda i, j=j: (jnp.clip(i - j * each, 0, each - 1), 0))
            for j in range(outs)
        ),
        compiler_params=params("arbitrary"),
        name="pack",
        cost_estimate=cost(1, 1),
    )(slots.reshape(1, length), *rows, *waits)


def unpack_body(parts, *refs):
    out_ref = refs[-1]
    step = out_ref.shape[0]
    made = None
    for slots_ref, rows_ref in zip(refs[:parts], refs[parts : 2 * parts]):
        count = rows_ref.shape[0]
        held = lax.broadcasted_iota(jnp.int32, (step, count), 1)
        chosen = jnp.where(slots_ref[...] == held, 1.0, 0.0).astype(jnp.bfloat16)
        more = dot(chosen, rows_ref[...], NN)
        made = more if made is None else made + more
    out_ref[...] = made.astype(out_ref.dtype)


def unpack(slots, rows, step, waits=()):
    length = slots[0].shape[0]
    width = rows[0].shape[1]
    count = sum(r.shape[0] for r in rows)
    return pl.pallas_call(
        functools.partial(unpack_body, len(rows)),
        out_shape=jax.ShapeDtypeStruct((length, width), jnp.bfloat16),
        grid=(length // step,),
        in_specs=[pl.BlockSpec((step, 1), lambda i: (i, 0))] * len(rows)
        + [pl.BlockSpec(r.shape, lambda i: (0, 0)) for r in rows]
        + [pl.BlockSpec(memory_space=pl.ANY)] * len(waits),
        out_specs=pl.BlockSpec((step, width), lambda i: (i, 0)),
        compiler_params=params("arbitrary"),
        name="unpack",
        cost_estimate=cost(2 * count * length * width, 2 * (length + count) * width),
    )(*(at.reshape(length, 1) for at in slots), *rows, *waits)


def middle_body(full_ref, out_ref, tokens_ref, gain_ref, bias_ref, middle_ref, routed_ref, all_ref):
    cols, _, width = full_ref.shape

    @pl.when(pl.program_id(0) == 0)
    def _():
        for z in range(cols):
            all_ref[:, z * width : (z + 1) * width] = out_ref[z]

    context = jnp.concatenate([full_ref[z] for z in range(cols)], axis=1)
    total = tokens_ref[...].astype(jnp.float32) + dot(context, all_ref[...], NT)
    middle_ref[...] = total
    mean = jnp.mean(total, axis=1, keepdims=True)
    centered = total - mean
    inverse = lax.rsqrt(jnp.mean(centered * centered, axis=1, keepdims=True) + EPSILON)
    routed_ref[...] = (centered * inverse * gain_ref[...] + bias_ref[...]).astype(jnp.bfloat16)


def middle_pass(full, out_full, tokens, gain, bias):
    cols, rows, width = full.shape
    depth = tokens.shape[1]
    step = min(256, rows)
    row = pl.BlockSpec((1, depth), lambda i: (0, 0))
    block = pl.BlockSpec((step, depth), lambda i: (i, 0))
    return pl.pallas_call(
        middle_body,
        out_shape=(
            jax.ShapeDtypeStruct((rows, depth), jnp.float32),
            jax.ShapeDtypeStruct((rows, depth), jnp.bfloat16),
        ),
        grid=(rows // step,),
        in_specs=[
            pl.BlockSpec((cols, step, width), lambda i: (0, i, 0)),
            pl.BlockSpec((cols, depth, width), lambda i: (0, 0, 0)),
            block,
            row,
            row,
        ],
        out_specs=(block, block),
        scratch_shapes=[pltpu.VMEM((depth, cols * width), jnp.bfloat16)],
        compiler_params=params("arbitrary"),
        name="middle_pass",
        cost_estimate=cost(2 * rows * depth * width * cols, 10 * rows * depth),
    )(full, out_full, tokens, gain, bias)


def forward_body(blocks, block, q_ref, k_ref, v_ref, *rest):
    o_ref, lse_ref = rest[-2:]
    width = q_ref.shape[1]
    heads = width // HEAD_DIM
    lane = lax.broadcasted_iota(jnp.int32, (block, width), 1)
    hidden = lax.broadcasted_iota(jnp.int32, (block, block), 1) > lax.broadcasted_iota(
        jnp.int32, (block, block), 0
    )
    for at, i in enumerate(blocks):
        span = (i + 1) * block
        here = pl.ds(at * block, block)
        o_ref[here, :] = jnp.zeros((block, width), o_ref.dtype)

        def one_head(h, carry, here=here, span=span, i=i):
            mine = (lane >= h * HEAD_DIM) & (lane < (h + 1) * HEAD_DIM)
            query = q_ref[pl.ds(i * block, block), :].astype(jnp.float32) * 0.125
            query = jnp.where(mine, query, 0.0).astype(jnp.bfloat16)
            edge = jnp.where(hidden, MASKED, dot(query, k_ref[pl.ds(span - block, block), :], NT))
            peak = jnp.max(edge, axis=1, keepdims=True)
            if i:
                past = dot(query, k_ref[pl.ds(0, span - block), :], NT)
                peak = jnp.maximum(peak, jnp.max(past, axis=1, keepdims=True))
            edge = jnp.exp(edge - peak)
            total = jnp.sum(edge, axis=1, keepdims=True)
            if i:
                past = jnp.exp(past - peak)
                total = total + jnp.sum(past, axis=1, keepdims=True)
            share = 1.0 / total
            mixed = dot((edge * share).astype(jnp.bfloat16), v_ref[pl.ds(span - block, block), :], NN)
            if i:
                mixed = mixed + dot(
                    (past * share).astype(jnp.bfloat16), v_ref[pl.ds(0, span - block), :], NN
                )
            o_ref[here, :] = jnp.where(mine, mixed.astype(o_ref.dtype), o_ref[here, :])
            logsum = jnp.broadcast_to(peak + jnp.log(total), (block, 128))
            lse_ref[pl.ds(h, 1), here] = logsum.T[0:1, :]
            return carry

        lax.fori_loop(0, heads, one_head, 0, unroll=heads)


def attend_forward(projected, blocks, block, waits=()):
    length, triple = projected.shape
    width = triple // 3
    heads = width // HEAD_DIM
    rows = len(blocks) * block
    spec = [pl.BlockSpec((length, width), lambda i, j=j: (0, j)) for j in range(3)]
    return pl.pallas_call(
        functools.partial(forward_body, blocks, block),
        out_shape=(
            jax.ShapeDtypeStruct((rows, width), jnp.bfloat16),
            jax.ShapeDtypeStruct((heads, rows), jnp.float32),
        ),
        grid=(1,),
        in_specs=spec + [pl.BlockSpec(memory_space=pl.ANY)] * len(waits),
        out_specs=(
            pl.BlockSpec((rows, width), lambda i: (0, 0)),
            pl.BlockSpec((heads, rows), lambda i: (0, 0)),
        ),
        compiler_params=params("arbitrary"),
        name="attend_forward",
        cost_estimate=cost(rows * width, rows * width),
    )(projected, projected, projected, *waits)


def backward_body(block, first, given, *refs):
    q_ref, do_ref, o_ref, lse_ref, k_ref, v_ref = refs[:6]
    outs = refs[6 + given :]
    out_ref, p_ref, ds_ref, qm_ref, dom_ref, dk_ref, dv_ref = outs[:1] + outs[-6:]
    width = q_ref.shape[1]
    heads = width // HEAD_DIM
    count = q_ref.shape[0] // block
    lane = lax.broadcasted_iota(jnp.int32, (block, width), 1)
    hidden = lax.broadcasted_iota(jnp.int32, (block, block), 0) > lax.broadcasted_iota(
        jnp.int32, (block, block), 1
    )
    for at in reversed(range(count)):
        i = first + at
        span = (i + 1) * block
        here = pl.ds(at * block, block)

        def one_head(h, carry, here=here, span=span, i=i):
            mine = (lane >= h * HEAD_DIM) & (lane < (h + 1) * HEAD_DIM)
            query = q_ref[here, :].astype(jnp.float32) * 0.125
            query = jnp.where(mine, query, 0.0).astype(jnp.bfloat16)
            grad = jnp.where(mine, do_ref[here, :].astype(jnp.float32), 0.0)
            delta = jnp.sum(grad * o_ref[here, :].astype(jnp.float32), axis=1, keepdims=True)
            delta = jnp.broadcast_to(delta, (block, 128)).T[0:1, :]
            grad = grad.astype(jnp.bfloat16)
            logsum = lse_ref[pl.ds(h, 1), here]
            column = pl.ds(pl.multiple_of(h * block, block), block)
            qm_ref[column, :] = query
            dom_ref[column, :] = grad

            def part(rows, edge):
                scores = dot(k_ref[rows, :], query, NT)
                if edge:
                    scores = jnp.where(hidden, MASKED, scores)
                probs = jnp.exp(scores - logsum)
                p_ref[rows, column] = probs.astype(jnp.bfloat16)
                grad_probs = dot(v_ref[rows, :], grad, NT)
                ds_ref[rows, column] = (probs * (grad_probs - delta)).astype(jnp.bfloat16)

            if i:
                part(pl.ds(0, span - block), False)
            part(pl.ds(span - block, block), True)
            dq = dot(ds_ref[pl.ds(0, span), column], k_ref[pl.ds(0, span), :], TN)
            out_ref[here, pl.ds(0, width)] = jnp.where(
                mine, (dq * 0.125).astype(out_ref.dtype), out_ref[here, pl.ds(0, width)]
            )
            return carry

        lax.fori_loop(0, heads, one_head, 0, unroll=heads)
        new_v = dot(p_ref[pl.ds(0, span), :], dom_ref[...], NN)
        new_k = dot(ds_ref[pl.ds(0, span), :], qm_ref[...], NN)
        if at == count - 1:
            old_k, old_v = (refs[6][...], refs[7][...]) if given > 1 else (0.0, 0.0)
            dv_ref[...] = old_v + new_v
            dk_ref[...] = old_k + new_k
        else:
            dv_ref[pl.ds(0, span), :] += new_v
            dk_ref[pl.ds(0, span), :] += new_k
        low = pl.ds(i * block, block)
        out_ref[here, pl.ds(width, width)] = dk_ref[low, :].astype(out_ref.dtype)
        out_ref[here, pl.ds(2 * width, width)] = dv_ref[low, :].astype(out_ref.dtype)
    if first:
        outs[1][...] = dk_ref[pl.ds(0, first * block), :]
        outs[2][...] = dv_ref[pl.ds(0, first * block), :]


def attend_backward(projected, grad_context, context, logsum, block, first, carried=()):
    rows, width = context.shape
    heads = width // HEAD_DIM
    length = first * block + rows
    half = lambda j: pl.BlockSpec((rows, width), lambda i: (first * block // rows, j))
    own = pl.BlockSpec((rows, width), lambda i: (0, 0))
    low = pl.BlockSpec((first * block, width), lambda i: (0, 0))
    rest = jax.ShapeDtypeStruct((first * block, width), jnp.float32)
    more = bool(first)
    return pl.pallas_call(
        functools.partial(backward_body, block, first, len(carried)),
        out_shape=(jax.ShapeDtypeStruct((rows, 3 * width), jnp.bfloat16),) + (rest,) * (2 * more),
        grid=(1,),
        in_specs=[
            half(0),
            own,
            own,
            pl.BlockSpec((heads, rows), lambda i: (0, 0)),
            pl.BlockSpec((length, width), lambda i: (0, 1)),
            pl.BlockSpec((length, width), lambda i: (0, 2)),
        ]
        + [own] * len(carried),
        out_specs=(pl.BlockSpec((rows, 3 * width), lambda i: (0, 0)),) + (low,) * (2 * more),
        scratch_shapes=[
            pltpu.VMEM((length, heads * block), jnp.bfloat16),
            pltpu.VMEM((length, heads * block), jnp.bfloat16),
            pltpu.VMEM((heads * block, width), jnp.bfloat16),
            pltpu.VMEM((heads * block, width), jnp.bfloat16),
            pltpu.VMEM((length, width), jnp.float32),
            pltpu.VMEM((length, width), jnp.float32),
        ],
        compiler_params=params("arbitrary"),
        name="attend_backward",
        cost_estimate=cost(
            20 * rows * length * width, 16 * length * width, rows * length * heads
        ),
    )(projected, grad_context, context, logsum, projected, projected, *carried)


ROOT = math.sqrt(2.0 / math.pi)
CUBE = 0.044715


def expert_body(given, x_ref, gy_ref, win_ref, wback_ref, *rest):
    out_ref, active_ref, slope_ref, *sent = rest[given:]
    rows, depth = x_ref.shape
    hidden = dot(x_ref[...], win_ref[...], NN)
    square = hidden * hidden
    bent = jnp.tanh(ROOT * hidden * (1.0 + CUBE * square))
    active = (0.5 * hidden * (1.0 + bent)).astype(jnp.bfloat16)
    slope = 0.5 * (1.0 + bent) + 0.5 * hidden * (1.0 - bent * bent) * (
        ROOT * (1.0 + 3.0 * CUBE * square)
    )
    active_ref[...] = active.reshape(active_ref.shape)
    parts = out_ref.shape[0]
    wide = depth // parts
    made = dot(active, wback_ref[...], NN).astype(jnp.bfloat16)
    for j in range(parts):
        out_ref[j] = made[:, j * wide : (j + 1) * wide]
    grad_active = dot(gy_ref[...].reshape(rows, depth), wback_ref[...], NT)
    grad_hidden = (grad_active * slope).astype(jnp.bfloat16)
    slope_ref[...] = grad_hidden.reshape(slope_ref.shape)
    back = dot(grad_hidden, win_ref[...], NT).astype(jnp.bfloat16)
    first = 0
    for ref in sent:
        wide = ref.shape[-1]
        ref[...] = back[:, first : first + wide].reshape(ref.shape)
        first += wide


def expert_pass(chunk, x, grad_y, w_in, w_back, kept, sent, members, parts, pieces, waits=()):
    e, low, size = chunk
    sources, cap, depth = grad_y.shape
    rows = sources * size
    width = w_in.shape[2]
    step = min(256, rows)
    group = step // size
    at = low // size
    given = [*kept, *sent]
    aliases = {4 + j: (1 if kept else 3) + j for j in range(len(given))}
    keep = jax.ShapeDtypeStruct((sources, cap, width), jnp.bfloat16)
    keep_spec = pl.BlockSpec((group, size, width), lambda i: (i, at, 0))
    piece = tuple(jax.ShapeDtypeStruct((sources, members, cap, w), jnp.bfloat16) for w in pieces)
    piece_spec = tuple(
        pl.BlockSpec((group, None, size, w), lambda i: (i, e % members, at, 0)) for w in pieces
    )
    made = pl.pallas_call(
        functools.partial(expert_body, len(given) + len(waits)),
        out_shape=(jax.ShapeDtypeStruct((parts, rows, depth // parts), jnp.bfloat16), keep, keep)
        + piece,
        grid=(rows // step,),
        in_specs=[
            pl.BlockSpec((step, depth), lambda i: (i, 0)),
            pl.BlockSpec((group, size, depth), lambda i: (i, at, 0)),
            pl.BlockSpec((None, depth, width), lambda i: (e, 0, 0)),
            pl.BlockSpec((None, width, depth), lambda i: (e, 0, 0)),
        ]
        + [pl.BlockSpec(memory_space=pl.ANY)] * (len(given) + len(waits)),
        out_specs=(
            pl.BlockSpec((parts, step, depth // parts), lambda i: (0, i, 0)),
            keep_spec,
            keep_spec,
        )
        + piece_spec,
        input_output_aliases=aliases,
        compiler_params=params("arbitrary"),
        name="expert_pass",
        cost_estimate=cost(
            8 * rows * depth * width, 4 * width * depth + 12 * rows * depth, rows * width
        ),
    )(x, grad_y, w_in, w_back, *given, *waits)
    return made[0], made[1:3], list(made[3:])


def weight_body(given, x_ref, gy_ref, router_ref, pick_ref, active_ref, slope_ref, *rest):
    gin_ref, gback_ref, token_ref, xt_ref, gyg_ref = rest[given:]
    token_ref[...] = jnp.zeros_like(token_ref)
    rows, depth = x_ref.shape

    @pl.when(pl.program_id(0) == 0)
    def _():
        logits = dot(x_ref[...], router_ref[...], NN)
        raised = jnp.exp(logits - jnp.max(logits, axis=1, keepdims=True))
        gate = jnp.sum(raised * pick_ref[...], axis=1, keepdims=True)
        gate = gate / jnp.sum(raised, axis=1, keepdims=True)
        xt_ref[...] = (x_ref[...].astype(jnp.float32) * gate).T.astype(jnp.bfloat16)
        gyg_ref[...] = (gy_ref[...].astype(jnp.float32) * gate).astype(jnp.bfloat16)

    gin_ref[...] = dot(xt_ref[...], slope_ref[...], NN)
    gback_ref[...] = dot(active_ref[...], gyg_ref[...], TN)


def weight_pass(e, local, x, grad_y, router, pick, active, slope, sent, waits=()):
    rows, width = active.shape
    depth = x.shape[1]
    step = min(256, width)
    sent = list(sent or [])
    return pl.pallas_call(
        functools.partial(weight_body, len(sent) + len(waits)),
        out_shape=(
            jax.ShapeDtypeStruct((local, depth, width), jnp.float32),
            jax.ShapeDtypeStruct((local, width, depth), jnp.float32),
            jax.ShapeDtypeStruct((8, 128), jnp.float32),
        ),
        grid=(width // step,),
        in_specs=[
            pl.BlockSpec((rows, depth), lambda i: (0, 0)),
            pl.BlockSpec((rows, depth), lambda i: (0, 0)),
            pl.BlockSpec(router.shape, lambda i: (0, 0)),
            pl.BlockSpec(pick.shape, lambda i: (0, 0)),
            pl.BlockSpec((rows, step), lambda i: (0, i)),
            pl.BlockSpec((rows, step), lambda i: (0, i)),
        ]
        + [pl.BlockSpec(memory_space=pl.ANY)] * (len(sent) + len(waits)),
        out_specs=(
            pl.BlockSpec((None, depth, step), lambda i: (e, 0, i)),
            pl.BlockSpec((None, step, depth), lambda i: (e, i, 0)),
            pl.BlockSpec((8, 128), lambda i: (0, 0)),
        ),
        scratch_shapes=[
            pltpu.VMEM((depth, rows), jnp.bfloat16),
            pltpu.VMEM((rows, depth), jnp.bfloat16),
        ],
        input_output_aliases={6 + j: j for j in range(len(sent))},
        compiler_params=params("arbitrary"),
        name="weight_pass",
        cost_estimate=cost(4 * rows * depth * width, 8 * width * depth + 8 * rows * depth),
    )(x, grad_y, router, pick, active, slope, *sent, *waits)


def swap(blocks, axis):
    return lax.all_to_all(blocks, axis, split_axis=0, concat_axis=0, tiled=True)


def tie(*values):
    return lax.optimization_barrier(values)


def row_stats(values):
    mean = jnp.mean(values, axis=-1, keepdims=True)
    centered = values - mean
    variance = jnp.mean(centered * centered, axis=-1, keepdims=True)
    return (mean, lax.rsqrt(variance + EPSILON))


def layer_stats(values):
    mean = jnp.mean(values, axis=-1, keepdims=True)
    centered = values - mean
    variance = jnp.mean(centered * centered, axis=-1, keepdims=True)
    inverse = lax.rsqrt(variance + EPSILON)
    return (centered * inverse, inverse)


def norm_back(grad_normed, normed, inverse, gain):
    grad_hat = grad_normed * gain
    centred_grad = grad_hat - jnp.mean(grad_hat, axis=-1, keepdims=True)
    return inverse * (centred_grad - normed * jnp.mean(grad_hat * normed, axis=-1, keepdims=True))


def slot_layout(expert_ids, experts, cap):
    chosen = expert_ids[:, 0]
    length = chosen.shape[0]
    table = chosen[:, None] == jnp.arange(experts, dtype=jnp.int32)[None, :]
    order = jnp.arange(length, dtype=jnp.int32)
    before = (order[:, None] > order[None, :]).astype(jnp.bfloat16)
    counted = jnp.dot(before, table.astype(jnp.bfloat16), preferred_element_type=jnp.float32)
    ranks = jnp.sum(jnp.where(table, counted, 0.0), axis=1).astype(jnp.int32)
    return (chosen, ranks, table.astype(jnp.float32))


def per_device(
    tokens, w_qkv, w_out, w_router, ln_gains, ln_biases, w_in, w_back, expert_ids, cotangent
):
    rows_all, cols_all = lax.axis_size("row"), lax.axis_size("col")
    col = lax.axis_index("col")
    length, depth = tokens.shape
    share = depth // rows_all
    width = w_qkv.shape[2]
    experts = w_router.shape[1]
    local = w_in.shape[0]
    cap = 2 * length // experts
    block_rows = rows_all * cap
    block = min(256, length // 2)
    part = length // cols_all
    members = max(1, local // 2)
    pieces = (depth * 5 // 8, depth * 3 // 8)

    def own(values, axis=0):
        return lax.dynamic_slice_in_dim(values, col * part, part, axis)

    def send(packed):
        return swap(packed.reshape(rows_all, cap, depth), "row").reshape(block_rows, depth)

    stacked = w_qkv.transpose(1, 0, 2).reshape(share, 3 * width)
    weights = jnp.concatenate([stacked, w_router, ln_gains.T, ln_biases.T], axis=1)
    weights = lax.all_gather(weights, "row", axis=0, tiled=True)
    mean_one, inverse_one = row_stats(tokens.astype(jnp.float32))

    chosen, ranks, select = slot_layout(expert_ids, experts, cap)
    out_block, ranks = tie(w_out.T, ranks)
    out_block = swap(jnp.broadcast_to(out_block[None], (cols_all, share, width)), "col")
    slots = chosen * cap + ranks
    slots_by_local = ((chosen % local) * rows_all + chosen // local) * cap + ranks
    member = chosen % local
    slots_by_group = [
        jnp.where(
            member // members == g,
            ((chosen // local) * members + member % members) * cap + ranks,
            -1,
        )
        for g in range(local // members)
    ]

    early = min(2, local)
    grad_packed = list(pack(slots_by_local, [cotangent], 0, block_rows, early))
    weights, grad_packed[0], out_block, mean_one, inverse_one = tie(
        weights, grad_packed[0], out_block, mean_one, inverse_one
    )
    qkv_full = weights[:, : 3 * width]
    router_full = weights[:, 3 * width : 3 * width + experts]
    norms = weights[:, 3 * width + experts :].astype(jnp.float32).T
    gains, biases = norms[0:2], norms[2:4]

    resid_in = tokens.astype(jnp.float32)
    normed_one = (resid_in - mean_one) * inverse_one
    normal_in = (normed_one * gains[0] + biases[0]).astype(jnp.bfloat16)
    projected = jnp.dot(normal_in, qkv_full, preferred_element_type=jnp.float32).astype(jnp.bfloat16)

    context, logsum = attend_forward(projected, tuple(range(length // block)), block)
    context, grad_packed[0] = tie(context, grad_packed[0])
    full = lax.all_gather(context, "col", axis=0)
    grad_arrived = [send(grad_packed[0])]
    if local > early:
        grad_packed += pack(
            slots_by_local, [cotangent], early * block_rows, block_rows, local - early, [context]
        )
    grad_arrived[0], *grad_packed[1:] = tie(grad_arrived[0], *grad_packed[1:])
    out_full = lax.all_gather(out_block, "row", axis=1, tiled=True)
    for e in range(1, local):
        grad_arrived.append(send(grad_packed[e]))
        if e + 1 < local:
            grad_arrived[e], grad_packed[e + 1] = tie(grad_arrived[e], grad_packed[e + 1])
    full, out_full = tie(full, out_full)
    middle, routed = middle_pass(full, out_full, tokens, gains[1:2], biases[1:2])

    short = cap // 2
    chunks = [(0, 0, short), (0, short, short)] + [(e, 0, cap) for e in range(1, local)]
    split = (ranks // short * rows_all + chosen // local) * short + ranks % short
    slots_by_chunk = jnp.where(chosen % local == 0, split, slots_by_local)

    def pack_chunk(k, waits):
        e, low, size = chunks[k]
        base = (e * cap + low) * rows_all
        return pack(slots_by_chunk, [routed], base, size * rows_all, 1, waits)[0]

    packed = [pack_chunk(k, []) for k in range(2)]
    packed[0], grad_arrived[-1] = tie(packed[0], grad_arrived[-1])

    logits = jnp.dot(routed, router_full, preferred_element_type=jnp.float32)
    probs = jax.nn.softmax(logits, axis=-1)
    gate = jnp.sum(probs * select, axis=-1, keepdims=True)

    arrived, summed, kept, sent = [], [], [], []
    final = len(chunks) - 1
    for k, (e, low, size) in enumerate(chunks):
        moved = swap(packed[k].reshape(rows_all, size, depth), "row")
        arrived.append(moved.reshape(rows_all * size, depth))
        if k < final:
            packed[k + 1], arrived[k] = tie(packed[k + 1], arrived[k])
        if k:
            then = packed[k + 1] if k < final else sent[0][0]
            then, summed[k - 1], arrived[k] = tie(then, summed[k - 1], arrived[k])
            summed[k - 1] = lax.psum_scatter(
                summed[k - 1], "col", scatter_dimension=0, tiled=True
            )
            if k < final:
                packed[k + 1] = then
            else:
                sent[0][0] = then
        waits = packed[1:2] if k == 0 else summed[:1] if k == final else []
        made, both, pair = expert_pass(
            chunks[k],
            arrived[k],
            grad_arrived[e].reshape(rows_all, cap, depth),
            w_in,
            w_back,
            kept.pop() if low else [],
            sent.pop() if low or e % members else [],
            members,
            cols_all,
            pieces,
            waits,
        )
        kept.append(both)
        summed.append(made)
        sent.append(pair)
        if k + 2 <= final:
            packed.append(pack_chunk(k + 2, [made]))
    active = [v[0].reshape(block_rows, -1) for v in kept]
    slope = [v[1].reshape(block_rows, -1) for v in kept]

    def joined(values):
        first = [v.reshape(rows_all, short, -1) for v in values[:2]]
        whole = [v.reshape(rows_all, cap, -1) for v in values[2:]]
        return [jnp.concatenate(first, axis=1)] + whole

    arrived = [v.reshape(block_rows, depth) for v in joined(arrived)]

    step = min(256, length)
    order = [(g, f) for f in range(len(pieces)) for g in range(len(sent))]
    grad_sent = []
    grad_weights = None
    token = None
    row = lax.axis_index("row")

    def weigh(e, waits):
        pick = jnp.arange(experts, dtype=jnp.int32)[None, :] == row * local + e
        return weight_pass(
            e,
            local,
            arrived[e],
            grad_arrived[e],
            router_full,
            pick.astype(jnp.float32),
            active[e],
            slope[e],
            grad_weights,
            waits,
        )

    waits = slope[-1:]
    last = None
    for f, wide in enumerate(pieces):
        for e in range(f * local // len(pieces), (f + 1) * local // len(pieces)):
            *grad_weights, token = weigh(e, waits)
            waits = [token]
        rows = []
        for g in range(len(sent)):
            piece = sent[g][f]
            if last is not None:
                piece, last = tie(piece, last)
                if rows:
                    rows[-1] = last
                else:
                    ended[-1] = last
            if f == 0 and g == len(sent) - 1:
                piece, slope[-1] = tie(piece, slope[-1])
            if f and g == len(sent) - 1:
                piece, whole = tie(piece, whole)
            last = swap(piece, "row")
            if f == 0 and g == 0:
                last, made = tie(last, summed[-1])
                summed[-1] = lax.psum_scatter(made, "col", scatter_dimension=0, tiled=True)
            rows.append(last)
        if f == 0:
            ended = rows
            sent[0][1], token = tie(sent[0][1], token)
            waits = [token]
        else:
            homed = jnp.stack(joined(summed), axis=1)
            waits = [token, homed]
            grad_sent.append(lax.psum_scatter(whole, "col", scatter_dimension=0, tiled=True))
        whole = unpack(slots_by_group, [v.reshape(-1, wide) for v in rows], step, waits)
        waits = [whole]
    grad_sent.append(lax.psum_scatter(whole, "col", scatter_dimension=0, tiled=True))

    grad_in, grad_back = grad_weights
    homed = swap(homed, "row")
    returned = unpack(
        [slots], [homed.reshape(experts * cap, depth // cols_all)], step, grad_sent[:1]
    ).astype(jnp.float32)
    columns = depth // cols_all

    def own_columns(values):
        return lax.dynamic_slice_in_dim(values, col * columns, columns, 1)

    mixed = (own_columns(middle) + gate * returned).astype(jnp.bfloat16)
    grad_gate = jnp.sum(own_columns(cotangent).astype(jnp.float32) * returned, axis=-1)
    grad_gate = swap(grad_gate.reshape(cols_all, part), "col")
    grad_gate = jnp.sum(grad_gate, axis=0)[:, None]
    mixed_full = lax.all_gather(mixed, "col", axis=0)

    own_gate, own_probs, own_select = own(gate), own(probs), own(select)
    grad_logits = (grad_gate * own_probs * (own_select - own_gate)).astype(jnp.bfloat16)
    own_routed = own(routed)
    grad_router = jnp.einsum(
        "td,te->de", own_routed, grad_logits, preferred_element_type=jnp.float32
    )
    grad_y = own(cotangent).astype(jnp.float32)
    normed_own, inverse_own = layer_stats(own(middle))
    grad_sent = jnp.concatenate(grad_sent, axis=1).astype(jnp.float32) * own_gate
    grad_routed = grad_sent + jnp.einsum(
        "te,de->td", grad_logits, router_full, preferred_element_type=jnp.float32
    )
    gain_two = jnp.sum(grad_routed * normed_own, axis=0)
    bias_two = jnp.sum(grad_routed, axis=0)
    grad_middle = grad_y + norm_back(grad_routed, normed_own, inverse_own, gains[1])
    grad_attn = grad_middle.astype(jnp.bfloat16)
    grad_context = jnp.einsum(
        "td,zdc->ztc", grad_attn, out_full, preferred_element_type=jnp.float32
    ).astype(jnp.bfloat16)
    grad_context = swap(grad_context, "col")
    grad_context = grad_context.reshape(length, width)
    grad_proj = attend_backward(projected, grad_context, context, logsum, block, 0)[0]
    grad_proj, grad_attn, mixed_full = tie(grad_proj, grad_attn, mixed_full)

    def spread(grads):
        made = jnp.einsum("tc,dc->td", grads, qkv_full, preferred_element_type=jnp.float32)
        return lax.psum_scatter(
            made.astype(jnp.bfloat16), "col", scatter_dimension=0, tiled=True
        ).astype(jnp.float32)

    grad_normal = spread(grad_proj)
    context_own = own(full, 1)
    grad_out = jnp.einsum("td,ztc->dzc", grad_attn, context_own, preferred_element_type=jnp.float32)
    plane = jnp.concatenate([grad_out.reshape(depth, cols_all * width), grad_router], axis=1)
    plane = swap(plane.astype(jnp.bfloat16).reshape(rows_all, share, -1), "row")
    mixed_out = mixed_full.transpose(1, 0, 2).reshape(length, depth)
    grad_qkv = jnp.einsum("td,tc->dc", normal_in, grad_proj, preferred_element_type=jnp.float32)
    grad_normal, plane, mixed_out, grad_qkv = tie(grad_normal, plane, mixed_out, grad_qkv)

    plane = jnp.sum(plane.astype(jnp.float32), axis=0)
    router_share = plane[:, cols_all * width :].reshape(1, share, experts)
    out_share = plane[:, : cols_all * width].reshape(share, cols_all, width).transpose(1, 0, 2)
    router_share = jnp.broadcast_to(router_share, (cols_all, share, experts))
    plane = jnp.concatenate([out_share, router_share], axis=2).astype(jnp.bfloat16)
    plane = jnp.sum(swap(plane, "col").astype(jnp.float32), axis=0)
    out_share, router_share = plane[:, :width].T, plane[:, width:]

    own_normed, own_inverse = layer_stats(own(tokens).astype(jnp.float32))
    grad_tokens = (
        grad_middle + norm_back(grad_normal, own_normed, own_inverse, gains[0])
    ).astype(jnp.bfloat16)
    grad_tokens = lax.all_gather(grad_tokens, "col", axis=0, tiled=True)
    small = [
        jnp.sum(grad_normal * own_normed, axis=0),
        jnp.sum(grad_normal, axis=0),
        gain_two,
        bias_two,
    ]
    small = swap(jnp.stack(small).reshape(4, rows_all, share).transpose(1, 0, 2), "row")
    small = jnp.sum(small, axis=0)
    small = jnp.sum(swap(jnp.broadcast_to(small[None], (cols_all, 4, share)), "col"), axis=0)
    qkv_share = swap(grad_qkv.astype(jnp.bfloat16).reshape(rows_all, share, -1), "row")
    qkv_share = jnp.sum(qkv_share.astype(jnp.float32), axis=0)
    qkv_share = qkv_share.reshape(share, 3, width).transpose(1, 0, 2)
    return (
        mixed_out,
        grad_tokens,
        qkv_share,
        out_share,
        router_share,
        jnp.stack([small[0], small[2]]),
        small[1],
        small[3],
        grad_in,
        grad_back,
    )


def solution(mesh):
    return jax.shard_map(
        per_device,
        mesh=mesh,
        in_specs=(
            P("row", None),
            P(None, "row", "col"),
            P("col", "row"),
            P("row", None),
            P(None, "row"),
            P(None, "row"),
            P("row", None, "col"),
            P("row", "col", None),
            P("row", None),
            P("row", None),
        ),
        out_specs=(
            P("row", None),
            P("row", None),
            P(None, "row", "col"),
            P("col", "row"),
            P("row", None),
            P(None, "row"),
            P("row"),
            P("row"),
            P("row", None, "col"),
            P("row", "col", None),
        ),
        check_vma=False,
    )
```

```python
import functools, math
import jax, jax.numpy as jnp
from jax import lax
from jax.experimental import pallas as pl
from jax.experimental.pallas import tpu as pltpu
from jax.sharding import PartitionSpec as P

HEAD_DIM = 64
EPSILON = 1e-05
MASKED = -1e30
VMEM = 60 << 20


def params(*kinds):
    return pltpu.CompilerParams(dimension_semantics=kinds or None, vmem_limit_bytes=VMEM)


def cost(flops, moved, special=0):
    return pl.CostEstimate(flops=flops, bytes_accessed=moved, transcendentals=special)


def dot(a, b, dims):
    return lax.dot_general(a, b, (dims, ((), ())), preferred_element_type=jnp.float32)

NN = ((1,), (0,))
NT = ((1,), (1,))
TN = ((0,), (0,))


def pack_body(base, step, each, parts, slots_ref, *rest):
    rows_refs, outs = rest[:parts], rest[-((pl.num_programs(0)) // each) :]
    at = pl.program_id(0)
    made = None
    first = 0
    for rows_ref in rows_refs:
        length = rows_ref.shape[0]
        wanted = base + at * step + lax.broadcasted_iota(jnp.int32, (step, length), 0)
        chosen = jnp.where(slots_ref[:, pl.ds(first, length)] == wanted, 1.0, 0.0)
        more = dot(chosen.astype(jnp.bfloat16), rows_ref[...], NN)
        made = more if made is None else made + more
        first += length
    made = made.astype(jnp.bfloat16)
    for j, out_ref in enumerate(outs):

        @pl.when(at // each == j)
        def _(out_ref=out_ref):
            out_ref[...] = made


def pack(slots, rows, base, count, outs, waits=()):
    length = slots.shape[0]
    width = rows[0].shape[1]
    step = min(512, count)
    each = count // step
    return pl.pallas_call(
        functools.partial(pack_body, base, step, each, len(rows)),
        out_shape=(jax.ShapeDtypeStruct((count, width), jnp.bfloat16),) * outs,
        grid=(each * outs,),
        in_specs=[pl.BlockSpec((1, length), lambda i: (0, 0))]
        + [pl.BlockSpec(r.shape, lambda i: (0, 0)) for r in rows]
        + [pl.BlockSpec(memory_space=pl.ANY)] * len(waits),
        out_specs=tuple(
            pl.BlockSpec((step, width), lambda i, j=j: (jnp.clip(i - j * each, 0, each - 1), 0))
            for j in range(outs)
        ),
        compiler_params=params("arbitrary"),
        name="pack",
        cost_estimate=cost(1, 1),
    )(slots.reshape(1, length), *rows, *waits)


def unpack_body(parts, *refs):
    out_ref = refs[-1]
    step = out_ref.shape[0]
    made = None
    for slots_ref, rows_ref in zip(refs[:parts], refs[parts : 2 * parts]):
        count = rows_ref.shape[0]
        held = lax.broadcasted_iota(jnp.int32, (step, count), 1)
        chosen = jnp.where(slots_ref[...] == held, 1.0, 0.0).astype(jnp.bfloat16)
        more = dot(chosen, rows_ref[...], NN)
        made = more if made is None else made + more
    out_ref[...] = made.astype(out_ref.dtype)


def unpack(slots, rows, step, waits=()):
    length = slots[0].shape[0]
    width = rows[0].shape[1]
    count = sum(r.shape[0] for r in rows)
    return pl.pallas_call(
        functools.partial(unpack_body, len(rows)),
        out_shape=jax.ShapeDtypeStruct((length, width), jnp.bfloat16),
        grid=(length // step,),
        in_specs=[pl.BlockSpec((step, 1), lambda i: (i, 0))] * len(rows)
        + [pl.BlockSpec(r.shape, lambda i: (0, 0)) for r in rows]
        + [pl.BlockSpec(memory_space=pl.ANY)] * len(waits),
        out_specs=pl.BlockSpec((step, width), lambda i: (i, 0)),
        compiler_params=params("arbitrary"),
        name="unpack",
        cost_estimate=cost(2 * count * length * width, 2 * (length + count) * width),
    )(*(at.reshape(length, 1) for at in slots), *rows, *waits)


def middle_body(full_ref, out_ref, tokens_ref, gain_ref, bias_ref, middle_ref, routed_ref, all_ref):
    cols, _, width = full_ref.shape

    @pl.when(pl.program_id(0) == 0)
    def _():
        for z in range(cols):
            all_ref[:, z * width : (z + 1) * width] = out_ref[z]

    context = jnp.concatenate([full_ref[z] for z in range(cols)], axis=1)
    total = tokens_ref[...].astype(jnp.float32) + dot(context, all_ref[...], NT)
    middle_ref[...] = total
    mean = jnp.mean(total, axis=1, keepdims=True)
    centered = total - mean
    inverse = lax.rsqrt(jnp.mean(centered * centered, axis=1, keepdims=True) + EPSILON)
    routed_ref[...] = (centered * inverse * gain_ref[...] + bias_ref[...]).astype(jnp.bfloat16)


def middle_pass(full, out_full, tokens, gain, bias):
    cols, rows, width = full.shape
    depth = tokens.shape[1]
    step = min(256, rows)
    row = pl.BlockSpec((1, depth), lambda i: (0, 0))
    block = pl.BlockSpec((step, depth), lambda i: (i, 0))
    return pl.pallas_call(
        middle_body,
        out_shape=(
            jax.ShapeDtypeStruct((rows, depth), jnp.float32),
            jax.ShapeDtypeStruct((rows, depth), jnp.bfloat16),
        ),
        grid=(rows // step,),
        in_specs=[
            pl.BlockSpec((cols, step, width), lambda i: (0, i, 0)),
            pl.BlockSpec((cols, depth, width), lambda i: (0, 0, 0)),
            block,
            row,
            row,
        ],
        out_specs=(block, block),
        scratch_shapes=[pltpu.VMEM((depth, cols * width), jnp.bfloat16)],
        compiler_params=params("arbitrary"),
        name="middle_pass",
        cost_estimate=cost(2 * rows * depth * width * cols, 10 * rows * depth),
    )(full, out_full, tokens, gain, bias)


def forward_body(blocks, block, q_ref, k_ref, v_ref, *rest):
    o_ref, lse_ref = rest[-2:]
    width = q_ref.shape[1]
    heads = width // HEAD_DIM
    lane = lax.broadcasted_iota(jnp.int32, (block, width), 1)
    hidden = lax.broadcasted_iota(jnp.int32, (block, block), 1) > lax.broadcasted_iota(
        jnp.int32, (block, block), 0
    )
    for at, i in enumerate(blocks):
        span = (i + 1) * block
        here = pl.ds(at * block, block)
        o_ref[here, :] = jnp.zeros((block, width), o_ref.dtype)

        def one_head(h, carry, here=here, span=span, i=i):
            mine = (lane >= h * HEAD_DIM) & (lane < (h + 1) * HEAD_DIM)
            query = q_ref[pl.ds(i * block, block), :].astype(jnp.float32) * 0.125
            query = jnp.where(mine, query, 0.0).astype(jnp.bfloat16)
            edge = jnp.where(hidden, MASKED, dot(query, k_ref[pl.ds(span - block, block), :], NT))
            peak = jnp.max(edge, axis=1, keepdims=True)
            if i:
                past = dot(query, k_ref[pl.ds(0, span - block), :], NT)
                peak = jnp.maximum(peak, jnp.max(past, axis=1, keepdims=True))
            edge = jnp.exp(edge - peak)
            total = jnp.sum(edge, axis=1, keepdims=True)
            if i:
                past = jnp.exp(past - peak)
                total = total + jnp.sum(past, axis=1, keepdims=True)
            share = 1.0 / total
            mixed = dot((edge * share).astype(jnp.bfloat16), v_ref[pl.ds(span - block, block), :], NN)
            if i:
                mixed = mixed + dot(
                    (past * share).astype(jnp.bfloat16), v_ref[pl.ds(0, span - block), :], NN
                )
            o_ref[here, :] = jnp.where(mine, mixed.astype(o_ref.dtype), o_ref[here, :])
            logsum = jnp.broadcast_to(peak + jnp.log(total), (block, 128))
            lse_ref[pl.ds(h, 1), here] = logsum.T[0:1, :]
            return carry

        lax.fori_loop(0, heads, one_head, 0, unroll=heads)


def attend_forward(projected, blocks, block, waits=()):
    length, triple = projected.shape
    width = triple // 3
    heads = width // HEAD_DIM
    rows = len(blocks) * block
    spec = [pl.BlockSpec((length, width), lambda i, j=j: (0, j)) for j in range(3)]
    return pl.pallas_call(
        functools.partial(forward_body, blocks, block),
        out_shape=(
            jax.ShapeDtypeStruct((rows, width), jnp.bfloat16),
            jax.ShapeDtypeStruct((heads, rows), jnp.float32),
        ),
        grid=(1,),
        in_specs=spec + [pl.BlockSpec(memory_space=pl.ANY)] * len(waits),
        out_specs=(
            pl.BlockSpec((rows, width), lambda i: (0, 0)),
            pl.BlockSpec((heads, rows), lambda i: (0, 0)),
        ),
        compiler_params=params("arbitrary"),
        name="attend_forward",
        cost_estimate=cost(rows * width, rows * width),
    )(projected, projected, projected, *waits)


def backward_body(block, first, given, *refs):
    q_ref, do_ref, o_ref, lse_ref, k_ref, v_ref = refs[:6]
    outs = refs[6 + given :]
    out_ref, p_ref, ds_ref, qm_ref, dom_ref, dk_ref, dv_ref = outs[:1] + outs[-6:]
    width = q_ref.shape[1]
    heads = width // HEAD_DIM
    count = q_ref.shape[0] // block
    lane = lax.broadcasted_iota(jnp.int32, (block, width), 1)
    hidden = lax.broadcasted_iota(jnp.int32, (block, block), 0) > lax.broadcasted_iota(
        jnp.int32, (block, block), 1
    )
    for at in reversed(range(count)):
        i = first + at
        span = (i + 1) * block
        here = pl.ds(at * block, block)

        def one_head(h, carry, here=here, span=span, i=i):
            mine = (lane >= h * HEAD_DIM) & (lane < (h + 1) * HEAD_DIM)
            query = q_ref[here, :].astype(jnp.float32) * 0.125
            query = jnp.where(mine, query, 0.0).astype(jnp.bfloat16)
            grad = jnp.where(mine, do_ref[here, :].astype(jnp.float32), 0.0)
            delta = jnp.sum(grad * o_ref[here, :].astype(jnp.float32), axis=1, keepdims=True)
            delta = jnp.broadcast_to(delta, (block, 128)).T[0:1, :]
            grad = grad.astype(jnp.bfloat16)
            logsum = lse_ref[pl.ds(h, 1), here]
            column = pl.ds(pl.multiple_of(h * block, block), block)
            qm_ref[column, :] = query
            dom_ref[column, :] = grad

            def part(rows, edge):
                scores = dot(k_ref[rows, :], query, NT)
                if edge:
                    scores = jnp.where(hidden, MASKED, scores)
                probs = jnp.exp(scores - logsum)
                p_ref[rows, column] = probs.astype(jnp.bfloat16)
                grad_probs = dot(v_ref[rows, :], grad, NT)
                ds_ref[rows, column] = (probs * (grad_probs - delta)).astype(jnp.bfloat16)

            if i:
                part(pl.ds(0, span - block), False)
            part(pl.ds(span - block, block), True)
            dq = dot(ds_ref[pl.ds(0, span), column], k_ref[pl.ds(0, span), :], TN)
            out_ref[here, pl.ds(0, width)] = jnp.where(
                mine, (dq * 0.125).astype(out_ref.dtype), out_ref[here, pl.ds(0, width)]
            )
            return carry

        lax.fori_loop(0, heads, one_head, 0, unroll=heads)
        new_v = dot(p_ref[pl.ds(0, span), :], dom_ref[...], NN)
        new_k = dot(ds_ref[pl.ds(0, span), :], qm_ref[...], NN)
        if at == count - 1:
            old_k, old_v = (refs[6][...], refs[7][...]) if given > 1 else (0.0, 0.0)
            dv_ref[...] = old_v + new_v
            dk_ref[...] = old_k + new_k
        else:
            dv_ref[pl.ds(0, span), :] += new_v
            dk_ref[pl.ds(0, span), :] += new_k
        low = pl.ds(i * block, block)
        out_ref[here, pl.ds(width, width)] = dk_ref[low, :].astype(out_ref.dtype)
        out_ref[here, pl.ds(2 * width, width)] = dv_ref[low, :].astype(out_ref.dtype)
    if first:
        outs[1][...] = dk_ref[pl.ds(0, first * block), :]
        outs[2][...] = dv_ref[pl.ds(0, first * block), :]


def attend_backward(projected, grad_context, context, logsum, block, first, carried=()):
    rows, width = context.shape
    heads = width // HEAD_DIM
    length = first * block + rows
    half = lambda j: pl.BlockSpec((rows, width), lambda i: (first * block // rows, j))
    own = pl.BlockSpec((rows, width), lambda i: (0, 0))
    low = pl.BlockSpec((first * block, width), lambda i: (0, 0))
    rest = jax.ShapeDtypeStruct((first * block, width), jnp.float32)
    more = bool(first)
    return pl.pallas_call(
        functools.partial(backward_body, block, first, len(carried)),
        out_shape=(jax.ShapeDtypeStruct((rows, 3 * width), jnp.bfloat16),) + (rest,) * (2 * more),
        grid=(1,),
        in_specs=[
            half(0),
            own,
            own,
            pl.BlockSpec((heads, rows), lambda i: (0, 0)),
            pl.BlockSpec((length, width), lambda i: (0, 1)),
            pl.BlockSpec((length, width), lambda i: (0, 2)),
        ]
        + [own] * len(carried),
        out_specs=(pl.BlockSpec((rows, 3 * width), lambda i: (0, 0)),) + (low,) * (2 * more),
        scratch_shapes=[
            pltpu.VMEM((length, heads * block), jnp.bfloat16),
            pltpu.VMEM((length, heads * block), jnp.bfloat16),
            pltpu.VMEM((heads * block, width), jnp.bfloat16),
            pltpu.VMEM((heads * block, width), jnp.bfloat16),
            pltpu.VMEM((length, width), jnp.float32),
            pltpu.VMEM((length, width), jnp.float32),
        ],
        compiler_params=params("arbitrary"),
        name="attend_backward",
        cost_estimate=cost(
            20 * rows * length * width, 16 * length * width, rows * length * heads
        ),
    )(projected, grad_context, context, logsum, projected, projected, *carried)


ROOT = math.sqrt(2.0 / math.pi)
CUBE = 0.044715


def expert_body(given, x_ref, gy_ref, win_ref, wback_ref, *rest):
    out_ref, active_ref, slope_ref, *sent = rest[given:]
    rows, depth = x_ref.shape
    hidden = dot(x_ref[...], win_ref[...], NN)
    square = hidden * hidden
    bent = jnp.tanh(ROOT * hidden * (1.0 + CUBE * square))
    active = (0.5 * hidden * (1.0 + bent)).astype(jnp.bfloat16)
    slope = 0.5 * (1.0 + bent) + 0.5 * hidden * (1.0 - bent * bent) * (
        ROOT * (1.0 + 3.0 * CUBE * square)
    )
    active_ref[...] = active.reshape(active_ref.shape)
    parts = out_ref.shape[0]
    wide = depth // parts
    made = dot(active, wback_ref[...], NN).astype(jnp.bfloat16)
    for j in range(parts):
        out_ref[j] = made[:, j * wide : (j + 1) * wide]
    grad_active = dot(gy_ref[...].reshape(rows, depth), wback_ref[...], NT)
    grad_hidden = (grad_active * slope).astype(jnp.bfloat16)
    slope_ref[...] = grad_hidden.reshape(slope_ref.shape)
    back = dot(grad_hidden, win_ref[...], NT).astype(jnp.bfloat16)
    first = 0
    for ref in sent:
        wide = ref.shape[-1]
        ref[...] = back[:, first : first + wide].reshape(ref.shape)
        first += wide


def expert_pass(chunk, x, grad_y, w_in, w_back, kept, sent, parts, pieces, waits=()):
    e, low, size = chunk
    sources, members, cap, depth = grad_y.shape
    rows = sources * size
    width = w_in.shape[2]
    step = min(256, rows)
    group = step // size
    at = low // size
    given = [*kept, *sent]
    aliases = {4 + j: (1 if kept else 3) + j for j in range(len(given))}
    keep = jax.ShapeDtypeStruct((sources, cap, width), jnp.bfloat16)
    keep_spec = pl.BlockSpec((group, size, width), lambda i: (i, at, 0))
    piece = tuple(jax.ShapeDtypeStruct((sources, members, cap, w), jnp.bfloat16) for w in pieces)
    piece_spec = tuple(
        pl.BlockSpec((group, None, size, w), lambda i: (i, e % members, at, 0)) for w in pieces
    )
    made = pl.pallas_call(
        functools.partial(expert_body, len(given) + len(waits)),
        out_shape=(jax.ShapeDtypeStruct((parts, rows, depth // parts), jnp.bfloat16), keep, keep)
        + piece,
        grid=(rows // step,),
        in_specs=[
            pl.BlockSpec((step, depth), lambda i: (i, 0)),
            pl.BlockSpec((group, None, size, depth), lambda i: (i, e % members, at, 0)),
            pl.BlockSpec((None, depth, width), lambda i: (e, 0, 0)),
            pl.BlockSpec((None, width, depth), lambda i: (e, 0, 0)),
        ]
        + [pl.BlockSpec(memory_space=pl.ANY)] * (len(given) + len(waits)),
        out_specs=(
            pl.BlockSpec((parts, step, depth // parts), lambda i: (0, i, 0)),
            keep_spec,
            keep_spec,
        )
        + piece_spec,
        input_output_aliases=aliases,
        compiler_params=params("arbitrary"),
        name="expert_pass",
        cost_estimate=cost(
            8 * rows * depth * width, 4 * width * depth + 12 * rows * depth, rows * width
        ),
    )(x, grad_y, w_in, w_back, *given, *waits)
    return made[0], made[1:3], list(made[3:])


def weight_body(given, x_ref, gy_ref, router_ref, pick_ref, active_ref, slope_ref, *rest):
    gin_ref, gback_ref, token_ref, xt_ref, gyg_ref = rest[given:]
    token_ref[...] = jnp.zeros_like(token_ref)
    rows, depth = x_ref.shape

    @pl.when(pl.program_id(0) == 0)
    def _():
        logits = dot(x_ref[...], router_ref[...], NN)
        raised = jnp.exp(logits - jnp.max(logits, axis=1, keepdims=True))
        gate = jnp.sum(raised * pick_ref[...], axis=1, keepdims=True)
        gate = gate / jnp.sum(raised, axis=1, keepdims=True)
        xt_ref[...] = (x_ref[...].astype(jnp.float32) * gate).T.astype(jnp.bfloat16)
        grad_y = gy_ref[...].reshape(rows, depth).astype(jnp.float32)
        gyg_ref[...] = (grad_y * gate).astype(jnp.bfloat16)

    gin_ref[...] = dot(xt_ref[...], slope_ref[...], NN)
    gback_ref[...] = dot(active_ref[...], gyg_ref[...], TN)


def weight_pass(e, local, x, grad_y, router, pick, active, slope, sent, waits=()):
    rows, width = active.shape
    sources, members, cap, depth = grad_y.shape
    step = min(256, width)
    sent = list(sent or [])
    return pl.pallas_call(
        functools.partial(weight_body, len(sent) + len(waits)),
        out_shape=(
            jax.ShapeDtypeStruct((local, depth, width), jnp.float32),
            jax.ShapeDtypeStruct((local, width, depth), jnp.float32),
            jax.ShapeDtypeStruct((8, 128), jnp.float32),
        ),
        grid=(width // step,),
        in_specs=[
            pl.BlockSpec((rows, depth), lambda i: (0, 0)),
            pl.BlockSpec((sources, None, cap, depth), lambda i: (0, e % members, 0, 0)),
            pl.BlockSpec(router.shape, lambda i: (0, 0)),
            pl.BlockSpec(pick.shape, lambda i: (0, 0)),
            pl.BlockSpec((rows, step), lambda i: (0, i)),
            pl.BlockSpec((rows, step), lambda i: (0, i)),
        ]
        + [pl.BlockSpec(memory_space=pl.ANY)] * (len(sent) + len(waits)),
        out_specs=(
            pl.BlockSpec((None, depth, step), lambda i: (e, 0, i)),
            pl.BlockSpec((None, step, depth), lambda i: (e, i, 0)),
            pl.BlockSpec((8, 128), lambda i: (0, 0)),
        ),
        scratch_shapes=[
            pltpu.VMEM((depth, rows), jnp.bfloat16),
            pltpu.VMEM((rows, depth), jnp.bfloat16),
        ],
        input_output_aliases={6 + j: j for j in range(len(sent))},
        compiler_params=params("arbitrary"),
        name="weight_pass",
        cost_estimate=cost(4 * rows * depth * width, 8 * width * depth + 8 * rows * depth),
    )(x, grad_y, router, pick, active, slope, *sent, *waits)


def swap(blocks, axis):
    return lax.all_to_all(blocks, axis, split_axis=0, concat_axis=0, tiled=True)


def tie(*values):
    return lax.optimization_barrier(values)


def row_stats(values):
    mean = jnp.mean(values, axis=-1, keepdims=True)
    centered = values - mean
    variance = jnp.mean(centered * centered, axis=-1, keepdims=True)
    return (mean, lax.rsqrt(variance + EPSILON))


def layer_stats(values):
    mean = jnp.mean(values, axis=-1, keepdims=True)
    centered = values - mean
    variance = jnp.mean(centered * centered, axis=-1, keepdims=True)
    inverse = lax.rsqrt(variance + EPSILON)
    return (centered * inverse, inverse)


def norm_back(grad_normed, normed, inverse, gain):
    grad_hat = grad_normed * gain
    centred_grad = grad_hat - jnp.mean(grad_hat, axis=-1, keepdims=True)
    return inverse * (centred_grad - normed * jnp.mean(grad_hat * normed, axis=-1, keepdims=True))


def slot_layout(expert_ids, experts, cap):
    chosen = expert_ids[:, 0]
    length = chosen.shape[0]
    table = chosen[:, None] == jnp.arange(experts, dtype=jnp.int32)[None, :]
    order = jnp.arange(length, dtype=jnp.int32)
    before = (order[:, None] > order[None, :]).astype(jnp.bfloat16)
    counted = jnp.dot(before, table.astype(jnp.bfloat16), preferred_element_type=jnp.float32)
    ranks = jnp.sum(jnp.where(table, counted, 0.0), axis=1).astype(jnp.int32)
    return (chosen, ranks, table.astype(jnp.float32))


def per_device(
    tokens, w_qkv, w_out, w_router, ln_gains, ln_biases, w_in, w_back, expert_ids, cotangent
):
    rows_all, cols_all = lax.axis_size("row"), lax.axis_size("col")
    col = lax.axis_index("col")
    length, depth = tokens.shape
    share = depth // rows_all
    width = w_qkv.shape[2]
    experts = w_router.shape[1]
    local = w_in.shape[0]
    cap = 2 * length // experts
    block_rows = rows_all * cap
    block = min(256, length // 2)
    part = length // cols_all
    members = max(1, local // 2)
    pieces = (depth * 5 // 8, depth * 3 // 8)

    def own(values, axis=0):
        return lax.dynamic_slice_in_dim(values, col * part, part, axis)

    def send(packed):
        return swap(packed.reshape(rows_all, cap, depth), "row").reshape(block_rows, depth)

    stacked = w_qkv.transpose(1, 0, 2).reshape(share, 3 * width)
    weights = jnp.concatenate([stacked, w_router, ln_gains.T, ln_biases.T], axis=1)
    weights = lax.all_gather(weights, "row", axis=0, tiled=True)
    mean_one, inverse_one = row_stats(tokens.astype(jnp.float32))

    chosen, ranks, select = slot_layout(expert_ids, experts, cap)
    out_block, ranks = tie(w_out.T, ranks)
    out_block = swap(jnp.broadcast_to(out_block[None], (cols_all, share, width)), "col")
    slots = chosen * cap + ranks
    slots_by_local = ((chosen % local) * rows_all + chosen // local) * cap + ranks
    member = chosen % local
    slots_by_group = [
        jnp.where(
            member // members == g,
            ((chosen // local) * members + member % members) * cap + ranks,
            -1,
        )
        for g in range(local // members)
    ]

    slots_by_pair = slots_by_local - slots_by_local
    for g, at in enumerate(slots_by_group):
        slots_by_pair = jnp.where(at >= 0, at + g * members * block_rows, slots_by_pair)

    def pack_group(g, waits):
        rows = members * block_rows
        return pack(slots_by_pair, [cotangent], g * rows, rows, 1, waits)[0]

    grad_packed = [pack_group(0, [])]
    weights, grad_packed[0], out_block, mean_one, inverse_one = tie(
        weights, grad_packed[0], out_block, mean_one, inverse_one
    )
    qkv_full = weights[:, : 3 * width]
    router_full = weights[:, 3 * width : 3 * width + experts]
    norms = weights[:, 3 * width + experts :].astype(jnp.float32).T
    gains, biases = norms[0:2], norms[2:4]

    resid_in = tokens.astype(jnp.float32)
    normed_one = (resid_in - mean_one) * inverse_one
    normal_in = (normed_one * gains[0] + biases[0]).astype(jnp.bfloat16)
    projected = jnp.dot(normal_in, qkv_full, preferred_element_type=jnp.float32).astype(jnp.bfloat16)

    context, logsum = attend_forward(projected, tuple(range(length // block)), block)
    context, grad_packed[0] = tie(context, grad_packed[0])
    full = lax.all_gather(context, "col", axis=0)
    grad_packed += [pack_group(g, [context]) for g in range(1, local // members)]
    out_full = lax.all_gather(out_block, "row", axis=1, tiled=True)
    grad_arrived = []
    for g in range(local // members):
        if g:
            grad_arrived[-1], grad_packed[g] = tie(grad_arrived[-1], grad_packed[g])
        grad_arrived.append(swap(grad_packed[g].reshape(rows_all, members, cap, depth), "row"))
    full, out_full = tie(full, out_full)
    middle, routed = middle_pass(full, out_full, tokens, gains[1:2], biases[1:2])

    short = cap // 2
    chunks = [(0, 0, short), (0, short, short)] + [(e, 0, cap) for e in range(1, local)]
    split = (ranks // short * rows_all + chosen // local) * short + ranks % short
    slots_by_chunk = jnp.where(chosen % local == 0, split, slots_by_local)

    def pack_chunk(k, waits):
        e, low, size = chunks[k]
        base = (e * cap + low) * rows_all
        return pack(slots_by_chunk, [routed], base, size * rows_all, 1, waits)[0]

    packed = [pack_chunk(k, []) for k in range(2)]
    packed[0], grad_arrived[-1] = tie(packed[0], grad_arrived[-1])

    logits = jnp.dot(routed, router_full, preferred_element_type=jnp.float32)
    probs = jax.nn.softmax(logits, axis=-1)
    gate = jnp.sum(probs * select, axis=-1, keepdims=True)

    arrived, summed, kept, sent = [], [], [], []
    final = len(chunks) - 1
    for k, (e, low, size) in enumerate(chunks):
        moved = swap(packed[k].reshape(rows_all, size, depth), "row")
        arrived.append(moved.reshape(rows_all * size, depth))
        if k < final:
            packed[k + 1], arrived[k] = tie(packed[k + 1], arrived[k])
        if k:
            then = packed[k + 1] if k < final else sent[0][0]
            then, summed[k - 1], arrived[k] = tie(then, summed[k - 1], arrived[k])
            summed[k - 1] = lax.psum_scatter(
                summed[k - 1], "col", scatter_dimension=0, tiled=True
            )
            if k < final:
                packed[k + 1] = then
            else:
                sent[0][0] = then
        waits = packed[1:2] if k == 0 else summed[:1] if k == final else []
        made, both, pair = expert_pass(
            chunks[k],
            arrived[k],
            grad_arrived[e // members],
            w_in,
            w_back,
            kept.pop() if low else [],
            sent.pop() if low or e % members else [],
            cols_all,
            pieces,
            waits,
        )
        kept.append(both)
        summed.append(made)
        sent.append(pair)
        if k + 2 <= final:
            packed.append(pack_chunk(k + 2, [made]))
    active = [v[0].reshape(block_rows, -1) for v in kept]
    slope = [v[1].reshape(block_rows, -1) for v in kept]

    def joined(values):
        first = [v.reshape(rows_all, short, -1) for v in values[:2]]
        whole = [v.reshape(rows_all, cap, -1) for v in values[2:]]
        return [jnp.concatenate(first, axis=1)] + whole

    arrived = [v.reshape(block_rows, depth) for v in joined(arrived)]

    step = min(256, length)
    order = [(g, f) for f in range(len(pieces)) for g in range(len(sent))]
    grad_sent = []
    grad_weights = None
    token = None
    row = lax.axis_index("row")

    def weigh(e, waits):
        pick = jnp.arange(experts, dtype=jnp.int32)[None, :] == row * local + e
        return weight_pass(
            e,
            local,
            arrived[e],
            grad_arrived[e // members],
            router_full,
            pick.astype(jnp.float32),
            active[e],
            slope[e],
            grad_weights,
            waits,
        )

    waits = slope[-1:]
    last = None
    for f, wide in enumerate(pieces):
        for e in range(f * local // len(pieces), (f + 1) * local // len(pieces)):
            *grad_weights, token = weigh(e, waits)
            waits = [token]
        rows = []
        for g in range(len(sent)):
            piece = sent[g][f]
            if last is not None:
                piece, last = tie(piece, last)
                if rows:
                    rows[-1] = last
                else:
                    ended[-1] = last
            if f == 0 and g == len(sent) - 1:
                piece, slope[-1] = tie(piece, slope[-1])
            if f and g == len(sent) - 1:
                piece, whole = tie(piece, whole)
            last = swap(piece, "row")
            if f == 0 and g == 0:
                last, made = tie(last, summed[-1])
                summed[-1] = lax.psum_scatter(made, "col", scatter_dimension=0, tiled=True)
            rows.append(last)
        if f == 0:
            ended = rows
            sent[0][1], token = tie(sent[0][1], token)
            waits = [token]
        else:
            homed = jnp.stack(joined(summed), axis=1)
            homed, token = tie(homed, token)
            waits = [token]
            grad_sent.append(lax.psum_scatter(whole, "col", scatter_dimension=0, tiled=True))
        whole = unpack(slots_by_group, [v.reshape(-1, wide) for v in rows], step, waits)
        if f:
            rows[-1], homed = tie(rows[-1], homed)
            homed = swap(homed, "row")
            whole, homed = tie(whole, homed)
        waits = [whole]
    grad_sent.append(lax.psum_scatter(whole, "col", scatter_dimension=0, tiled=True))

    grad_in, grad_back = grad_weights
    returned = unpack(
        [slots], [homed.reshape(experts * cap, depth // cols_all)], step, grad_sent[:1]
    ).astype(jnp.float32)
    columns = depth // cols_all

    def own_columns(values):
        return lax.dynamic_slice_in_dim(values, col * columns, columns, 1)

    mixed = (own_columns(middle) + gate * returned).astype(jnp.bfloat16)
    grad_gate = jnp.sum(own_columns(cotangent).astype(jnp.float32) * returned, axis=-1)
    grad_gate = swap(grad_gate.reshape(cols_all, part), "col")
    grad_gate = jnp.sum(grad_gate, axis=0)[:, None]
    mixed_full = lax.all_gather(mixed, "col", axis=0)

    own_gate, own_probs, own_select = own(gate), own(probs), own(select)
    grad_logits = (grad_gate * own_probs * (own_select - own_gate)).astype(jnp.bfloat16)
    own_routed = own(routed)
    grad_router = jnp.einsum(
        "td,te->de", own_routed, grad_logits, preferred_element_type=jnp.float32
    )
    grad_y = own(cotangent).astype(jnp.float32)
    normed_own, inverse_own = layer_stats(own(middle))
    grad_sent = jnp.concatenate(grad_sent, axis=1).astype(jnp.float32) * own_gate
    grad_routed = grad_sent + jnp.einsum(
        "te,de->td", grad_logits, router_full, preferred_element_type=jnp.float32
    )
    gain_two = jnp.sum(grad_routed * normed_own, axis=0)
    bias_two = jnp.sum(grad_routed, axis=0)
    grad_middle = grad_y + norm_back(grad_routed, normed_own, inverse_own, gains[1])
    grad_attn = grad_middle.astype(jnp.bfloat16)
    grad_context = jnp.einsum(
        "td,zdc->ztc", grad_attn, out_full, preferred_element_type=jnp.float32
    ).astype(jnp.bfloat16)
    grad_context = swap(grad_context, "col")
    context_own = own(full, 1)
    grad_out = jnp.einsum("td,ztc->dzc", grad_attn, context_own, preferred_element_type=jnp.float32)
    plane = jnp.concatenate([grad_out.reshape(depth, cols_all * width), grad_router], axis=1)
    plane = swap(plane.astype(jnp.bfloat16).reshape(rows_all, share, -1), "row")
    grad_context = grad_context.reshape(length, width)
    grad_proj = attend_backward(projected, grad_context, context, logsum, block, 0)[0]
    grad_proj, plane, mixed_full = tie(grad_proj, plane, mixed_full)

    def spread(grads):
        made = jnp.einsum("tc,dc->td", grads, qkv_full, preferred_element_type=jnp.float32)
        return lax.psum_scatter(
            made.astype(jnp.bfloat16), "col", scatter_dimension=0, tiled=True
        ).astype(jnp.float32)

    grad_normal = spread(grad_proj)
    mixed_out = mixed_full.transpose(1, 0, 2).reshape(length, depth)
    grad_qkv = jnp.einsum("td,tc->dc", normal_in, grad_proj, preferred_element_type=jnp.float32)
    plane = jnp.sum(plane.astype(jnp.float32), axis=0)
    router_share = plane[:, cols_all * width :].reshape(1, share, experts)
    out_share = plane[:, : cols_all * width].reshape(share, cols_all, width).transpose(1, 0, 2)
    router_share = jnp.broadcast_to(router_share, (cols_all, share, experts))
    plane = jnp.concatenate([out_share, router_share], axis=2).astype(jnp.bfloat16)
    plane = jnp.sum(swap(plane, "col").astype(jnp.float32), axis=0)
    out_share, router_share = plane[:, :width].T, plane[:, width:]
    grad_normal, out_share, mixed_out, grad_qkv = tie(
        grad_normal, out_share, mixed_out, grad_qkv
    )

    own_normed, own_inverse = layer_stats(own(tokens).astype(jnp.float32))
    grad_tokens = (
        grad_middle + norm_back(grad_normal, own_normed, own_inverse, gains[0])
    ).astype(jnp.bfloat16)
    grad_tokens = lax.all_gather(grad_tokens, "col", axis=0, tiled=True)
    small = [
        jnp.sum(grad_normal * own_normed, axis=0),
        jnp.sum(grad_normal, axis=0),
        gain_two,
        bias_two,
    ]
    small = swap(jnp.stack(small).reshape(4, rows_all, share).transpose(1, 0, 2), "row")
    small = jnp.sum(small, axis=0)
    small = jnp.sum(swap(jnp.broadcast_to(small[None], (cols_all, 4, share)), "col"), axis=0)
    qkv_share = swap(grad_qkv.astype(jnp.bfloat16).reshape(rows_all, share, -1), "row")
    qkv_share = jnp.sum(qkv_share.astype(jnp.float32), axis=0)
    qkv_share = qkv_share.reshape(share, 3, width).transpose(1, 0, 2)
    return (
        mixed_out,
        grad_tokens,
        qkv_share,
        out_share,
        router_share,
        jnp.stack([small[0], small[2]]),
        small[1],
        small[3],
        grad_in,
        grad_back,
    )


def solution(mesh):
    return jax.shard_map(
        per_device,
        mesh=mesh,
        in_specs=(
            P("row", None),
            P(None, "row", "col"),
            P("col", "row"),
            P("row", None),
            P(None, "row"),
            P(None, "row"),
            P("row", None, "col"),
            P("row", "col", None),
            P("row", None),
            P("row", None),
        ),
        out_specs=(
            P("row", None),
            P("row", None),
            P(None, "row", "col"),
            P("col", "row"),
            P("row", None),
            P(None, "row"),
            P("row"),
            P("row"),
            P("row", None, "col"),
            P("row", "col", None),
        ),
        check_vma=False,
    )
```

```python
import functools, math
import jax, jax.numpy as jnp
from jax import lax
from jax.experimental import pallas as pl
from jax.experimental.pallas import tpu as pltpu
from jax.sharding import PartitionSpec as P

HEAD_DIM = 64
EPSILON = 1e-05
MASKED = -1e30
VMEM = 60 << 20


def params(*kinds):
    return pltpu.CompilerParams(dimension_semantics=kinds or None, vmem_limit_bytes=VMEM)


def cost(flops, moved, special=0):
    return pl.CostEstimate(flops=flops, bytes_accessed=moved, transcendentals=special)


def dot(a, b, dims):
    return lax.dot_general(a, b, (dims, ((), ())), preferred_element_type=jnp.float32)

NN = ((1,), (0,))
NT = ((1,), (1,))
TN = ((0,), (0,))


def pack_body(base, step, each, parts, slots_ref, *rest):
    rows_refs, outs = rest[:parts], rest[-((pl.num_programs(0)) // each) :]
    at = pl.program_id(0)
    made = None
    first = 0
    for rows_ref in rows_refs:
        length = rows_ref.shape[0]
        wanted = base + at * step + lax.broadcasted_iota(jnp.int32, (step, length), 0)
        chosen = jnp.where(slots_ref[:, pl.ds(first, length)] == wanted, 1.0, 0.0)
        more = dot(chosen.astype(jnp.bfloat16), rows_ref[...], NN)
        made = more if made is None else made + more
        first += length
    made = made.astype(jnp.bfloat16)
    for j, out_ref in enumerate(outs):

        @pl.when(at // each == j)
        def _(out_ref=out_ref):
            out_ref[...] = made


def pack(slots, rows, base, count, outs, waits=()):
    length = slots.shape[0]
    width = rows[0].shape[1]
    step = min(512, count)
    each = count // step
    return pl.pallas_call(
        functools.partial(pack_body, base, step, each, len(rows)),
        out_shape=(jax.ShapeDtypeStruct((count, width), jnp.bfloat16),) * outs,
        grid=(each * outs,),
        in_specs=[pl.BlockSpec((1, length), lambda i: (0, 0))]
        + [pl.BlockSpec(r.shape, lambda i: (0, 0)) for r in rows]
        + [pl.BlockSpec(memory_space=pl.ANY)] * len(waits),
        out_specs=tuple(
            pl.BlockSpec((step, width), lambda i, j=j: (jnp.clip(i - j * each, 0, each - 1), 0))
            for j in range(outs)
        ),
        compiler_params=params("arbitrary"),
        name="pack",
        cost_estimate=cost(1, 1),
    )(slots.reshape(1, length), *rows, *waits)


def unpack_body(parts, *refs):
    out_ref = refs[-1]
    step = out_ref.shape[0]
    made = None
    for slots_ref, rows_ref in zip(refs[:parts], refs[parts : 2 * parts]):
        count = rows_ref.shape[0]
        held = lax.broadcasted_iota(jnp.int32, (step, count), 1)
        chosen = jnp.where(slots_ref[...] == held, 1.0, 0.0).astype(jnp.bfloat16)
        more = dot(chosen, rows_ref[...], NN)
        made = more if made is None else made + more
    out_ref[...] = made.astype(out_ref.dtype)


def unpack(slots, rows, step, waits=()):
    length = slots[0].shape[0]
    width = rows[0].shape[1]
    count = sum(r.shape[0] for r in rows)
    return pl.pallas_call(
        functools.partial(unpack_body, len(rows)),
        out_shape=jax.ShapeDtypeStruct((length, width), jnp.bfloat16),
        grid=(length // step,),
        in_specs=[pl.BlockSpec((step, 1), lambda i: (i, 0))] * len(rows)
        + [pl.BlockSpec(r.shape, lambda i: (0, 0)) for r in rows]
        + [pl.BlockSpec(memory_space=pl.ANY)] * len(waits),
        out_specs=pl.BlockSpec((step, width), lambda i: (i, 0)),
        compiler_params=params("arbitrary"),
        name="unpack",
        cost_estimate=cost(2 * count * length * width, 2 * (length + count) * width),
    )(*(at.reshape(length, 1) for at in slots), *rows, *waits)


def middle_body(full_ref, out_ref, tokens_ref, gain_ref, bias_ref, middle_ref, routed_ref, all_ref):
    cols, _, width = full_ref.shape

    @pl.when(pl.program_id(0) == 0)
    def _():
        for z in range(cols):
            all_ref[:, z * width : (z + 1) * width] = out_ref[z]

    context = jnp.concatenate([full_ref[z] for z in range(cols)], axis=1)
    total = tokens_ref[...].astype(jnp.float32) + dot(context, all_ref[...], NT)
    middle_ref[...] = total
    mean = jnp.mean(total, axis=1, keepdims=True)
    centered = total - mean
    inverse = lax.rsqrt(jnp.mean(centered * centered, axis=1, keepdims=True) + EPSILON)
    routed_ref[...] = (centered * inverse * gain_ref[...] + bias_ref[...]).astype(jnp.bfloat16)


def middle_pass(full, out_full, tokens, gain, bias):
    cols, rows, width = full.shape
    depth = tokens.shape[1]
    step = min(512, rows)
    row = pl.BlockSpec((1, depth), lambda i: (0, 0))
    block = pl.BlockSpec((step, depth), lambda i: (i, 0))
    return pl.pallas_call(
        middle_body,
        out_shape=(
            jax.ShapeDtypeStruct((rows, depth), jnp.float32),
            jax.ShapeDtypeStruct((rows, depth), jnp.bfloat16),
        ),
        grid=(rows // step,),
        in_specs=[
            pl.BlockSpec((cols, step, width), lambda i: (0, i, 0)),
            pl.BlockSpec((cols, depth, width), lambda i: (0, 0, 0)),
            block,
            row,
            row,
        ],
        out_specs=(block, block),
        scratch_shapes=[pltpu.VMEM((depth, cols * width), jnp.bfloat16)],
        compiler_params=params("arbitrary"),
        name="middle_pass",
        cost_estimate=cost(2 * rows * depth * width * cols, 10 * rows * depth),
    )(full, out_full, tokens, gain, bias)


def forward_body(blocks, block, q_ref, k_ref, v_ref, *rest):
    o_ref, lse_ref = rest[-2:]
    width = q_ref.shape[1]
    heads = width // HEAD_DIM
    lane = lax.broadcasted_iota(jnp.int32, (block, width), 1)
    hidden = lax.broadcasted_iota(jnp.int32, (block, block), 1) > lax.broadcasted_iota(
        jnp.int32, (block, block), 0
    )
    for at, i in enumerate(blocks):
        span = (i + 1) * block
        here = pl.ds(at * block, block)
        o_ref[here, :] = jnp.zeros((block, width), o_ref.dtype)

        def one_head(h, carry, here=here, span=span, i=i):
            mine = (lane >= h * HEAD_DIM) & (lane < (h + 1) * HEAD_DIM)
            query = q_ref[pl.ds(i * block, block), :].astype(jnp.float32) * 0.125
            query = jnp.where(mine, query, 0.0).astype(jnp.bfloat16)
            edge = jnp.where(hidden, MASKED, dot(query, k_ref[pl.ds(span - block, block), :], NT))
            peak = jnp.max(edge, axis=1, keepdims=True)
            if i:
                past = dot(query, k_ref[pl.ds(0, span - block), :], NT)
                peak = jnp.maximum(peak, jnp.max(past, axis=1, keepdims=True))
            edge = jnp.exp(edge - peak)
            total = jnp.sum(edge, axis=1, keepdims=True)
            if i:
                past = jnp.exp(past - peak)
                total = total + jnp.sum(past, axis=1, keepdims=True)
            share = 1.0 / total
            mixed = dot((edge * share).astype(jnp.bfloat16), v_ref[pl.ds(span - block, block), :], NN)
            if i:
                mixed = mixed + dot(
                    (past * share).astype(jnp.bfloat16), v_ref[pl.ds(0, span - block), :], NN
                )
            o_ref[here, :] = jnp.where(mine, mixed.astype(o_ref.dtype), o_ref[here, :])
            logsum = jnp.broadcast_to(peak + jnp.log(total), (block, 128))
            lse_ref[pl.ds(h, 1), here] = logsum.T[0:1, :]
            return carry

        lax.fori_loop(0, heads, one_head, 0, unroll=heads)


def attend_forward(projected, blocks, block, waits=()):
    length, triple = projected.shape
    width = triple // 3
    heads = width // HEAD_DIM
    rows = len(blocks) * block
    spec = [pl.BlockSpec((length, width), lambda i, j=j: (0, j)) for j in range(3)]
    return pl.pallas_call(
        functools.partial(forward_body, blocks, block),
        out_shape=(
            jax.ShapeDtypeStruct((rows, width), jnp.bfloat16),
            jax.ShapeDtypeStruct((heads, rows), jnp.float32),
        ),
        grid=(1,),
        in_specs=spec + [pl.BlockSpec(memory_space=pl.ANY)] * len(waits),
        out_specs=(
            pl.BlockSpec((rows, width), lambda i: (0, 0)),
            pl.BlockSpec((heads, rows), lambda i: (0, 0)),
        ),
        compiler_params=params("arbitrary"),
        name="attend_forward",
        cost_estimate=cost(rows * width, rows * width),
    )(projected, projected, projected, *waits)


def backward_body(block, first, given, *refs):
    q_ref, do_ref, o_ref, lse_ref, k_ref, v_ref = refs[:6]
    outs = refs[6 + given :]
    out_ref, p_ref, ds_ref, qm_ref, dom_ref, dk_ref, dv_ref = outs[:1] + outs[-6:]
    width = q_ref.shape[1]
    heads = width // HEAD_DIM
    count = q_ref.shape[0] // block
    lane = lax.broadcasted_iota(jnp.int32, (block, width), 1)
    hidden = lax.broadcasted_iota(jnp.int32, (block, block), 0) > lax.broadcasted_iota(
        jnp.int32, (block, block), 1
    )
    for at in reversed(range(count)):
        i = first + at
        span = (i + 1) * block
        here = pl.ds(at * block, block)

        def one_head(h, carry, here=here, span=span, i=i):
            mine = (lane >= h * HEAD_DIM) & (lane < (h + 1) * HEAD_DIM)
            query = q_ref[here, :].astype(jnp.float32) * 0.125
            query = jnp.where(mine, query, 0.0).astype(jnp.bfloat16)
            grad = jnp.where(mine, do_ref[here, :].astype(jnp.float32), 0.0)
            delta = jnp.sum(grad * o_ref[here, :].astype(jnp.float32), axis=1, keepdims=True)
            delta = jnp.broadcast_to(delta, (block, 128)).T[0:1, :]
            grad = grad.astype(jnp.bfloat16)
            logsum = lse_ref[pl.ds(h, 1), here]
            column = pl.ds(pl.multiple_of(h * block, block), block)
            qm_ref[column, :] = query
            dom_ref[column, :] = grad

            def part(rows, edge):
                scores = dot(k_ref[rows, :], query, NT)
                if edge:
                    scores = jnp.where(hidden, MASKED, scores)
                probs = jnp.exp(scores - logsum)
                p_ref[rows, column] = probs.astype(jnp.bfloat16)
                grad_probs = dot(v_ref[rows, :], grad, NT)
                ds_ref[rows, column] = (probs * (grad_probs - delta)).astype(jnp.bfloat16)

            if i:
                part(pl.ds(0, span - block), False)
            part(pl.ds(span - block, block), True)
            dq = dot(ds_ref[pl.ds(0, span), column], k_ref[pl.ds(0, span), :], TN)
            out_ref[here, pl.ds(0, width)] = jnp.where(
                mine, (dq * 0.125).astype(out_ref.dtype), out_ref[here, pl.ds(0, width)]
            )
            return carry

        lax.fori_loop(0, heads, one_head, 0, unroll=heads)
        new_v = dot(p_ref[pl.ds(0, span), :], dom_ref[...], NN)
        new_k = dot(ds_ref[pl.ds(0, span), :], qm_ref[...], NN)
        if at == count - 1:
            old_k, old_v = (refs[6][...], refs[7][...]) if given > 1 else (0.0, 0.0)
            dv_ref[...] = old_v + new_v
            dk_ref[...] = old_k + new_k
        else:
            dv_ref[pl.ds(0, span), :] += new_v
            dk_ref[pl.ds(0, span), :] += new_k
        low = pl.ds(i * block, block)
        out_ref[here, pl.ds(width, width)] = dk_ref[low, :].astype(out_ref.dtype)
        out_ref[here, pl.ds(2 * width, width)] = dv_ref[low, :].astype(out_ref.dtype)
    if first:
        outs[1][...] = dk_ref[pl.ds(0, first * block), :]
        outs[2][...] = dv_ref[pl.ds(0, first * block), :]


def attend_backward(projected, grad_context, context, logsum, block, first, carried=()):
    rows, width = context.shape
    heads = width // HEAD_DIM
    length = first * block + rows
    half = lambda j: pl.BlockSpec((rows, width), lambda i: (first * block // rows, j))
    own = pl.BlockSpec((rows, width), lambda i: (0, 0))
    low = pl.BlockSpec((first * block, width), lambda i: (0, 0))
    rest = jax.ShapeDtypeStruct((first * block, width), jnp.float32)
    more = bool(first)
    return pl.pallas_call(
        functools.partial(backward_body, block, first, len(carried)),
        out_shape=(jax.ShapeDtypeStruct((rows, 3 * width), jnp.bfloat16),) + (rest,) * (2 * more),
        grid=(1,),
        in_specs=[
            half(0),
            own,
            own,
            pl.BlockSpec((heads, rows), lambda i: (0, 0)),
            pl.BlockSpec((length, width), lambda i: (0, 1)),
            pl.BlockSpec((length, width), lambda i: (0, 2)),
        ]
        + [own] * len(carried),
        out_specs=(pl.BlockSpec((rows, 3 * width), lambda i: (0, 0)),) + (low,) * (2 * more),
        scratch_shapes=[
            pltpu.VMEM((length, heads * block), jnp.bfloat16),
            pltpu.VMEM((length, heads * block), jnp.bfloat16),
            pltpu.VMEM((heads * block, width), jnp.bfloat16),
            pltpu.VMEM((heads * block, width), jnp.bfloat16),
            pltpu.VMEM((length, width), jnp.float32),
            pltpu.VMEM((length, width), jnp.float32),
        ],
        compiler_params=params("arbitrary"),
        name="attend_backward",
        cost_estimate=cost(
            20 * rows * length * width, 16 * length * width, rows * length * heads
        ),
    )(projected, grad_context, context, logsum, projected, projected, *carried)


ROOT = math.sqrt(2.0 / math.pi)
CUBE = 0.044715


def expert_body(given, x_ref, gy_ref, win_ref, wback_ref, *rest):
    out_ref, active_ref, slope_ref, *sent = rest[given:]
    rows, depth = x_ref.shape
    hidden = dot(x_ref[...], win_ref[...], NN)
    square = hidden * hidden
    bent = jnp.tanh(ROOT * hidden * (1.0 + CUBE * square))
    active = (0.5 * hidden * (1.0 + bent)).astype(jnp.bfloat16)
    slope = 0.5 * (1.0 + bent) + 0.5 * hidden * (1.0 - bent * bent) * (
        ROOT * (1.0 + 3.0 * CUBE * square)
    )
    active_ref[...] = active.reshape(active_ref.shape)
    parts = out_ref.shape[0]
    wide = depth // parts
    made = dot(active, wback_ref[...], NN).astype(jnp.bfloat16)
    for j in range(parts):
        out_ref[j] = made[:, j * wide : (j + 1) * wide]
    grad_active = dot(gy_ref[...].reshape(rows, depth), wback_ref[...], NT)
    grad_hidden = (grad_active * slope).astype(jnp.bfloat16)
    slope_ref[...] = grad_hidden.reshape(slope_ref.shape)
    back = dot(grad_hidden, win_ref[...], NT).astype(jnp.bfloat16)
    first = 0
    for ref in sent:
        wide = ref.shape[-1]
        ref[...] = back[:, first : first + wide].reshape(ref.shape)
        first += wide


def expert_pass(chunk, x, grad_y, w_in, w_back, kept, sent, parts, pieces, waits=()):
    e, low, size = chunk
    sources, members, cap, depth = grad_y.shape
    rows = sources * size
    width = w_in.shape[2]
    step = min(256, rows)
    group = step // size
    at = low // size
    given = [*kept, *sent]
    aliases = {4 + j: (1 if kept else 3) + j for j in range(len(given))}
    keep = jax.ShapeDtypeStruct((sources, cap, width), jnp.bfloat16)
    keep_spec = pl.BlockSpec((group, size, width), lambda i: (i, at, 0))
    piece = tuple(jax.ShapeDtypeStruct((sources, members, cap, w), jnp.bfloat16) for w in pieces)
    piece_spec = tuple(
        pl.BlockSpec((group, None, size, w), lambda i: (i, e % members, at, 0)) for w in pieces
    )
    made = pl.pallas_call(
        functools.partial(expert_body, len(given) + len(waits)),
        out_shape=(jax.ShapeDtypeStruct((parts, rows, depth // parts), jnp.bfloat16), keep, keep)
        + piece,
        grid=(rows // step,),
        in_specs=[
            pl.BlockSpec((step, depth), lambda i: (i, 0)),
            pl.BlockSpec((group, None, size, depth), lambda i: (i, e % members, at, 0)),
            pl.BlockSpec((None, depth, width), lambda i: (e, 0, 0)),
            pl.BlockSpec((None, width, depth), lambda i: (e, 0, 0)),
        ]
        + [pl.BlockSpec(memory_space=pl.ANY)] * (len(given) + len(waits)),
        out_specs=(
            pl.BlockSpec((parts, step, depth // parts), lambda i: (0, i, 0)),
            keep_spec,
            keep_spec,
        )
        + piece_spec,
        input_output_aliases=aliases,
        compiler_params=params("arbitrary"),
        name="expert_pass",
        cost_estimate=cost(
            8 * rows * depth * width, 4 * width * depth + 12 * rows * depth, rows * width
        ),
    )(x, grad_y, w_in, w_back, *given, *waits)
    return made[0], made[1:3], list(made[3:])


def weight_body(given, x_ref, gy_ref, router_ref, pick_ref, active_ref, slope_ref, *rest):
    gin_ref, gback_ref, token_ref, xt_ref, gyg_ref = rest[given:]
    token_ref[...] = jnp.zeros_like(token_ref)
    rows, depth = x_ref.shape

    @pl.when(pl.program_id(0) == 0)
    def _():
        logits = dot(x_ref[...], router_ref[...], NN)
        raised = jnp.exp(logits - jnp.max(logits, axis=1, keepdims=True))
        gate = jnp.sum(raised * pick_ref[...], axis=1, keepdims=True)
        gate = gate / jnp.sum(raised, axis=1, keepdims=True)
        xt_ref[...] = (x_ref[...].astype(jnp.float32) * gate).T.astype(jnp.bfloat16)
        grad_y = gy_ref[...].reshape(rows, depth).astype(jnp.float32)
        gyg_ref[...] = (grad_y * gate).astype(jnp.bfloat16)

    gin_ref[...] = dot(xt_ref[...], slope_ref[...], NN)
    gback_ref[...] = dot(active_ref[...], gyg_ref[...], TN)


def weight_pass(e, local, x, grad_y, router, pick, active, slope, sent, waits=()):
    rows, width = active.shape
    sources, members, cap, depth = grad_y.shape
    step = min(256, width)
    sent = list(sent or [])
    return pl.pallas_call(
        functools.partial(weight_body, len(sent) + len(waits)),
        out_shape=(
            jax.ShapeDtypeStruct((local, depth, width), jnp.float32),
            jax.ShapeDtypeStruct((local, width, depth), jnp.float32),
            jax.ShapeDtypeStruct((8, 128), jnp.float32),
        ),
        grid=(width // step,),
        in_specs=[
            pl.BlockSpec((rows, depth), lambda i: (0, 0)),
            pl.BlockSpec((sources, None, cap, depth), lambda i: (0, e % members, 0, 0)),
            pl.BlockSpec(router.shape, lambda i: (0, 0)),
            pl.BlockSpec(pick.shape, lambda i: (0, 0)),
            pl.BlockSpec((rows, step), lambda i: (0, i)),
            pl.BlockSpec((rows, step), lambda i: (0, i)),
        ]
        + [pl.BlockSpec(memory_space=pl.ANY)] * (len(sent) + len(waits)),
        out_specs=(
            pl.BlockSpec((None, depth, step), lambda i: (e, 0, i)),
            pl.BlockSpec((None, step, depth), lambda i: (e, i, 0)),
            pl.BlockSpec((8, 128), lambda i: (0, 0)),
        ),
        scratch_shapes=[
            pltpu.VMEM((depth, rows), jnp.bfloat16),
            pltpu.VMEM((rows, depth), jnp.bfloat16),
        ],
        input_output_aliases={6 + j: j for j in range(len(sent))},
        compiler_params=params("arbitrary"),
        name="weight_pass",
        cost_estimate=cost(4 * rows * depth * width, 8 * width * depth + 8 * rows * depth),
    )(x, grad_y, router, pick, active, slope, *sent, *waits)


def swap(blocks, axis):
    return lax.all_to_all(blocks, axis, split_axis=0, concat_axis=0, tiled=True)


def tie(*values):
    return lax.optimization_barrier(values)


def row_stats(values):
    mean = jnp.mean(values, axis=-1, keepdims=True)
    centered = values - mean
    variance = jnp.mean(centered * centered, axis=-1, keepdims=True)
    return (mean, lax.rsqrt(variance + EPSILON))


def layer_stats(values):
    mean = jnp.mean(values, axis=-1, keepdims=True)
    centered = values - mean
    variance = jnp.mean(centered * centered, axis=-1, keepdims=True)
    inverse = lax.rsqrt(variance + EPSILON)
    return (centered * inverse, inverse)


def norm_back(grad_normed, normed, inverse, gain):
    grad_hat = grad_normed * gain
    centred_grad = grad_hat - jnp.mean(grad_hat, axis=-1, keepdims=True)
    return inverse * (centred_grad - normed * jnp.mean(grad_hat * normed, axis=-1, keepdims=True))


def slot_layout(expert_ids, experts, cap):
    chosen = expert_ids[:, 0]
    length = chosen.shape[0]
    table = chosen[:, None] == jnp.arange(experts, dtype=jnp.int32)[None, :]
    order = jnp.arange(length, dtype=jnp.int32)
    before = (order[:, None] > order[None, :]).astype(jnp.bfloat16)
    counted = jnp.dot(before, table.astype(jnp.bfloat16), preferred_element_type=jnp.float32)
    ranks = jnp.sum(jnp.where(table, counted, 0.0), axis=1).astype(jnp.int32)
    return (chosen, ranks, table.astype(jnp.float32))


def per_device(
    tokens, w_qkv, w_out, w_router, ln_gains, ln_biases, w_in, w_back, expert_ids, cotangent
):
    rows_all, cols_all = lax.axis_size("row"), lax.axis_size("col")
    col = lax.axis_index("col")
    length, depth = tokens.shape
    share = depth // rows_all
    width = w_qkv.shape[2]
    experts = w_router.shape[1]
    local = w_in.shape[0]
    cap = 2 * length // experts
    block_rows = rows_all * cap
    block = min(256, length // 2)
    part = length // cols_all
    members = max(1, local // 2)
    pieces = (depth * 5 // 8, depth * 3 // 8)

    def own(values, axis=0):
        return lax.dynamic_slice_in_dim(values, col * part, part, axis)

    def send(packed):
        return swap(packed.reshape(rows_all, cap, depth), "row").reshape(block_rows, depth)

    stacked = w_qkv.transpose(1, 0, 2).reshape(share, 3 * width)
    weights = jnp.concatenate([stacked, w_router, ln_gains.T, ln_biases.T], axis=1)
    weights = lax.all_gather(weights, "row", axis=0, tiled=True)
    mean_one, inverse_one = row_stats(tokens.astype(jnp.float32))

    chosen, ranks, select = slot_layout(expert_ids, experts, cap)
    out_block, ranks = tie(w_out.T, ranks)
    out_block = swap(jnp.broadcast_to(out_block[None], (cols_all, share, width)), "col")
    slots = chosen * cap + ranks
    slots_by_local = ((chosen % local) * rows_all + chosen // local) * cap + ranks
    member = chosen % local
    slots_by_group = [
        jnp.where(
            member // members == g,
            ((chosen // local) * members + member % members) * cap + ranks,
            -1,
        )
        for g in range(local // members)
    ]

    slots_by_pair = slots_by_local - slots_by_local
    for g, at in enumerate(slots_by_group):
        slots_by_pair = jnp.where(at >= 0, at + g * members * block_rows, slots_by_pair)

    def pack_group(g, waits):
        rows = members * block_rows
        return pack(slots_by_pair, [cotangent], g * rows, rows, 1, waits)[0]

    grad_packed = [pack_group(0, [])]
    weights, grad_packed[0], out_block, mean_one, inverse_one = tie(
        weights, grad_packed[0], out_block, mean_one, inverse_one
    )
    qkv_full = weights[:, : 3 * width]
    router_full = weights[:, 3 * width : 3 * width + experts]
    norms = weights[:, 3 * width + experts :].astype(jnp.float32).T
    gains, biases = norms[0:2], norms[2:4]

    resid_in = tokens.astype(jnp.float32)
    normed_one = (resid_in - mean_one) * inverse_one
    normal_in = (normed_one * gains[0] + biases[0]).astype(jnp.bfloat16)
    projected = jnp.dot(normal_in, qkv_full, preferred_element_type=jnp.float32).astype(jnp.bfloat16)

    context, logsum = attend_forward(projected, tuple(range(length // block)), block)
    context, grad_packed[0] = tie(context, grad_packed[0])
    full = lax.all_gather(context, "col", axis=0)
    grad_packed += [pack_group(g, [context]) for g in range(1, local // members)]
    out_full = lax.all_gather(out_block, "row", axis=1, tiled=True)
    grad_arrived = []
    for g in range(local // members):
        if g:
            grad_arrived[-1], grad_packed[g] = tie(grad_arrived[-1], grad_packed[g])
        grad_arrived.append(swap(grad_packed[g].reshape(rows_all, members, cap, depth), "row"))
    full, out_full = tie(full, out_full)
    middle, routed = middle_pass(full, out_full, tokens, gains[1:2], biases[1:2])

    short = cap // 2
    chunks = [(0, 0, short), (0, short, short)] + [(e, 0, cap) for e in range(1, local)]
    split = (ranks // short * rows_all + chosen // local) * short + ranks % short
    slots_by_chunk = jnp.where(chosen % local == 0, split, slots_by_local)

    def pack_chunk(k, waits):
        e, low, size = chunks[k]
        base = (e * cap + low) * rows_all
        return pack(slots_by_chunk, [routed], base, size * rows_all, 1, waits)[0]

    packed = [pack_chunk(k, []) for k in range(min(3, len(chunks)))]
    packed[0], grad_arrived[-1] = tie(packed[0], grad_arrived[-1])

    logits = jnp.dot(routed, router_full, preferred_element_type=jnp.float32)
    probs = jax.nn.softmax(logits, axis=-1)
    gate = jnp.sum(probs * select, axis=-1, keepdims=True)

    arrived, summed, kept, sent = [], [], [], []
    final = len(chunks) - 1
    for k, (e, low, size) in enumerate(chunks):
        moved = swap(packed[k].reshape(rows_all, size, depth), "row")
        arrived.append(moved.reshape(rows_all * size, depth))
        if k < final:
            packed[k + 1], arrived[k], *more = tie(
                packed[k + 1], arrived[k], *(packed[2:3] if k == 0 else [])
            )
            packed[2:3] = more or packed[2:3]
        if k:
            then = packed[k + 1] if k < final else sent[0][0]
            then, summed[k - 1], arrived[k] = tie(then, summed[k - 1], arrived[k])
            summed[k - 1] = lax.psum_scatter(
                summed[k - 1], "col", scatter_dimension=0, tiled=True
            )
            if k < final:
                packed[k + 1] = then
            else:
                sent[0][0] = then
        waits = summed[:1] if k == final else []
        made, both, pair = expert_pass(
            chunks[k],
            arrived[k],
            grad_arrived[e // members],
            w_in,
            w_back,
            kept.pop() if low else [],
            sent.pop() if low or e % members else [],
            cols_all,
            pieces,
            waits,
        )
        kept.append(both)
        summed.append(made)
        sent.append(pair)
        if 1 <= k and k + 2 <= final:
            packed.append(pack_chunk(k + 2, [made]))
    active = [v[0].reshape(block_rows, -1) for v in kept]
    slope = [v[1].reshape(block_rows, -1) for v in kept]

    def joined(values):
        first = [v.reshape(rows_all, short, -1) for v in values[:2]]
        whole = [v.reshape(rows_all, cap, -1) for v in values[2:]]
        return [jnp.concatenate(first, axis=1)] + whole

    arrived = [v.reshape(block_rows, depth) for v in joined(arrived)]

    step = min(256, length)
    order = [(g, f) for f in range(len(pieces)) for g in range(len(sent))]
    grad_sent = []
    grad_weights = None
    token = None
    row = lax.axis_index("row")

    def weigh(e, waits):
        pick = jnp.arange(experts, dtype=jnp.int32)[None, :] == row * local + e
        return weight_pass(
            e,
            local,
            arrived[e],
            grad_arrived[e // members],
            router_full,
            pick.astype(jnp.float32),
            active[e],
            slope[e],
            grad_weights,
            waits,
        )

    waits = slope[-1:]
    last = None
    for f, wide in enumerate(pieces):
        early = max(1, local * 3 // 4)
        for e in range(early) if f == 0 else range(early, local):
            *grad_weights, token = weigh(e, waits)
            waits = [token]
        rows = []
        for g in range(len(sent)):
            piece = sent[g][f]
            if last is not None:
                piece, last = tie(piece, last)
                if rows:
                    rows[-1] = last
                else:
                    ended[-1] = last
            if f == 0 and g == len(sent) - 1:
                piece, slope[-1] = tie(piece, slope[-1])
            if f and g == len(sent) - 1:
                piece, whole = tie(piece, whole)
            last = swap(piece, "row")
            if f == 0 and g == 0:
                last, made = tie(last, summed[-1])
                summed[-1] = lax.psum_scatter(made, "col", scatter_dimension=0, tiled=True)
            rows.append(last)
        if f == 0:
            ended = rows
            sent[0][1], token = tie(sent[0][1], token)
            waits = [token]
        else:
            homed = jnp.stack(joined(summed), axis=1)
            homed, token = tie(homed, token)
            waits = [token]
            grad_sent.append(lax.psum_scatter(whole, "col", scatter_dimension=0, tiled=True))
        whole = unpack(slots_by_group, [v.reshape(-1, wide) for v in rows], step, waits)
        if f:
            rows[-1], homed = tie(rows[-1], homed)
            homed = swap(homed, "row")
            whole, homed = tie(whole, homed)
        waits = [whole]
    grad_sent.append(lax.psum_scatter(whole, "col", scatter_dimension=0, tiled=True))

    grad_in, grad_back = grad_weights
    returned = unpack(
        [slots], [homed.reshape(experts * cap, depth // cols_all)], step, grad_sent[:1]
    ).astype(jnp.float32)
    columns = depth // cols_all

    def own_columns(values):
        return lax.dynamic_slice_in_dim(values, col * columns, columns, 1)

    mixed = (own_columns(middle) + gate * returned).astype(jnp.bfloat16)
    grad_gate = jnp.sum(own_columns(cotangent).astype(jnp.float32) * returned, axis=-1)
    grad_gate = swap(grad_gate.reshape(cols_all, part), "col")
    grad_gate = jnp.sum(grad_gate, axis=0)[:, None]
    mixed_full = lax.all_gather(mixed, "col", axis=0)

    own_gate, own_probs, own_select = own(gate), own(probs), own(select)
    grad_logits = (grad_gate * own_probs * (own_select - own_gate)).astype(jnp.bfloat16)
    own_routed = own(routed)
    grad_router = jnp.einsum(
        "td,te->de", own_routed, grad_logits, preferred_element_type=jnp.float32
    )
    grad_y = own(cotangent).astype(jnp.float32)
    normed_own, inverse_own = layer_stats(own(middle))
    grad_sent = jnp.concatenate(grad_sent, axis=1).astype(jnp.float32) * own_gate
    grad_routed = grad_sent + jnp.einsum(
        "te,de->td", grad_logits, router_full, preferred_element_type=jnp.float32
    )
    gain_two = jnp.sum(grad_routed * normed_own, axis=0)
    bias_two = jnp.sum(grad_routed, axis=0)
    grad_middle = grad_y + norm_back(grad_routed, normed_own, inverse_own, gains[1])
    grad_attn = grad_middle.astype(jnp.bfloat16)
    grad_context = jnp.einsum(
        "td,zdc->ztc", grad_attn, out_full, preferred_element_type=jnp.float32
    ).astype(jnp.bfloat16)
    grad_context = swap(grad_context, "col")
    context_own = own(full, 1)
    grad_out = jnp.einsum("td,ztc->dzc", grad_attn, context_own, preferred_element_type=jnp.float32)
    plane = jnp.concatenate([grad_out.reshape(depth, cols_all * width), grad_router], axis=1)
    plane = swap(plane.astype(jnp.bfloat16).reshape(rows_all, share, -1), "row")
    grad_context = grad_context.reshape(length, width)
    grad_proj = attend_backward(projected, grad_context, context, logsum, block, 0)[0]
    grad_proj, plane = tie(grad_proj, plane)

    shares = jnp.einsum("tc,dc->td", grad_proj, qkv_full, preferred_element_type=jnp.float32)
    shares, mixed_full = tie(shares.astype(jnp.bfloat16), mixed_full)
    grad_normal = lax.psum_scatter(shares, "col", scatter_dimension=0, tiled=True)
    grad_normal = grad_normal.astype(jnp.float32)
    mixed_out = mixed_full.transpose(1, 0, 2).reshape(length, depth)
    grad_qkv = jnp.einsum("td,tc->dc", normal_in, grad_proj, preferred_element_type=jnp.float32)
    plane = jnp.sum(plane.astype(jnp.float32), axis=0)
    router_share = plane[:, cols_all * width :].reshape(1, share, experts)
    out_share = plane[:, : cols_all * width].reshape(share, cols_all, width).transpose(1, 0, 2)
    router_share = jnp.broadcast_to(router_share, (cols_all, share, experts))
    plane = jnp.concatenate([out_share, router_share], axis=2).astype(jnp.bfloat16)
    plane = jnp.sum(swap(plane, "col").astype(jnp.float32), axis=0)
    out_share, router_share = plane[:, :width].T, plane[:, width:]
    grad_normal, out_share, mixed_out, grad_qkv = tie(
        grad_normal, out_share, mixed_out, grad_qkv
    )

    own_normed, own_inverse = layer_stats(own(tokens).astype(jnp.float32))
    grad_tokens = (
        grad_middle + norm_back(grad_normal, own_normed, own_inverse, gains[0])
    ).astype(jnp.bfloat16)
    grad_tokens = lax.all_gather(grad_tokens, "col", axis=0, tiled=True)
    small = [
        jnp.sum(grad_normal * own_normed, axis=0),
        jnp.sum(grad_normal, axis=0),
        gain_two,
        bias_two,
    ]
    small = swap(jnp.stack(small).reshape(4, rows_all, share).transpose(1, 0, 2), "row")
    small = jnp.sum(small, axis=0)
    small = jnp.sum(swap(jnp.broadcast_to(small[None], (cols_all, 4, share)), "col"), axis=0)
    qkv_share = swap(grad_qkv.astype(jnp.bfloat16).reshape(rows_all, share, -1), "row")
    qkv_share = jnp.sum(qkv_share.astype(jnp.float32), axis=0)
    qkv_share = qkv_share.reshape(share, 3, width).transpose(1, 0, 2)
    return (
        mixed_out,
        grad_tokens,
        qkv_share,
        out_share,
        router_share,
        jnp.stack([small[0], small[2]]),
        small[1],
        small[3],
        grad_in,
        grad_back,
    )


def solution(mesh):
    return jax.shard_map(
        per_device,
        mesh=mesh,
        in_specs=(
            P("row", None),
            P(None, "row", "col"),
            P("col", "row"),
            P("row", None),
            P(None, "row"),
            P(None, "row"),
            P("row", None, "col"),
            P("row", "col", None),
            P("row", None),
            P("row", None),
        ),
        out_specs=(
            P("row", None),
            P("row", None),
            P(None, "row", "col"),
            P("col", "row"),
            P("row", None),
            P(None, "row"),
            P("row"),
            P("row"),
            P("row", None, "col"),
            P("row", "col", None),
        ),
        check_vma=False,
    )
```

```python
import functools, math
import jax, jax.numpy as jnp
from jax import lax
from jax.experimental import pallas as pl
from jax.experimental.pallas import tpu as pltpu
from jax.sharding import PartitionSpec as P

HEAD_DIM = 64
EPSILON = 1e-05
MASKED = -1e30
VMEM = 60 << 20


def params(*kinds):
    return pltpu.CompilerParams(dimension_semantics=kinds or None, vmem_limit_bytes=VMEM)


def cost(flops, moved, special=0):
    return pl.CostEstimate(flops=flops, bytes_accessed=moved, transcendentals=special)


def dot(a, b, dims):
    return lax.dot_general(a, b, (dims, ((), ())), preferred_element_type=jnp.float32)

NN = ((1,), (0,))
NT = ((1,), (1,))
TN = ((0,), (0,))


def pack_body(base, step, each, parts, slots_ref, *rest):
    rows_refs, outs = rest[:parts], rest[-((pl.num_programs(0)) // each) :]
    at = pl.program_id(0)
    made = None
    first = 0
    for rows_ref in rows_refs:
        length = rows_ref.shape[0]
        wanted = base + at * step + lax.broadcasted_iota(jnp.int32, (step, length), 0)
        chosen = jnp.where(slots_ref[:, pl.ds(first, length)] == wanted, 1.0, 0.0)
        more = dot(chosen.astype(jnp.bfloat16), rows_ref[...], NN)
        made = more if made is None else made + more
        first += length
    made = made.astype(jnp.bfloat16)
    for j, out_ref in enumerate(outs):

        @pl.when(at // each == j)
        def _(out_ref=out_ref):
            out_ref[...] = made


def pack(slots, rows, base, count, outs, waits=()):
    length = slots.shape[0]
    width = rows[0].shape[1]
    step = min(512, count)
    each = count // step
    return pl.pallas_call(
        functools.partial(pack_body, base, step, each, len(rows)),
        out_shape=(jax.ShapeDtypeStruct((count, width), jnp.bfloat16),) * outs,
        grid=(each * outs,),
        in_specs=[pl.BlockSpec((1, length), lambda i: (0, 0))]
        + [pl.BlockSpec(r.shape, lambda i: (0, 0)) for r in rows]
        + [pl.BlockSpec(memory_space=pl.ANY)] * len(waits),
        out_specs=tuple(
            pl.BlockSpec((step, width), lambda i, j=j: (jnp.clip(i - j * each, 0, each - 1), 0))
            for j in range(outs)
        ),
        compiler_params=params("arbitrary"),
        name="pack",
        cost_estimate=cost(1, 1),
    )(slots.reshape(1, length), *rows, *waits)


def unpack_body(parts, *refs):
    out_ref = refs[-1]
    step = out_ref.shape[0]
    made = None
    for slots_ref, rows_ref in zip(refs[:parts], refs[parts : 2 * parts]):
        count = rows_ref.shape[0]
        held = lax.broadcasted_iota(jnp.int32, (step, count), 1)
        chosen = jnp.where(slots_ref[...] == held, 1.0, 0.0).astype(jnp.bfloat16)
        more = dot(chosen, rows_ref[...], NN)
        made = more if made is None else made + more
    out_ref[...] = made.astype(out_ref.dtype)


def unpack(slots, rows, step, waits=()):
    length = slots[0].shape[0]
    width = rows[0].shape[1]
    count = sum(r.shape[0] for r in rows)
    return pl.pallas_call(
        functools.partial(unpack_body, len(rows)),
        out_shape=jax.ShapeDtypeStruct((length, width), jnp.bfloat16),
        grid=(length // step,),
        in_specs=[pl.BlockSpec((step, 1), lambda i: (i, 0))] * len(rows)
        + [pl.BlockSpec(r.shape, lambda i: (0, 0)) for r in rows]
        + [pl.BlockSpec(memory_space=pl.ANY)] * len(waits),
        out_specs=pl.BlockSpec((step, width), lambda i: (i, 0)),
        compiler_params=params("arbitrary"),
        name="unpack",
        cost_estimate=cost(2 * count * length * width, 2 * (length + count) * width),
    )(*(at.reshape(length, 1) for at in slots), *rows, *waits)


def middle_body(full_ref, out_ref, tokens_ref, gain_ref, bias_ref, middle_ref, routed_ref, all_ref):
    cols, _, width = full_ref.shape

    @pl.when(pl.program_id(0) == 0)
    def _():
        for z in range(cols):
            all_ref[:, z * width : (z + 1) * width] = out_ref[z]

    context = jnp.concatenate([full_ref[z] for z in range(cols)], axis=1)
    total = tokens_ref[...].astype(jnp.float32) + dot(context, all_ref[...], NT)
    middle_ref[...] = total
    mean = jnp.mean(total, axis=1, keepdims=True)
    centered = total - mean
    inverse = lax.rsqrt(jnp.mean(centered * centered, axis=1, keepdims=True) + EPSILON)
    routed_ref[...] = (centered * inverse * gain_ref[...] + bias_ref[...]).astype(jnp.bfloat16)


def middle_pass(full, out_full, tokens, gain, bias):
    cols, rows, width = full.shape
    depth = tokens.shape[1]
    step = min(512, rows)
    row = pl.BlockSpec((1, depth), lambda i: (0, 0))
    block = pl.BlockSpec((step, depth), lambda i: (i, 0))
    return pl.pallas_call(
        middle_body,
        out_shape=(
            jax.ShapeDtypeStruct((rows, depth), jnp.float32),
            jax.ShapeDtypeStruct((rows, depth), jnp.bfloat16),
        ),
        grid=(rows // step,),
        in_specs=[
            pl.BlockSpec((cols, step, width), lambda i: (0, i, 0)),
            pl.BlockSpec((cols, depth, width), lambda i: (0, 0, 0)),
            block,
            row,
            row,
        ],
        out_specs=(block, block),
        scratch_shapes=[pltpu.VMEM((depth, cols * width), jnp.bfloat16)],
        compiler_params=params("arbitrary"),
        name="middle_pass",
        cost_estimate=cost(2 * rows * depth * width * cols, 10 * rows * depth),
    )(full, out_full, tokens, gain, bias)


def forward_body(blocks, block, q_ref, k_ref, v_ref, *rest):
    o_ref, lse_ref = rest[-2:]
    width = q_ref.shape[1]
    heads = width // HEAD_DIM
    lane = lax.broadcasted_iota(jnp.int32, (block, width), 1)
    hidden = lax.broadcasted_iota(jnp.int32, (block, block), 1) > lax.broadcasted_iota(
        jnp.int32, (block, block), 0
    )
    for at, i in enumerate(blocks):
        span = (i + 1) * block
        here = pl.ds(at * block, block)
        o_ref[here, :] = jnp.zeros((block, width), o_ref.dtype)

        def one_head(h, carry, here=here, span=span, i=i):
            mine = (lane >= h * HEAD_DIM) & (lane < (h + 1) * HEAD_DIM)
            query = q_ref[pl.ds(i * block, block), :].astype(jnp.float32) * 0.125
            query = jnp.where(mine, query, 0.0).astype(jnp.bfloat16)
            edge = jnp.where(hidden, MASKED, dot(query, k_ref[pl.ds(span - block, block), :], NT))
            peak = jnp.max(edge, axis=1, keepdims=True)
            if i:
                past = dot(query, k_ref[pl.ds(0, span - block), :], NT)
                peak = jnp.maximum(peak, jnp.max(past, axis=1, keepdims=True))
            edge = jnp.exp(edge - peak)
            total = jnp.sum(edge, axis=1, keepdims=True)
            if i:
                past = jnp.exp(past - peak)
                total = total + jnp.sum(past, axis=1, keepdims=True)
            share = 1.0 / total
            mixed = dot((edge * share).astype(jnp.bfloat16), v_ref[pl.ds(span - block, block), :], NN)
            if i:
                mixed = mixed + dot(
                    (past * share).astype(jnp.bfloat16), v_ref[pl.ds(0, span - block), :], NN
                )
            o_ref[here, :] = jnp.where(mine, mixed.astype(o_ref.dtype), o_ref[here, :])
            logsum = jnp.broadcast_to(peak + jnp.log(total), (block, 128))
            lse_ref[pl.ds(h, 1), here] = logsum.T[0:1, :]
            return carry

        lax.fori_loop(0, heads, one_head, 0, unroll=heads)


def attend_forward(projected, blocks, block, waits=()):
    length, triple = projected.shape
    width = triple // 3
    heads = width // HEAD_DIM
    rows = len(blocks) * block
    spec = [pl.BlockSpec((length, width), lambda i, j=j: (0, j)) for j in range(3)]
    return pl.pallas_call(
        functools.partial(forward_body, blocks, block),
        out_shape=(
            jax.ShapeDtypeStruct((rows, width), jnp.bfloat16),
            jax.ShapeDtypeStruct((heads, rows), jnp.float32),
        ),
        grid=(1,),
        in_specs=spec + [pl.BlockSpec(memory_space=pl.ANY)] * len(waits),
        out_specs=(
            pl.BlockSpec((rows, width), lambda i: (0, 0)),
            pl.BlockSpec((heads, rows), lambda i: (0, 0)),
        ),
        compiler_params=params("arbitrary"),
        name="attend_forward",
        cost_estimate=cost(rows * width, rows * width),
    )(projected, projected, projected, *waits)


def backward_body(block, first, given, *refs):
    q_ref, do_ref, o_ref, lse_ref, k_ref, v_ref = refs[:6]
    outs = refs[6 + given :]
    out_ref, p_ref, ds_ref, qm_ref, dom_ref, dk_ref, dv_ref = outs[:1] + outs[-6:]
    width = q_ref.shape[1]
    heads = width // HEAD_DIM
    count = q_ref.shape[0] // block
    lane = lax.broadcasted_iota(jnp.int32, (block, width), 1)
    hidden = lax.broadcasted_iota(jnp.int32, (block, block), 0) > lax.broadcasted_iota(
        jnp.int32, (block, block), 1
    )
    for at in reversed(range(count)):
        i = first + at
        span = (i + 1) * block
        here = pl.ds(at * block, block)

        def one_head(h, carry, here=here, span=span, i=i):
            mine = (lane >= h * HEAD_DIM) & (lane < (h + 1) * HEAD_DIM)
            query = q_ref[here, :].astype(jnp.float32) * 0.125
            query = jnp.where(mine, query, 0.0).astype(jnp.bfloat16)
            grad = jnp.where(mine, do_ref[here, :].astype(jnp.float32), 0.0)
            delta = jnp.sum(grad * o_ref[here, :].astype(jnp.float32), axis=1, keepdims=True)
            delta = jnp.broadcast_to(delta, (block, 128)).T[0:1, :]
            grad = grad.astype(jnp.bfloat16)
            logsum = lse_ref[pl.ds(h, 1), here]
            column = pl.ds(pl.multiple_of(h * block, block), block)
            qm_ref[column, :] = query
            dom_ref[column, :] = grad

            def part(rows, edge):
                scores = dot(k_ref[rows, :], query, NT)
                if edge:
                    scores = jnp.where(hidden, MASKED, scores)
                probs = jnp.exp(scores - logsum)
                p_ref[rows, column] = probs.astype(jnp.bfloat16)
                grad_probs = dot(v_ref[rows, :], grad, NT)
                ds_ref[rows, column] = (probs * (grad_probs - delta)).astype(jnp.bfloat16)

            if i:
                part(pl.ds(0, span - block), False)
            part(pl.ds(span - block, block), True)
            dq = dot(ds_ref[pl.ds(0, span), column], k_ref[pl.ds(0, span), :], TN)
            out_ref[here, pl.ds(0, width)] = jnp.where(
                mine, (dq * 0.125).astype(out_ref.dtype), out_ref[here, pl.ds(0, width)]
            )
            return carry

        lax.fori_loop(0, heads, one_head, 0, unroll=heads)
        new_v = dot(p_ref[pl.ds(0, span), :], dom_ref[...], NN)
        new_k = dot(ds_ref[pl.ds(0, span), :], qm_ref[...], NN)
        if at == count - 1:
            dv_ref[...] = new_v
            dk_ref[...] = new_k
        else:
            dv_ref[pl.ds(0, span), :] += new_v
            dk_ref[pl.ds(0, span), :] += new_k
        low = pl.ds(i * block, block)
        out_ref[here, pl.ds(width, width)] = dk_ref[low, :].astype(out_ref.dtype)
        out_ref[here, pl.ds(2 * width, width)] = dv_ref[low, :].astype(out_ref.dtype)
    if first:
        outs[1][...] = dk_ref[pl.ds(0, first * block), :]
        outs[2][...] = dv_ref[pl.ds(0, first * block), :]


def attend_backward(projected, grad_context, context, logsum, block, first, waits=()):
    rows, width = context.shape
    heads = width // HEAD_DIM
    length = first * block + rows
    half = lambda j: pl.BlockSpec((rows, width), lambda i: (first * block // rows, j))
    own = pl.BlockSpec((rows, width), lambda i: (0, 0))
    low = pl.BlockSpec((first * block, width), lambda i: (0, 0))
    rest = jax.ShapeDtypeStruct((first * block, width), jnp.float32)
    more = bool(first)
    return pl.pallas_call(
        functools.partial(backward_body, block, first, len(waits)),
        out_shape=(jax.ShapeDtypeStruct((rows, 3 * width), jnp.bfloat16),) + (rest,) * (2 * more),
        grid=(1,),
        in_specs=[
            half(0),
            own,
            own,
            pl.BlockSpec((heads, rows), lambda i: (0, 0)),
            pl.BlockSpec((length, width), lambda i: (0, 1)),
            pl.BlockSpec((length, width), lambda i: (0, 2)),
        ]
        + [pl.BlockSpec(memory_space=pl.ANY)] * len(waits),
        out_specs=(pl.BlockSpec((rows, 3 * width), lambda i: (0, 0)),) + (low,) * (2 * more),
        scratch_shapes=[
            pltpu.VMEM((length, heads * block), jnp.bfloat16),
            pltpu.VMEM((length, heads * block), jnp.bfloat16),
            pltpu.VMEM((heads * block, width), jnp.bfloat16),
            pltpu.VMEM((heads * block, width), jnp.bfloat16),
            pltpu.VMEM((length, width), jnp.float32),
            pltpu.VMEM((length, width), jnp.float32),
        ],
        compiler_params=params("arbitrary"),
        name="attend_backward",
        cost_estimate=cost(
            20 * rows * length * width, 16 * length * width, rows * length * heads
        ),
    )(projected, grad_context, context, logsum, projected, projected, *waits)


def normed_rows(values):
    mean = jnp.mean(values, axis=1, keepdims=True)
    centered = values - mean
    inverse = lax.rsqrt(jnp.mean(centered * centered, axis=1, keepdims=True) + EPSILON)
    return centered * inverse, inverse


def norm_back_rows(grads, normed, inverse, gain):
    hat = grads * gain
    inner = jnp.mean(hat * normed, axis=1, keepdims=True)
    return inverse * (hat - jnp.mean(hat, axis=1, keepdims=True) - normed * inner)


def add_sums(sums_ref, grads, normed):
    @pl.when(pl.program_id(0) == 0)
    def _():
        sums_ref[...] = jnp.zeros_like(sums_ref)

    sums_ref[0:1, :] += jnp.sum(grads * normed, axis=0, keepdims=True)
    sums_ref[1:2, :] += jnp.sum(grads, axis=0, keepdims=True)


def settle_body(
    col_ref, low_ref, high_ref, gate_ref, logit_ref, router_ref, cot_ref, middle_ref, gain_ref,
    weight_ref, grad_ref, low_grad_ref, context_ref, sums_ref
):
    sent = jnp.concatenate([low_ref[...], high_ref[...]], axis=1).astype(jnp.float32)
    grads = sent * gate_ref[...] + dot(logit_ref[...], router_ref[...], NT)
    normed, inverse = normed_rows(middle_ref[...])
    add_sums(sums_ref, grads, normed)
    made = cot_ref[...].astype(jnp.float32) + norm_back_rows(
        grads, normed, inverse, gain_ref[...]
    )
    grad_ref[...] = made
    low = made.astype(jnp.bfloat16)
    low_grad_ref[...] = low
    for z in range(weight_ref.shape[0]):
        context_ref[z] = dot(low, weight_ref[z], NN).astype(jnp.bfloat16)


def settle_pass(col, low, high, gate, logits, router, cotangent, middle, gain, weights):
    part, experts = logits.shape
    cols, depth, width = weights.shape
    step = min(256, part)
    block = pl.BlockSpec((step, depth), lambda i, c: (i, 0))
    mine = pl.BlockSpec((step, depth), lambda i, c: (c[0] * (part // step) + i, 0))
    return pl.pallas_call(
        settle_body,
        out_shape=(
            jax.ShapeDtypeStruct((part, depth), jnp.float32),
            jax.ShapeDtypeStruct((part, depth), jnp.bfloat16),
            jax.ShapeDtypeStruct((cols, part, width), jnp.bfloat16),
            jax.ShapeDtypeStruct((8, depth), jnp.float32),
        ),
        grid_spec=pltpu.PrefetchScalarGridSpec(
            num_scalar_prefetch=1,
            grid=(part // step,),
            in_specs=[
                pl.BlockSpec((step, low.shape[1]), lambda i, c: (i, 0)),
                pl.BlockSpec((step, high.shape[1]), lambda i, c: (i, 0)),
                pl.BlockSpec((step, 1), lambda i, c: (i, 0)),
                pl.BlockSpec((step, experts), lambda i, c: (i, 0)),
                pl.BlockSpec((depth, experts), lambda i, c: (0, 0)),
                mine,
                mine,
                pl.BlockSpec((1, depth), lambda i, c: (0, 0)),
                pl.BlockSpec((cols, depth, width), lambda i, c: (0, 0, 0)),
            ],
            out_specs=(
                block,
                block,
                pl.BlockSpec((cols, step, width), lambda i, c: (0, i, 0)),
                pl.BlockSpec((8, depth), lambda i, c: (0, 0)),
            ),
        ),
        compiler_params=params("arbitrary"),
        name="settle_pass",
        cost_estimate=cost(2 * part * depth * width * cols, 20 * part * depth),
    )(col, low, high, gate, logits, router, cotangent, middle, gain, weights)


def close_body(col_ref, share_ref, tokens_ref, grad_ref, gain_ref, out_ref, sums_ref):
    grads = share_ref[...].astype(jnp.float32)
    normed, inverse = normed_rows(tokens_ref[...].astype(jnp.float32))
    made = grad_ref[...] + norm_back_rows(grads, normed, inverse, gain_ref[...])
    out_ref[...] = made.astype(jnp.bfloat16)
    add_sums(sums_ref, grads, normed)


def close_pass(col, shares, tokens, grads, gain):
    part, depth = shares.shape
    step = min(128, part)
    block = pl.BlockSpec((step, depth), lambda i, c: (i, 0))
    mine = pl.BlockSpec((step, depth), lambda i, c: (c[0] * (part // step) + i, 0))
    return pl.pallas_call(
        close_body,
        out_shape=(
            jax.ShapeDtypeStruct((part, depth), jnp.bfloat16),
            jax.ShapeDtypeStruct((8, depth), jnp.float32),
        ),
        grid_spec=pltpu.PrefetchScalarGridSpec(
            num_scalar_prefetch=1,
            grid=(part // step,),
            in_specs=[block, mine, block, pl.BlockSpec((1, depth), lambda i, c: (0, 0))],
            out_specs=(block, pl.BlockSpec((8, depth), lambda i, c: (0, 0))),
        ),
        compiler_params=params("arbitrary"),
        name="close_pass",
        cost_estimate=cost(30 * part * depth, 12 * part * depth),
    )(col, shares, tokens, grads, gain)


ROOT = math.sqrt(2.0 / math.pi)
CUBE = 0.044715


def expert_body(given, x_ref, gy_ref, win_ref, wback_ref, *rest):
    out_ref, active_ref, slope_ref, *sent = rest[given:]
    rows, depth = x_ref.shape
    hidden = dot(x_ref[...], win_ref[...], NN)
    square = hidden * hidden
    bent = jnp.tanh(ROOT * hidden * (1.0 + CUBE * square))
    active = (0.5 * hidden * (1.0 + bent)).astype(jnp.bfloat16)
    slope = 0.5 * (1.0 + bent) + 0.5 * hidden * (1.0 - bent * bent) * (
        ROOT * (1.0 + 3.0 * CUBE * square)
    )
    active_ref[...] = active.reshape(active_ref.shape)
    parts = out_ref.shape[0]
    wide = depth // parts
    made = dot(active, wback_ref[...], NN).astype(jnp.bfloat16)
    for j in range(parts):
        out_ref[j] = made[:, j * wide : (j + 1) * wide]
    grad_active = dot(gy_ref[...].reshape(rows, depth), wback_ref[...], NT)
    grad_hidden = (grad_active * slope).astype(jnp.bfloat16)
    slope_ref[...] = grad_hidden.reshape(slope_ref.shape)
    back = dot(grad_hidden, win_ref[...], NT).astype(jnp.bfloat16)
    first = 0
    for ref in sent:
        wide = ref.shape[-1]
        ref[...] = back[:, first : first + wide].reshape(ref.shape)
        first += wide


def expert_pass(chunk, x, grad_y, w_in, w_back, kept, sent, parts, pieces, waits=()):
    e, low, size = chunk
    sources, members, cap, depth = grad_y.shape
    rows = sources * size
    width = w_in.shape[2]
    step = min(256, rows)
    group = step // size
    at = low // size
    given = [*kept, *sent]
    aliases = {4 + j: (1 if kept else 3) + j for j in range(len(given))}
    keep = jax.ShapeDtypeStruct((sources, cap, width), jnp.bfloat16)
    keep_spec = pl.BlockSpec((group, size, width), lambda i: (i, at, 0))
    piece = tuple(jax.ShapeDtypeStruct((sources, members, cap, w), jnp.bfloat16) for w in pieces)
    piece_spec = tuple(
        pl.BlockSpec((group, None, size, w), lambda i: (i, e % members, at, 0)) for w in pieces
    )
    made = pl.pallas_call(
        functools.partial(expert_body, len(given) + len(waits)),
        out_shape=(jax.ShapeDtypeStruct((parts, rows, depth // parts), jnp.bfloat16), keep, keep)
        + piece,
        grid=(rows // step,),
        in_specs=[
            pl.BlockSpec((step, depth), lambda i: (i, 0)),
            pl.BlockSpec((group, None, size, depth), lambda i: (i, e % members, at, 0)),
            pl.BlockSpec((None, depth, width), lambda i: (e, 0, 0)),
            pl.BlockSpec((None, width, depth), lambda i: (e, 0, 0)),
        ]
        + [pl.BlockSpec(memory_space=pl.ANY)] * (len(given) + len(waits)),
        out_specs=(
            pl.BlockSpec((parts, step, depth // parts), lambda i: (0, i, 0)),
            keep_spec,
            keep_spec,
        )
        + piece_spec,
        input_output_aliases=aliases,
        compiler_params=params("arbitrary"),
        name="expert_pass",
        cost_estimate=cost(
            8 * rows * depth * width, 4 * width * depth + 12 * rows * depth, rows * width
        ),
    )(x, grad_y, w_in, w_back, *given, *waits)
    return made[0], made[1:3], list(made[3:])


def weight_body(given, x_ref, gy_ref, router_ref, pick_ref, active_ref, slope_ref, *rest):
    gin_ref, gback_ref, token_ref, xt_ref, gyg_ref = rest[given:]
    token_ref[...] = jnp.zeros_like(token_ref)
    rows, depth = x_ref.shape

    @pl.when(pl.program_id(0) == 0)
    def _():
        logits = dot(x_ref[...], router_ref[...], NN)
        raised = jnp.exp(logits - jnp.max(logits, axis=1, keepdims=True))
        gate = jnp.sum(raised * pick_ref[...], axis=1, keepdims=True)
        gate = gate / jnp.sum(raised, axis=1, keepdims=True)
        xt_ref[...] = (x_ref[...].astype(jnp.float32) * gate).T.astype(jnp.bfloat16)
        grad_y = gy_ref[...].reshape(rows, depth).astype(jnp.float32)
        gyg_ref[...] = (grad_y * gate).astype(jnp.bfloat16)

    gin_ref[...] = dot(xt_ref[...], slope_ref[...], NN)
    gback_ref[...] = dot(active_ref[...], gyg_ref[...], TN)


def weight_pass(e, local, x, grad_y, router, pick, active, slope, sent, waits=()):
    rows, width = active.shape
    sources, members, cap, depth = grad_y.shape
    step = min(256, width)
    sent = list(sent or [])
    return pl.pallas_call(
        functools.partial(weight_body, len(sent) + len(waits)),
        out_shape=(
            jax.ShapeDtypeStruct((local, depth, width), jnp.float32),
            jax.ShapeDtypeStruct((local, width, depth), jnp.float32),
            jax.ShapeDtypeStruct((8, 128), jnp.float32),
        ),
        grid=(width // step,),
        in_specs=[
            pl.BlockSpec((rows, depth), lambda i: (0, 0)),
            pl.BlockSpec((sources, None, cap, depth), lambda i: (0, e % members, 0, 0)),
            pl.BlockSpec(router.shape, lambda i: (0, 0)),
            pl.BlockSpec(pick.shape, lambda i: (0, 0)),
            pl.BlockSpec((rows, step), lambda i: (0, i)),
            pl.BlockSpec((rows, step), lambda i: (0, i)),
        ]
        + [pl.BlockSpec(memory_space=pl.ANY)] * (len(sent) + len(waits)),
        out_specs=(
            pl.BlockSpec((None, depth, step), lambda i: (e, 0, i)),
            pl.BlockSpec((None, step, depth), lambda i: (e, i, 0)),
            pl.BlockSpec((8, 128), lambda i: (0, 0)),
        ),
        scratch_shapes=[
            pltpu.VMEM((depth, rows), jnp.bfloat16),
            pltpu.VMEM((rows, depth), jnp.bfloat16),
        ],
        input_output_aliases={6 + j: j for j in range(len(sent))},
        compiler_params=params("arbitrary"),
        name="weight_pass",
        cost_estimate=cost(4 * rows * depth * width, 8 * width * depth + 8 * rows * depth),
    )(x, grad_y, router, pick, active, slope, *sent, *waits)


def swap(blocks, axis):
    return lax.all_to_all(blocks, axis, split_axis=0, concat_axis=0, tiled=True)


def tie(*values):
    return lax.optimization_barrier(values)


def row_stats(values):
    mean = jnp.mean(values, axis=-1, keepdims=True)
    centered = values - mean
    variance = jnp.mean(centered * centered, axis=-1, keepdims=True)
    return (mean, lax.rsqrt(variance + EPSILON))


def slot_layout(expert_ids, experts, cap):
    chosen = expert_ids[:, 0]
    length = chosen.shape[0]
    table = chosen[:, None] == jnp.arange(experts, dtype=jnp.int32)[None, :]
    order = jnp.arange(length, dtype=jnp.int32)
    before = (order[:, None] > order[None, :]).astype(jnp.bfloat16)
    counted = jnp.dot(before, table.astype(jnp.bfloat16), preferred_element_type=jnp.float32)
    ranks = jnp.sum(jnp.where(table, counted, 0.0), axis=1).astype(jnp.int32)
    return (chosen, ranks, table.astype(jnp.float32))


def per_device(
    tokens, w_qkv, w_out, w_router, ln_gains, ln_biases, w_in, w_back, expert_ids, cotangent
):
    rows_all, cols_all = lax.axis_size("row"), lax.axis_size("col")
    col = lax.axis_index("col")
    length, depth = tokens.shape
    share = depth // rows_all
    width = w_qkv.shape[2]
    experts = w_router.shape[1]
    local = w_in.shape[0]
    cap = 2 * length // experts
    block_rows = rows_all * cap
    block = min(256, length // 2)
    part = length // cols_all
    members = max(1, local // 2)
    pieces = (depth * 5 // 8, depth * 3 // 8)

    def own(values, axis=0):
        return lax.dynamic_slice_in_dim(values, col * part, part, axis)

    def send(packed):
        return swap(packed.reshape(rows_all, cap, depth), "row").reshape(block_rows, depth)

    stacked = w_qkv.transpose(1, 0, 2).reshape(share, 3 * width)
    weights = jnp.concatenate([stacked, w_router, ln_gains.T, ln_biases.T], axis=1)
    weights = lax.all_gather(weights, "row", axis=0, tiled=True)
    mean_one, inverse_one = row_stats(tokens.astype(jnp.float32))

    chosen, ranks, select = slot_layout(expert_ids, experts, cap)
    out_block, ranks = tie(w_out.T, ranks)
    out_block = swap(jnp.broadcast_to(out_block[None], (cols_all, share, width)), "col")
    slots = chosen * cap + ranks
    slots_by_local = ((chosen % local) * rows_all + chosen // local) * cap + ranks
    member = chosen % local
    slots_by_group = [
        jnp.where(
            member // members == g,
            ((chosen // local) * members + member % members) * cap + ranks,
            -1,
        )
        for g in range(local // members)
    ]

    slots_by_pair = slots_by_local - slots_by_local
    for g, at in enumerate(slots_by_group):
        slots_by_pair = jnp.where(at >= 0, at + g * members * block_rows, slots_by_pair)

    def pack_group(g, waits):
        rows = members * block_rows
        return pack(slots_by_pair, [cotangent], g * rows, rows, 1, waits)[0]

    grad_packed = [pack_group(0, [])]
    weights, grad_packed[0], out_block, mean_one, inverse_one = tie(
        weights, grad_packed[0], out_block, mean_one, inverse_one
    )
    qkv_full = weights[:, : 3 * width]
    router_full = weights[:, 3 * width : 3 * width + experts]
    norms = weights[:, 3 * width + experts :].astype(jnp.float32).T
    gains, biases = norms[0:2], norms[2:4]

    resid_in = tokens.astype(jnp.float32)
    normed_one = (resid_in - mean_one) * inverse_one
    normal_in = (normed_one * gains[0] + biases[0]).astype(jnp.bfloat16)
    projected = jnp.dot(normal_in, qkv_full, preferred_element_type=jnp.float32).astype(jnp.bfloat16)

    context, logsum = attend_forward(projected, tuple(range(length // block)), block)
    context, grad_packed[0] = tie(context, grad_packed[0])
    full = lax.all_gather(context, "col", axis=0)
    grad_packed += [pack_group(g, [context]) for g in range(1, local // members)]
    out_full = lax.all_gather(out_block, "row", axis=1, tiled=True)
    grad_arrived = []
    for g in range(local // members):
        if g:
            grad_arrived[-1], grad_packed[g] = tie(grad_arrived[-1], grad_packed[g])
        grad_arrived.append(swap(grad_packed[g].reshape(rows_all, members, cap, depth), "row"))
    full, out_full = tie(full, out_full)
    middle, routed = middle_pass(full, out_full, tokens, gains[1:2], biases[1:2])

    short = cap // 2
    chunks = [(0, 0, short), (0, short, short)] + [(e, 0, cap) for e in range(1, local)]
    split = (ranks // short * rows_all + chosen // local) * short + ranks % short
    slots_by_chunk = jnp.where(chosen % local == 0, split, slots_by_local)

    def pack_chunk(k, waits):
        e, low, size = chunks[k]
        base = (e * cap + low) * rows_all
        return pack(slots_by_chunk, [routed], base, size * rows_all, 1, waits)[0]

    packed = [pack_chunk(k, []) for k in range(min(3, len(chunks)))]
    packed[0], grad_arrived[-1] = tie(packed[0], grad_arrived[-1])

    logits = jnp.dot(routed, router_full, preferred_element_type=jnp.float32)
    probs = jax.nn.softmax(logits, axis=-1)
    gate = jnp.sum(probs * select, axis=-1, keepdims=True)

    arrived, summed, kept, sent = [], [], [], []
    final = len(chunks) - 1
    for k, (e, low, size) in enumerate(chunks):
        moved = swap(packed[k].reshape(rows_all, size, depth), "row")
        arrived.append(moved.reshape(rows_all * size, depth))
        if k < final:
            packed[k + 1], arrived[k], *more = tie(
                packed[k + 1], arrived[k], *(packed[2:3] if k == 0 else [])
            )
            packed[2:3] = more or packed[2:3]
        if k:
            then = packed[k + 1] if k < final else sent[0][0]
            then, summed[k - 1], arrived[k] = tie(then, summed[k - 1], arrived[k])
            summed[k - 1] = lax.psum_scatter(
                summed[k - 1], "col", scatter_dimension=0, tiled=True
            )
            if k < final:
                packed[k + 1] = then
            else:
                sent[0][0] = then
        waits = summed[:1] if k == final else []
        made, both, pair = expert_pass(
            chunks[k],
            arrived[k],
            grad_arrived[e // members],
            w_in,
            w_back,
            kept.pop() if low else [],
            sent.pop() if low or e % members else [],
            cols_all,
            pieces,
            waits,
        )
        kept.append(both)
        summed.append(made)
        sent.append(pair)
        if 1 <= k and k + 2 <= final:
            packed.append(pack_chunk(k + 2, [made]))
    active = [v[0].reshape(block_rows, -1) for v in kept]
    slope = [v[1].reshape(block_rows, -1) for v in kept]

    def joined(values):
        first = [v.reshape(rows_all, short, -1) for v in values[:2]]
        whole = [v.reshape(rows_all, cap, -1) for v in values[2:]]
        return [jnp.concatenate(first, axis=1)] + whole

    arrived = [v.reshape(block_rows, depth) for v in joined(arrived)]

    step = min(256, length)
    order = [(g, f) for f in range(len(pieces)) for g in range(len(sent))]
    grad_sent = []
    grad_weights = None
    token = None
    row = lax.axis_index("row")

    def weigh(e, waits):
        pick = jnp.arange(experts, dtype=jnp.int32)[None, :] == row * local + e
        return weight_pass(
            e,
            local,
            arrived[e],
            grad_arrived[e // members],
            router_full,
            pick.astype(jnp.float32),
            active[e],
            slope[e],
            grad_weights,
            waits,
        )

    early = max(1, local // 2)
    late = max(early, local - 1)
    waits = slope[-1:]
    last = None
    for f, wide in enumerate(pieces):
        for e in range(early) if f == 0 else range(early, late):
            *grad_weights, token = weigh(e, waits)
            waits = [token]
        rows = []
        for g in range(len(sent)):
            piece = sent[g][f]
            if last is not None:
                piece, last = tie(piece, last)
                if rows:
                    rows[-1] = last
                else:
                    ended[-1] = last
            if f == 0 and g == len(sent) - 1:
                piece, slope[-1] = tie(piece, slope[-1])
            if f and g == len(sent) - 1:
                piece, whole = tie(piece, whole)
            last = swap(piece, "row")
            if f == 0 and g == 0:
                last, made = tie(last, summed[-1])
                summed[-1] = lax.psum_scatter(made, "col", scatter_dimension=0, tiled=True)
            rows.append(last)
        if f == 0:
            ended = rows
            sent[0][1], token = tie(sent[0][1], token)
            waits = [token]
        else:
            homed = jnp.stack(joined(summed), axis=1)
            homed, token = tie(homed, token)
            waits = [token]
            grad_sent.append(lax.psum_scatter(whole, "col", scatter_dimension=0, tiled=True))
        whole = unpack(slots_by_group, [v.reshape(-1, wide) for v in rows], step, waits)
        if f:
            rows[-1], homed = tie(rows[-1], homed)
            homed = swap(homed, "row")
            whole, homed = tie(whole, homed)
        waits = [whole]
    grad_sent.append(lax.psum_scatter(whole, "col", scatter_dimension=0, tiled=True))

    returned = unpack(
        [slots], [homed.reshape(experts * cap, depth // cols_all)], step, grad_sent[:1]
    ).astype(jnp.float32)
    columns = depth // cols_all

    def own_columns(values):
        return lax.dynamic_slice_in_dim(values, col * columns, columns, 1)

    mixed = (own_columns(middle) + gate * returned).astype(jnp.bfloat16)
    grad_gate = jnp.sum(own_columns(cotangent).astype(jnp.float32) * returned, axis=-1)
    grad_gate = swap(grad_gate.reshape(cols_all, part), "col")
    grad_gate = jnp.sum(grad_gate, axis=0)[:, None]
    mixed_full = lax.all_gather(mixed, "col", axis=0)

    own_gate, own_probs, own_select = own(gate), own(probs), own(select)
    grad_logits = (grad_gate * own_probs * (own_select - own_gate)).astype(jnp.bfloat16)
    own_routed = own(routed)
    grad_router = jnp.einsum(
        "td,te->de", own_routed, grad_logits, preferred_element_type=jnp.float32
    )
    place = jnp.reshape(col, (1,)).astype(jnp.int32)
    grad_middle, grad_attn, grad_context, sums_two = settle_pass(
        place,
        *grad_sent,
        own_gate,
        grad_logits,
        router_full,
        cotangent,
        middle,
        gains[1:2],
        out_full,
    )
    grad_context = swap(grad_context, "col")
    context_own = own(full, 1)
    grad_out = jnp.einsum("td,ztc->dzc", grad_attn, context_own, preferred_element_type=jnp.float32)
    plane = jnp.concatenate([grad_out.reshape(depth, cols_all * width), grad_router], axis=1)
    plane = swap(plane.astype(jnp.bfloat16).reshape(rows_all, share, -1), "row")
    grad_context = grad_context.reshape(length, width)
    waits = [grad_attn]
    for e in range(late, local):
        *grad_weights, token = weigh(e, waits)
        waits = [token]
    grad_in, grad_back = grad_weights
    grad_proj = attend_backward(projected, grad_context, context, logsum, block, 0, waits)[0]
    grad_proj, plane = tie(grad_proj, plane)

    shares = jnp.einsum("tc,dc->td", grad_proj, qkv_full, preferred_element_type=jnp.float32)
    shares, mixed_full = tie(shares.astype(jnp.bfloat16), mixed_full)
    grad_normal = lax.psum_scatter(shares, "col", scatter_dimension=0, tiled=True)
    mixed_out = mixed_full.transpose(1, 0, 2).reshape(length, depth)
    grad_qkv = jnp.einsum("td,tc->dc", normal_in, grad_proj, preferred_element_type=jnp.float32)
    plane = jnp.sum(plane.astype(jnp.float32), axis=0)
    router_share = plane[:, cols_all * width :].reshape(1, share, experts)
    out_share = plane[:, : cols_all * width].reshape(share, cols_all, width).transpose(1, 0, 2)
    router_share = jnp.broadcast_to(router_share, (cols_all, share, experts))
    plane = jnp.concatenate([out_share, router_share], axis=2).astype(jnp.bfloat16)
    plane = jnp.sum(swap(plane, "col").astype(jnp.float32), axis=0)
    out_share, router_share = plane[:, :width].T, plane[:, width:]
    grad_normal, out_share, mixed_out, grad_qkv = tie(
        grad_normal, out_share, mixed_out, grad_qkv
    )

    grad_tokens, sums_one = close_pass(place, grad_normal, tokens, grad_middle, gains[0:1])
    grad_tokens = lax.all_gather(grad_tokens, "col", axis=0, tiled=True)
    small = jnp.concatenate([sums_one[0:2], sums_two[0:2]], axis=0)
    small = swap(small.reshape(4, rows_all, share).transpose(1, 0, 2), "row")
    small = jnp.sum(small, axis=0)
    small = jnp.sum(swap(jnp.broadcast_to(small[None], (cols_all, 4, share)), "col"), axis=0)
    qkv_share = swap(grad_qkv.astype(jnp.bfloat16).reshape(rows_all, share, -1), "row")
    qkv_share = jnp.sum(qkv_share.astype(jnp.float32), axis=0)
    qkv_share = qkv_share.reshape(share, 3, width).transpose(1, 0, 2)
    return (
        mixed_out,
        grad_tokens,
        qkv_share,
        out_share,
        router_share,
        jnp.stack([small[0], small[2]]),
        small[1],
        small[3],
        grad_in,
        grad_back,
    )


def solution(mesh):
    return jax.shard_map(
        per_device,
        mesh=mesh,
        in_specs=(
            P("row", None),
            P(None, "row", "col"),
            P("col", "row"),
            P("row", None),
            P(None, "row"),
            P(None, "row"),
            P("row", None, "col"),
            P("row", "col", None),
            P("row", None),
            P("row", None),
        ),
        out_specs=(
            P("row", None),
            P("row", None),
            P(None, "row", "col"),
            P("col", "row"),
            P("row", None),
            P(None, "row"),
            P("row"),
            P("row"),
            P("row", None, "col"),
            P("row", "col", None),
        ),
        check_vma=False,
    )
```

```python
import functools, math
import jax, jax.numpy as jnp
from jax import lax
from jax.experimental import pallas as pl
from jax.experimental.pallas import tpu as pltpu
from jax.sharding import PartitionSpec as P

HEAD_DIM = 64
EPSILON = 1e-05
MASKED = -1e30
VMEM = 60 << 20


def params(*kinds):
    return pltpu.CompilerParams(dimension_semantics=kinds or None, vmem_limit_bytes=VMEM)


def cost(flops, moved, special=0):
    return pl.CostEstimate(flops=flops, bytes_accessed=moved, transcendentals=special)


def dot(a, b, dims):
    return lax.dot_general(a, b, (dims, ((), ())), preferred_element_type=jnp.float32)

NN = ((1,), (0,))
NT = ((1,), (1,))
TN = ((0,), (0,))


def pack_body(base, step, each, parts, slots_ref, *rest):
    rows_refs, outs = rest[:parts], rest[-((pl.num_programs(0)) // each) :]
    at = pl.program_id(0)
    made = None
    first = 0
    for rows_ref in rows_refs:
        length = rows_ref.shape[0]
        wanted = base + at * step + lax.broadcasted_iota(jnp.int32, (step, length), 0)
        chosen = jnp.where(slots_ref[:, pl.ds(first, length)] == wanted, 1.0, 0.0)
        more = dot(chosen.astype(jnp.bfloat16), rows_ref[...], NN)
        made = more if made is None else made + more
        first += length
    made = made.astype(jnp.bfloat16)
    for j, out_ref in enumerate(outs):

        @pl.when(at // each == j)
        def _(out_ref=out_ref):
            out_ref[...] = made


def pack(slots, rows, base, count, outs, waits=()):
    length = slots.shape[0]
    width = rows[0].shape[1]
    step = min(512, count)
    each = count // step
    return pl.pallas_call(
        functools.partial(pack_body, base, step, each, len(rows)),
        out_shape=(jax.ShapeDtypeStruct((count, width), jnp.bfloat16),) * outs,
        grid=(each * outs,),
        in_specs=[pl.BlockSpec((1, length), lambda i: (0, 0))]
        + [pl.BlockSpec(r.shape, lambda i: (0, 0)) for r in rows]
        + [pl.BlockSpec(memory_space=pl.ANY)] * len(waits),
        out_specs=tuple(
            pl.BlockSpec((step, width), lambda i, j=j: (jnp.clip(i - j * each, 0, each - 1), 0))
            for j in range(outs)
        ),
        compiler_params=params("arbitrary"),
        name="pack",
        cost_estimate=cost(1, 1),
    )(slots.reshape(1, length), *rows, *waits)


def unpack_body(parts, *refs):
    out_ref = refs[-1]
    step = out_ref.shape[0]
    made = None
    for slots_ref, rows_ref in zip(refs[:parts], refs[parts : 2 * parts]):
        count = rows_ref.shape[0]
        held = lax.broadcasted_iota(jnp.int32, (step, count), 1)
        chosen = jnp.where(slots_ref[...] == held, 1.0, 0.0).astype(jnp.bfloat16)
        more = dot(chosen, rows_ref[...], NN)
        made = more if made is None else made + more
    out_ref[...] = made.astype(out_ref.dtype)


def unpack(slots, rows, step, waits=()):
    length = slots[0].shape[0]
    width = rows[0].shape[1]
    count = sum(r.shape[0] for r in rows)
    return pl.pallas_call(
        functools.partial(unpack_body, len(rows)),
        out_shape=jax.ShapeDtypeStruct((length, width), jnp.bfloat16),
        grid=(length // step,),
        in_specs=[pl.BlockSpec((step, 1), lambda i: (i, 0))] * len(rows)
        + [pl.BlockSpec(r.shape, lambda i: (0, 0)) for r in rows]
        + [pl.BlockSpec(memory_space=pl.ANY)] * len(waits),
        out_specs=pl.BlockSpec((step, width), lambda i: (i, 0)),
        compiler_params=params("arbitrary"),
        name="unpack",
        cost_estimate=cost(2 * count * length * width, 2 * (length + count) * width),
    )(*(at.reshape(length, 1) for at in slots), *rows, *waits)


def middle_body(full_ref, out_ref, tokens_ref, gain_ref, bias_ref, middle_ref, routed_ref, all_ref):
    cols, _, width = full_ref.shape

    @pl.when(pl.program_id(0) == 0)
    def _():
        for z in range(cols):
            all_ref[:, z * width : (z + 1) * width] = out_ref[z]

    context = jnp.concatenate([full_ref[z] for z in range(cols)], axis=1)
    total = tokens_ref[...].astype(jnp.float32) + dot(context, all_ref[...], NT)
    middle_ref[...] = total
    mean = jnp.mean(total, axis=1, keepdims=True)
    centered = total - mean
    inverse = lax.rsqrt(jnp.mean(centered * centered, axis=1, keepdims=True) + EPSILON)
    routed_ref[...] = (centered * inverse * gain_ref[...] + bias_ref[...]).astype(jnp.bfloat16)


def middle_pass(full, out_full, tokens, gain, bias):
    cols, rows, width = full.shape
    depth = tokens.shape[1]
    step = min(512, rows)
    row = pl.BlockSpec((1, depth), lambda i: (0, 0))
    block = pl.BlockSpec((step, depth), lambda i: (i, 0))
    return pl.pallas_call(
        middle_body,
        out_shape=(
            jax.ShapeDtypeStruct((rows, depth), jnp.float32),
            jax.ShapeDtypeStruct((rows, depth), jnp.bfloat16),
        ),
        grid=(rows // step,),
        in_specs=[
            pl.BlockSpec((cols, step, width), lambda i: (0, i, 0)),
            pl.BlockSpec((cols, depth, width), lambda i: (0, 0, 0)),
            block,
            row,
            row,
        ],
        out_specs=(block, block),
        scratch_shapes=[pltpu.VMEM((depth, cols * width), jnp.bfloat16)],
        compiler_params=params("arbitrary"),
        name="middle_pass",
        cost_estimate=cost(2 * rows * depth * width * cols, 10 * rows * depth),
    )(full, out_full, tokens, gain, bias)


def forward_body(blocks, block, q_ref, k_ref, v_ref, *rest):
    o_ref, lse_ref = rest[-2:]
    width = q_ref.shape[1]
    heads = width // HEAD_DIM
    lane = lax.broadcasted_iota(jnp.int32, (block, width), 1)
    hidden = lax.broadcasted_iota(jnp.int32, (block, block), 1) > lax.broadcasted_iota(
        jnp.int32, (block, block), 0
    )
    for at, i in enumerate(blocks):
        span = (i + 1) * block
        here = pl.ds(at * block, block)
        o_ref[here, :] = jnp.zeros((block, width), o_ref.dtype)

        def one_head(h, carry, here=here, span=span, i=i):
            mine = (lane >= h * HEAD_DIM) & (lane < (h + 1) * HEAD_DIM)
            query = q_ref[pl.ds(i * block, block), :].astype(jnp.float32) * 0.125
            query = jnp.where(mine, query, 0.0).astype(jnp.bfloat16)
            edge = jnp.where(hidden, MASKED, dot(query, k_ref[pl.ds(span - block, block), :], NT))
            peak = jnp.max(edge, axis=1, keepdims=True)
            if i:
                past = dot(query, k_ref[pl.ds(0, span - block), :], NT)
                peak = jnp.maximum(peak, jnp.max(past, axis=1, keepdims=True))
            edge = jnp.exp(edge - peak)
            total = jnp.sum(edge, axis=1, keepdims=True)
            if i:
                past = jnp.exp(past - peak)
                total = total + jnp.sum(past, axis=1, keepdims=True)
            share = 1.0 / total
            mixed = dot((edge * share).astype(jnp.bfloat16), v_ref[pl.ds(span - block, block), :], NN)
            if i:
                mixed = mixed + dot(
                    (past * share).astype(jnp.bfloat16), v_ref[pl.ds(0, span - block), :], NN
                )
            o_ref[here, :] = jnp.where(mine, mixed.astype(o_ref.dtype), o_ref[here, :])
            logsum = jnp.broadcast_to(peak + jnp.log(total), (block, 128))
            lse_ref[pl.ds(h, 1), here] = logsum.T[0:1, :]
            return carry

        lax.fori_loop(0, heads, one_head, 0, unroll=heads)


def attend_forward(projected, blocks, block, waits=()):
    length, triple = projected.shape
    width = triple // 3
    heads = width // HEAD_DIM
    rows = len(blocks) * block
    spec = [pl.BlockSpec((length, width), lambda i, j=j: (0, j)) for j in range(3)]
    return pl.pallas_call(
        functools.partial(forward_body, blocks, block),
        out_shape=(
            jax.ShapeDtypeStruct((rows, width), jnp.bfloat16),
            jax.ShapeDtypeStruct((heads, rows), jnp.float32),
        ),
        grid=(1,),
        in_specs=spec + [pl.BlockSpec(memory_space=pl.ANY)] * len(waits),
        out_specs=(
            pl.BlockSpec((rows, width), lambda i: (0, 0)),
            pl.BlockSpec((heads, rows), lambda i: (0, 0)),
        ),
        compiler_params=params("arbitrary"),
        name="attend_forward",
        cost_estimate=cost(rows * width, rows * width),
    )(projected, projected, projected, *waits)


def backward_body(block, given, *refs):
    q_ref, do_ref, o_ref, lse_ref, k_ref, v_ref, weight_ref = refs[:7]
    out_ref, share_ref, p_ref, ds_ref, qm_ref, dom_ref, dk_ref, dv_ref = refs[7 + given :]
    width = q_ref.shape[1]
    heads = width // HEAD_DIM
    count = q_ref.shape[0] // block
    lane = lax.broadcasted_iota(jnp.int32, (block, width), 1)
    hidden = lax.broadcasted_iota(jnp.int32, (block, block), 0) > lax.broadcasted_iota(
        jnp.int32, (block, block), 1
    )
    for i in reversed(range(count)):
        span = (i + 1) * block
        here = pl.ds(i * block, block)

        def one_head(h, carry, here=here, span=span, i=i):
            mine = (lane >= h * HEAD_DIM) & (lane < (h + 1) * HEAD_DIM)
            query = q_ref[here, :].astype(jnp.float32) * 0.125
            query = jnp.where(mine, query, 0.0).astype(jnp.bfloat16)
            grad = jnp.where(mine, do_ref[here, :].astype(jnp.float32), 0.0)
            delta = jnp.sum(grad * o_ref[here, :].astype(jnp.float32), axis=1, keepdims=True)
            delta = jnp.broadcast_to(delta, (block, 128)).T[0:1, :]
            grad = grad.astype(jnp.bfloat16)
            logsum = lse_ref[pl.ds(h, 1), here]
            column = pl.ds(pl.multiple_of(h * block, block), block)
            qm_ref[column, :] = query
            dom_ref[column, :] = grad

            def part(rows, edge):
                scores = dot(k_ref[rows, :], query, NT)
                if edge:
                    scores = jnp.where(hidden, MASKED, scores)
                probs = jnp.exp(scores - logsum)
                p_ref[rows, column] = probs.astype(jnp.bfloat16)
                grad_probs = dot(v_ref[rows, :], grad, NT)
                ds_ref[rows, column] = (probs * (grad_probs - delta)).astype(jnp.bfloat16)

            if i:
                part(pl.ds(0, span - block), False)
            part(pl.ds(span - block, block), True)
            dq = dot(ds_ref[pl.ds(0, span), column], k_ref[pl.ds(0, span), :], TN)
            out_ref[here, pl.ds(0, width)] = jnp.where(
                mine, (dq * 0.125).astype(out_ref.dtype), out_ref[here, pl.ds(0, width)]
            )
            return carry

        lax.fori_loop(0, heads, one_head, 0, unroll=heads)
        new_v = dot(p_ref[pl.ds(0, span), :], dom_ref[...], NN)
        new_k = dot(ds_ref[pl.ds(0, span), :], qm_ref[...], NN)
        if i == count - 1:
            dv_ref[...] = new_v
            dk_ref[...] = new_k
        else:
            dv_ref[pl.ds(0, span), :] += new_v
            dk_ref[pl.ds(0, span), :] += new_k
        low = pl.ds(i * block, block)
        out_ref[here, pl.ds(width, width)] = dk_ref[low, :].astype(out_ref.dtype)
        out_ref[here, pl.ds(2 * width, width)] = dv_ref[low, :].astype(out_ref.dtype)
        share_ref[here, :] = dot(out_ref[here, :], weight_ref[...], NT).astype(share_ref.dtype)


def attend_backward(projected, grad_context, context, logsum, weights, block, waits=()):
    length, width = context.shape
    heads = width // HEAD_DIM
    depth = weights.shape[0]
    third = [pl.BlockSpec((length, width), lambda i, j=j: (0, j)) for j in range(3)]
    whole = third[0]
    return pl.pallas_call(
        functools.partial(backward_body, block, len(waits)),
        out_shape=(
            jax.ShapeDtypeStruct((length, 3 * width), jnp.bfloat16),
            jax.ShapeDtypeStruct((length, depth), jnp.bfloat16),
        ),
        grid=(1,),
        in_specs=[
            third[0],
            whole,
            whole,
            pl.BlockSpec((heads, length), lambda i: (0, 0)),
            third[1],
            third[2],
            pl.BlockSpec((depth, 3 * width), lambda i: (0, 0)),
        ]
        + [pl.BlockSpec(memory_space=pl.ANY)] * len(waits),
        out_specs=(
            pl.BlockSpec((length, 3 * width), lambda i: (0, 0)),
            pl.BlockSpec((length, depth), lambda i: (0, 0)),
        ),
        scratch_shapes=[
            pltpu.VMEM((length, heads * block), jnp.bfloat16),
            pltpu.VMEM((length, heads * block), jnp.bfloat16),
            pltpu.VMEM((heads * block, width), jnp.bfloat16),
            pltpu.VMEM((heads * block, width), jnp.bfloat16),
            pltpu.VMEM((length, width), jnp.float32),
            pltpu.VMEM((length, width), jnp.float32),
        ],
        compiler_params=params("arbitrary"),
        name="attend_backward",
        cost_estimate=cost(
            20 * length * length * width, 16 * length * width, length * length * heads
        ),
    )(projected, grad_context, context, logsum, projected, projected, weights, *waits)


def normed_rows(values):
    mean = jnp.mean(values, axis=1, keepdims=True)
    centered = values - mean
    inverse = lax.rsqrt(jnp.mean(centered * centered, axis=1, keepdims=True) + EPSILON)
    return centered * inverse, inverse


def norm_back_rows(grads, normed, inverse, gain):
    hat = grads * gain
    inner = jnp.mean(hat * normed, axis=1, keepdims=True)
    return inverse * (hat - jnp.mean(hat, axis=1, keepdims=True) - normed * inner)


def add_sums(sums_ref, grads, normed):
    @pl.when(pl.program_id(0) == 0)
    def _():
        sums_ref[...] = jnp.zeros_like(sums_ref)

    sums_ref[0:1, :] += jnp.sum(grads * normed, axis=0, keepdims=True)
    sums_ref[1:2, :] += jnp.sum(grads, axis=0, keepdims=True)


def settle_body(
    col_ref, low_ref, high_ref, gate_ref, logit_ref, router_ref, cot_ref, middle_ref, gain_ref,
    weight_ref, grad_ref, low_grad_ref, context_ref, sums_ref
):
    sent = jnp.concatenate([low_ref[...], high_ref[...]], axis=1).astype(jnp.float32)
    grads = sent * gate_ref[...] + dot(logit_ref[...], router_ref[...], NT)
    normed, inverse = normed_rows(middle_ref[...])
    add_sums(sums_ref, grads, normed)
    made = cot_ref[...].astype(jnp.float32) + norm_back_rows(
        grads, normed, inverse, gain_ref[...]
    )
    grad_ref[...] = made
    low = made.astype(jnp.bfloat16)
    low_grad_ref[...] = low
    for z in range(weight_ref.shape[0]):
        context_ref[z] = dot(low, weight_ref[z], NN).astype(jnp.bfloat16)


def settle_pass(col, low, high, gate, logits, router, cotangent, middle, gain, weights):
    part, experts = logits.shape
    cols, depth, width = weights.shape
    step = min(256, part)
    block = pl.BlockSpec((step, depth), lambda i, c: (i, 0))
    mine = pl.BlockSpec((step, depth), lambda i, c: (c[0] * (part // step) + i, 0))
    return pl.pallas_call(
        settle_body,
        out_shape=(
            jax.ShapeDtypeStruct((part, depth), jnp.float32),
            jax.ShapeDtypeStruct((part, depth), jnp.bfloat16),
            jax.ShapeDtypeStruct((cols, part, width), jnp.bfloat16),
            jax.ShapeDtypeStruct((8, depth), jnp.float32),
        ),
        grid_spec=pltpu.PrefetchScalarGridSpec(
            num_scalar_prefetch=1,
            grid=(part // step,),
            in_specs=[
                pl.BlockSpec((step, low.shape[1]), lambda i, c: (i, 0)),
                pl.BlockSpec((step, high.shape[1]), lambda i, c: (i, 0)),
                pl.BlockSpec((step, 1), lambda i, c: (i, 0)),
                pl.BlockSpec((step, experts), lambda i, c: (i, 0)),
                pl.BlockSpec((depth, experts), lambda i, c: (0, 0)),
                mine,
                mine,
                pl.BlockSpec((1, depth), lambda i, c: (0, 0)),
                pl.BlockSpec((cols, depth, width), lambda i, c: (0, 0, 0)),
            ],
            out_specs=(
                block,
                block,
                pl.BlockSpec((cols, step, width), lambda i, c: (0, i, 0)),
                pl.BlockSpec((8, depth), lambda i, c: (0, 0)),
            ),
        ),
        compiler_params=params("arbitrary"),
        name="settle_pass",
        cost_estimate=cost(2 * part * depth * width * cols, 20 * part * depth),
    )(col, low, high, gate, logits, router, cotangent, middle, gain, weights)


def close_body(col_ref, share_ref, tokens_ref, grad_ref, gain_ref, out_ref, sums_ref):
    grads = share_ref[...].astype(jnp.float32)
    normed, inverse = normed_rows(tokens_ref[...].astype(jnp.float32))
    made = grad_ref[...] + norm_back_rows(grads, normed, inverse, gain_ref[...])
    out_ref[...] = made.astype(jnp.bfloat16)
    add_sums(sums_ref, grads, normed)


def close_pass(col, shares, tokens, grads, gain):
    part, depth = shares.shape
    step = min(256, part)
    block = pl.BlockSpec((step, depth), lambda i, c: (i, 0))
    mine = pl.BlockSpec((step, depth), lambda i, c: (c[0] * (part // step) + i, 0))
    return pl.pallas_call(
        close_body,
        out_shape=(
            jax.ShapeDtypeStruct((part, depth), jnp.bfloat16),
            jax.ShapeDtypeStruct((8, depth), jnp.float32),
        ),
        grid_spec=pltpu.PrefetchScalarGridSpec(
            num_scalar_prefetch=1,
            grid=(part // step,),
            in_specs=[block, mine, block, pl.BlockSpec((1, depth), lambda i, c: (0, 0))],
            out_specs=(block, pl.BlockSpec((8, depth), lambda i, c: (0, 0))),
        ),
        compiler_params=params("arbitrary"),
        name="close_pass",
        cost_estimate=cost(30 * part * depth, 12 * part * depth),
    )(col, shares, tokens, grads, gain)


ROOT = math.sqrt(2.0 / math.pi)
CUBE = 0.044715


def expert_body(given, x_ref, gy_ref, win_ref, wback_ref, *rest):
    out_ref, active_ref, slope_ref, *sent = rest[given:]
    rows, depth = x_ref.shape
    hidden = dot(x_ref[...], win_ref[...], NN)
    square = hidden * hidden
    bent = jnp.tanh(ROOT * hidden * (1.0 + CUBE * square))
    active = (0.5 * hidden * (1.0 + bent)).astype(jnp.bfloat16)
    slope = 0.5 * (1.0 + bent) + 0.5 * hidden * (1.0 - bent * bent) * (
        ROOT * (1.0 + 3.0 * CUBE * square)
    )
    active_ref[...] = active.reshape(active_ref.shape)
    parts = out_ref.shape[0]
    wide = depth // parts
    made = dot(active, wback_ref[...], NN).astype(jnp.bfloat16)
    for j in range(parts):
        out_ref[j] = made[:, j * wide : (j + 1) * wide]
    grad_active = dot(gy_ref[...].reshape(rows, depth), wback_ref[...], NT)
    grad_hidden = (grad_active * slope).astype(jnp.bfloat16)
    slope_ref[...] = grad_hidden.reshape(slope_ref.shape)
    back = dot(grad_hidden, win_ref[...], NT).astype(jnp.bfloat16)
    first = 0
    for ref in sent:
        wide = ref.shape[-1]
        ref[...] = back[:, first : first + wide].reshape(ref.shape)
        first += wide


def expert_pass(chunk, x, grad_y, w_in, w_back, kept, sent, parts, pieces, waits=()):
    e, low, size = chunk
    sources, members, cap, depth = grad_y.shape
    rows = sources * size
    width = w_in.shape[2]
    step = min(256, rows)
    group = step // size
    at = low // size
    given = [*kept, *sent]
    aliases = {4 + j: (1 if kept else 3) + j for j in range(len(given))}
    keep = jax.ShapeDtypeStruct((sources, cap, width), jnp.bfloat16)
    keep_spec = pl.BlockSpec((group, size, width), lambda i: (i, at, 0))
    piece = tuple(jax.ShapeDtypeStruct((sources, members, cap, w), jnp.bfloat16) for w in pieces)
    piece_spec = tuple(
        pl.BlockSpec((group, None, size, w), lambda i: (i, e % members, at, 0)) for w in pieces
    )
    made = pl.pallas_call(
        functools.partial(expert_body, len(given) + len(waits)),
        out_shape=(jax.ShapeDtypeStruct((parts, rows, depth // parts), jnp.bfloat16), keep, keep)
        + piece,
        grid=(rows // step,),
        in_specs=[
            pl.BlockSpec((step, depth), lambda i: (i, 0)),
            pl.BlockSpec((group, None, size, depth), lambda i: (i, e % members, at, 0)),
            pl.BlockSpec((None, depth, width), lambda i: (e, 0, 0)),
            pl.BlockSpec((None, width, depth), lambda i: (e, 0, 0)),
        ]
        + [pl.BlockSpec(memory_space=pl.ANY)] * (len(given) + len(waits)),
        out_specs=(
            pl.BlockSpec((parts, step, depth // parts), lambda i: (0, i, 0)),
            keep_spec,
            keep_spec,
        )
        + piece_spec,
        input_output_aliases=aliases,
        compiler_params=params("arbitrary"),
        name="expert_pass",
        cost_estimate=cost(
            8 * rows * depth * width, 4 * width * depth + 12 * rows * depth, rows * width
        ),
    )(x, grad_y, w_in, w_back, *given, *waits)
    return made[0], made[1:3], list(made[3:])


def weight_body(given, x_ref, gy_ref, router_ref, pick_ref, active_ref, slope_ref, *rest):
    gin_ref, gback_ref, token_ref, xt_ref, gyg_ref = rest[given:]
    token_ref[...] = jnp.zeros_like(token_ref)
    rows, depth = x_ref.shape

    @pl.when(pl.program_id(0) == 0)
    def _():
        logits = dot(x_ref[...], router_ref[...], NN)
        raised = jnp.exp(logits - jnp.max(logits, axis=1, keepdims=True))
        gate = jnp.sum(raised * pick_ref[...], axis=1, keepdims=True)
        gate = gate / jnp.sum(raised, axis=1, keepdims=True)
        xt_ref[...] = (x_ref[...].astype(jnp.float32) * gate).T.astype(jnp.bfloat16)
        grad_y = gy_ref[...].reshape(rows, depth).astype(jnp.float32)
        gyg_ref[...] = (grad_y * gate).astype(jnp.bfloat16)

    gin_ref[...] = dot(xt_ref[...], slope_ref[...], NN)
    gback_ref[...] = dot(active_ref[...], gyg_ref[...], TN)


def weight_pass(e, local, x, grad_y, router, pick, active, slope, sent, waits=()):
    rows, width = active.shape
    sources, members, cap, depth = grad_y.shape
    step = min(256, width)
    sent = list(sent or [])
    return pl.pallas_call(
        functools.partial(weight_body, len(sent) + len(waits)),
        out_shape=(
            jax.ShapeDtypeStruct((local, depth, width), jnp.float32),
            jax.ShapeDtypeStruct((local, width, depth), jnp.float32),
            jax.ShapeDtypeStruct((8, 128), jnp.float32),
        ),
        grid=(width // step,),
        in_specs=[
            pl.BlockSpec((rows, depth), lambda i: (0, 0)),
            pl.BlockSpec((sources, None, cap, depth), lambda i: (0, e % members, 0, 0)),
            pl.BlockSpec(router.shape, lambda i: (0, 0)),
            pl.BlockSpec(pick.shape, lambda i: (0, 0)),
            pl.BlockSpec((rows, step), lambda i: (0, i)),
            pl.BlockSpec((rows, step), lambda i: (0, i)),
        ]
        + [pl.BlockSpec(memory_space=pl.ANY)] * (len(sent) + len(waits)),
        out_specs=(
            pl.BlockSpec((None, depth, step), lambda i: (e, 0, i)),
            pl.BlockSpec((None, step, depth), lambda i: (e, i, 0)),
            pl.BlockSpec((8, 128), lambda i: (0, 0)),
        ),
        scratch_shapes=[
            pltpu.VMEM((depth, rows), jnp.bfloat16),
            pltpu.VMEM((rows, depth), jnp.bfloat16),
        ],
        input_output_aliases={6 + j: j for j in range(len(sent))},
        compiler_params=params("arbitrary"),
        name="weight_pass",
        cost_estimate=cost(4 * rows * depth * width, 8 * width * depth + 8 * rows * depth),
    )(x, grad_y, router, pick, active, slope, *sent, *waits)


def swap(blocks, axis):
    return lax.all_to_all(blocks, axis, split_axis=0, concat_axis=0, tiled=True)


def tie(*values):
    return lax.optimization_barrier(values)


def row_stats(values):
    mean = jnp.mean(values, axis=-1, keepdims=True)
    centered = values - mean
    variance = jnp.mean(centered * centered, axis=-1, keepdims=True)
    return (mean, lax.rsqrt(variance + EPSILON))


def slot_layout(expert_ids, experts, cap):
    chosen = expert_ids[:, 0]
    length = chosen.shape[0]
    table = chosen[:, None] == jnp.arange(experts, dtype=jnp.int32)[None, :]
    order = jnp.arange(length, dtype=jnp.int32)
    before = (order[:, None] > order[None, :]).astype(jnp.bfloat16)
    counted = jnp.dot(before, table.astype(jnp.bfloat16), preferred_element_type=jnp.float32)
    ranks = jnp.sum(jnp.where(table, counted, 0.0), axis=1).astype(jnp.int32)
    return (chosen, ranks, table.astype(jnp.float32))


def per_device(
    tokens, w_qkv, w_out, w_router, ln_gains, ln_biases, w_in, w_back, expert_ids, cotangent
):
    rows_all, cols_all = lax.axis_size("row"), lax.axis_size("col")
    col = lax.axis_index("col")
    length, depth = tokens.shape
    share = depth // rows_all
    width = w_qkv.shape[2]
    experts = w_router.shape[1]
    local = w_in.shape[0]
    cap = 2 * length // experts
    block_rows = rows_all * cap
    block = min(256, length // 2)
    part = length // cols_all
    members = max(1, local // 2)
    pieces = (depth * 5 // 8, depth * 3 // 8)

    def own(values, axis=0):
        return lax.dynamic_slice_in_dim(values, col * part, part, axis)

    def send(packed):
        return swap(packed.reshape(rows_all, cap, depth), "row").reshape(block_rows, depth)

    stacked = w_qkv.transpose(1, 0, 2).reshape(share, 3 * width)
    weights = jnp.concatenate([stacked, w_router, ln_gains.T, ln_biases.T], axis=1)
    weights = lax.all_gather(weights, "row", axis=0, tiled=True)
    mean_one, inverse_one = row_stats(tokens.astype(jnp.float32))

    chosen, ranks, select = slot_layout(expert_ids, experts, cap)
    out_block, ranks = tie(w_out.T, ranks)
    out_block = swap(jnp.broadcast_to(out_block[None], (cols_all, share, width)), "col")
    slots = chosen * cap + ranks
    slots_by_local = ((chosen % local) * rows_all + chosen // local) * cap + ranks
    member = chosen % local
    slots_by_group = [
        jnp.where(
            member // members == g,
            ((chosen // local) * members + member % members) * cap + ranks,
            -1,
        )
        for g in range(local // members)
    ]

    slots_by_pair = slots_by_local - slots_by_local
    for g, at in enumerate(slots_by_group):
        slots_by_pair = jnp.where(at >= 0, at + g * members * block_rows, slots_by_pair)

    def pack_group(g, waits):
        rows = members * block_rows
        return pack(slots_by_pair, [cotangent], g * rows, rows, 1, waits)[0]

    grad_packed = [pack_group(0, [])]
    weights, grad_packed[0], out_block, mean_one, inverse_one = tie(
        weights, grad_packed[0], out_block, mean_one, inverse_one
    )
    qkv_full = weights[:, : 3 * width]
    router_full = weights[:, 3 * width : 3 * width + experts]
    norms = weights[:, 3 * width + experts :].astype(jnp.float32).T
    gains, biases = norms[0:2], norms[2:4]

    resid_in = tokens.astype(jnp.float32)
    normed_one = (resid_in - mean_one) * inverse_one
    normal_in = (normed_one * gains[0] + biases[0]).astype(jnp.bfloat16)
    projected = jnp.dot(normal_in, qkv_full, preferred_element_type=jnp.float32).astype(jnp.bfloat16)

    context, logsum = attend_forward(projected, tuple(range(length // block)), block)
    context, grad_packed[0] = tie(context, grad_packed[0])
    full = lax.all_gather(context, "col", axis=0)
    grad_packed += [pack_group(g, [context]) for g in range(1, local // members)]
    out_full = lax.all_gather(out_block, "row", axis=1, tiled=True)
    grad_arrived = []
    for g in range(local // members):
        if g:
            grad_arrived[-1], grad_packed[g] = tie(grad_arrived[-1], grad_packed[g])
        grad_arrived.append(swap(grad_packed[g].reshape(rows_all, members, cap, depth), "row"))
    full, out_full = tie(full, out_full)
    middle, routed = middle_pass(full, out_full, tokens, gains[1:2], biases[1:2])

    short = cap // 2
    chunks = [(0, 0, short), (0, short, short)] + [(e, 0, cap) for e in range(1, local)]
    split = (ranks // short * rows_all + chosen // local) * short + ranks % short
    slots_by_chunk = jnp.where(chosen % local == 0, split, slots_by_local)

    def pack_chunk(k, waits):
        e, low, size = chunks[k]
        base = (e * cap + low) * rows_all
        return pack(slots_by_chunk, [routed], base, size * rows_all, 1, waits)[0]

    packed = [pack_chunk(k, []) for k in range(min(3, len(chunks)))]
    packed[0], grad_arrived[-1] = tie(packed[0], grad_arrived[-1])

    logits = jnp.dot(routed, router_full, preferred_element_type=jnp.float32)
    probs = jax.nn.softmax(logits, axis=-1)
    gate = jnp.sum(probs * select, axis=-1, keepdims=True)

    arrived, summed, kept, sent = [], [], [], []
    final = len(chunks) - 1
    for k, (e, low, size) in enumerate(chunks):
        moved = swap(packed[k].reshape(rows_all, size, depth), "row")
        arrived.append(moved.reshape(rows_all * size, depth))
        if k < final:
            packed[k + 1], arrived[k], *more = tie(
                packed[k + 1], arrived[k], *(packed[2:3] if k == 0 else [])
            )
            packed[2:3] = more or packed[2:3]
        if k:
            then = packed[k + 1] if k < final else sent[0][0]
            then, summed[k - 1], arrived[k] = tie(then, summed[k - 1], arrived[k])
            summed[k - 1] = lax.psum_scatter(
                summed[k - 1], "col", scatter_dimension=0, tiled=True
            )
            if k < final:
                packed[k + 1] = then
            else:
                sent[0][0] = then
        waits = summed[:1] if k == final else []
        made, both, pair = expert_pass(
            chunks[k],
            arrived[k],
            grad_arrived[e // members],
            w_in,
            w_back,
            kept.pop() if low else [],
            sent.pop() if low or e % members else [],
            cols_all,
            pieces,
            waits,
        )
        kept.append(both)
        summed.append(made)
        sent.append(pair)
        if 1 <= k and k + 2 <= final:
            packed.append(pack_chunk(k + 2, [made]))
    active = [v[0].reshape(block_rows, -1) for v in kept]
    slope = [v[1].reshape(block_rows, -1) for v in kept]

    def joined(values):
        first = [v.reshape(rows_all, short, -1) for v in values[:2]]
        whole = [v.reshape(rows_all, cap, -1) for v in values[2:]]
        return [jnp.concatenate(first, axis=1)] + whole

    arrived = [v.reshape(block_rows, depth) for v in joined(arrived)]

    step = min(256, length)
    order = [(g, f) for f in range(len(pieces)) for g in range(len(sent))]
    grad_sent = []
    grad_weights = None
    token = None
    row = lax.axis_index("row")

    def weigh(e, waits):
        pick = jnp.arange(experts, dtype=jnp.int32)[None, :] == row * local + e
        return weight_pass(
            e,
            local,
            arrived[e],
            grad_arrived[e // members],
            router_full,
            pick.astype(jnp.float32),
            active[e],
            slope[e],
            grad_weights,
            waits,
        )

    early = max(1, local // 2)
    late = max(early, local - 1)
    waits = slope[-1:]
    last = None
    for f, wide in enumerate(pieces):
        for e in range(early) if f == 0 else range(early, late):
            *grad_weights, token = weigh(e, waits)
            waits = [token]
        rows = []
        for g in range(len(sent)):
            piece = sent[g][f]
            if last is not None:
                piece, last = tie(piece, last)
                if rows:
                    rows[-1] = last
                else:
                    ended[-1] = last
            if f == 0 and g == len(sent) - 1:
                piece, slope[-1] = tie(piece, slope[-1])
            if f and g == len(sent) - 1:
                piece, whole = tie(piece, whole)
            last = swap(piece, "row")
            if f == 0 and g == 0:
                last, made = tie(last, summed[-1])
                summed[-1] = lax.psum_scatter(made, "col", scatter_dimension=0, tiled=True)
            rows.append(last)
        if f == 0:
            ended = rows
            sent[0][1], token = tie(sent[0][1], token)
            waits = [token]
        else:
            homed = jnp.stack(joined(summed), axis=1)
            homed, token = tie(homed, token)
            waits = [token]
            grad_sent.append(lax.psum_scatter(whole, "col", scatter_dimension=0, tiled=True))
        whole = unpack(slots_by_group, [v.reshape(-1, wide) for v in rows], step, waits)
        if f:
            rows[-1], homed = tie(rows[-1], homed)
            homed = swap(homed, "row")
            whole, homed = tie(whole, homed)
        waits = [whole]
    grad_sent.append(lax.psum_scatter(whole, "col", scatter_dimension=0, tiled=True))

    returned = unpack(
        [slots], [homed.reshape(experts * cap, depth // cols_all)], step, grad_sent[:1]
    ).astype(jnp.float32)
    columns = depth // cols_all

    def own_columns(values):
        return lax.dynamic_slice_in_dim(values, col * columns, columns, 1)

    mixed = (own_columns(middle) + gate * returned).astype(jnp.bfloat16)
    grad_gate = jnp.sum(own_columns(cotangent).astype(jnp.float32) * returned, axis=-1)
    grad_gate = swap(grad_gate.reshape(cols_all, part), "col")
    grad_gate = jnp.sum(grad_gate, axis=0)[:, None]
    mixed_full = lax.all_gather(mixed, "col", axis=0)

    own_gate, own_probs, own_select = own(gate), own(probs), own(select)
    grad_logits = (grad_gate * own_probs * (own_select - own_gate)).astype(jnp.bfloat16)
    own_routed = own(routed)
    grad_router = jnp.einsum(
        "td,te->de", own_routed, grad_logits, preferred_element_type=jnp.float32
    )
    place = jnp.reshape(col, (1,)).astype(jnp.int32)
    grad_middle, grad_attn, grad_context, sums_two = settle_pass(
        place,
        *grad_sent,
        own_gate,
        grad_logits,
        router_full,
        cotangent,
        middle,
        gains[1:2],
        out_full,
    )
    grad_context = swap(grad_context, "col")
    context_own = own(full, 1)
    grad_out = jnp.einsum("td,ztc->dzc", grad_attn, context_own, preferred_element_type=jnp.float32)
    plane = jnp.concatenate([grad_out.reshape(depth, cols_all * width), grad_router], axis=1)
    plane = swap(plane.astype(jnp.bfloat16).reshape(rows_all, share, -1), "row")
    grad_context = grad_context.reshape(length, width)
    waits = [grad_attn]
    for e in range(late, local):
        *grad_weights, token = weigh(e, waits)
        waits = [token]
    grad_in, grad_back = grad_weights
    grad_proj, shares = attend_backward(
        projected, grad_context, context, logsum, qkv_full, block, waits
    )
    shares, plane = tie(shares, plane)

    shares, mixed_full = tie(shares, mixed_full)
    grad_normal = lax.psum_scatter(shares, "col", scatter_dimension=0, tiled=True)
    mixed_out = mixed_full.transpose(1, 0, 2).reshape(length, depth)
    grad_qkv = jnp.einsum("td,tc->dc", normal_in, grad_proj, preferred_element_type=jnp.float32)
    plane = jnp.sum(plane.astype(jnp.float32), axis=0)
    router_share = plane[:, cols_all * width :].reshape(1, share, experts)
    out_share = plane[:, : cols_all * width].reshape(share, cols_all, width).transpose(1, 0, 2)
    router_share = jnp.broadcast_to(router_share, (cols_all, share, experts))
    plane = jnp.concatenate([out_share, router_share], axis=2).astype(jnp.bfloat16)
    plane = jnp.sum(swap(plane, "col").astype(jnp.float32), axis=0)
    out_share, router_share = plane[:, :width].T, plane[:, width:]
    grad_normal, out_share, mixed_out, grad_qkv = tie(
        grad_normal, out_share, mixed_out, grad_qkv
    )

    grad_tokens, sums_one = close_pass(place, grad_normal, tokens, grad_middle, gains[0:1])
    grad_tokens = lax.all_gather(grad_tokens, "col", axis=0, tiled=True)
    small = jnp.concatenate([sums_one[0:2], sums_two[0:2]], axis=0)
    small = swap(small.reshape(4, rows_all, share).transpose(1, 0, 2), "row")
    small = jnp.sum(small, axis=0)
    small = jnp.sum(swap(jnp.broadcast_to(small[None], (cols_all, 4, share)), "col"), axis=0)
    qkv_share = swap(grad_qkv.astype(jnp.bfloat16).reshape(rows_all, share, -1), "row")
    qkv_share = jnp.sum(qkv_share.astype(jnp.float32), axis=0)
    qkv_share = qkv_share.reshape(share, 3, width).transpose(1, 0, 2)
    return (
        mixed_out,
        grad_tokens,
        qkv_share,
        out_share,
        router_share,
        jnp.stack([small[0], small[2]]),
        small[1],
        small[3],
        grad_in,
        grad_back,
    )


def solution(mesh):
    return jax.shard_map(
        per_device,
        mesh=mesh,
        in_specs=(
            P("row", None),
            P(None, "row", "col"),
            P("col", "row"),
            P("row", None),
            P(None, "row"),
            P(None, "row"),
            P("row", None, "col"),
            P("row", "col", None),
            P("row", None),
            P("row", None),
        ),
        out_specs=(
            P("row", None),
            P("row", None),
            P(None, "row", "col"),
            P("col", "row"),
            P("row", None),
            P(None, "row"),
            P("row"),
            P("row"),
            P("row", None, "col"),
            P("row", "col", None),
        ),
        check_vma=False,
    )
```

```python
import functools, math
import jax, jax.numpy as jnp
from jax import lax
from jax.experimental import pallas as pl
from jax.experimental.pallas import tpu as pltpu
from jax.sharding import PartitionSpec as P

HEAD_DIM = 64
EPSILON = 1e-05
MASKED = -1e30
VMEM = 60 << 20


def params(*kinds):
    return pltpu.CompilerParams(dimension_semantics=kinds or None, vmem_limit_bytes=VMEM)


def cost(flops, moved, special=0):
    return pl.CostEstimate(flops=flops, bytes_accessed=moved, transcendentals=special)


def dot(a, b, dims):
    return lax.dot_general(a, b, (dims, ((), ())), preferred_element_type=jnp.float32)

NN = ((1,), (0,))
NT = ((1,), (1,))
TN = ((0,), (0,))


def pack_body(base, step, each, parts, slots_ref, *rest):
    rows_refs, outs = rest[:parts], rest[-((pl.num_programs(0)) // each) :]
    at = pl.program_id(0)
    made = None
    first = 0
    for rows_ref in rows_refs:
        length = rows_ref.shape[0]
        wanted = base + at * step + lax.broadcasted_iota(jnp.int32, (step, length), 0)
        chosen = jnp.where(slots_ref[:, pl.ds(first, length)] == wanted, 1.0, 0.0)
        more = dot(chosen.astype(jnp.bfloat16), rows_ref[...], NN)
        made = more if made is None else made + more
        first += length
    made = made.astype(jnp.bfloat16)
    for j, out_ref in enumerate(outs):

        @pl.when(at // each == j)
        def _(out_ref=out_ref):
            out_ref[...] = made


def pack(slots, rows, base, count, outs, waits=()):
    length = slots.shape[0]
    width = rows[0].shape[1]
    step = min(512, count)
    each = count // step
    return pl.pallas_call(
        functools.partial(pack_body, base, step, each, len(rows)),
        out_shape=(jax.ShapeDtypeStruct((count, width), jnp.bfloat16),) * outs,
        grid=(each * outs,),
        in_specs=[pl.BlockSpec((1, length), lambda i: (0, 0))]
        + [pl.BlockSpec(r.shape, lambda i: (0, 0)) for r in rows]
        + [pl.BlockSpec(memory_space=pl.ANY)] * len(waits),
        out_specs=tuple(
            pl.BlockSpec((step, width), lambda i, j=j: (jnp.clip(i - j * each, 0, each - 1), 0))
            for j in range(outs)
        ),
        compiler_params=params("arbitrary"),
        name="pack",
        cost_estimate=cost(1, 1),
    )(slots.reshape(1, length), *rows, *waits)


def unpack_body(parts, *refs):
    out_ref = refs[-1]
    step = out_ref.shape[0]
    made = None
    for slots_ref, rows_ref in zip(refs[:parts], refs[parts : 2 * parts]):
        count = rows_ref.shape[0]
        held = lax.broadcasted_iota(jnp.int32, (step, count), 1)
        chosen = jnp.where(slots_ref[...] == held, 1.0, 0.0).astype(jnp.bfloat16)
        more = dot(chosen, rows_ref[...], NN)
        made = more if made is None else made + more
    out_ref[...] = made.astype(out_ref.dtype)


def unpack(slots, rows, step, waits=()):
    length = slots[0].shape[0]
    width = rows[0].shape[1]
    count = sum(r.shape[0] for r in rows)
    return pl.pallas_call(
        functools.partial(unpack_body, len(rows)),
        out_shape=jax.ShapeDtypeStruct((length, width), jnp.bfloat16),
        grid=(length // step,),
        in_specs=[pl.BlockSpec((step, 1), lambda i: (i, 0))] * len(rows)
        + [pl.BlockSpec(r.shape, lambda i: (0, 0)) for r in rows]
        + [pl.BlockSpec(memory_space=pl.ANY)] * len(waits),
        out_specs=pl.BlockSpec((step, width), lambda i: (i, 0)),
        compiler_params=params("arbitrary"),
        name="unpack",
        cost_estimate=cost(2 * count * length * width, 2 * (length + count) * width),
    )(*(at.reshape(length, 1) for at in slots), *rows, *waits)


def middle_body(full_ref, out_ref, tokens_ref, gain_ref, bias_ref, middle_ref, routed_ref, all_ref):
    cols, _, width = full_ref.shape

    @pl.when(pl.program_id(0) == 0)
    def _():
        for z in range(cols):
            all_ref[:, z * width : (z + 1) * width] = out_ref[z]

    context = jnp.concatenate([full_ref[z] for z in range(cols)], axis=1)
    total = tokens_ref[...].astype(jnp.float32) + dot(context, all_ref[...], NT)
    middle_ref[...] = total
    mean = jnp.mean(total, axis=1, keepdims=True)
    centered = total - mean
    inverse = lax.rsqrt(jnp.mean(centered * centered, axis=1, keepdims=True) + EPSILON)
    routed_ref[...] = (centered * inverse * gain_ref[...] + bias_ref[...]).astype(jnp.bfloat16)


def middle_pass(full, out_full, tokens, gain, bias):
    cols, rows, width = full.shape
    depth = tokens.shape[1]
    step = min(512, rows)
    row = pl.BlockSpec((1, depth), lambda i: (0, 0))
    block = pl.BlockSpec((step, depth), lambda i: (i, 0))
    return pl.pallas_call(
        middle_body,
        out_shape=(
            jax.ShapeDtypeStruct((rows, depth), jnp.float32),
            jax.ShapeDtypeStruct((rows, depth), jnp.bfloat16),
        ),
        grid=(rows // step,),
        in_specs=[
            pl.BlockSpec((cols, step, width), lambda i: (0, i, 0)),
            pl.BlockSpec((cols, depth, width), lambda i: (0, 0, 0)),
            block,
            row,
            row,
        ],
        out_specs=(block, block),
        scratch_shapes=[pltpu.VMEM((depth, cols * width), jnp.bfloat16)],
        compiler_params=params("arbitrary"),
        name="middle_pass",
        cost_estimate=cost(2 * rows * depth * width * cols, 10 * rows * depth),
    )(full, out_full, tokens, gain, bias)


def forward_body(blocks, block, q_ref, k_ref, v_ref, *rest):
    o_ref, lse_ref = rest[-2:]
    width = q_ref.shape[1]
    heads = width // HEAD_DIM
    lane = lax.broadcasted_iota(jnp.int32, (block, width), 1)
    hidden = lax.broadcasted_iota(jnp.int32, (block, block), 1) > lax.broadcasted_iota(
        jnp.int32, (block, block), 0
    )
    for at, i in enumerate(blocks):
        span = (i + 1) * block
        here = pl.ds(at * block, block)
        o_ref[here, :] = jnp.zeros((block, width), o_ref.dtype)

        def one_head(h, carry, here=here, span=span, i=i):
            mine = (lane >= h * HEAD_DIM) & (lane < (h + 1) * HEAD_DIM)
            query = q_ref[pl.ds(i * block, block), :].astype(jnp.float32) * 0.125
            query = jnp.where(mine, query, 0.0).astype(jnp.bfloat16)
            edge = jnp.where(hidden, MASKED, dot(query, k_ref[pl.ds(span - block, block), :], NT))
            peak = jnp.max(edge, axis=1, keepdims=True)
            if i:
                past = dot(query, k_ref[pl.ds(0, span - block), :], NT)
                peak = jnp.maximum(peak, jnp.max(past, axis=1, keepdims=True))
            edge = jnp.exp(edge - peak)
            total = jnp.sum(edge, axis=1, keepdims=True)
            if i:
                past = jnp.exp(past - peak)
                total = total + jnp.sum(past, axis=1, keepdims=True)
            share = 1.0 / total
            mixed = dot((edge * share).astype(jnp.bfloat16), v_ref[pl.ds(span - block, block), :], NN)
            if i:
                mixed = mixed + dot(
                    (past * share).astype(jnp.bfloat16), v_ref[pl.ds(0, span - block), :], NN
                )
            o_ref[here, :] = jnp.where(mine, mixed.astype(o_ref.dtype), o_ref[here, :])
            logsum = jnp.broadcast_to(peak + jnp.log(total), (block, 128))
            lse_ref[pl.ds(h, 1), here] = logsum.T[0:1, :]
            return carry

        lax.fori_loop(0, heads, one_head, 0, unroll=heads)


def attend_forward(projected, blocks, block, waits=()):
    length, triple = projected.shape
    width = triple // 3
    heads = width // HEAD_DIM
    rows = len(blocks) * block
    spec = [pl.BlockSpec((length, width), lambda i, j=j: (0, j)) for j in range(3)]
    return pl.pallas_call(
        functools.partial(forward_body, blocks, block),
        out_shape=(
            jax.ShapeDtypeStruct((rows, width), jnp.bfloat16),
            jax.ShapeDtypeStruct((heads, rows), jnp.float32),
        ),
        grid=(1,),
        in_specs=spec + [pl.BlockSpec(memory_space=pl.ANY)] * len(waits),
        out_specs=(
            pl.BlockSpec((rows, width), lambda i: (0, 0)),
            pl.BlockSpec((heads, rows), lambda i: (0, 0)),
        ),
        compiler_params=params("arbitrary"),
        name="attend_forward",
        cost_estimate=cost(rows * width, rows * width),
    )(projected, projected, projected, *waits)


def backward_body(block, given, *refs):
    q_ref, do_ref, o_ref, lse_ref, k_ref, v_ref, weight_ref = refs[:7]
    out_ref, share_ref, p_ref, ds_ref, qm_ref, dom_ref, dk_ref, dv_ref = refs[7 + given :]
    width = q_ref.shape[1]
    heads = width // HEAD_DIM
    count = q_ref.shape[0] // block
    lane = lax.broadcasted_iota(jnp.int32, (block, width), 1)
    hidden = lax.broadcasted_iota(jnp.int32, (block, block), 0) > lax.broadcasted_iota(
        jnp.int32, (block, block), 1
    )
    for i in reversed(range(count)):
        span = (i + 1) * block
        here = pl.ds(i * block, block)

        def one_head(h, carry, here=here, span=span, i=i):
            mine = (lane >= h * HEAD_DIM) & (lane < (h + 1) * HEAD_DIM)
            query = q_ref[here, :].astype(jnp.float32) * 0.125
            query = jnp.where(mine, query, 0.0).astype(jnp.bfloat16)
            grad = jnp.where(mine, do_ref[here, :].astype(jnp.float32), 0.0)
            delta = jnp.sum(grad * o_ref[here, :].astype(jnp.float32), axis=1, keepdims=True)
            delta = jnp.broadcast_to(delta, (block, 128)).T[0:1, :]
            grad = grad.astype(jnp.bfloat16)
            logsum = lse_ref[pl.ds(h, 1), here]
            column = pl.ds(pl.multiple_of(h * block, block), block)
            qm_ref[column, :] = query
            dom_ref[column, :] = grad

            def part(rows, edge):
                scores = dot(k_ref[rows, :], query, NT)
                if edge:
                    scores = jnp.where(hidden, MASKED, scores)
                probs = jnp.exp(scores - logsum)
                p_ref[rows, column] = probs.astype(jnp.bfloat16)
                grad_probs = dot(v_ref[rows, :], grad, NT)
                ds_ref[rows, column] = (probs * (grad_probs - delta)).astype(jnp.bfloat16)

            if i:
                part(pl.ds(0, span - block), False)
            part(pl.ds(span - block, block), True)
            dq = dot(ds_ref[pl.ds(0, span), column], k_ref[pl.ds(0, span), :], TN)
            out_ref[here, pl.ds(0, width)] = jnp.where(
                mine, (dq * 0.125).astype(out_ref.dtype), out_ref[here, pl.ds(0, width)]
            )
            return carry

        lax.fori_loop(0, heads, one_head, 0, unroll=heads)
        new_v = dot(p_ref[pl.ds(0, span), :], dom_ref[...], NN)
        new_k = dot(ds_ref[pl.ds(0, span), :], qm_ref[...], NN)
        if i == count - 1:
            dv_ref[...] = new_v
            dk_ref[...] = new_k
        else:
            dv_ref[pl.ds(0, span), :] += new_v
            dk_ref[pl.ds(0, span), :] += new_k
        low = pl.ds(i * block, block)
        out_ref[here, pl.ds(width, width)] = dk_ref[low, :].astype(out_ref.dtype)
        out_ref[here, pl.ds(2 * width, width)] = dv_ref[low, :].astype(out_ref.dtype)
        share_ref[here, :] = dot(out_ref[here, :], weight_ref[...], NT).astype(share_ref.dtype)


def attend_backward(projected, grad_context, context, logsum, weights, block, waits=()):
    length, width = context.shape
    heads = width // HEAD_DIM
    depth = weights.shape[0]
    third = [pl.BlockSpec((length, width), lambda i, j=j: (0, j)) for j in range(3)]
    whole = third[0]
    return pl.pallas_call(
        functools.partial(backward_body, block, len(waits)),
        out_shape=(
            jax.ShapeDtypeStruct((length, 3 * width), jnp.bfloat16),
            jax.ShapeDtypeStruct((length, depth), jnp.bfloat16),
        ),
        grid=(1,),
        in_specs=[
            third[0],
            whole,
            whole,
            pl.BlockSpec((heads, length), lambda i: (0, 0)),
            third[1],
            third[2],
            pl.BlockSpec((depth, 3 * width), lambda i: (0, 0)),
        ]
        + [pl.BlockSpec(memory_space=pl.ANY)] * len(waits),
        out_specs=(
            pl.BlockSpec((length, 3 * width), lambda i: (0, 0)),
            pl.BlockSpec((length, depth), lambda i: (0, 0)),
        ),
        scratch_shapes=[
            pltpu.VMEM((length, heads * block), jnp.bfloat16),
            pltpu.VMEM((length, heads * block), jnp.bfloat16),
            pltpu.VMEM((heads * block, width), jnp.bfloat16),
            pltpu.VMEM((heads * block, width), jnp.bfloat16),
            pltpu.VMEM((length, width), jnp.float32),
            pltpu.VMEM((length, width), jnp.float32),
        ],
        compiler_params=params("arbitrary"),
        name="attend_backward",
        cost_estimate=cost(
            20 * length * length * width, 16 * length * width, length * length * heads
        ),
    )(projected, grad_context, context, logsum, projected, projected, weights, *waits)


def normed_rows(values):
    mean = jnp.mean(values, axis=1, keepdims=True)
    centered = values - mean
    inverse = lax.rsqrt(jnp.mean(centered * centered, axis=1, keepdims=True) + EPSILON)
    return centered * inverse, inverse


def norm_back_rows(grads, normed, inverse, gain):
    hat = grads * gain
    inner = jnp.mean(hat * normed, axis=1, keepdims=True)
    return inverse * (hat - jnp.mean(hat, axis=1, keepdims=True) - normed * inner)


def add_sums(sums_ref, grads, normed):
    @pl.when(pl.program_id(0) == 0)
    def _():
        sums_ref[...] = jnp.zeros_like(sums_ref)

    sums_ref[0:1, :] += jnp.sum(grads * normed, axis=0, keepdims=True)
    sums_ref[1:2, :] += jnp.sum(grads, axis=0, keepdims=True)


def settle_body(
    col_ref, low_ref, high_ref, gate_ref, logit_ref, router_ref, cot_ref, middle_ref, gain_ref,
    weight_ref, grad_ref, low_grad_ref, context_ref, sums_ref
):
    sent = jnp.concatenate([low_ref[...], high_ref[...]], axis=1).astype(jnp.float32)
    grads = sent * gate_ref[...] + dot(logit_ref[...], router_ref[...], NT)
    normed, inverse = normed_rows(middle_ref[...])
    add_sums(sums_ref, grads, normed)
    made = cot_ref[...].astype(jnp.float32) + norm_back_rows(
        grads, normed, inverse, gain_ref[...]
    )
    grad_ref[...] = made
    low = made.astype(jnp.bfloat16)
    low_grad_ref[...] = low
    for z in range(weight_ref.shape[0]):
        context_ref[z] = dot(low, weight_ref[z], NN).astype(jnp.bfloat16)


def settle_pass(col, low, high, gate, logits, router, cotangent, middle, gain, weights):
    part, experts = logits.shape
    cols, depth, width = weights.shape
    step = min(256, part)
    block = pl.BlockSpec((step, depth), lambda i, c: (i, 0))
    mine = pl.BlockSpec((step, depth), lambda i, c: (c[0] * (part // step) + i, 0))
    return pl.pallas_call(
        settle_body,
        out_shape=(
            jax.ShapeDtypeStruct((part, depth), jnp.float32),
            jax.ShapeDtypeStruct((part, depth), jnp.bfloat16),
            jax.ShapeDtypeStruct((cols, part, width), jnp.bfloat16),
            jax.ShapeDtypeStruct((8, depth), jnp.float32),
        ),
        grid_spec=pltpu.PrefetchScalarGridSpec(
            num_scalar_prefetch=1,
            grid=(part // step,),
            in_specs=[
                pl.BlockSpec((step, low.shape[1]), lambda i, c: (i, 0)),
                pl.BlockSpec((step, high.shape[1]), lambda i, c: (i, 0)),
                pl.BlockSpec((step, 1), lambda i, c: (i, 0)),
                pl.BlockSpec((step, experts), lambda i, c: (i, 0)),
                pl.BlockSpec((depth, experts), lambda i, c: (0, 0)),
                mine,
                mine,
                pl.BlockSpec((1, depth), lambda i, c: (0, 0)),
                pl.BlockSpec((cols, depth, width), lambda i, c: (0, 0, 0)),
            ],
            out_specs=(
                block,
                block,
                pl.BlockSpec((cols, step, width), lambda i, c: (0, i, 0)),
                pl.BlockSpec((8, depth), lambda i, c: (0, 0)),
            ),
        ),
        compiler_params=params("arbitrary"),
        name="settle_pass",
        cost_estimate=cost(2 * part * depth * width * cols, 20 * part * depth),
    )(col, low, high, gate, logits, router, cotangent, middle, gain, weights)


def close_body(col_ref, share_ref, tokens_ref, grad_ref, gain_ref, out_ref, sums_ref):
    grads = share_ref[...].astype(jnp.float32)
    normed, inverse = normed_rows(tokens_ref[...].astype(jnp.float32))
    made = grad_ref[...] + norm_back_rows(grads, normed, inverse, gain_ref[...])
    out_ref[...] = made.astype(jnp.bfloat16)
    add_sums(sums_ref, grads, normed)


def close_pass(col, shares, tokens, grads, gain):
    part, depth = shares.shape
    step = min(256, part)
    block = pl.BlockSpec((step, depth), lambda i, c: (i, 0))
    mine = pl.BlockSpec((step, depth), lambda i, c: (c[0] * (part // step) + i, 0))
    return pl.pallas_call(
        close_body,
        out_shape=(
            jax.ShapeDtypeStruct((part, depth), jnp.bfloat16),
            jax.ShapeDtypeStruct((8, depth), jnp.float32),
        ),
        grid_spec=pltpu.PrefetchScalarGridSpec(
            num_scalar_prefetch=1,
            grid=(part // step,),
            in_specs=[block, mine, block, pl.BlockSpec((1, depth), lambda i, c: (0, 0))],
            out_specs=(block, pl.BlockSpec((8, depth), lambda i, c: (0, 0))),
        ),
        compiler_params=params("arbitrary"),
        name="close_pass",
        cost_estimate=cost(30 * part * depth, 12 * part * depth),
    )(col, shares, tokens, grads, gain)


def move_body(source_ref, target_ref, sems):
    rows = source_ref.shape[0] // sems.shape[0]
    copies = []
    for j in range(sems.shape[0]):
        part = pl.ds(j * rows, rows)
        copies.append(
            pltpu.make_async_copy(source_ref.at[part], target_ref.at[part], sems.at[j])
        )
    for copy in copies:
        copy.start()
    for copy in copies:
        copy.wait()


def move(values):
    return pl.pallas_call(
        move_body,
        out_shape=jax.ShapeDtypeStruct(values.shape, values.dtype),
        in_specs=[pl.BlockSpec(memory_space=pl.ANY)],
        out_specs=pl.BlockSpec(memory_space=pl.ANY),
        scratch_shapes=[pltpu.SemaphoreType.DMA((8,))],
        compiler_params=params(),
        name="move",
    )(values)


ROOT = math.sqrt(2.0 / math.pi)
CUBE = 0.044715


def expert_body(given, x_ref, gy_ref, win_ref, wback_ref, *rest):
    out_ref, active_ref, slope_ref, *sent = rest[given:]
    rows, depth = x_ref.shape
    hidden = dot(x_ref[...], win_ref[...], NN)
    square = hidden * hidden
    bent = jnp.tanh(ROOT * hidden * (1.0 + CUBE * square))
    active = (0.5 * hidden * (1.0 + bent)).astype(jnp.bfloat16)
    slope = 0.5 * (1.0 + bent) + 0.5 * hidden * (1.0 - bent * bent) * (
        ROOT * (1.0 + 3.0 * CUBE * square)
    )
    active_ref[...] = active.reshape(active_ref.shape)
    parts = out_ref.shape[0]
    wide = depth // parts
    made = dot(active, wback_ref[...], NN).astype(jnp.bfloat16)
    for j in range(parts):
        out_ref[j] = made[:, j * wide : (j + 1) * wide]
    grad_active = dot(gy_ref[...].reshape(rows, depth), wback_ref[...], NT)
    grad_hidden = (grad_active * slope).astype(jnp.bfloat16)
    slope_ref[...] = grad_hidden.reshape(slope_ref.shape)
    back = dot(grad_hidden, win_ref[...], NT).astype(jnp.bfloat16)
    first = 0
    for ref in sent:
        wide = ref.shape[-1]
        ref[...] = back[:, first : first + wide].reshape(ref.shape)
        first += wide


def expert_pass(chunk, x, grad_y, w_in, w_back, kept, sent, parts, pieces, waits=()):
    e, low, size = chunk
    sources, members, cap, depth = grad_y.shape
    rows = sources * size
    width = w_in.shape[2]
    step = min(256, rows)
    group = step // size
    at = low // size
    given = [*kept, *sent]
    aliases = {4 + j: (1 if kept else 3) + j for j in range(len(given))}
    keep = jax.ShapeDtypeStruct((sources, cap, width), jnp.bfloat16)
    keep_spec = pl.BlockSpec((group, size, width), lambda i: (i, at, 0))
    piece = tuple(jax.ShapeDtypeStruct((sources, members, cap, w), jnp.bfloat16) for w in pieces)
    piece_spec = tuple(
        pl.BlockSpec((group, None, size, w), lambda i: (i, e % members, at, 0)) for w in pieces
    )
    made = pl.pallas_call(
        functools.partial(expert_body, len(given) + len(waits)),
        out_shape=(jax.ShapeDtypeStruct((parts, rows, depth // parts), jnp.bfloat16), keep, keep)
        + piece,
        grid=(rows // step,),
        in_specs=[
            pl.BlockSpec((step, depth), lambda i: (i, 0)),
            pl.BlockSpec((group, None, size, depth), lambda i: (i, e % members, at, 0)),
            pl.BlockSpec((None, depth, width), lambda i: (e, 0, 0)),
            pl.BlockSpec((None, width, depth), lambda i: (e, 0, 0)),
        ]
        + [pl.BlockSpec(memory_space=pl.ANY)] * (len(given) + len(waits)),
        out_specs=(
            pl.BlockSpec((parts, step, depth // parts), lambda i: (0, i, 0)),
            keep_spec,
            keep_spec,
        )
        + piece_spec,
        input_output_aliases=aliases,
        compiler_params=params("arbitrary"),
        name="expert_pass",
        cost_estimate=cost(
            8 * rows * depth * width, 4 * width * depth + 12 * rows * depth, rows * width
        ),
    )(x, grad_y, w_in, w_back, *given, *waits)
    return made[0], made[1:3], list(made[3:])


def weight_body(given, x_ref, gy_ref, router_ref, pick_ref, active_ref, slope_ref, *rest):
    gin_ref, gback_ref, token_ref, xt_ref, gyg_ref = rest[given:]
    token_ref[...] = jnp.zeros_like(token_ref)
    rows, depth = x_ref.shape

    @pl.when(pl.program_id(0) == 0)
    def _():
        logits = dot(x_ref[...], router_ref[...], NN)
        raised = jnp.exp(logits - jnp.max(logits, axis=1, keepdims=True))
        gate = jnp.sum(raised * pick_ref[...], axis=1, keepdims=True)
        gate = gate / jnp.sum(raised, axis=1, keepdims=True)
        xt_ref[...] = (x_ref[...].astype(jnp.float32) * gate).T.astype(jnp.bfloat16)
        grad_y = gy_ref[...].reshape(rows, depth).astype(jnp.float32)
        gyg_ref[...] = (grad_y * gate).astype(jnp.bfloat16)

    gin_ref[...] = dot(xt_ref[...], slope_ref[...], NN)
    gback_ref[...] = dot(active_ref[...], gyg_ref[...], TN)


def weight_pass(e, local, x, grad_y, router, pick, active, slope, sent, waits=()):
    rows, width = active.shape
    sources, members, cap, depth = grad_y.shape
    step = min(256, width)
    sent = list(sent or [])
    return pl.pallas_call(
        functools.partial(weight_body, len(sent) + len(waits)),
        out_shape=(
            jax.ShapeDtypeStruct((local, depth, width), jnp.float32),
            jax.ShapeDtypeStruct((local, width, depth), jnp.float32),
            jax.ShapeDtypeStruct((8, 128), jnp.float32),
        ),
        grid=(width // step,),
        in_specs=[
            pl.BlockSpec((rows, depth), lambda i: (0, 0)),
            pl.BlockSpec((sources, None, cap, depth), lambda i: (0, e % members, 0, 0)),
            pl.BlockSpec(router.shape, lambda i: (0, 0)),
            pl.BlockSpec(pick.shape, lambda i: (0, 0)),
            pl.BlockSpec((rows, step), lambda i: (0, i)),
            pl.BlockSpec((rows, step), lambda i: (0, i)),
        ]
        + [pl.BlockSpec(memory_space=pl.ANY)] * (len(sent) + len(waits)),
        out_specs=(
            pl.BlockSpec((None, depth, step), lambda i: (e, 0, i)),
            pl.BlockSpec((None, step, depth), lambda i: (e, i, 0)),
            pl.BlockSpec((8, 128), lambda i: (0, 0)),
        ),
        scratch_shapes=[
            pltpu.VMEM((depth, rows), jnp.bfloat16),
            pltpu.VMEM((rows, depth), jnp.bfloat16),
        ],
        input_output_aliases={6 + j: j for j in range(len(sent))},
        compiler_params=params("arbitrary"),
        name="weight_pass",
        cost_estimate=cost(4 * rows * depth * width, 8 * width * depth + 8 * rows * depth),
    )(x, grad_y, router, pick, active, slope, *sent, *waits)


def swap(blocks, axis):
    return lax.all_to_all(blocks, axis, split_axis=0, concat_axis=0, tiled=True)


def tie(*values):
    return lax.optimization_barrier(values)


def row_stats(values):
    mean = jnp.mean(values, axis=-1, keepdims=True)
    centered = values - mean
    variance = jnp.mean(centered * centered, axis=-1, keepdims=True)
    return (mean, lax.rsqrt(variance + EPSILON))


def slot_layout(expert_ids, experts, cap):
    chosen = expert_ids[:, 0]
    length = chosen.shape[0]
    table = chosen[:, None] == jnp.arange(experts, dtype=jnp.int32)[None, :]
    order = jnp.arange(length, dtype=jnp.int32)
    before = (order[:, None] > order[None, :]).astype(jnp.bfloat16)
    counted = jnp.dot(before, table.astype(jnp.bfloat16), preferred_element_type=jnp.float32)
    ranks = jnp.sum(jnp.where(table, counted, 0.0), axis=1).astype(jnp.int32)
    return (chosen, ranks, table.astype(jnp.float32))


def per_device(
    tokens, w_qkv, w_out, w_router, ln_gains, ln_biases, w_in, w_back, expert_ids, cotangent
):
    rows_all, cols_all = lax.axis_size("row"), lax.axis_size("col")
    col = lax.axis_index("col")
    length, depth = tokens.shape
    share = depth // rows_all
    width = w_qkv.shape[2]
    experts = w_router.shape[1]
    local = w_in.shape[0]
    cap = 2 * length // experts
    block_rows = rows_all * cap
    block = min(256, length // 2)
    part = length // cols_all
    members = max(1, local // 2)
    pieces = (depth * 5 // 8, depth * 3 // 8)

    def own(values, axis=0):
        return lax.dynamic_slice_in_dim(values, col * part, part, axis)

    def send(packed):
        return swap(packed.reshape(rows_all, cap, depth), "row").reshape(block_rows, depth)

    stacked = w_qkv.transpose(1, 0, 2).reshape(share, 3 * width)
    weights = jnp.concatenate([stacked, w_router, ln_gains.T, ln_biases.T], axis=1)
    weights = lax.all_gather(weights, "row", axis=0, tiled=True)
    mean_one, inverse_one = row_stats(tokens.astype(jnp.float32))

    chosen, ranks, select = slot_layout(expert_ids, experts, cap)
    out_block, ranks = tie(w_out.T, ranks)
    out_block = swap(jnp.broadcast_to(out_block[None], (cols_all, share, width)), "col")
    slots = chosen * cap + ranks
    slots_by_local = ((chosen % local) * rows_all + chosen // local) * cap + ranks
    member = chosen % local
    slots_by_group = [
        jnp.where(
            member // members == g,
            ((chosen // local) * members + member % members) * cap + ranks,
            -1,
        )
        for g in range(local // members)
    ]

    slots_by_pair = slots_by_local - slots_by_local
    for g, at in enumerate(slots_by_group):
        slots_by_pair = jnp.where(at >= 0, at + g * members * block_rows, slots_by_pair)

    def pack_group(g, waits):
        rows = members * block_rows
        return pack(slots_by_pair, [cotangent], g * rows, rows, 1, waits)[0]

    grad_packed = [pack_group(0, [])]
    weights, grad_packed[0], out_block, mean_one, inverse_one = tie(
        weights, grad_packed[0], out_block, mean_one, inverse_one
    )
    qkv_full = weights[:, : 3 * width]
    router_full = weights[:, 3 * width : 3 * width + experts]
    norms = weights[:, 3 * width + experts :].astype(jnp.float32).T
    gains, biases = norms[0:2], norms[2:4]

    resid_in = tokens.astype(jnp.float32)
    normed_one = (resid_in - mean_one) * inverse_one
    normal_in = (normed_one * gains[0] + biases[0]).astype(jnp.bfloat16)
    projected = jnp.dot(normal_in, qkv_full, preferred_element_type=jnp.float32).astype(jnp.bfloat16)

    context, logsum = attend_forward(projected, tuple(range(length // block)), block)
    context, grad_packed[0] = tie(context, grad_packed[0])
    full = lax.all_gather(context, "col", axis=0)
    grad_packed += [pack_group(g, [context]) for g in range(1, local // members)]
    out_full = lax.all_gather(out_block, "row", axis=1, tiled=True)
    grad_arrived = []
    for g in range(local // members):
        if g:
            grad_arrived[-1], grad_packed[g] = tie(grad_arrived[-1], grad_packed[g])
        grad_arrived.append(swap(grad_packed[g].reshape(rows_all, members, cap, depth), "row"))
    full, out_full = tie(full, out_full)
    middle, routed = middle_pass(full, out_full, tokens, gains[1:2], biases[1:2])

    short = cap // 2
    chunks = [(0, 0, short), (0, short, short)] + [(e, 0, cap) for e in range(1, local)]
    split = (ranks // short * rows_all + chosen // local) * short + ranks % short
    slots_by_chunk = jnp.where(chosen % local == 0, split, slots_by_local)

    def pack_chunk(k, waits):
        e, low, size = chunks[k]
        base = (e * cap + low) * rows_all
        return pack(slots_by_chunk, [routed], base, size * rows_all, 1, waits)[0]

    packed = [pack_chunk(k, []) for k in range(min(3, len(chunks)))]
    packed[0], grad_arrived[-1] = tie(packed[0], grad_arrived[-1])

    logits = jnp.dot(routed, router_full, preferred_element_type=jnp.float32)
    probs = jax.nn.softmax(logits, axis=-1)
    gate = jnp.sum(probs * select, axis=-1, keepdims=True)

    arrived, summed, kept, sent = [], [], [], []
    final = len(chunks) - 1
    for k, (e, low, size) in enumerate(chunks):
        moved = swap(packed[k].reshape(rows_all, size, depth), "row")
        arrived.append(moved.reshape(rows_all * size, depth))
        if k < final:
            packed[k + 1], arrived[k], *more = tie(
                packed[k + 1], arrived[k], *(packed[2:3] if k == 0 else [])
            )
            packed[2:3] = more or packed[2:3]
        if k:
            then = packed[k + 1] if k < final else sent[0][0]
            then, summed[k - 1], arrived[k] = tie(then, summed[k - 1], arrived[k])
            summed[k - 1] = lax.psum_scatter(
                summed[k - 1], "col", scatter_dimension=0, tiled=True
            )
            if k < final:
                packed[k + 1] = then
            else:
                sent[0][0] = then
        waits = summed[:1] if k == final else []
        made, both, pair = expert_pass(
            chunks[k],
            arrived[k],
            grad_arrived[e // members],
            w_in,
            w_back,
            kept.pop() if low else [],
            sent.pop() if low or e % members else [],
            cols_all,
            pieces,
            waits,
        )
        kept.append(both)
        summed.append(made)
        sent.append(pair)
        if 1 <= k and k + 2 <= final:
            packed.append(pack_chunk(k + 2, [made]))
    active = [v[0].reshape(block_rows, -1) for v in kept]
    slope = [v[1].reshape(block_rows, -1) for v in kept]

    def joined(values):
        first = [v.reshape(rows_all, short, -1) for v in values[:2]]
        whole = [v.reshape(rows_all, cap, -1) for v in values[2:]]
        return [jnp.concatenate(first, axis=1)] + whole

    arrived = [v.reshape(block_rows, depth) for v in joined(arrived)]

    step = min(256, length)
    order = [(g, f) for f in range(len(pieces)) for g in range(len(sent))]
    grad_sent = []
    grad_weights = None
    token = None
    row = lax.axis_index("row")

    def weigh(e, waits):
        pick = jnp.arange(experts, dtype=jnp.int32)[None, :] == row * local + e
        return weight_pass(
            e,
            local,
            arrived[e],
            grad_arrived[e // members],
            router_full,
            pick.astype(jnp.float32),
            active[e],
            slope[e],
            grad_weights,
            waits,
        )

    early = max(1, local // 2)
    late = max(early, local - 1)
    waits = slope[-1:]
    last = None
    for f, wide in enumerate(pieces):
        for e in range(early) if f == 0 else range(early, late):
            *grad_weights, token = weigh(e, waits)
            waits = [token]
        rows = []
        for g in range(len(sent)):
            piece = sent[g][f]
            if last is not None:
                piece, last = tie(piece, last)
                if rows:
                    rows[-1] = last
                else:
                    ended[-1] = last
            if f == 0 and g == len(sent) - 1:
                piece, slope[-1] = tie(piece, slope[-1])
            if f and g == len(sent) - 1:
                piece, whole = tie(piece, whole)
            last = swap(piece, "row")
            if f == 0 and g == 0:
                last, made = tie(last, summed[-1])
                summed[-1] = lax.psum_scatter(made, "col", scatter_dimension=0, tiled=True)
            rows.append(last)
        if f == 0:
            ended = rows
            sent[0][1], token = tie(sent[0][1], token)
            waits = [token]
        else:
            homed = jnp.stack(joined(summed), axis=1)
            homed, token = tie(homed, token)
            waits = [token]
            grad_sent.append(lax.psum_scatter(whole, "col", scatter_dimension=0, tiled=True))
        whole = unpack(slots_by_group, [v.reshape(-1, wide) for v in rows], step, waits)
        if f:
            rows[-1], homed = tie(rows[-1], homed)
            homed = swap(homed, "row")
            whole, homed = tie(whole, homed)
        waits = [whole]
    grad_sent.append(lax.psum_scatter(whole, "col", scatter_dimension=0, tiled=True))

    returned = unpack(
        [slots], [homed.reshape(experts * cap, depth // cols_all)], step, grad_sent[:1]
    ).astype(jnp.float32)
    columns = depth // cols_all

    def own_columns(values):
        return lax.dynamic_slice_in_dim(values, col * columns, columns, 1)

    mixed = (own_columns(middle) + gate * returned).astype(jnp.bfloat16)
    grad_gate = jnp.sum(own_columns(cotangent).astype(jnp.float32) * returned, axis=-1)
    grad_gate = swap(grad_gate.reshape(cols_all, part), "col")
    grad_gate = jnp.sum(grad_gate, axis=0)[:, None]
    mixed_full = lax.all_gather(mixed, "col", axis=0)

    own_gate, own_probs, own_select = own(gate), own(probs), own(select)
    grad_logits = (grad_gate * own_probs * (own_select - own_gate)).astype(jnp.bfloat16)
    own_routed = own(routed)
    grad_router = jnp.einsum(
        "td,te->de", own_routed, grad_logits, preferred_element_type=jnp.float32
    )
    place = jnp.reshape(col, (1,)).astype(jnp.int32)
    grad_middle, grad_attn, grad_context, sums_two = settle_pass(
        place,
        *grad_sent,
        own_gate,
        grad_logits,
        router_full,
        cotangent,
        middle,
        gains[1:2],
        out_full,
    )
    grad_context = swap(grad_context, "col")
    context_own = own(full, 1)
    grad_out = jnp.einsum("td,ztc->dzc", grad_attn, context_own, preferred_element_type=jnp.float32)
    plane = jnp.concatenate([grad_out.reshape(depth, cols_all * width), grad_router], axis=1)
    plane = swap(plane.astype(jnp.bfloat16).reshape(rows_all, share, -1), "row")
    grad_context = grad_context.reshape(length, width)
    waits = [grad_attn]
    for e in range(late, local):
        *grad_weights, token = weigh(e, waits)
        waits = [token]
    grad_in, grad_back = grad_weights
    grad_proj, shares = attend_backward(
        projected, grad_context, context, logsum, qkv_full, block, waits
    )
    shares, plane = tie(shares, plane)

    shares, mixed_full = tie(shares, mixed_full)
    grad_normal = lax.psum_scatter(shares, "col", scatter_dimension=0, tiled=True)
    mixed_out = mixed_full.transpose(1, 0, 2).reshape(length, depth)
    grad_qkv = jnp.einsum("td,tc->dc", normal_in, grad_proj, preferred_element_type=jnp.float32)
    plane = jnp.sum(plane.astype(jnp.float32), axis=0)
    router_share = plane[:, cols_all * width :].reshape(1, share, experts)
    out_share = plane[:, : cols_all * width].reshape(share, cols_all, width).transpose(1, 0, 2)
    router_share = jnp.broadcast_to(router_share, (cols_all, share, experts))
    plane = jnp.concatenate([out_share, router_share], axis=2).astype(jnp.bfloat16)
    plane = jnp.sum(swap(plane, "col").astype(jnp.float32), axis=0)
    out_share, router_share = plane[:, :width].T, plane[:, width:]
    grad_normal, out_share, mixed_out, grad_qkv = tie(
        grad_normal, out_share, mixed_out, grad_qkv
    )

    grad_tokens, sums_one = close_pass(place, grad_normal, tokens, grad_middle, gains[0:1])
    grad_tokens = move(lax.all_gather(grad_tokens, "col", axis=0, tiled=True))
    small = jnp.concatenate([sums_one[0:2], sums_two[0:2]], axis=0)
    small = swap(small.reshape(4, rows_all, share).transpose(1, 0, 2), "row")
    small = jnp.sum(small, axis=0)
    small = jnp.sum(swap(jnp.broadcast_to(small[None], (cols_all, 4, share)), "col"), axis=0)
    qkv_share = swap(grad_qkv.astype(jnp.bfloat16).reshape(rows_all, share, -1), "row")
    qkv_share = jnp.sum(qkv_share.astype(jnp.float32), axis=0)
    qkv_share = qkv_share.reshape(share, 3, width).transpose(1, 0, 2)
    return (
        mixed_out,
        grad_tokens,
        qkv_share,
        out_share,
        router_share,
        jnp.stack([small[0], small[2]]),
        small[1],
        small[3],
        grad_in,
        grad_back,
    )


def solution(mesh):
    return jax.shard_map(
        per_device,
        mesh=mesh,
        in_specs=(
            P("row", None),
            P(None, "row", "col"),
            P("col", "row"),
            P("row", None),
            P(None, "row"),
            P(None, "row"),
            P("row", None, "col"),
            P("row", "col", None),
            P("row", None),
            P("row", None),
        ),
        out_specs=(
            P("row", None),
            P("row", None),
            P(None, "row", "col"),
            P("col", "row"),
            P("row", None),
            P(None, "row"),
            P("row"),
            P("row"),
            P("row", None, "col"),
            P("row", "col", None),
        ),
        check_vma=False,
    )
```
